32 devices in a mesh: img: 4 (over y, x), tile: 8 (over z, core).
Axes of the slice: x: 2, y: 2, z: 4, core: 2. Of those that a mesh axis runs over, the one named last changes fastest.
Arguments:
- images: bfloat16 [8, 2, 256, 1024], P('img', None, 'tile'), may hold values from -6 to 6
- nucleus: int32 [8], P('img'), may hold values 0 or 1
- target_flow: int32 [8, 2, 256, 1024], P('img', None, 'tile'), may hold values from -4 to 4
- cell_label: int32 [8, 256, 1024], P('img', 'tile'), may hold values 0 or 1
- step_count: int32 [1], replicated, may hold values from 1 to 20
- conv1_weight: float32 [3, 3, 2, 32], replicated, may hold values from -1.5 to 1.5
- conv1_momentum: float32 [3, 3, 2, 32], replicated, may hold values from -6 to 6
- conv1_average: float32 [3, 3, 2, 32], replicated, may hold values from -1.5 to 1.5
- conv2_weight: float32 [3, 3, 32, 64], replicated, may hold values from -0.375 to 0.375
- conv2_momentum: float32 [3, 3, 32, 64], replicated, may hold values from -6 to 6
- conv2_average: float32 [3, 3, 32, 64], replicated, may hold values from -0.375 to 0.375
- conv3_weight: float32 [3, 3, 64, 32], replicated, may hold values from -0.25 to 0.25
- conv3_momentum: float32 [3, 3, 64, 32], replicated, may hold values from -6 to 6
- conv3_average: float32 [3, 3, 64, 32], replicated, may hold values from -0.25 to 0.25
- style_weight: float32 [64, 32], replicated, may hold values from -0.75 to 0.75
- style_momentum: float32 [64, 32], replicated, may hold values from -6 to 6
- style_average: float32 [64, 32], replicated, may hold values from -0.75 to 0.75
- head_weight: float32 [32, 3], replicated, may hold values from -1 to 1
- head_momentum: float32 [32, 3], replicated, may hold values from -6 to 6
- head_average: float32 [32, 3], replicated, may hold values from -1 to 1
- biases: float32 [163], replicated, may hold values from -1.8 to 1.8
- bias_momentum: float32 [163], replicated, may hold values from -6 to 6
- bias_average: float32 [163], replicated, may hold values from -1.8 to 1.8
Outputs:
- loss: float32 [1], replicated
- conv1_weight_out: float32 [3, 3, 2, 32], replicated
- conv1_momentum_out: float32 [3, 3, 2, 32], replicated
- conv1_average_out: float32 [3, 3, 2, 32], replicated
- conv2_weight_out: float32 [3, 3, 32, 64], replicated
- conv2_momentum_out: float32 [3, 3, 32, 64], replicated
- conv2_average_out: float32 [3, 3, 32, 64], replicated
- conv3_weight_out: float32 [3, 3, 64, 32], replicated
- conv3_momentum_out: float32 [3, 3, 64, 32], replicated
- conv3_average_out: float32 [3, 3, 64, 32], replicated
- style_weight_out: float32 [64, 32], replicated
- style_momentum_out: float32 [64, 32], replicated
- style_average_out: float32 [64, 32], replicated
- head_weight_out: float32 [32, 3], replicated
- head_momentum_out: float32 [32, 3], replicated
- head_average_out: float32 [32, 3], replicated
- biases_out: float32 [163], replicated
- bias_momentum_out: float32 [163], replicated
- bias_average_out: float32 [163], replicated
The draws below stay inside these ranges and needn't reach their ends.
All inputs are finite; a program needn't handle non-finite values. No bound on the sum of `nucleus` or of `cell_label` on one device may be relied on, other than what follows from the above.
Results may differ from the reference program's by a relative error of at most 0.00075.
The reference program's roundings to bfloat16 on the way count: a program that leaves them out, or rounds other values in their place, can miss the bound.
Values may be sent and summed in bfloat16 or wider, within the bound.
A program may use at most 384 MiB of HBM per device.

```python
import math
import jax
import jax.numpy as jnp
from jax import lax

IN_CH = 2
CH_ONE = 32
CH_TWO = 64
OUT_CH = 3
CROPS_DEV = 2
COLS = 1024
CROPS = 8
HEIGHT = 256
NPIX = 2097152
BIAS_LEN = 163


def place_ends(drawn, key, least, top_value):
    longest = drawn.shape.index(max(drawn.shape))
    spots = []
    for shift in (0, 1):
        where = [jax.random.randint(jax.random.fold_in(key, axis), (), 0, length) for axis, length in enumerate(drawn.shape)]
        where[longest] = (where[longest] + shift) % drawn.shape[longest]
        spots.append(tuple(where))
    return drawn.at[spots[0]].set(least).at[spots[1]].set(top_value)


def levels(own_key, dims, cuts, smallest, high):
    level, own = 1.0, jax.random.fold_in(own_key, 6)
    for axis_at, blocks in cuts:
        draws = jnp.exp(jax.random.uniform(jax.random.fold_in(own, axis_at), (blocks,), jnp.float32, smallest / len(cuts), high / len(cuts)))
        level = level * jnp.repeat(draws, dims[axis_at] // blocks).reshape([-1 if axis == axis_at else 1 for axis in range(len(dims))])
    return level


def noise(stream_key, extent, scale, limit, cuts=(), dtype=jnp.bfloat16):
    entries = jax.random.normal(stream_key, extent, jnp.float32) * scale
    if len(cuts) > 0:
        entries = levels(stream_key, extent, cuts, -0.22, 0.18) * entries
    return jnp.clip(entries, min=-limit, max=limit).astype(dtype)


def setup_inputs(seed: int = 0) -> dict:
    keys = jax.random.split(jax.random.key(seed), 24)
    return {
        "images": noise(keys[0], (CROPS, IN_CH, HEIGHT, COLS), 1.0, 6.0, ((0, 4), (2, 8))),
        "nucleus": place_ends((jax.random.randint(keys[1], (CROPS,), 0, 2) < 1).astype(jnp.int32), jax.random.fold_in(keys[1], 1), 0, 1),
        "target_flow": place_ends(jax.random.randint(keys[2], (CROPS, 2, HEIGHT, COLS), -4, 5), jax.random.fold_in(keys[2], 1), -4, 4).astype(jnp.int32),
        "cell_label": place_ends((jax.random.randint(keys[3], (CROPS, HEIGHT, COLS), 0, 2) < 1).astype(jnp.int32), jax.random.fold_in(keys[3], 1), 0, 1),
        "step_count": jax.random.randint(keys[4], (1,), 1, 21).astype(jnp.int32),
        "conv1_weight": noise(keys[5], (3, 3, IN_CH, CH_ONE), (9 * IN_CH) ** -0.5, 1.5, (), jnp.float32),
        "conv1_momentum": noise(keys[6], (3, 3, IN_CH, CH_ONE), 1.0, 6.0, (), jnp.float32),
        "conv1_average": noise(keys[7], (3, 3, IN_CH, CH_ONE), (9 * IN_CH) ** -0.5, 1.5, (), jnp.float32),
        "conv2_weight": noise(keys[8], (3, 3, CH_ONE, CH_TWO), (9 * CH_ONE) ** -0.5, 0.375, (), jnp.float32),
        "conv2_momentum": noise(keys[9], (3, 3, CH_ONE, CH_TWO), 1.0, 6.0, (), jnp.float32),
        "conv2_average": noise(keys[10], (3, 3, CH_ONE, CH_TWO), (9 * CH_ONE) ** -0.5, 0.375, (), jnp.float32),
        "conv3_weight": noise(keys[11], (3, 3, CH_TWO, CH_ONE), (9 * CH_TWO) ** -0.5, 0.25, (), jnp.float32),
        "conv3_momentum": noise(keys[12], (3, 3, CH_TWO, CH_ONE), 1.0, 6.0, (), jnp.float32),
        "conv3_average": noise(keys[13], (3, 3, CH_TWO, CH_ONE), (9 * CH_TWO) ** -0.5, 0.25, (), jnp.float32),
        "style_weight": noise(keys[14], (CH_TWO, CH_ONE), CH_TWO ** -0.5, 0.75, (), jnp.float32),
        "style_momentum": noise(keys[15], (CH_TWO, CH_ONE), 1.0, 6.0, (), jnp.float32),
        "style_average": noise(keys[16], (CH_TWO, CH_ONE), CH_TWO ** -0.5, 0.75, (), jnp.float32),
        "head_weight": noise(keys[17], (CH_ONE, OUT_CH), CH_ONE ** -0.5, 1.0, (), jnp.float32),
        "head_momentum": noise(keys[18], (CH_ONE, OUT_CH), 1.0, 6.0, (), jnp.float32),
        "head_average": noise(keys[19], (CH_ONE, OUT_CH), CH_ONE ** -0.5, 1.0, (), jnp.float32),
        "biases": noise(keys[20], (BIAS_LEN,), 0.3, 1.8, (), jnp.float32),
        "bias_momentum": noise(keys[21], (BIAS_LEN,), 1.0, 6.0, (), jnp.float32),
        "bias_average": noise(keys[22], (BIAS_LEN,), 0.3, 1.8, (), jnp.float32),
    }


@jax.custom_vjp
def low(v):
    return lax.optimization_barrier(v.astype(jnp.bfloat16)).astype(jnp.float32)

@jax.custom_vjp
def low_back(v):
    return v

def low_keep(v):
    return (low(v), None)

def low_pass(kept, grad):
    return (grad,)

def back_keep(v):
    return (v, None)

def back_low(kept, grad):
    return (low(grad),)
low.defvjp(low_keep, low_pass)
low_back.defvjp(back_keep, back_low)
momentum_rate = 0.9
learn_rate = 0.02
decay_rate = 0.0001
norm_eps = 1e-05
highest = lax.Precision.HIGHEST

def convolve(values, kernel):
    return lax.conv_general_dilated(values, kernel, (1, 1), 'SAME', dimension_numbers=('NCHW', 'HWIO', 'NCHW'), precision=highest)

def pool_mean(values):
    in_shape = values.shape
    return lax.optimization_barrier(jnp.mean(values.reshape(in_shape[0], in_shape[1], in_shape[2] // 2, 2, in_shape[3] // 2, 2), axis=(3, 5)))

def upsample(values):
    return jnp.repeat(jnp.repeat(values, 2, axis=2), 2, axis=3)

def row_diff(values):
    padded = jnp.pad(values, ((0, 0), (1, 1), (0, 0)))
    return 0.5 * (padded[:, 2:] - padded[:, :-2])

def col_diff(values):
    padded = jnp.pad(values, ((0, 0), (0, 0), (1, 1)))
    return 0.5 * (padded[:, :, 2:] - padded[:, :, :-2])

def forward(weights, pixels, gate_block, target_block, label_block):
    kernel_one, kernel_two, kernel_three, style_kernel, head_kernel, bias_all = weights
    bias_one = bias_all[0:CH_ONE][None, :, None, None]
    bias_two = bias_all[CH_ONE:CH_ONE + CH_TWO][None, :, None, None]
    bias_three = bias_all[CH_ONE + CH_TWO:2 * CH_ONE + CH_TWO][None, :, None, None]
    bias_style = bias_all[2 * CH_ONE + CH_TWO:3 * CH_ONE + CH_TWO]
    bias_head = bias_all[3 * CH_ONE + CH_TWO:BIAS_LEN][None, :, None, None]
    inputs = jnp.stack([pixels[:, 0], pixels[:, 1] * gate_block[:, None, None]], axis=1)
    hidden_one = low_back(low(jax.nn.relu(convolve(inputs, low(kernel_one)) + bias_one)))
    pooled = low_back(low(pool_mean(hidden_one)))
    hidden_two = low_back(low(jax.nn.relu(convolve(pooled, low(kernel_two)) + bias_two)))
    style_raw = lax.optimization_barrier(jnp.mean(hidden_two, axis=(2, 3)))
    style_unit = style_raw * lax.rsqrt(lax.optimization_barrier(jnp.mean(style_raw * style_raw, axis=1, keepdims=True)) + norm_eps)
    style_vec = jnp.dot(style_unit, style_kernel, precision=highest) + bias_style
    pre_three = convolve(upsample(hidden_two), low(kernel_three)) + bias_three + style_vec[:, :, None, None]
    hidden_three = low_back(low(jax.nn.relu(pre_three) + hidden_one))
    output = low_back(jnp.einsum('cirw,io->corw', hidden_three, low(head_kernel), precision=highest) + bias_head)
    flow_error = output[:, 0:2] - target_block
    spread = row_diff(flow_error[:, 0]) + col_diff(flow_error[:, 1])
    logits = output[:, 2]
    return jnp.sum(flow_error * flow_error) + jnp.sum(spread * spread) + jnp.sum(jax.nn.softplus(logits) - label_block * logits)

def nesterov(weight, gradient, momentum, average, count):
    decayed = gradient + decay_rate * weight
    momentum_new = momentum_rate * momentum + decayed
    weight_new = weight - learn_rate * (decayed + momentum_rate * momentum_new)
    average_new = average + (weight_new - average) / (count + 1.0)
    return (weight_new, momentum_new, average_new)

def reference(images, nucleus, target_flow, cell_label, step_count, conv1_weight, conv1_momentum, conv1_average, conv2_weight, conv2_momentum, conv2_average, conv3_weight, conv3_momentum, conv3_average, style_weight, style_momentum, style_average, head_weight, head_momentum, head_average, biases, bias_momentum, bias_average):
    params = (conv1_weight, conv2_weight, conv3_weight, style_weight, head_weight, biases)
    block_count = CROPS // CROPS_DEV

    def by_block(array_in):
        return array_in.reshape((block_count, CROPS_DEV) + array_in.shape[1:])
    batches = (by_block(images.astype(jnp.float32)), by_block(nucleus.astype(jnp.float32)), by_block(0.25 * target_flow.astype(jnp.float32)), by_block(cell_label.astype(jnp.float32)))
    grad_scale = 1.0 / math.sqrt(NPIX)

    def accumulate(carry, block):
        loss_total, gradients = carry
        block_value, pullback = jax.vjp(lambda weights_in: forward(weights_in, *block), params)
        block_grads, = pullback(jnp.ones_like(block_value) * grad_scale)
        return ((loss_total + block_value, jax.tree.map(jnp.add, gradients, block_grads)), None)
    start = (jnp.zeros((), jnp.float32), jax.tree.map(jnp.zeros_like, params))
    (loss_total, gradients), unused = lax.scan(accumulate, start, batches)
    count = step_count[0].astype(jnp.float32)
    olds = ((conv1_weight, conv1_momentum, conv1_average), (conv2_weight, conv2_momentum, conv2_average), (conv3_weight, conv3_momentum, conv3_average), (style_weight, style_momentum, style_average), (head_weight, head_momentum, head_average), (biases, bias_momentum, bias_average))
    results = [(loss_total / NPIX).reshape(1)]
    for state, gradient in zip(olds, gradients):
        results.extend(nesterov(state[0], gradient, state[1], state[2], count))
    return tuple(results)
```

```python
import math

import numpy as np
import jax
import jax.numpy as jnp
from jax import lax
from jax.experimental import pallas as pl
from jax.experimental.pallas import tpu as pltpu
from jax.sharding import PartitionSpec as P

CH_ONE = 32
CH_TWO = 64
OUT_CH = 3

momentum_rate = 0.9
learn_rate = 0.02
decay_rate = 0.0001
norm_eps = 1e-05
highest = lax.Precision.HIGHEST
f32 = jnp.float32
bf16 = jnp.bfloat16

IN_HALO = 7
LABEL_HALO = 2
VMEM = pl.BlockSpec(memory_space=pltpu.VMEM)
SMEM = pl.BlockSpec(memory_space=pltpu.SMEM)


def tap_select(kind):
    table = np.zeros(kind[0], np.float32)
    for spot in kind[1]:
        table[spot] = 1.0
    return table


SEL_ONE = tap_select(((2, 4, 3), [(p, p + a, a) for p in range(2) for a in range(3)]))
SEL_UP = tap_select(((2, 3, 3), [(p, (p + a + 1) // 2, a) for p in range(2) for a in range(3)]))
SEL_DOWN = tap_select(((4, 3), [(x - a + 2, a) for x in range(2) for a in range(3)]))


def dot(a, b):
    return jnp.dot(a, b, preferred_element_type=f32)


def dot_nt(a, b):
    return lax.dot_general(a, b, (((1,), (1,)), ((), ())), preferred_element_type=f32)


def from_left(x):
    lane = lax.broadcasted_iota(jnp.int32, x.shape, 1)
    return jnp.where(lane == 0, 0.0, pltpu.roll(x, 1, 1))


def from_right(x):
    width = x.shape[1]
    lane = lax.broadcasted_iota(jnp.int32, x.shape, 1)
    return jnp.where(lane == width - 1, 0.0, pltpu.roll(x, width - 1, 1))


def fold_lanes(x):
    total = x[:, 0:128]
    for k in range(1, x.shape[1] // 128):
        total = total + x[:, 128 * k : 128 * (k + 1)]
    return total


def wide(tile, width):
    return jnp.concatenate([tile] * (width // 128), axis=1)


def rows_of(ref, crop, start, size, align=16):
    return ref[crop, pl.ds(pl.multiple_of(start, align), size), :]


def put_lanes(ref, crop, start, size, value):
    for k in range(value.shape[1] // 128):
        ref[crop, k, pl.ds(pl.multiple_of(start, 8), size), :] = value[:, 128 * k : 128 * (k + 1)]


def get_lanes(ref, crop, start, size, stride=None):
    parts = []
    for k in range(ref.shape[1]):
        spot = pl.ds(start, size, stride=stride) if stride else pl.ds(pl.multiple_of(start, 8), size)
        parts.append(ref[crop, k, spot, :])
    return jnp.concatenate(parts, axis=1)


def valid(row, edge_ref):
    return jnp.where((row >= edge_ref[0]) & (row < edge_ref[1]), 1.0, 0.0).astype(f32)


def split_columns(x, select):
    even, odd = [], []
    for k in range(x.shape[1] // 256):
        piece = dot(x[:, 256 * k : 256 * (k + 1)], select)
        even.append(piece[:, 0:128])
        odd.append(piece[:, 128:256])
    return jnp.concatenate(even, axis=1), jnp.concatenate(odd, axis=1)


def first_kernel(
    edge_ref, nucleus_ref, x_ref, t_ref, w1_ref, b1_ref, w2_ref, b2_ref,
    y_ref, t_out, h1_ref, pool_ref, h2_ref, style_ref, x2_ref,
):
    crops = x_ref.shape[0]
    width = x_ref.shape[2] // 2
    rows = h2_ref.shape[1] // CH_TWO - 4
    top = IN_HALO // 2
    r_id = lax.broadcasted_iota(jnp.int32, (256, 256), 0)
    c_id = lax.broadcasted_iota(jnp.int32, (256, 256), 1)
    select = jnp.where(r_id == 2 * (c_id % 128) + c_id // 128, 1.0, 0.0).astype(bf16)
    x_rows = x_ref.shape[1]
    per_ch = x_rows // 2
    y_rows = y_ref.shape[1]
    ri = lax.broadcasted_iota(jnp.int32, (y_rows, 4 * x_rows), 0)
    ci = lax.broadcasted_iota(jnp.int32, (y_rows, 4 * x_rows), 1)
    source = (ri % 4) * x_rows + ((ri // 4) % 2) * per_ch + 2 * (ri // 16) + (ri // 8) % 2
    perm_x = jnp.where(ci == source, 1.0, 0.0).astype(bf16)
    t_rows = t_ref.shape[1]
    per_t = t_rows // 3
    ri = lax.broadcasted_iota(jnp.int32, (t_out.shape[2], 2 * t_rows), 0)
    ci = lax.broadcasted_iota(jnp.int32, (t_out.shape[2], 2 * t_rows), 1)
    part = (ri // 4) % 4
    source = (ri % 2) * t_rows + part * per_t + 2 * (ri // 16) + (ri // 2) % 2
    perm_t = jnp.where((ci == source) & (part < 3), 1.0, 0.0).astype(bf16)
    for c in range(crops):
        even, odd = split_columns(x_ref[c], select)
        row = lax.broadcasted_iota(jnp.int32, (x_rows, width), 0)
        gate = jnp.where(row >= per_ch, nucleus_ref[c].astype(f32), 1.0)
        even, odd = even * gate, odd * gate
        stack = jnp.concatenate([from_left(odd), even, odd, from_right(even)], axis=0)
        y_ref[c] = dot(perm_x, stack.astype(bf16)).astype(bf16)
        even, odd = split_columns(t_ref[c], select)
        put_lanes(t_out, c, 0, t_out.shape[2], dot(perm_t, jnp.concatenate([even, odd], axis=0).astype(bf16)))
    style_ref[...] = jnp.zeros_like(style_ref)
    bias1 = jnp.broadcast_to(b1_ref[...], (4 * CH_ONE, 128))
    bias2 = jnp.broadcast_to(b2_ref[...], (CH_TWO, 128))

    def conv_one(k):
        row = k - top
        keep = valid(row, edge_ref)
        spot = jnp.clip(row + 1, 0, rows + 2)
        pre = [dot(w1_ref[...], rows_of(y_ref, c, k * 16, 32)) for c in range(crops)]
        for c in range(crops):
            hidden = (jnp.maximum(pre[c] + wide(bias1, width), 0.0) * keep).astype(bf16)
            h1_ref[c, pl.ds(pl.multiple_of(spot * 128, 128), 128), :] = hidden
            h = hidden.astype(f32)
            pooled = (0.25 * ((h[0:32] + h[32:64]) + (h[64:96] + h[96:128]))).astype(bf16)
            pool_ref[c, pl.ds(pl.multiple_of(spot * 32, 32), 32), :] = pooled
            p = pooled.astype(f32)
            both = jnp.concatenate([from_left(p).astype(bf16), pooled, from_right(p).astype(bf16)], axis=0)
            x2_ref[c, pl.ds(pl.multiple_of(k * 96, 96), 96), :] = both

    def conv_two(q):
        row = q - 2
        keep = valid(row, edge_ref)
        own = jnp.where((row >= 0) & (row < rows), 1.0, 0.0).astype(f32)
        pre = [dot(w2_ref[...], rows_of(x2_ref, c, q * 96, 288)) for c in range(crops)]
        for c in range(crops):
            hidden = (jnp.maximum(pre[c] + wide(bias2, width), 0.0) * keep).astype(bf16)
            h2_ref[c, pl.ds(pl.multiple_of(q * 64, 64), 64), :] = hidden
            style_ref[c] += fold_lanes(hidden.astype(f32)) * own

    def loop_one(k, carry):
        conv_one(k)
        return carry

    def loop_both(k, carry):
        conv_two(k - 3)
        conv_one(k)
        return carry

    lax.fori_loop(0, 3, loop_one, 0)
    lax.fori_loop(3, rows + 6, loop_both, 0)
    conv_two(rows + 3)


def second_kernel(
    scale, edge_ref, h1_ref, h2_ref, t_ref, bs_ref, w3_ref, wh_ref, wht_ref, wd3_ref, bh_ref,
    gc_ref, go_out, d3_ref, head_ref, small_ref, sg_ref, loss_ref,
    x3_ref, h3_ref, m_ref, fe_ref, go_ref, g3_ref,
):
    crops = h1_ref.shape[0]
    width = h1_ref.shape[2]
    rows = go_out.shape[1] // 16

    def shift(k, carry):
        for c in range(crops):
            mid = rows_of(h2_ref, c, k * 64, 64)
            x = mid.astype(f32)
            x3_ref[c, pl.ds(pl.multiple_of(k * 192, 192), 192), :] = jnp.concatenate(
                [from_left(x).astype(bf16), mid, from_right(x).astype(bf16)], axis=0
            )
        return carry

    lax.fori_loop(0, rows + 4, shift, 0)
    bias3 = [jnp.broadcast_to(bs_ref[c], (4 * CH_ONE, 128)) for c in range(crops)]
    bias_h = jnp.broadcast_to(bh_ref[...], (16, 128))

    def forward(k, carry):
        row = k - 1
        keep = valid(row, edge_ref)
        pre = [dot(w3_ref[...], rows_of(x3_ref, c, k * 192, 576)) for c in range(crops)]
        hs = []
        for c in range(crops):
            p = pre[c][0:128] + pre[c][128:256] + wide(bias3[c], width)
            h1 = rows_of(h1_ref, c, k * 128, 128).astype(f32)
            h3 = (jnp.maximum(p, 0.0) + h1).astype(bf16)
            h3_ref[c, pl.ds(pl.multiple_of(k * 128, 128), 128), :] = h3
            m_ref[c, pl.ds(pl.multiple_of(k * 128, 128), 128), :] = jnp.where(p > 0, 1.0, 0.0).astype(bf16)
            hs.append(h3)
        outs = [dot(wh_ref[...], h) for h in hs]
        for c in range(crops):
            o = outs[c] + wide(bias_h, width)
            t = get_lanes(t_ref, c, k * 16, 16)
            fe = (o[0:8] - 0.25 * t[0:8]) * keep
            put_lanes(fe_ref, c, k * 16, 16, jnp.concatenate([fe, o[8:16]], axis=0))
        return carry

    lax.fori_loop(0, rows + 2, forward, 0)

    r_id = lax.broadcasted_iota(jnp.int32, (rows, width), 0)
    above = jnp.where(r_id - 1 >= edge_ref[0], 1.0, 0.0)
    below = jnp.where(r_id + 1 < edge_ref[1], 1.0, 0.0)
    loss = jnp.zeros((rows, 128), f32)
    go_ref[...] = jnp.zeros_like(go_ref)
    for c in range(crops):

        def at(part, off):
            return get_lanes(fe_ref, c, 16 * (1 + off) + part, rows, 16)

        def column_part(pr, off):
            odd, even = at(4 + 2 * pr + 1, off), at(4 + 2 * pr, off)
            return 0.5 * (odd - from_left(odd)), 0.5 * (from_right(even) - even)

        e0 = [at(k, 0) for k in range(4)]
        e1 = [at(4 + k, 0) for k in range(4)]
        cols0, cols1 = column_part(0, 0), column_part(1, 0)
        cols_up, cols_dn = column_part(1, -1), column_part(0, 1)
        spread = [None] * 4
        g_up, g_dn = [None] * 2, [None] * 2
        for pc in range(2):
            f_up, f_dn = at(2 + pc, -1), at(pc, 1)
            spread[pc] = 0.5 * (e0[2 + pc] - f_up) + cols0[pc]
            spread[2 + pc] = 0.5 * (f_dn - e0[pc]) + cols1[pc]
            g_up[pc] = 2.0 * scale * above * (0.5 * (e0[pc] - at(pc, -1)) + cols_up[pc])
            g_dn[pc] = 2.0 * scale * below * (0.5 * (at(2 + pc, 1) - e0[2 + pc]) + cols_dn[pc])
        g = [2.0 * scale * v for v in spread]
        for pr in range(2):
            even, odd = g[2 * pr], g[2 * pr + 1]
            col = [0.5 * (odd - from_left(odd)), 0.5 * (from_right(even) - even)]
            for pc in range(2):
                k = 2 * pr + pc
                if pr == 0:
                    row_part = 0.5 * (g[2 + pc] - g_up[pc])
                else:
                    row_part = 0.5 * (g_dn[pc] - g[pc])
                logit = at(8 + k, 0)
                label = get_lanes(t_ref, c, 16 + 8 + k, rows, 16)
                ex = jnp.exp(-jnp.abs(logit))
                sig = jnp.where(logit >= 0, 1.0, ex) / (1.0 + ex)
                grads = (2.0 * scale * e0[k] - row_part, 2.0 * scale * e1[k] - col[pc], scale * (sig - label))
                for part in range(OUT_CH):
                    for j in range(width // 128):
                        go_ref[c, j, pl.ds(4 * part + k, rows, stride=16), :] = grads[part][:, 128 * j : 128 * (j + 1)]
                term = jnp.maximum(logit, 0.0) + jnp.log1p(ex) - label * logit
                loss = loss + fold_lanes(e0[k] * e0[k] + e1[k] * e1[k] + spread[k] * spread[k] + term)
    loss_ref[...] = loss

    head_ref[...] = jnp.zeros_like(head_ref)
    small_ref[...] = jnp.zeros_like(small_ref)
    sg_ref[...] = jnp.zeros_like(sg_ref)
    d3_ref[...] = jnp.zeros_like(d3_ref)
    edge = jnp.zeros((256, width), bf16)
    for c in range(crops):
        for k in (0, 1, rows + 2, rows + 3):
            g3_ref[c, 256 * k : 256 * (k + 1), :] = edge

    def backward(r, carry):
        gos, gts = [], []
        for c in range(crops):
            go = get_lanes(go_ref, c, r * 16, 16).astype(bf16)
            go_out[c, pl.ds(pl.multiple_of(r * 16, 16), 16), :] = go
            gos.append(go)
            gts.append(dot(wht_ref[...], go))
        for c in range(crops):
            spot = (r + 1) * 128
            head_ref[...] += dot_nt(gos[c], rows_of(h3_ref, c, spot, 128))
            small_ref[...] += fold_lanes(gos[c].astype(f32))
            g = gts[c].astype(bf16).astype(f32) * rows_of(m_ref, c, spot, 128).astype(f32)
            sg_ref[c] += fold_lanes(g)
            parts = []
            gb = g.astype(bf16)
            for pr in range(2):
                even, odd = g[64 * pr : 64 * pr + 32], g[64 * pr + 32 : 64 * pr + 64]
                parts += [from_left(odd).astype(bf16), gb[64 * pr : 64 * pr + 64], from_right(even).astype(bf16)]
            g3_ref[c, pl.ds(pl.multiple_of((r + 2) * 256, 256), 256), :] = jnp.concatenate(parts, axis=0)
            d3_ref[...] += dot_nt(gb, rows_of(x3_ref, c, (r + 1) * 192, 576))
        return carry

    lax.fori_loop(0, rows, backward, 0)

    def down(k, carry):
        both = [dot(wd3_ref[...], rows_of(g3_ref, c, k * 256 + 128, 512)) for c in range(crops)]
        for c in range(crops):
            gc_ref[c, pl.ds(pl.multiple_of(k * 64, 64), 64), :] = both[c][0:64] + both[c][64:128]
        return carry

    lax.fori_loop(0, rows + 2, down, 0)


def third_kernel(
    gc_ref, up_ref, dn_ref, raw_ref, h2_ref, pool_ref, h1_ref, y_ref, go_ref, wd2_ref, wht_ref,
    d2_ref, d1_ref, b2_ref, b1_ref,
    g2_ref, x2_ref,
):
    crops = h1_ref.shape[0]
    width = h1_ref.shape[2]
    rows = go_ref.shape[1] // 16
    raw = [jnp.broadcast_to(raw_ref[c], (CH_TWO, 128)) for c in range(crops)]
    b2_ref[...] = jnp.zeros_like(b2_ref)
    b1_ref[...] = jnp.zeros_like(b1_ref)
    d2_ref[...] = jnp.zeros_like(d2_ref)
    d1_ref[...] = jnp.zeros_like(d1_ref)

    def masked(k, c, extra, own):
        coarse = rows_of(gc_ref, c, k * 64, 64)
        if extra is not None:
            coarse = coarse + extra.astype(f32)
        grad = (coarse + wide(raw[c], width)).astype(bf16)
        h2 = rows_of(h2_ref, c, (k + 1) * 64, 64).astype(f32)
        g = jnp.where(h2 > 0, grad.astype(f32), 0.0)
        if own:
            b2_ref[...] += fold_lanes(g)
        g2_ref[c, pl.ds(pl.multiple_of(k * 192, 192), 192), :] = jnp.concatenate(
            [from_left(g).astype(bf16), g.astype(bf16), from_right(g).astype(bf16)], axis=0
        )

    def widen(k, carry):
        for c in range(crops):
            mid = rows_of(pool_ref, c, k * 32, 32)
            x = mid.astype(f32)
            x2_ref[c, pl.ds(pl.multiple_of(k * 96, 96), 96), :] = jnp.concatenate(
                [from_left(x).astype(bf16), mid, from_right(x).astype(bf16)], axis=0
            )
        return carry

    lax.fori_loop(0, rows + 2, widen, 0)
    for c in range(crops):
        masked(0, c, up_ref[c, 0:64], False)
        masked(1, c, up_ref[c, 64:128], True)
        masked(rows, c, dn_ref[c, 0:64], True)
        masked(rows + 1, c, dn_ref[c, 64:128], False)

    def inner(k, carry):
        for c in range(crops):
            masked(k, c, None, True)
        return carry

    lax.fori_loop(2, rows, inner, 0)

    def backward(r, carry):
        gps = [dot(wd2_ref[...], rows_of(g2_ref, c, r * 192, 576)) for c in range(crops)]
        gts = [dot(wht_ref[...], rows_of(go_ref, c, r * 16, 16)) for c in range(crops)]
        for c in range(crops):
            d2_ref[...] += dot_nt(rows_of(g2_ref, c, (r + 1) * 192 + 64, 64), rows_of(x2_ref, c, r * 96, 288))
            gp = 0.25 * gps[c].astype(bf16).astype(f32)
            g1 = (jnp.concatenate([gp] * 4, axis=0) + gts[c].astype(bf16).astype(f32)).astype(bf16).astype(f32)
            h1 = rows_of(h1_ref, c, (r + 1) * 128, 128).astype(f32)
            g1 = jnp.where(h1 > 0, g1, 0.0)
            b1_ref[...] += fold_lanes(g1)
            d1_ref[...] += dot_nt(g1.astype(bf16), rows_of(y_ref, c, (r + 3) * 16, 32))
        return carry

    lax.fori_loop(0, rows, backward, 0)


def neighbours(block_low, block_high, axis):
    count = lax.axis_size(axis)
    forward = [(i, i + 1) for i in range(count - 1)]
    backward = [(i + 1, i) for i in range(count - 1)]
    return lax.ppermute(block_high, axis, forward), lax.ppermute(block_low, axis, backward)


def nesterov(weight, gradient, momentum, average, count):
    decayed = gradient + decay_rate * weight
    momentum_new = momentum_rate * momentum + decayed
    weight_new = weight - learn_rate * (decayed + momentum_rate * momentum_new)
    average_new = average + (weight_new - average) / (count + 1.0)
    return (weight_new, momentum_new, average_new)


def on_device(
    images, nucleus, target_flow, cell_label, step_count,
    conv1_weight, conv1_momentum, conv1_average,
    conv2_weight, conv2_momentum, conv2_average,
    conv3_weight, conv3_momentum, conv3_average,
    style_weight, style_momentum, style_average,
    head_weight, head_momentum, head_average,
    biases, bias_momentum, bias_average,
):
    tiles = lax.axis_size("tile")
    me = lax.axis_index("tile")
    crops, _, height, cols = images.shape
    rows, width = height // 2, cols // 2
    pixel_count = lax.axis_size("img") * tiles * crops * height * cols
    grad_scale = 1.0 / math.sqrt(pixel_count)
    coarse_count = tiles * rows * width

    def sds(shape, dtype=f32):
        return jax.ShapeDtypeStruct(shape, dtype)

    k1, k2, k3, kh = (w.astype(bf16) for w in (conv1_weight, conv2_weight, conv3_weight, head_weight))
    bias_one = biases[0:CH_ONE]
    bias_two = biases[CH_ONE : CH_ONE + CH_TWO]
    bias_three = biases[CH_ONE + CH_TWO : 2 * CH_ONE + CH_TWO]
    bias_style = biases[2 * CH_ONE + CH_TWO : 3 * CH_ONE + CH_TWO]
    bias_head = biases[3 * CH_ONE + CH_TWO :]

    w1 = jnp.einsum("pja,qlb,abio->pqojil", SEL_ONE, SEL_ONE, k1.astype(f32), precision=highest)
    w1 = w1.reshape(4 * CH_ONE, 32).astype(bf16)
    w2 = jnp.transpose(k2, (3, 0, 1, 2)).reshape(CH_TWO, 9 * CH_ONE)
    w3 = jnp.einsum("pra,qcb,abio->pqorci", SEL_UP, SEL_UP, k3.astype(f32), precision=highest)
    w3 = w3.reshape(4 * CH_ONE, 9 * CH_TWO)
    w3_hi = lax.reduce_precision(w3, 8, 7)
    w3 = jnp.concatenate([w3_hi.astype(bf16), (w3 - w3_hi).astype(bf16)], axis=0)
    wd3 = jnp.einsum("ra,cb,abio->irco", SEL_DOWN, SEL_DOWN, k3.astype(f32), precision=highest)
    wd3 = wd3.reshape(CH_TWO, 16 * CH_ONE)
    wd3_hi = lax.reduce_precision(wd3, 8, 7)
    wd3 = jnp.concatenate([wd3_hi.astype(bf16), (wd3 - wd3_hi).astype(bf16)], axis=0)
    wd2 = jnp.transpose(k2[::-1, ::-1], (2, 0, 1, 3)).reshape(CH_ONE, 9 * CH_TWO)
    wht = jnp.einsum("pq,io->piqo", jnp.eye(4, dtype=f32), kh.astype(f32)).transpose(0, 1, 3, 2)
    wht = jnp.pad(wht.reshape(4 * CH_ONE, 4 * OUT_CH), ((0, 0), (0, 4))).astype(bf16)
    wh = wht.T
    bh = jnp.pad(jnp.repeat(bias_head, 4), (0, 4)).reshape(16, 1)
    b1 = jnp.tile(bias_one, 4).reshape(4 * CH_ONE, 1)
    b2 = bias_two.reshape(CH_TWO, 1)

    edges = jnp.stack([-me * rows, (tiles - me) * rows]).astype(jnp.int32)
    low, high = neighbours(images[:, :, :IN_HALO], images[:, :, -IN_HALO:], "tile")
    pad = jnp.zeros((crops, 2, 2, cols), bf16)
    x = jnp.concatenate([low, images, high, pad], axis=2).reshape(crops, 2 * (height + 16), cols)
    flow = target_flow.astype(bf16)
    low, high = neighbours(flow[:, :, :LABEL_HALO], flow[:, :, -LABEL_HALO:], "tile")
    flow = jnp.concatenate([low, flow, high], axis=2)
    label = jnp.pad(cell_label.astype(bf16), ((0, 0), (2, 2), (0, 0)))[:, None]
    t = jnp.pad(jnp.concatenate([flow, label], axis=1), ((0, 0), (0, 0), (0, 4), (0, 0)))
    t = t.reshape(crops, 3 * (height + 8), cols)

    limit = pltpu.CompilerParams(vmem_limit_bytes=60 * 2**20)
    y, targets, h1, pool, h2, style_part = pl.pallas_call(
        first_kernel,
        out_shape=(
            sds((crops, 16 * (rows + 7), width), bf16),
            sds((crops, width // 128, 16 * (rows + 2), 128)),
            sds((crops, 128 * (rows + 3), width), bf16),
            sds((crops, 32 * (rows + 3), width), bf16),
            sds((crops, 64 * (rows + 4), width), bf16),
            sds((crops, CH_TWO, 128)),
        ),
        in_specs=[SMEM, SMEM] + [VMEM] * 6,
        out_specs=[VMEM] * 6,
        scratch_shapes=[pltpu.VMEM((crops, 96 * (rows + 6), width), bf16)],
        compiler_params=limit,
        name="forward_one_two",
    )(edges, nucleus, x, t, w1, b1, w2, b2)

    style_raw = lax.psum(jnp.sum(style_part, axis=2), "tile") / coarse_count
    style_inv = lax.rsqrt(jnp.mean(style_raw * style_raw, axis=1, keepdims=True) + norm_eps)
    style_unit = style_raw * style_inv
    style_vec = jnp.dot(style_unit, style_weight, precision=highest) + bias_style
    bs = jnp.tile(style_vec + bias_three, (1, 4))[:, :, None]

    def second(*refs):
        second_kernel(grad_scale, *refs)

    gc, go, d3, head, small, sg, loss = pl.pallas_call(
        second,
        out_shape=(
            sds((crops, 64 * (rows + 2), width)),
            sds((crops, 16 * rows, width), bf16),
            sds((4 * CH_ONE, 9 * CH_TWO)),
            sds((16, 128)),
            sds((16, 128)),
            sds((crops, 4 * CH_ONE, 128)),
            sds((rows, 128)),
        ),
        in_specs=[SMEM] + [VMEM] * 9,
        out_specs=[VMEM] * 7,
        scratch_shapes=[
            pltpu.VMEM((crops, 192 * (rows + 4), width), bf16),
            pltpu.VMEM((crops, 128 * (rows + 2), width), bf16),
            pltpu.VMEM((crops, 128 * (rows + 2), width), bf16),
            pltpu.VMEM((crops, width // 128, 16 * (rows + 2), 128), f32),
            pltpu.VMEM((crops, width // 128, 16 * rows, 128), f32),
            pltpu.VMEM((crops, 256 * (rows + 4), width), bf16),
        ],
        compiler_params=limit,
        name="forward_three_back",
    )(edges, h1, h2, targets, bs, w3, wh, wht, wd3, bh)

    style_grad_part = jnp.sum(sg.reshape(crops, 4, CH_ONE, 128), axis=(1, 3))
    grad_bias_three = jnp.sum(style_grad_part, axis=0)
    grad_style_weight = jnp.dot(style_unit.T, style_grad_part, precision=highest)
    style_grad = lax.psum(style_grad_part, "tile")
    grad_unit = jnp.dot(style_grad, style_weight.T, precision=highest)
    grad_raw = style_inv * grad_unit - style_inv**3 * style_raw * jnp.mean(
        style_raw * grad_unit, axis=1, keepdims=True
    )
    raw = (grad_raw / coarse_count)[:, :, None]
    rim = gc.reshape(crops, rows + 2, CH_TWO, width)
    rim_low = rim[:, 0:2].reshape(crops, 128, width).astype(bf16)
    rim_high = rim[:, rows : rows + 2].reshape(crops, 128, width).astype(bf16)
    from_up, from_dn = neighbours(rim_low, rim_high, "tile")

    d2, d1, gb2, gb1 = pl.pallas_call(
        third_kernel,
        out_shape=(
            sds((CH_TWO, 9 * CH_ONE)),
            sds((4 * CH_ONE, 32)),
            sds((CH_TWO, 128)),
            sds((4 * CH_ONE, 128)),
        ),
        in_specs=[VMEM] * 11,
        out_specs=[VMEM] * 4,
        scratch_shapes=[
            pltpu.VMEM((crops, 192 * (rows + 2), width), bf16),
            pltpu.VMEM((crops, 96 * (rows + 2), width), bf16),
        ],
        compiler_params=limit,
        name="back_two_one",
    )(gc, from_up, from_dn, raw, h2, pool, h1, y, go, wd2, wht)

    d1 = d1.reshape(2, 2, CH_ONE, 4, 2, 4)
    grad_kernel_one = jnp.einsum("pqojil,pja,qlb->abio", d1, SEL_ONE, SEL_ONE, precision=highest)
    grad_kernel_two = jnp.transpose(d2.reshape(CH_TWO, 3, 3, CH_ONE), (1, 2, 3, 0))
    d3 = d3.reshape(2, 2, CH_ONE, 3, 3, CH_TWO)
    grad_kernel_three = jnp.einsum("pqorci,pra,qcb->abio", d3, SEL_UP, SEL_UP, precision=highest)
    head = head.reshape(4, 4, 4, CH_ONE)[:OUT_CH]
    grad_head = jnp.einsum("oppi->io", head)
    grad_bias_head = jnp.sum(small.reshape(4, 4, 128), axis=(1, 2))[:OUT_CH]
    grad_bias_two = jnp.sum(gb2, axis=1)
    grad_bias_one = jnp.sum(gb1.reshape(4, CH_ONE, 128), axis=(0, 2))
    grad_bias = jnp.concatenate([grad_bias_one, grad_bias_two, grad_bias_three, grad_bias_three, grad_bias_head])
    summed = lax.psum(
        (grad_kernel_one, grad_kernel_two, grad_kernel_three, grad_style_weight, grad_head, grad_bias, jnp.sum(loss)),
        ("img", "tile"),
    )
    count = step_count[0].astype(f32)
    olds = (
        (conv1_weight, conv1_momentum, conv1_average),
        (conv2_weight, conv2_momentum, conv2_average),
        (conv3_weight, conv3_momentum, conv3_average),
        (style_weight, style_momentum, style_average),
        (head_weight, head_momentum, head_average),
        (biases, bias_momentum, bias_average),
    )
    results = [(summed[6] / pixel_count).reshape(1)]
    for k, state in enumerate(olds):
        results.extend(nesterov(state[0], summed[k], state[1], state[2], count))
    return tuple(results)


def solution(mesh):
    return jax.shard_map(
        on_device,
        mesh=mesh,
        in_specs=(
            P("img", None, "tile", None),
            P("img"),
            P("img", None, "tile", None),
            P("img", "tile", None),
        )
        + (P(),) * 19,
        out_specs=(P(),) * 19,
        check_vma=False,
    )
```

```python
import math

import jax
import jax.numpy as jnp
from jax import lax
from jax.experimental import pallas as pl
from jax.experimental.pallas import tpu as pltpu
from jax.sharding import PartitionSpec as P

CH_ONE = 32
CH_TWO = 64
OUT_CH = 3

momentum_rate = 0.9
learn_rate = 0.02
decay_rate = 0.0001
norm_eps = 1e-05
highest = lax.Precision.HIGHEST
f32 = jnp.float32
bf16 = jnp.bfloat16

HALO = 8
VMEM = pl.BlockSpec(memory_space=pltpu.VMEM)
SMEM = pl.BlockSpec(memory_space=pltpu.SMEM)
ANY = pl.BlockSpec(memory_space=pl.ANY)
MESH = pl.DeviceIdType.MESH
DMA = pltpu.SemaphoreType.DMA

PART_ROWS = (144, 160, 32, 16, 16, 8)


def dot(a, b):
    return jnp.dot(a, b, preferred_element_type=f32)


def dot_nt(a, b, precision=None):
    return lax.dot_general(a, b, (((1,), (1,)), ((), ())), preferred_element_type=f32, precision=precision)


def from_left(x):
    lane = lax.broadcasted_iota(jnp.int32, x.shape, 1)
    return jnp.where(lane == 0, 0.0, pltpu.roll(x, 1, 1))


def from_right(x):
    width = x.shape[1]
    lane = lax.broadcasted_iota(jnp.int32, x.shape, 1)
    return jnp.where(lane == width - 1, 0.0, pltpu.roll(x, width - 1, 1))


def turn(x, by, axis):
    by = by % x.shape[axis]
    return pltpu.roll(x, by, axis) if by else x


def lane_group(x, group, size=32):
    lane = lax.broadcasted_iota(jnp.int32, x.shape, 1)
    return jnp.where(lane // size == group, x, 0.0)


def over_phases(x):
    return (x + turn(x, 32, 1)) + (turn(x, 64, 1) + turn(x, 96, 1))


def as_column(row):
    return jnp.transpose(jnp.broadcast_to(row, (128, 128)))


def fold_lanes(x):
    total = x[:, 0:128]
    for k in range(1, x.shape[1] // 128):
        total = total + x[:, 128 * k : 128 * (k + 1)]
    return total


def wide(tile, width):
    return jnp.concatenate([tile] * (width // 128), axis=1)


def rows_of(ref, crop, start, size, align=16):
    return ref[crop, pl.ds(pl.multiple_of(start, align), size), :]


def put_lanes(ref, crop, start, size, value):
    for k in range(value.shape[1] // 128):
        ref[crop, k, pl.ds(pl.multiple_of(start, 8), size), :] = value[:, 128 * k : 128 * (k + 1)]


def get_lanes(ref, crop, start, size, stride=None):
    parts = []
    for k in range(ref.shape[1]):
        spot = pl.ds(start, size, stride=stride) if stride else pl.ds(pl.multiple_of(start, 8), size)
        parts.append(ref[crop, k, spot, :])
    return jnp.concatenate(parts, axis=1)


def valid(row, edge_ref):
    return jnp.where((row >= edge_ref[0]) & (row < edge_ref[1]), 1.0, 0.0).astype(f32)


def meet(sizes):
    gate = pltpu.get_barrier_semaphore()
    for axis, count in sizes:
        me = lax.axis_index(axis)
        for j in range(1, count):
            pl.semaphore_signal(gate, inc=1, device_id={axis: lax.rem(me + j, count)}, device_id_type=MESH)
    pl.semaphore_wait(gate, sum(count - 1 for _, count in sizes))


def send_all(count, axis, source, target, send_sem, recv_sem):
    me = lax.axis_index(axis)
    copies = []
    for j in range(1, count):
        to = lax.rem(me + j, count)
        copy = pltpu.make_async_remote_copy(
            src_ref=source(to), dst_ref=target, send_sem=send_sem.at[j - 1], recv_sem=recv_sem.at[j - 1],
            device_id={axis: to}, device_id_type=MESH,
        )
        copy.start()
        copies.append(copy)
    return copies


def in_order(ref, count):
    total = ref[0]
    for k in range(1, count):
        total = total + ref[k]
    return total


def meet_next(tiles):
    gate = pltpu.get_barrier_semaphore()
    me = lax.axis_index("tile")

    @pl.when(me > 0)
    def _():
        pl.semaphore_signal(gate, inc=1, device_id={"tile": me - 1}, device_id_type=MESH)

    @pl.when(me < tiles - 1)
    def _():
        pl.semaphore_signal(gate, inc=1, device_id={"tile": me + 1}, device_id_type=MESH)

    pl.semaphore_wait(gate, jnp.minimum(me, 1) + jnp.minimum(tiles - 1 - me, 1))


def swap_edges(tiles, pairs, send_sem, recv_sem):
    me = lax.axis_index("tile")
    copies = []
    for k, (low, high, from_before, from_after) in enumerate(pairs):
        down = pltpu.make_async_remote_copy(
            src_ref=high, dst_ref=from_before, send_sem=send_sem.at[2 * k], recv_sem=recv_sem.at[2 * k],
            device_id={"tile": jnp.minimum(me + 1, tiles - 1)}, device_id_type=MESH,
        )
        up = pltpu.make_async_remote_copy(
            src_ref=low, dst_ref=from_after, send_sem=send_sem.at[2 * k + 1], recv_sem=recv_sem.at[2 * k + 1],
            device_id={"tile": jnp.maximum(me - 1, 0)}, device_id_type=MESH,
        )
        copies.append((down, up))

    @pl.when(me < tiles - 1)
    def _():
        for down, _up in copies:
            down.start()

    @pl.when(me > 0)
    def _():
        for _down, up in copies:
            up.start()

    def finish():
        @pl.when(me < tiles - 1)
        def _():
            for down, up in copies:
                down.wait_send()
                up.wait_recv()

        @pl.when(me > 0)
        def _():
            for down, up in copies:
                up.wait_send()
                down.wait_recv()

    return finish


def halo_kernel(tiles, x_ref, t_ref, x_lo, x_hi, t_lo, t_hi, send_sem, recv_sem):
    meet_next(tiles)
    last = x_ref.shape[2] - HALO
    finish = swap_edges(
        tiles,
        [
            (ref.at[:, :, pl.ds(0, HALO), :], ref.at[:, :, pl.ds(last, HALO), :], lo, hi)
            for ref, lo, hi in ((x_ref, x_lo, x_hi), (t_ref, t_lo, t_hi))
        ],
        send_sem, recv_sem,
    )
    finish()


def sum_kernel(tiles, x_ref, o_ref, got, send_sem, recv_sem):
    me = lax.axis_index("tile")
    got[me] = x_ref[...]
    meet((("tile", tiles),))
    copies = send_all(tiles, "tile", lambda to: x_ref, got.at[me], send_sem, recv_sem)
    for copy in copies:
        copy.wait()
    o_ref[...] = in_order(got, tiles)


def sum_rim_kernel(tiles, x_ref, lo_ref, hi_ref, o_ref, up_ref, dn_ref, got, send_sem, recv_sem, rim_send, rim_recv):
    me = lax.axis_index("tile")
    got[me] = x_ref[...]
    meet((("tile", tiles),))
    finish = swap_edges(tiles, [(lo_ref, hi_ref, up_ref, dn_ref)], rim_send, rim_recv)
    copies = send_all(tiles, "tile", lambda to: x_ref, got.at[me], send_sem, recv_sem)
    for copy in copies:
        copy.wait()
    o_ref[...] = in_order(got, tiles)
    finish()


def reduce_kernel(
    tiles, images, part, k3_ref, k2_ref, k1_ref, head_ref, style_ref, sums_a, sums_b, o_ref,
    pay, got, own, met, full, send_one, recv_one, send_two, recv_two, send_three, recv_three,
):
    me, mine = lax.axis_index("tile"), lax.axis_index("img")
    start = 0
    for ref, rows in zip((k3_ref, k2_ref, k1_ref, head_ref, style_ref), PART_ROWS):
        pay[start : start + rows, :] = ref[...]
        start += rows
    pay[start : start + 8, :] = sums_a[...] + sums_b[...]
    start += 8
    if start < part * tiles:
        pay[start : part * tiles, :] = jnp.zeros((part * tiles - start, 128), f32)
    meet((("tile", tiles), ("img", images)))

    def block(ref, k):
        return ref.at[pl.ds(pl.multiple_of(k * part, 8), part), :]

    got[me] = pay[pl.ds(pl.multiple_of(me * part, 8), part), :]
    for copy in send_all(tiles, "tile", lambda to: block(pay, to), got.at[me], send_one, recv_one):
        copy.wait()
    own[...] = in_order(got, tiles)
    met[mine] = own[...]
    for copy in send_all(images, "img", lambda to: own, met.at[mine], send_two, recv_two):
        copy.wait()
    total = in_order(met, images)
    full[pl.ds(pl.multiple_of(me * part, 8), part), :] = total
    copies = send_all(tiles, "tile", lambda to: block(full, me), block(full, me), send_three, recv_three)
    for copy in copies:
        copy.wait()
    o_ref[...] = full[...]


def weight_kernel(
    k1_ref, k2_ref, k3_ref, kh_ref, bias_ref,
    w1_ref, w2_ref, w3_ref, wd3_ref, wd2_ref, wh_ref, wht_ref, b1_ref, b2_ref, bh_ref,
    base_ref,
):
    base_ref[...] = jnp.zeros_like(base_ref)
    for a in range(3):
        for b in range(3):
            for i in range(2):
                base_ref[8 * a + 4 * i + b : 8 * a + 4 * i + b + 1, 0:32] = k1_ref[a, b, i : i + 1, :]
    base = base_ref[...]
    w1t = jnp.zeros((32, 128), f32)
    for p in range(4):
        w1t = w1t + turn(turn(base, 8 * (p // 2) + p % 2, 0), 32 * p, 1)
    w1_ref[...] = jnp.transpose(w1t).astype(bf16)

    k2 = [[k2_ref[a, b].astype(bf16).astype(f32) for b in range(3)] for a in range(3)]
    w2t = jnp.concatenate([k2[a][b] for a in range(3) for b in range(3)], axis=0)
    w2_ref[...] = jnp.transpose(w2t).astype(bf16)
    wd2_ref[...] = jnp.concatenate([k2[2 - s][2 - t] for s in range(3) for t in range(3)], axis=1).astype(bf16)

    def tap_sum(first, second):
        total = None
        for a in first:
            for b in second:
                total = k3[a][b] if total is None else total + k3[a][b]
        return jnp.zeros((CH_TWO, CH_ONE), f32) if total is None else total

    k3 = [[k3_ref[a, b].astype(bf16).astype(f32) for b in range(3)] for a in range(3)]
    up = [[[a for a in range(3) if (p + a + 1) // 2 == r] for r in range(3)] for p in range(2)]
    w3t = jnp.concatenate(
        [
            jnp.concatenate([tap_sum(up[p // 2][r], up[p % 2][c]) for p in range(4)], axis=1)
            for r in range(3)
            for c in range(3)
        ],
        axis=0,
    )
    w3 = jnp.transpose(w3t)
    w3_hi = w3.astype(bf16)
    w3_ref[0:128, :] = w3_hi
    w3_ref[128:256, :] = (w3 - w3_hi.astype(f32)).astype(bf16)
    down = ((2,), (1, 2), (0, 1), (0,))
    wd3 = jnp.concatenate([tap_sum(down[r], down[c]) for r in range(4) for c in range(4)], axis=1)
    wd3_hi = wd3.astype(bf16)
    wd3_ref[0:64, :] = wd3_hi
    wd3_ref[64:128, :] = (wd3 - wd3_hi.astype(f32)).astype(bf16)

    kht = jnp.transpose(jnp.concatenate([kh_ref[...], jnp.zeros((CH_ONE, 5), f32)], axis=1))
    row = lax.broadcasted_iota(jnp.int32, (16, 128), 0)
    lane = lax.broadcasted_iota(jnp.int32, (16, 128), 1)
    wh = jnp.zeros((16, 128), f32)
    for o in range(OUT_CH):
        one = jnp.concatenate([kht[o : o + 1, :]] * 4, axis=1)
        wh = jnp.where(row // 4 == o, jnp.broadcast_to(one, (16, 128)), wh)
    wh = jnp.where(row % 4 == lane // 32, wh, 0.0)
    wh_ref[...] = wh.astype(bf16)
    wht_ref[...] = jnp.transpose(wh).astype(bf16)

    b1 = bias_ref[0:1, 0:32]
    b1_ref[...] = as_column(jnp.concatenate([b1] * 4, axis=1))
    b2 = bias_ref[0:1, 32:96]
    b2_ref[...] = as_column(jnp.concatenate([b2] * 2, axis=1))[0:64]
    bh = jnp.zeros((16, 128), f32)
    for o in range(OUT_CH):
        bh = jnp.where(row // 4 == o, jnp.broadcast_to(bias_ref[0:1, 160 + o : 161 + o], (16, 128)), bh)
    bh_ref[...] = bh


def split_columns(x, select):
    even, odd = [], []
    for k in range(x.shape[1] // 256):
        piece = dot(x[:, 256 * k : 256 * (k + 1)], select)
        even.append(piece[:, 0:128])
        odd.append(piece[:, 128:256])
    return jnp.concatenate(even, axis=1), jnp.concatenate(odd, axis=1)


def first_kernel(
    edge_ref, nucleus_ref, x_ref, x_lo, x_hi, t_ref, t_lo, t_hi, label_ref, w1_ref, b1_ref, w2_ref, b2_ref,
    y_ref, t_out, h1_ref, pool_ref, h2_ref, style_ref, x2_ref,
):
    crops = x_ref.shape[0]
    width = x_ref.shape[3] // 2
    rows = h2_ref.shape[1] // CH_TWO - 4
    height = 2 * rows
    top = 3
    r_id = lax.broadcasted_iota(jnp.int32, (256, 256), 0)
    c_id = lax.broadcasted_iota(jnp.int32, (256, 256), 1)
    select = jnp.where(r_id == 2 * (c_id % 128) + c_id // 128, 1.0, 0.0).astype(bf16)
    x_rows = 2 * (height + 2 * HALO)
    y_rows = y_ref.shape[1]
    ri = lax.broadcasted_iota(jnp.int32, (y_rows, 4 * x_rows), 0)
    ci = lax.broadcasted_iota(jnp.int32, (y_rows, 4 * x_rows), 1)
    fine = 2 * (ri // 16) + (ri // 8) % 2 - 7
    channel = (ri // 4) % 2
    source = jnp.where(
        fine < 0,
        channel * HALO + fine + HALO,
        jnp.where(
            fine < height,
            2 * HALO + channel * height + fine,
            2 * HALO + 2 * height + channel * HALO + fine - height,
        ),
    )
    perm_x = jnp.where(ci == (ri % 4) * x_rows + source, 1.0, 0.0).astype(bf16)
    t_rows = 3 * height + 4 * HALO
    ri = lax.broadcasted_iota(jnp.int32, (t_out.shape[2], 2 * t_rows), 0)
    ci = lax.broadcasted_iota(jnp.int32, (t_out.shape[2], 2 * t_rows), 1)
    part = (ri // 4) % 4
    fine = 2 * (ri // 16) + (ri // 2) % 2 - 2
    source = jnp.where(
        fine < 0,
        3 * height + part * HALO + fine + HALO,
        jnp.where(fine < height, part * height + fine, 3 * height + 2 * HALO + part * HALO + fine - height),
    )
    outside = (fine < 0) | (fine >= height)
    known = (part < 2) | ((part == 2) & jnp.logical_not(outside))
    perm_t = jnp.where((ci == (ri % 2) * t_rows + source) & known, 1.0, 0.0).astype(bf16)
    has_up, has_dn = edge_ref[0] < 0, edge_ref[1] > rows
    for c in range(crops):
        pieces = [jnp.where(has_up, x_lo[c, k].astype(f32), 0.0) for k in range(2)]
        pieces += [x_ref[c, k].astype(f32) for k in range(2)]
        pieces += [jnp.where(has_dn, x_hi[c, k].astype(f32), 0.0) for k in range(2)]
        even, odd = split_columns(jnp.concatenate(pieces, axis=0).astype(bf16), select)
        row = lax.broadcasted_iota(jnp.int32, (x_rows, width), 0)
        second = ((row >= HALO) & (row < 2 * HALO)) | (row >= x_rows - HALO)
        second = second | ((row >= 2 * HALO + height) & (row < 2 * HALO + 2 * height))
        gate = jnp.where(second, nucleus_ref[c].astype(f32), 1.0)
        even, odd = even * gate, odd * gate
        stack = jnp.concatenate([from_left(odd), even, odd, from_right(even)], axis=0)
        y_ref[c] = dot(perm_x, stack.astype(bf16)).astype(bf16)
        pieces = [t_ref[c, 0].astype(f32), t_ref[c, 1].astype(f32), label_ref[c].astype(f32)]
        pieces += [jnp.where(has_up, t_lo[c, k], 0).astype(f32) for k in range(2)]
        pieces += [jnp.where(has_dn, t_hi[c, k], 0).astype(f32) for k in range(2)]
        even, odd = split_columns(jnp.concatenate(pieces, axis=0).astype(bf16), select)
        put_lanes(t_out, c, 0, t_out.shape[2], dot(perm_t, jnp.concatenate([even, odd], axis=0).astype(bf16)))
    style_ref[...] = jnp.zeros_like(style_ref)
    ones = jnp.ones((8, width), bf16)

    def conv_one(k):
        row = k - top
        keep = valid(row, edge_ref)
        spot = jnp.clip(row + 1, 0, rows + 2)
        pre = [dot(w1_ref[...], rows_of(y_ref, c, k * 16, 32)) for c in range(crops)]
        for c in range(crops):
            hidden = (jnp.maximum(pre[c] + wide(b1_ref[...], width), 0.0) * keep).astype(bf16)
            h1_ref[c, pl.ds(pl.multiple_of(spot * 128, 128), 128), :] = hidden
            h = hidden.astype(f32)
            pooled = (0.25 * ((h[0:32] + h[32:64]) + (h[64:96] + h[96:128]))).astype(bf16)
            pool_ref[c, pl.ds(pl.multiple_of(spot * 32, 32), 32), :] = pooled
            p = pooled.astype(f32)
            both = jnp.concatenate([from_left(p).astype(bf16), pooled, from_right(p).astype(bf16)], axis=0)
            x2_ref[c, pl.ds(pl.multiple_of(k * 96, 96), 96), :] = both

    def conv_two(q):
        row = q - 2
        keep = valid(row, edge_ref)
        own = jnp.where((row >= 0) & (row < rows), 1.0, 0.0).astype(f32)
        pre = [dot(w2_ref[...], rows_of(x2_ref, c, q * 96, 288)) for c in range(crops)]
        for c in range(crops):
            hidden = (jnp.maximum(pre[c] + wide(b2_ref[...], width), 0.0) * keep).astype(bf16)
            h2_ref[c, pl.ds(pl.multiple_of(q * 64, 64), 64), :] = hidden
            style_ref[c : c + 1, 0:64] += dot_nt(ones, hidden)[0:1] * own

    def loop_one(k, carry):
        conv_one(k)
        return carry

    def loop_both(k, carry):
        conv_two(k - 3)
        conv_one(k)
        return carry

    lax.fori_loop(0, 3, loop_one, 0)
    lax.fori_loop(3, rows + 6, loop_both, 0)
    conv_two(rows + 3)


def second_kernel(
    scale, coarse_count,
    edge_ref, h1_ref, h2_ref, t_ref, total_ref, bias_ref, ws_ref, w3_ref, wh_ref, wht_ref, wd3_ref, bh_ref,
    gc_ref, rim_lo, rim_hi, go_out, k3_ref, head_ref, style_ref, sums_ref, sg_ref,
    x3_ref, h3_ref, m_ref, fe_ref, go_ref, g3_ref, d3_ref,
):
    crops = h1_ref.shape[0]
    width = h1_ref.shape[2]
    rows = go_out.shape[1] // 16

    def shift(k, carry):
        for c in range(crops):
            mid = rows_of(h2_ref, c, k * 64, 64)
            x = mid.astype(f32)
            x3_ref[c, pl.ds(pl.multiple_of(k * 192, 192), 192), :] = jnp.concatenate(
                [from_left(x).astype(bf16), mid, from_right(x).astype(bf16)], axis=0
            )
        return carry

    lax.fori_loop(0, rows + 4, shift, 0)
    raw = total_ref[:, 0:64] / coarse_count
    unit = raw * lax.rsqrt(jnp.mean(raw * raw, axis=1, keepdims=True) + norm_eps)
    vec = jnp.dot(unit, ws_ref[...], precision=highest, preferred_element_type=f32) + bias_ref[0:1, 128:160]
    vec = jnp.concatenate([vec + bias_ref[0:1, 96:128]] * 4, axis=1)
    bias3 = [as_column(vec[c : c + 1]) for c in range(crops)]
    ones = jnp.ones((8, width), bf16)

    def forward(k, carry):
        row = k - 1
        keep = valid(row, edge_ref)
        pre = [dot(w3_ref[...], rows_of(x3_ref, c, k * 192, 576)) for c in range(crops)]
        hs = []
        for c in range(crops):
            p = pre[c][0:128] + pre[c][128:256] + wide(bias3[c], width)
            h1 = rows_of(h1_ref, c, k * 128, 128).astype(f32)
            h3 = (jnp.maximum(p, 0.0) + h1).astype(bf16)
            h3_ref[c, pl.ds(pl.multiple_of(k * 128, 128), 128), :] = h3
            m_ref[c, pl.ds(pl.multiple_of(k * 128, 128), 128), :] = jnp.where(p > 0, 1.0, 0.0).astype(bf16)
            hs.append(h3)
        outs = [dot(wh_ref[...], h) for h in hs]
        for c in range(crops):
            o = outs[c] + wide(bh_ref[...], width)
            t = get_lanes(t_ref, c, k * 16, 16)
            fe = (o[0:8] - 0.25 * t[0:8]) * keep
            put_lanes(fe_ref, c, k * 16, 16, jnp.concatenate([fe, o[8:16]], axis=0))
        return carry

    lax.fori_loop(0, rows + 2, forward, 0)

    r_id = lax.broadcasted_iota(jnp.int32, (rows, width), 0)
    above = jnp.where(r_id - 1 >= edge_ref[0], 1.0, 0.0)
    below = jnp.where(r_id + 1 < edge_ref[1], 1.0, 0.0)
    loss = jnp.zeros((rows, 128), f32)
    go_ref[...] = jnp.zeros_like(go_ref)
    for c in range(crops):

        def at(part, off):
            return get_lanes(fe_ref, c, 16 * (1 + off) + part, rows, 16)

        def column_part(pr, off):
            odd, even = at(4 + 2 * pr + 1, off), at(4 + 2 * pr, off)
            return 0.5 * (odd - from_left(odd)), 0.5 * (from_right(even) - even)

        e0 = [at(k, 0) for k in range(4)]
        e1 = [at(4 + k, 0) for k in range(4)]
        cols0, cols1 = column_part(0, 0), column_part(1, 0)
        cols_up, cols_dn = column_part(1, -1), column_part(0, 1)
        spread = [None] * 4
        g_up, g_dn = [None] * 2, [None] * 2
        for pc in range(2):
            f_up, f_dn = at(2 + pc, -1), at(pc, 1)
            spread[pc] = 0.5 * (e0[2 + pc] - f_up) + cols0[pc]
            spread[2 + pc] = 0.5 * (f_dn - e0[pc]) + cols1[pc]
            g_up[pc] = 2.0 * scale * above * (0.5 * (e0[pc] - at(pc, -1)) + cols_up[pc])
            g_dn[pc] = 2.0 * scale * below * (0.5 * (at(2 + pc, 1) - e0[2 + pc]) + cols_dn[pc])
        g = [2.0 * scale * v for v in spread]
        for pr in range(2):
            even, odd = g[2 * pr], g[2 * pr + 1]
            col = [0.5 * (odd - from_left(odd)), 0.5 * (from_right(even) - even)]
            for pc in range(2):
                k = 2 * pr + pc
                if pr == 0:
                    row_part = 0.5 * (g[2 + pc] - g_up[pc])
                else:
                    row_part = 0.5 * (g_dn[pc] - g[pc])
                logit = at(8 + k, 0)
                label = get_lanes(t_ref, c, 16 + 8 + k, rows, 16)
                ex = jnp.exp(-jnp.abs(logit))
                sig = jnp.where(logit >= 0, 1.0, ex) / (1.0 + ex)
                grads = (2.0 * scale * e0[k] - row_part, 2.0 * scale * e1[k] - col[pc], scale * (sig - label))
                for part in range(OUT_CH):
                    for j in range(width // 128):
                        go_ref[c, j, pl.ds(4 * part + k, rows, stride=16), :] = grads[part][:, 128 * j : 128 * (j + 1)]
                term = jnp.maximum(logit, 0.0) + jnp.log1p(ex) - label * logit
                loss = loss + fold_lanes(e0[k] * e0[k] + e1[k] * e1[k] + spread[k] * spread[k] + term)
    sums_ref[...] = jnp.zeros_like(sums_ref)
    sums_ref[4:5, :] = jnp.sum(loss, axis=0, keepdims=True)
    head_ref[...] = jnp.zeros_like(head_ref)
    sg_ref[...] = jnp.zeros_like(sg_ref)
    d3_ref[...] = jnp.zeros_like(d3_ref)
    edge = jnp.zeros((256, width), bf16)
    for c in range(crops):
        for k in (0, 1, rows + 2, rows + 3):
            g3_ref[c, 256 * k : 256 * (k + 1), :] = edge

    def backward(r, carry):
        gos, gts = [], []
        for c in range(crops):
            go = get_lanes(go_ref, c, r * 16, 16).astype(bf16)
            go_out[c, pl.ds(pl.multiple_of(r * 16, 16), 16), :] = go
            gos.append(go)
            gts.append(dot(wht_ref[...], go))
        for c in range(crops):
            spot = (r + 1) * 128
            head_ref[...] += dot_nt(gos[c], rows_of(h3_ref, c, spot, 128))
            sums_ref[3:4, 0:16] += dot_nt(ones, gos[c])[0:1]
            g = gts[c].astype(bf16).astype(f32) * rows_of(m_ref, c, spot, 128).astype(f32)
            parts = []
            gb = g.astype(bf16)
            sg_ref[c : c + 1, :] += dot_nt(ones, gb)[0:1]
            for pr in range(2):
                even, odd = g[64 * pr : 64 * pr + 32], g[64 * pr + 32 : 64 * pr + 64]
                parts += [from_left(odd).astype(bf16), gb[64 * pr : 64 * pr + 64], from_right(even).astype(bf16)]
            g3_ref[c, pl.ds(pl.multiple_of((r + 2) * 256, 256), 256), :] = jnp.concatenate(parts, axis=0)
            d3_ref[...] += dot_nt(rows_of(x3_ref, c, (r + 1) * 192, 576), gb)
        return carry

    lax.fori_loop(0, rows, backward, 0)

    def down(k, carry):
        both = [dot(wd3_ref[...], rows_of(g3_ref, c, k * 256 + 128, 512)) for c in range(crops)]
        for c in range(crops):
            gc_ref[c, pl.ds(pl.multiple_of(k * 64, 64), 64), :] = both[c][0:64] + both[c][64:128]
        return carry

    lax.fori_loop(0, rows + 2, down, 0)
    for c in range(crops):
        rim_lo[c] = gc_ref[c, 0:128, :].astype(bf16)
        rim_hi[c] = gc_ref[c, 64 * rows : 64 * rows + 128, :].astype(bf16)

    for block in range(3):
        packed = jnp.zeros((CH_TWO, 128), f32)
        for tap in range(4 * block, min(4 * block + 4, 9)):
            a, b = tap // 3, tap % 3
            total = jnp.zeros((CH_TWO, 128), f32)
            for p in range(4):
                n = 3 * ((p // 2 + a + 1) // 2) + (p % 2 + b + 1) // 2
                total = total + turn(d3_ref[64 * n : 64 * (n + 1), :], 32 * (tap % 4 - p), 1)
            packed = packed + lane_group(total, tap % 4)
        if block < 2:
            k3_ref[64 * block : 64 * (block + 1), :] = packed
        else:
            last = packed[0:16]
            for k in range(1, 4):
                last = last + turn(packed[16 * k : 16 * (k + 1)], 32 * k, 1)
            k3_ref[128:144, :] = last
    outer = jnp.zeros((CH_TWO, 128), f32)
    for c in range(crops):
        column = as_column(jnp.concatenate([unit[c : c + 1]] * 2, axis=1))[0:64]
        outer = outer + column * over_phases(sg_ref[c : c + 1, :])
        sums_ref[2:3, :] += sg_ref[c : c + 1, :]
    packed = lane_group(outer[0:16], 0)
    for k in range(1, 4):
        packed = packed + lane_group(outer[16 * k : 16 * (k + 1)], k)
    style_ref[...] = packed


def third_kernel(
    coarse_count,
    edge_ref, gc_ref, up_ref, dn_ref, total_ref, sg_ref, ws_ref, h2_ref, pool_ref, h1_ref, y_ref, go_ref, wd2_ref, wht_ref,
    k2_ref, d1_ref, sums_ref,
    g2_ref, x2_ref, d2_ref,
):
    crops = h1_ref.shape[0]
    width = h1_ref.shape[2]
    rows = go_ref.shape[1] // 16
    style_raw = total_ref[:, 0:64] / coarse_count
    inv = lax.rsqrt(jnp.mean(style_raw * style_raw, axis=1, keepdims=True) + norm_eps)
    style_grad = over_phases(sg_ref[...])[:, 0:32]
    grad_unit = dot_nt(style_grad, ws_ref[...], highest)
    grad_raw = inv * grad_unit - inv * inv * inv * style_raw * jnp.mean(style_raw * grad_unit, axis=1, keepdims=True)
    grad_raw = jnp.concatenate([grad_raw / coarse_count] * 2, axis=1)
    raw = [as_column(grad_raw[c : c + 1])[0:64] for c in range(crops)]
    ones = jnp.ones((8, width), bf16)
    sums_ref[...] = jnp.zeros_like(sums_ref)
    d2_ref[...] = jnp.zeros_like(d2_ref)
    d1_ref[...] = jnp.zeros_like(d1_ref)

    def masked(k, c, extra, own):
        coarse = rows_of(gc_ref, c, k * 64, 64)
        if extra is not None:
            coarse = coarse + extra
        grad = (coarse + wide(raw[c], width)).astype(bf16)
        h2 = rows_of(h2_ref, c, (k + 1) * 64, 64).astype(f32)
        g = jnp.where(h2 > 0, grad.astype(f32), 0.0)
        gb = g.astype(bf16)
        if own:
            sums_ref[1:2, 0:64] += dot_nt(ones, gb)[0:1]
        g2_ref[c, pl.ds(pl.multiple_of(k * 192, 192), 192), :] = jnp.concatenate(
            [from_left(g).astype(bf16), gb, from_right(g).astype(bf16)], axis=0
        )

    def widen(k, carry):
        for c in range(crops):
            mid = rows_of(pool_ref, c, k * 32, 32)
            x = mid.astype(f32)
            x2_ref[c, pl.ds(pl.multiple_of(k * 96, 96), 96), :] = jnp.concatenate(
                [from_left(x).astype(bf16), mid, from_right(x).astype(bf16)], axis=0
            )
        return carry

    lax.fori_loop(0, rows + 2, widen, 0)
    for c in range(crops):
        up = jnp.where(edge_ref[0] < 0, up_ref[c].astype(f32), 0.0)
        dn = jnp.where(edge_ref[1] > rows, dn_ref[c].astype(f32), 0.0)
        masked(0, c, up[0:64], False)
        masked(1, c, up[64:128], True)
        masked(rows, c, dn[0:64], True)
        masked(rows + 1, c, dn[64:128], False)

    def inner(k, carry):
        for c in range(crops):
            masked(k, c, None, True)
        return carry

    lax.fori_loop(2, rows, inner, 0)

    def backward(r, carry):
        gps = [dot(wd2_ref[...], rows_of(g2_ref, c, r * 192, 576)) for c in range(crops)]
        gts = [dot(wht_ref[...], rows_of(go_ref, c, r * 16, 16)) for c in range(crops)]
        for c in range(crops):
            d2_ref[...] += dot_nt(rows_of(x2_ref, c, r * 96, 288), rows_of(g2_ref, c, (r + 1) * 192 + 64, 64))
            gp = 0.25 * gps[c].astype(bf16).astype(f32)
            g1 = (jnp.concatenate([gp] * 4, axis=0) + gts[c].astype(bf16).astype(f32)).astype(bf16).astype(f32)
            h1 = rows_of(h1_ref, c, (r + 1) * 128, 128).astype(f32)
            g1 = jnp.where(h1 > 0, g1, 0.0)
            gb = g1.astype(bf16)
            sums_ref[0:1, :] += dot_nt(ones, gb)[0:1]
            d1_ref[...] += dot_nt(rows_of(y_ref, c, (r + 3) * 16, 32), gb)
        return carry

    lax.fori_loop(0, rows, backward, 0)
    rest = jnp.concatenate([d2_ref[160:288, :], jnp.zeros((32, 64), f32)], axis=0)
    k2_ref[...] = jnp.concatenate([d2_ref[0:160, :], rest], axis=1)


def update_kernel(pixel_count, count_ref, sum_ref, *refs):
    olds, tail_ref, outs = refs[:15], refs[15], refs[16:]
    starts = [sum(PART_ROWS[:k]) for k in range(len(PART_ROWS))]
    rate = 1.0 / (jnp.zeros((8, 128), f32) + (count_ref[0].astype(f32) + 1.0))

    def step(index, spot, grad):
        weight, momentum, average = (olds[3 * index + k][spot] for k in range(3))
        decayed = grad + decay_rate * weight
        momentum = momentum_rate * momentum + decayed
        new = weight - learn_rate * (decayed + momentum_rate * momentum)
        outs[3 * index][spot] = new
        outs[3 * index + 1][spot] = momentum
        outs[3 * index + 2][spot] = average + (new - average) * rate[0:1, 0:1]

    d1 = sum_ref[starts[2] : starts[2] + 32, :]
    total = jnp.zeros((32, 128), f32)
    for p in range(4):
        total = total + turn(turn(d1, -32 * p, 1), -(8 * (p // 2) + p % 2), 0)
    for a in range(3):
        for b in range(3):
            for i in range(2):
                k = 8 * a + 4 * i + b
                step(0, (a, b, slice(i, i + 1), slice(None)), total[k : k + 1, 0:32])
    for tap in range(9):
        a, b = tap // 3, tap % 3
        first = starts[1] + 32 * (tap % 5)
        half = 64 * (tap // 5)
        step(1, (a, b), sum_ref[first : first + 32, half : half + 64])
        if tap < 8:
            first = starts[0] + 64 * (tap // 4)
            lane = 32 * (tap % 4)
            grad = sum_ref[first : first + 64, lane : lane + 32]
        else:
            first = starts[0] + 128
            grad = jnp.concatenate([sum_ref[first : first + 16, 32 * k : 32 * (k + 1)] for k in range(4)], axis=0)
        step(2, (a, b), grad)
    first = starts[4]
    grad = jnp.concatenate([sum_ref[first : first + 16, 32 * k : 32 * (k + 1)] for k in range(4)], axis=0)
    step(3, (slice(None), slice(None)), grad)
    head = sum_ref[starts[3] : starts[3] + 16, :]
    total = jnp.zeros((16, 128), f32)
    for p in range(4):
        total = total + turn(turn(head, -32 * p, 1), -p, 0)
    total = jnp.concatenate([total[4 * o : 4 * o + 1] for o in range(OUT_CH)] + [jnp.zeros((5, 128), f32)], axis=0)
    step(4, (slice(None), slice(None)), jnp.transpose(total)[0:32, 0:OUT_CH])
    sums = sum_ref[starts[5] : starts[5] + 8, :]
    one, three = over_phases(sums[0:1]), over_phases(sums[2:3])
    lane = lax.broadcasted_iota(jnp.int32, (1, 128), 1)
    low = jnp.where(lane < 32, one, jnp.where(lane < 96, turn(sums[1:2], 32, 1), three))
    ends = sums[3:4]
    ends = (ends + turn(ends, -1, 1)) + (turn(ends, -2, 1) + turn(ends, -3, 1))
    high = jnp.where(lane < 32, three, 0.0)
    for o in range(OUT_CH):
        high = jnp.where(lane == 32 + o, turn(ends, 32 + o - 4 * o, 1), high)
    tail_ref[...] = jnp.zeros_like(tail_ref)
    tail_ref[0:1, :] = jnp.concatenate([low, high], axis=1)
    tail_ref[1:2, 0:1] = jnp.sum(sums[4:5], axis=1, keepdims=True) / pixel_count


def nesterov(weight, gradient, momentum, average, count):
    decayed = gradient + decay_rate * weight
    momentum_new = momentum_rate * momentum + decayed
    weight_new = weight - learn_rate * (decayed + momentum_rate * momentum_new)
    average_new = average + (weight_new - average) / (count + 1.0)
    return (weight_new, momentum_new, average_new)


def on_device(
    images, nucleus, target_flow, cell_label, step_count,
    conv1_weight, conv1_momentum, conv1_average,
    conv2_weight, conv2_momentum, conv2_average,
    conv3_weight, conv3_momentum, conv3_average,
    style_weight, style_momentum, style_average,
    head_weight, head_momentum, head_average,
    biases, bias_momentum, bias_average,
):
    tiles = lax.axis_size("tile")
    me = lax.axis_index("tile")
    crops, _, height, cols = images.shape
    rows, width = height // 2, cols // 2
    pixel_count = lax.axis_size("img") * tiles * crops * height * cols
    grad_scale = 1.0 / math.sqrt(pixel_count)
    coarse_count = tiles * rows * width

    def sds(shape, dtype=f32):
        return jax.ShapeDtypeStruct(shape, dtype)

    def params(**more):
        return pltpu.CompilerParams(vmem_limit_bytes=60 * 2**20, **more)

    def remote(collective_id):
        return pltpu.CompilerParams(collective_id=collective_id, has_side_effects=True)

    images_count = lax.axis_size("img")
    edges = jnp.stack([-me * rows, (tiles - me) * rows]).astype(jnp.int32)
    bias_row = jnp.pad(biases.reshape(1, -1), ((0, 7), (0, 256 - biases.shape[0])))
    edge = (crops, 2, HALO, cols)
    x_lo, x_hi, t_lo, t_hi = pl.pallas_call(
        lambda *refs: halo_kernel(tiles, *refs),
        out_shape=(sds(edge, bf16), sds(edge, bf16), sds(edge, jnp.int32), sds(edge, jnp.int32)),
        in_specs=[ANY] * 2,
        out_specs=[ANY] * 4,
        scratch_shapes=[DMA((4,)), DMA((4,))],
        compiler_params=remote(1),
        name="halo",
    )(images, target_flow)
    w1, w2, w3, wd3, wd2, wh, wht, b1, b2, bh = pl.pallas_call(
        weight_kernel,
        out_shape=(
            sds((128, 32), bf16),
            sds((CH_TWO, 9 * CH_ONE), bf16),
            sds((256, 9 * CH_TWO), bf16),
            sds((128, 16 * CH_ONE), bf16),
            sds((CH_ONE, 9 * CH_TWO), bf16),
            sds((16, 128), bf16),
            sds((128, 16), bf16),
            sds((128, 128)),
            sds((64, 128)),
            sds((16, 128)),
        ),
        in_specs=[VMEM] * 5,
        out_specs=[VMEM] * 10,
        scratch_shapes=[pltpu.VMEM((32, 128), f32)],
        compiler_params=params(),
        name="weights",
    )(conv1_weight, conv2_weight, conv3_weight, head_weight, bias_row)

    y, targets, h1, pool, h2, style_part = pl.pallas_call(
        first_kernel,
        out_shape=(
            sds((crops, 16 * (rows + 7), width), bf16),
            sds((crops, width // 128, 16 * (rows + 2), 128)),
            sds((crops, 128 * (rows + 3), width), bf16),
            sds((crops, 32 * (rows + 3), width), bf16),
            sds((crops, 64 * (rows + 4), width), bf16),
            sds((8, 128)),
        ),
        in_specs=[SMEM, SMEM] + [VMEM] * 11,
        out_specs=[VMEM] * 6,
        scratch_shapes=[pltpu.VMEM((crops, 96 * (rows + 6), width), bf16)],
        compiler_params=params(),
        name="forward_one_two",
    )(edges, nucleus, images, x_lo, x_hi, target_flow, t_lo, t_hi, cell_label, w1, b1, w2, b2)

    style_total = pl.pallas_call(
        lambda *refs: sum_kernel(tiles, *refs),
        out_shape=sds((8, 128)),
        in_specs=[VMEM],
        out_specs=VMEM,
        scratch_shapes=[pltpu.VMEM((tiles, 8, 128), f32), DMA((tiles,)), DMA((tiles,))],
        compiler_params=remote(2),
        name="style_sum",
    )(style_part)

    rim = (crops, 128, width)
    gc, rim_lo, rim_hi, go, k3, head, style, sums_a, sg = pl.pallas_call(
        lambda *refs: second_kernel(grad_scale, float(coarse_count), *refs),
        out_shape=(
            sds((crops, 64 * (rows + 2), width)),
            sds(rim, bf16),
            sds(rim, bf16),
            sds((crops, 16 * rows, width), bf16),
            sds((144, 128)),
            sds((16, 128)),
            sds((16, 128)),
            sds((8, 128)),
            sds((8, 128)),
        ),
        in_specs=[SMEM] + [VMEM] * 11,
        out_specs=[VMEM] * 9,
        scratch_shapes=[
            pltpu.VMEM((crops, 192 * (rows + 4), width), bf16),
            pltpu.VMEM((crops, 128 * (rows + 2), width), bf16),
            pltpu.VMEM((crops, 128 * (rows + 2), width), bf16),
            pltpu.VMEM((crops, width // 128, 16 * (rows + 2), 128), f32),
            pltpu.VMEM((crops, width // 128, 16 * rows, 128), f32),
            pltpu.VMEM((crops, 256 * (rows + 4), width), bf16),
            pltpu.VMEM((9 * CH_TWO, 128), f32),
        ],
        compiler_params=params(),
        name="forward_three_back",
    )(edges, h1, h2, targets, style_total, bias_row, style_weight, w3, wh, wht, wd3, bh)

    sg_total, rim_up, rim_dn = pl.pallas_call(
        lambda *refs: sum_rim_kernel(tiles, *refs),
        out_shape=(sds((8, 128)), sds(rim, bf16), sds(rim, bf16)),
        in_specs=[VMEM, ANY, ANY],
        out_specs=[VMEM, ANY, ANY],
        scratch_shapes=[
            pltpu.VMEM((tiles, 8, 128), f32), DMA((tiles,)), DMA((tiles,)), DMA((2,)), DMA((2,)),
        ],
        compiler_params=remote(3),
        name="style_grad_sum",
    )(sg, rim_lo, rim_hi)

    k2, d1, sums_b = pl.pallas_call(
        lambda *refs: third_kernel(float(coarse_count), *refs),
        out_shape=(sds((160, 128)), sds((32, 128)), sds((8, 128))),
        in_specs=[SMEM] + [VMEM] * 13,
        out_specs=[VMEM] * 3,
        scratch_shapes=[
            pltpu.VMEM((crops, 192 * (rows + 2), width), bf16),
            pltpu.VMEM((crops, 96 * (rows + 2), width), bf16),
            pltpu.VMEM((9 * CH_ONE, CH_TWO), f32),
        ],
        compiler_params=params(),
        name="back_two_one",
    )(edges, gc, rim_up, rim_dn, style_total, sg_total, style_weight, h2, pool, h1, y, go, wd2, wht)

    part = 8 * pl.cdiv(sum(PART_ROWS), 8 * tiles)
    summed = pl.pallas_call(
        lambda *refs: reduce_kernel(tiles, images_count, part, *refs),
        out_shape=sds((part * tiles, 128)),
        in_specs=[VMEM] * 7,
        out_specs=VMEM,
        scratch_shapes=[
            pltpu.VMEM((part * tiles, 128), f32),
            pltpu.VMEM((tiles, part, 128), f32),
            pltpu.VMEM((part, 128), f32),
            pltpu.VMEM((images_count, part, 128), f32),
            pltpu.VMEM((part * tiles, 128), f32),
            DMA((tiles,)), DMA((tiles,)), DMA((images_count,)), DMA((images_count,)), DMA((tiles,)), DMA((tiles,)),
        ],
        compiler_params=remote(4),
        name="gradient_sum",
    )(k3, k2, d1, head, style, sums_a, sums_b)

    olds = (
        conv1_weight, conv1_momentum, conv1_average,
        conv2_weight, conv2_momentum, conv2_average,
        conv3_weight, conv3_momentum, conv3_average,
        style_weight, style_momentum, style_average,
        head_weight, head_momentum, head_average,
    )
    tail, *news = pl.pallas_call(
        lambda *refs: update_kernel(float(pixel_count), *refs),
        out_shape=(sds((8, 256)),) + tuple(sds(v.shape) for v in olds),
        in_specs=[SMEM] + [VMEM] * 16,
        out_specs=[VMEM] * 16,
        compiler_params=params(),
        name="update",
    )(step_count, summed, *olds)
    grad_bias = tail[0, 0 : biases.shape[0]]
    last = nesterov(biases, grad_bias, bias_momentum, bias_average, step_count[0].astype(f32))
    return (tail[1, 0:1], *news, *last)


def solution(mesh):
    return jax.shard_map(
        on_device,
        mesh=mesh,
        in_specs=(
            P("img", None, "tile", None),
            P("img"),
            P("img", None, "tile", None),
            P("img", "tile", None),
        )
        + (P(),) * 19,
        out_specs=(P(),) * 19,
        check_vma=False,
    )
```

```python
import math

import jax
import jax.numpy as jnp
from jax import lax
from jax.experimental import pallas as pl
from jax.experimental.pallas import tpu as pltpu
from jax.sharding import PartitionSpec as P

CH_ONE = 32
CH_TWO = 64
OUT_CH = 3

momentum_rate = 0.9
learn_rate = 0.02
decay_rate = 0.0001
norm_eps = 1e-05
highest = lax.Precision.HIGHEST
f32 = jnp.float32
bf16 = jnp.bfloat16

HALO = 8
VMEM = pl.BlockSpec(memory_space=pltpu.VMEM)
SMEM = pl.BlockSpec(memory_space=pltpu.SMEM)
ANY = pl.BlockSpec(memory_space=pl.ANY)
MESH = pl.DeviceIdType.MESH
DMA = pltpu.SemaphoreType.DMA

PART_ROWS = (144, 160, 32, 16, 16, 8)


def dot(a, b):
    return jnp.dot(a, b, preferred_element_type=f32)


def dot_nt(a, b, precision=None):
    return lax.dot_general(a, b, (((1,), (1,)), ((), ())), preferred_element_type=f32, precision=precision)


def from_left(x, crops=1):
    lane = lax.broadcasted_iota(jnp.int32, x.shape, 1)
    return jnp.where(lane % (x.shape[1] // crops) == 0, 0.0, pltpu.roll(x, 1, 1))


def from_right(x, crops=1):
    width = x.shape[1] // crops
    lane = lax.broadcasted_iota(jnp.int32, x.shape, 1)
    return jnp.where(lane % width == width - 1, 0.0, pltpu.roll(x, x.shape[1] - 1, 1))


def three_columns(mid, crops):
    x = mid.astype(f32)
    return jnp.concatenate([from_left(x, crops).astype(bf16), mid, from_right(x, crops).astype(bf16)], axis=0)


def crop_rows(crops, lanes):
    row = lax.broadcasted_iota(jnp.int32, (8, lanes), 0)
    lane = lax.broadcasted_iota(jnp.int32, (8, lanes), 1)
    return jnp.where(lane // (lanes // crops) == row, 1.0, 0.0).astype(bf16)


def repeat_rows(count, step, body):
    def run(k, carry):
        body([k * step + j for j in range(step)])
        return carry

    lax.fori_loop(0, count // step, run, 0)


def turn(x, by, axis):
    by = by % x.shape[axis]
    return pltpu.roll(x, by, axis) if by else x


def lane_group(x, group, size=32):
    lane = lax.broadcasted_iota(jnp.int32, x.shape, 1)
    return jnp.where(lane // size == group, x, 0.0)


def over_phases(x):
    return (x + turn(x, 32, 1)) + (turn(x, 64, 1) + turn(x, 96, 1))


def as_column(row):
    return jnp.transpose(jnp.broadcast_to(row, (128, 128)))


def fold_lanes(x):
    total = x[:, 0:128]
    for k in range(1, x.shape[1] // 128):
        total = total + x[:, 128 * k : 128 * (k + 1)]
    return total


def wide(tile, width):
    return jnp.concatenate([tile] * (width // 128), axis=1)


def rows_of(ref, start, size):
    return ref[pl.ds(pl.multiple_of(start, 16), size), :]


def put_rows(ref, start, value):
    ref[pl.ds(pl.multiple_of(start, 16), value.shape[0]), :] = value


def put_lanes(ref, start, value):
    for k in range(value.shape[1] // 128):
        ref[k, pl.ds(pl.multiple_of(start, 16), value.shape[0]), :] = value[:, 128 * k : 128 * (k + 1)]


def get_lanes(ref, start, size, stride=None):
    spot = pl.ds(start, size, stride=stride) if stride else pl.ds(pl.multiple_of(start, 16), size)
    return jnp.concatenate([ref[k, spot, :] for k in range(ref.shape[0])], axis=1)


def strip_edges(tiles, rows):
    me = lax.axis_index("tile")
    return -me * rows, (tiles - me) * rows


def valid(row, edge):
    return jnp.where((row >= edge[0]) & (row < edge[1]), 1.0, 0.0).astype(f32)


def meet(sizes):
    gate = pltpu.get_barrier_semaphore()
    for axis, count in sizes:
        me = lax.axis_index(axis)
        for j in range(1, count):
            pl.semaphore_signal(gate, inc=1, device_id={axis: lax.rem(me + j, count)}, device_id_type=MESH)
    pl.semaphore_wait(gate, sum(count - 1 for _, count in sizes))


def send_all(count, axis, source, target, send_sem, recv_sem):
    me = lax.axis_index(axis)
    copies = []
    for j in range(1, count):
        to = lax.rem(me + j, count)
        copy = pltpu.make_async_remote_copy(
            src_ref=source(to), dst_ref=target, send_sem=send_sem.at[j - 1], recv_sem=recv_sem.at[j - 1],
            device_id={axis: to}, device_id_type=MESH,
        )
        copy.start()
        copies.append(copy)
    return copies


def in_order(ref, count):
    total = ref[0]
    for k in range(1, count):
        total = total + ref[k]
    return total


def meet_next(tiles):
    gate = pltpu.get_barrier_semaphore()
    me = lax.axis_index("tile")

    @pl.when(me > 0)
    def _():
        pl.semaphore_signal(gate, inc=1, device_id={"tile": me - 1}, device_id_type=MESH)

    @pl.when(me < tiles - 1)
    def _():
        pl.semaphore_signal(gate, inc=1, device_id={"tile": me + 1}, device_id_type=MESH)

    pl.semaphore_wait(gate, jnp.minimum(me, 1) + jnp.minimum(tiles - 1 - me, 1))


def swap_edges(tiles, pairs, send_sem, recv_sem):
    me = lax.axis_index("tile")
    copies = []
    for k, (low, high, from_before, from_after) in enumerate(pairs):
        down = pltpu.make_async_remote_copy(
            src_ref=high, dst_ref=from_before, send_sem=send_sem.at[2 * k], recv_sem=recv_sem.at[2 * k],
            device_id={"tile": jnp.minimum(me + 1, tiles - 1)}, device_id_type=MESH,
        )
        up = pltpu.make_async_remote_copy(
            src_ref=low, dst_ref=from_after, send_sem=send_sem.at[2 * k + 1], recv_sem=recv_sem.at[2 * k + 1],
            device_id={"tile": jnp.maximum(me - 1, 0)}, device_id_type=MESH,
        )
        copies.append((down, up))

    @pl.when(me < tiles - 1)
    def _():
        for down, _up in copies:
            down.start()

    @pl.when(me > 0)
    def _():
        for _down, up in copies:
            up.start()

    def finish():
        @pl.when(me < tiles - 1)
        def _():
            for down, up in copies:
                down.wait_send()
                up.wait_recv()

        @pl.when(me > 0)
        def _():
            for down, up in copies:
                up.wait_send()
                down.wait_recv()

    return finish


def halo_kernel(tiles, x_ref, t_ref, x_lo, x_hi, t_lo, t_hi, send_sem, recv_sem):
    meet_next(tiles)
    last = x_ref.shape[2] - HALO
    finish = swap_edges(
        tiles,
        [
            (ref.at[:, :, pl.ds(0, HALO), :], ref.at[:, :, pl.ds(last, HALO), :], lo, hi)
            for ref, lo, hi in ((x_ref, x_lo, x_hi), (t_ref, t_lo, t_hi))
        ],
        send_sem, recv_sem,
    )
    finish()


def sum_kernel(tiles, x_ref, o_ref, got, send_sem, recv_sem):
    me = lax.axis_index("tile")
    got[me] = x_ref[...]
    meet((("tile", tiles),))
    copies = send_all(tiles, "tile", lambda to: x_ref, got.at[me], send_sem, recv_sem)
    for copy in copies:
        copy.wait()
    o_ref[...] = in_order(got, tiles)


def sum_rim_kernel(tiles, x_ref, lo_ref, hi_ref, o_ref, up_ref, dn_ref, got, send_sem, recv_sem, rim_send, rim_recv):
    me = lax.axis_index("tile")
    got[me] = x_ref[...]
    meet((("tile", tiles),))
    finish = swap_edges(tiles, [(lo_ref, hi_ref, up_ref, dn_ref)], rim_send, rim_recv)
    copies = send_all(tiles, "tile", lambda to: x_ref, got.at[me], send_sem, recv_sem)
    for copy in copies:
        copy.wait()
    o_ref[...] = in_order(got, tiles)
    finish()


def reduce_kernel(
    tiles, images, part, k3_ref, k2_ref, k1_ref, head_ref, style_ref, sums_a, sums_b, o_ref,
    pay, got, own, met, full, send_one, recv_one, send_two, recv_two, send_three, recv_three,
):
    me, mine = lax.axis_index("tile"), lax.axis_index("img")
    start = 0
    for ref, rows in zip((k3_ref, k2_ref, k1_ref, head_ref, style_ref), PART_ROWS):
        pay[start : start + rows, :] = ref[...]
        start += rows
    pay[start : start + 8, :] = sums_a[...] + sums_b[...]
    start += 8
    if start < part * tiles:
        pay[start : part * tiles, :] = jnp.zeros((part * tiles - start, 128), f32)
    meet((("tile", tiles), ("img", images)))

    def block(ref, k):
        return ref.at[pl.ds(pl.multiple_of(k * part, 8), part), :]

    got[me] = pay[pl.ds(pl.multiple_of(me * part, 8), part), :]
    for copy in send_all(tiles, "tile", lambda to: block(pay, to), got.at[me], send_one, recv_one):
        copy.wait()
    own[...] = in_order(got, tiles)
    met[mine] = own[...]
    for copy in send_all(images, "img", lambda to: own, met.at[mine], send_two, recv_two):
        copy.wait()
    total = in_order(met, images)
    full[pl.ds(pl.multiple_of(me * part, 8), part), :] = total
    copies = send_all(tiles, "tile", lambda to: block(full, me), block(full, me), send_three, recv_three)
    for copy in copies:
        copy.wait()
    o_ref[...] = full[...]


def weight_kernel(
    k1_ref, k2_ref, k3_ref, kh_ref, bias_ref,
    w1_ref, w2_ref, w3_ref, wd3_ref, wd2_ref, wh_ref, wht_ref, b1_ref, b2_ref, b3_ref, bh_ref,
    base_ref,
):
    base_ref[...] = jnp.zeros_like(base_ref)
    for a in range(3):
        for b in range(3):
            for i in range(2):
                base_ref[8 * a + 4 * i + b : 8 * a + 4 * i + b + 1, 0:32] = k1_ref[a, b, i : i + 1, :]
    base = base_ref[...]
    w1t = jnp.zeros((32, 128), f32)
    for p in range(4):
        w1t = w1t + turn(turn(base, 8 * (p // 2) + p % 2, 0), 32 * p, 1)
    w1_ref[...] = jnp.transpose(w1t).astype(bf16)

    k2 = [[k2_ref[a, b].astype(bf16).astype(f32) for b in range(3)] for a in range(3)]
    w2t = jnp.concatenate([k2[a][b] for a in range(3) for b in range(3)], axis=0)
    w2_ref[...] = jnp.transpose(w2t).astype(bf16)
    wd2_ref[...] = jnp.concatenate([k2[2 - s][2 - t] for s in range(3) for t in range(3)], axis=1).astype(bf16)

    def tap_sum(first, second):
        total = None
        for a in first:
            for b in second:
                total = k3[a][b] if total is None else total + k3[a][b]
        return jnp.zeros((CH_ONE, CH_TWO), f32) if total is None else total

    k3 = [[k3_ref[a, b].astype(bf16).astype(f32) for b in range(3)] for a in range(3)]
    up = [[[a for a in range(3) if (p + a + 1) // 2 == r] for r in range(3)] for p in range(2)]
    for p in range(4):
        w3 = jnp.concatenate([tap_sum(up[p // 2][r], up[p % 2][c]) for r in range(3) for c in range(3)], axis=1)
        w3_hi = w3.astype(bf16)
        w3_ref[32 * p : 32 * (p + 1), :] = w3_hi
        w3_ref[128 + 32 * p : 160 + 32 * p, :] = (w3 - w3_hi.astype(f32)).astype(bf16)
    down = ((2,), (1, 2), (0, 1), (0,))
    wd3 = jnp.transpose(jnp.concatenate([tap_sum(down[r], down[c]) for r in range(4) for c in range(4)], axis=0))
    wd3_hi = wd3.astype(bf16)
    wd3_ref[0:64, :] = wd3_hi
    wd3_ref[64:128, :] = (wd3 - wd3_hi.astype(f32)).astype(bf16)

    row = lax.broadcasted_iota(jnp.int32, (16, 128), 0)
    lane = lax.broadcasted_iota(jnp.int32, (16, 128), 1)
    wh = jnp.zeros((16, 128), f32)
    for o in range(OUT_CH):
        one = jnp.concatenate([kh_ref[o : o + 1, :]] * 4, axis=1)
        wh = jnp.where(row // 4 == o, jnp.broadcast_to(one, (16, 128)), wh)
    wh = jnp.where(row % 4 == lane // 32, wh, 0.0)
    wh_ref[...] = wh.astype(bf16)
    wht_ref[...] = jnp.transpose(wh).astype(bf16)

    bias = bias_ref[...].reshape(1, -1)
    b1 = bias[:, 0:32]
    b1_ref[...] = as_column(jnp.concatenate([b1] * 4, axis=1))
    b2 = bias[:, 32:96]
    b2_ref[...] = as_column(jnp.concatenate([b2] * 2, axis=1))[0:64]
    b3_ref[...] = jnp.zeros_like(b3_ref)
    b3_ref[0:1, :] = jnp.concatenate([bias[:, 96:128] + bias[:, 128:160]] * 4, axis=1)
    bh = jnp.zeros((16, 128), f32)
    for o in range(OUT_CH):
        bh = jnp.where(row // 4 == o, jnp.broadcast_to(bias[:, 160 + o : 161 + o], (16, 128)), bh)
    bh_ref[...] = bh


def split_columns(x, select):
    even, odd = [], []
    for k in range(x.shape[1] // 256):
        piece = dot(x[:, 256 * k : 256 * (k + 1)], select)
        even.append(piece[:, 0:128])
        odd.append(piece[:, 128:256])
    return jnp.concatenate(even, axis=1), jnp.concatenate(odd, axis=1)


def first_kernel(
    tiles,
    nucleus_ref, x_ref, x_lo, x_hi, t_ref, t_lo, t_hi, label_ref, w1_ref, b1_ref, w2_ref, b2_ref,
    y_ref, t_out, h1_ref, x2_ref, x3_ref, style_ref,
):
    crops = x_ref.shape[0]
    width = x_ref.shape[3] // 2
    lanes = crops * width
    height = x_ref.shape[2]
    rows = height // 2
    edge = strip_edges(tiles, rows)
    r_id = lax.broadcasted_iota(jnp.int32, (256, 256), 0)
    c_id = lax.broadcasted_iota(jnp.int32, (256, 256), 1)
    select = jnp.where(r_id == 2 * (c_id % 128) + c_id // 128, 1.0, 0.0).astype(bf16)
    x_rows = 2 * (height + 2 * HALO)
    y_rows = y_ref.shape[0]
    ri = lax.broadcasted_iota(jnp.int32, (y_rows, 4 * x_rows), 0)
    ci = lax.broadcasted_iota(jnp.int32, (y_rows, 4 * x_rows), 1)
    fine = 2 * (ri // 16) + (ri // 8) % 2 - 7
    channel = (ri // 4) % 2
    source = jnp.where(
        fine < 0,
        channel * HALO + fine + HALO,
        jnp.where(
            fine < height,
            2 * HALO + channel * height + fine,
            2 * HALO + 2 * height + channel * HALO + fine - height,
        ),
    )
    perm_x = jnp.where(ci == (ri % 4) * x_rows + source, 1.0, 0.0).astype(bf16)
    t_rows = 3 * height + 4 * HALO
    ri = lax.broadcasted_iota(jnp.int32, (t_out.shape[1], 2 * t_rows), 0)
    ci = lax.broadcasted_iota(jnp.int32, (t_out.shape[1], 2 * t_rows), 1)
    part = (ri // 4) % 4
    fine = 2 * (ri // 16) + (ri // 2) % 2 - 2
    source = jnp.where(
        fine < 0,
        3 * height + part * HALO + fine + HALO,
        jnp.where(fine < height, part * height + fine, 3 * height + 2 * HALO + part * HALO + fine - height),
    )
    outside = (fine < 0) | (fine >= height)
    known = (part < 2) | ((part == 2) & jnp.logical_not(outside))
    perm_t = jnp.where((ci == (ri % 2) * t_rows + source) & known, 1.0, 0.0).astype(bf16)
    has_up, has_dn = edge[0] < 0, edge[1] > rows

    def both_columns(of_crop):
        even, odd = [], []
        for c in range(crops):
            first, second = split_columns(of_crop(c), select)
            even.append(first)
            odd.append(second)
        return jnp.concatenate(even, axis=1), jnp.concatenate(odd, axis=1)

    def image_rows(c):
        pieces = [jnp.where(has_up, x_lo[c, k].astype(f32), 0.0) for k in range(2)]
        pieces += [x_ref[c, k].astype(f32) for k in range(2)]
        pieces += [jnp.where(has_dn, x_hi[c, k].astype(f32), 0.0) for k in range(2)]
        return jnp.concatenate(pieces, axis=0).astype(bf16)

    def target_rows(c):
        pieces = [t_ref[c, 0].astype(f32), t_ref[c, 1].astype(f32), label_ref[c].astype(f32)]
        pieces += [jnp.where(has_up, t_lo[c, k], 0).astype(f32) for k in range(2)]
        pieces += [jnp.where(has_dn, t_hi[c, k], 0).astype(f32) for k in range(2)]
        return jnp.concatenate(pieces, axis=0).astype(bf16)

    even, odd = both_columns(image_rows)
    row = lax.broadcasted_iota(jnp.int32, (x_rows, lanes), 0)
    crop = lax.broadcasted_iota(jnp.int32, (x_rows, lanes), 1) // width
    second = ((row >= HALO) & (row < 2 * HALO)) | (row >= x_rows - HALO)
    second = second | ((row >= 2 * HALO + height) & (row < 2 * HALO + 2 * height))
    gate = jnp.ones((x_rows, lanes), f32)
    for c in range(crops):
        gate = jnp.where(second & (crop == c), nucleus_ref[c].astype(f32), gate)
    even, odd = even * gate, odd * gate
    stack = jnp.concatenate([from_left(odd, crops), even, odd, from_right(even, crops)], axis=0)
    y_ref[...] = dot(perm_x, stack.astype(bf16)).astype(bf16)
    even, odd = both_columns(target_rows)
    put_lanes(t_out, 0, dot(perm_t, jnp.concatenate([even, odd], axis=0).astype(bf16)))
    ones = crop_rows(crops, lanes)
    style_ref[...] = jnp.zeros_like(style_ref)

    def conv_one(ks):
        pre = [dot(w1_ref[...], rows_of(y_ref, k * 16, 32)) for k in ks]
        for k, p in zip(ks, pre):
            keep = valid(k - 3, edge)
            hidden = (jnp.maximum(p + wide(b1_ref[...], lanes), 0.0) * keep).astype(bf16)
            put_rows(h1_ref, k * 128, hidden)
            h = hidden.astype(f32)
            pooled = (0.25 * ((h[0:32] + h[32:64]) + (h[64:96] + h[96:128]))).astype(bf16)
            put_rows(x2_ref, k * 96, three_columns(pooled, crops))

    def conv_two(qs):
        pre = [dot(w2_ref[...], rows_of(x2_ref, q * 96, 288)) for q in qs]
        sums = 0.0
        for q, p in zip(qs, pre):
            row = q - 2
            keep = valid(row, edge)
            own = jnp.where((row >= 0) & (row < rows), 1.0, 0.0).astype(f32)
            hidden = (jnp.maximum(p + wide(b2_ref[...], lanes), 0.0) * keep).astype(bf16)
            put_rows(x3_ref, q * 192, three_columns(hidden, crops))
            sums = sums + dot_nt(ones, hidden) * own
        style_ref[:, 0:64] += sums

    repeat_rows(rows + 6, 2, conv_one)
    repeat_rows(rows + 4, 2, conv_two)


def second_kernel(
    tiles, crops, scale, coarse_count,
    h1_ref, x3_ref, t_ref, total_ref, b3_ref, ws_ref, w3_ref, wh_ref, wht_ref, wd3_ref, bh_ref,
    gc_ref, rim_lo, rim_hi, go_out, k3_ref, head_ref, style_ref, sums_ref, sg_ref,
    h3_ref, m_ref, fe_ref, go_ref, g3_ref, d3_ref,
):
    lanes = h1_ref.shape[1]
    width = lanes // crops
    rows = go_out.shape[0] // 16
    edge = strip_edges(tiles, rows)
    raw = total_ref[:, 0:64] / coarse_count
    unit = raw * lax.rsqrt(jnp.mean(raw * raw, axis=1, keepdims=True) + norm_eps)
    vec = dot_nt(unit, ws_ref[...], highest)
    vec = jnp.concatenate([vec] * 4, axis=1) + b3_ref[0:1, :]
    bias3 = [as_column(vec[c : c + 1]) for c in range(crops)]
    bias3 = jnp.concatenate([wide(b, width) for b in bias3], axis=1)
    ones = crop_rows(crops, lanes)

    def forward(ks):
        pre = [dot(w3_ref[...], rows_of(x3_ref, k * 192, 576)) for k in ks]
        hs = []
        for k, both in zip(ks, pre):
            p = both[0:128] + both[128:256] + bias3
            h1 = rows_of(h1_ref, (k + 2) * 128, 128).astype(f32)
            h3 = (jnp.maximum(p, 0.0) + h1).astype(bf16)
            put_rows(h3_ref, k * 128, h3)
            put_rows(m_ref, k * 128, jnp.where(p > 0, 1.0, 0.0).astype(bf16))
            hs.append(h3)
        outs = [dot(wh_ref[...], h) for h in hs]
        for k, o in zip(ks, outs):
            o = o + wide(bh_ref[...], lanes)
            t = get_lanes(t_ref, k * 16, 16)
            fe = (o[0:8] - 0.25 * t[0:8]) * valid(k - 1, edge)
            put_lanes(fe_ref, k * 16, jnp.concatenate([fe, o[8:16]], axis=0))

    repeat_rows(rows + 2, 2, forward)

    r_id = lax.broadcasted_iota(jnp.int32, (rows, lanes), 0)
    above = jnp.where(r_id - 1 >= edge[0], 1.0, 0.0)
    below = jnp.where(r_id + 1 < edge[1], 1.0, 0.0)
    go_ref[...] = jnp.zeros_like(go_ref)

    def at(part, off):
        return get_lanes(fe_ref, 16 * (1 + off) + part, rows, 16)

    def column_part(pr, off):
        odd, even = at(4 + 2 * pr + 1, off), at(4 + 2 * pr, off)
        return 0.5 * (odd - from_left(odd, crops)), 0.5 * (from_right(even, crops) - even)

    loss = jnp.zeros((rows, 128), f32)
    e0 = [at(k, 0) for k in range(4)]
    e1 = [at(4 + k, 0) for k in range(4)]
    cols0, cols1 = column_part(0, 0), column_part(1, 0)
    cols_up, cols_dn = column_part(1, -1), column_part(0, 1)
    spread = [None] * 4
    g_up, g_dn = [None] * 2, [None] * 2
    for pc in range(2):
        f_up, f_dn = at(2 + pc, -1), at(pc, 1)
        spread[pc] = 0.5 * (e0[2 + pc] - f_up) + cols0[pc]
        spread[2 + pc] = 0.5 * (f_dn - e0[pc]) + cols1[pc]
        g_up[pc] = 2.0 * scale * above * (0.5 * (e0[pc] - at(pc, -1)) + cols_up[pc])
        g_dn[pc] = 2.0 * scale * below * (0.5 * (at(2 + pc, 1) - e0[2 + pc]) + cols_dn[pc])
    g = [2.0 * scale * v for v in spread]
    for pr in range(2):
        even, odd = g[2 * pr], g[2 * pr + 1]
        col = [0.5 * (odd - from_left(odd, crops)), 0.5 * (from_right(even, crops) - even)]
        for pc in range(2):
            k = 2 * pr + pc
            if pr == 0:
                row_part = 0.5 * (g[2 + pc] - g_up[pc])
            else:
                row_part = 0.5 * (g_dn[pc] - g[pc])
            logit = at(8 + k, 0)
            label = get_lanes(t_ref, 16 + 8 + k, rows, 16)
            ex = jnp.exp(-jnp.abs(logit))
            sig = jnp.where(logit >= 0, 1.0, ex) / (1.0 + ex)
            grads = (2.0 * scale * e0[k] - row_part, 2.0 * scale * e1[k] - col[pc], scale * (sig - label))
            for part in range(OUT_CH):
                for j in range(lanes // 128):
                    go_ref[j, pl.ds(4 * part + k, rows, stride=16), :] = grads[part][:, 128 * j : 128 * (j + 1)]
            term = jnp.maximum(logit, 0.0) + jnp.log1p(ex) - label * logit
            loss = loss + fold_lanes(e0[k] * e0[k] + e1[k] * e1[k] + spread[k] * spread[k] + term)

    sums_ref[...] = jnp.zeros_like(sums_ref)
    sums_ref[4:5, :] = jnp.sum(loss, axis=0, keepdims=True)
    head_ref[...] = jnp.zeros_like(head_ref)
    sg_ref[...] = jnp.zeros_like(sg_ref)
    d3_ref[...] = jnp.zeros_like(d3_ref)
    for k in (0, 1, rows + 2, rows + 3):
        g3_ref[256 * k : 256 * (k + 1), :] = jnp.zeros((256, lanes), bf16)

    def backward(rs):
        gos = [get_lanes(go_ref, r * 16, 16).astype(bf16) for r in rs]
        gts = [dot(wht_ref[...], go) for go in gos]
        head, gsum, sg, d3 = 0.0, 0.0, 0.0, 0.0
        for r, go, gt in zip(rs, gos, gts):
            put_rows(go_out, r * 16, go)
            spot = (r + 1) * 128
            head = head + dot_nt(go, rows_of(h3_ref, spot, 128))
            gsum = gsum + dot_nt(ones, go)
            g = gt.astype(bf16).astype(f32) * rows_of(m_ref, spot, 128).astype(f32)
            gb = g.astype(bf16)
            sg = sg + dot_nt(ones, gb)
            parts = []
            for pr in range(2):
                even, odd = g[64 * pr : 64 * pr + 32], g[64 * pr + 32 : 64 * pr + 64]
                parts += [
                    from_left(odd, crops).astype(bf16),
                    gb[64 * pr : 64 * pr + 64],
                    from_right(even, crops).astype(bf16),
                ]
            put_rows(g3_ref, (r + 2) * 256, jnp.concatenate(parts, axis=0))
            d3 = d3 + dot_nt(rows_of(x3_ref, (r + 1) * 192, 576), gb)
        head_ref[...] += head
        sums_ref[3:4, 0:16] += jnp.sum(gsum, axis=0, keepdims=True)
        sg_ref[...] += sg
        d3_ref[...] += d3

    repeat_rows(rows, 2, backward)

    def down(ks):
        both = [dot(wd3_ref[...], rows_of(g3_ref, k * 256 + 128, 512)) for k in ks]
        for k, b in zip(ks, both):
            put_rows(gc_ref, k * 64, b[0:64] + b[64:128])

    repeat_rows(rows + 2, 2, down)
    rim_lo[...] = gc_ref[0:128, :].astype(bf16)
    rim_hi[...] = gc_ref[64 * rows : 64 * rows + 128, :].astype(bf16)

    d3 = jnp.transpose(d3_ref[...])
    for block in range(5):
        packed = jnp.zeros((CH_ONE, 128), f32)
        for tap in range(2 * block, min(2 * block + 2, 9)):
            a, b = tap // 3, tap % 3
            total = jnp.zeros((CH_ONE, CH_TWO), f32)
            for p in range(4):
                n = 3 * ((p // 2 + a + 1) // 2) + (p % 2 + b + 1) // 2
                total = total + d3[32 * p : 32 * (p + 1), 64 * n : 64 * (n + 1)]
            if tap % 2 == 0:
                packed = jnp.concatenate([total, packed[:, 64:128]], axis=1)
            else:
                packed = jnp.concatenate([packed[:, 0:64], total], axis=1)
        if block < 4:
            k3_ref[32 * block : 32 * (block + 1), :] = packed
        else:
            k3_ref[128:144, :] = jnp.concatenate([packed[0:16, 0:64], packed[16:32, 0:64]], axis=1)
    outer = jnp.zeros((CH_ONE, 128), f32)
    for c in range(crops):
        outer = outer + as_column(over_phases(sg_ref[c : c + 1, :]))[0:32] * jnp.concatenate([unit[c : c + 1]] * 2, axis=1)
        sums_ref[2:3, :] += sg_ref[c : c + 1, :]
    style_ref[...] = jnp.concatenate([outer[0:16, 0:64], outer[16:32, 0:64]], axis=1)


def third_kernel(
    tiles, crops, coarse_count,
    gc_ref, up_ref, dn_ref, total_ref, sg_ref, ws_ref, x3_ref, x2_ref, h1_ref, y_ref, go_ref, wd2_ref, wht_ref,
    k2_ref, d1_ref, sums_ref,
    g2_ref, d2_ref,
):
    lanes = h1_ref.shape[1]
    width = lanes // crops
    rows = go_ref.shape[0] // 16
    edge = strip_edges(tiles, rows)
    style_raw = total_ref[:, 0:64] / coarse_count
    inv = lax.rsqrt(jnp.mean(style_raw * style_raw, axis=1, keepdims=True) + norm_eps)
    style_grad = over_phases(sg_ref[...])[:, 0:32]
    grad_unit = jnp.dot(style_grad, ws_ref[...], precision=highest, preferred_element_type=f32)
    grad_raw = inv * grad_unit - inv * inv * inv * style_raw * jnp.mean(style_raw * grad_unit, axis=1, keepdims=True)
    grad_raw = jnp.concatenate([grad_raw / coarse_count] * 2, axis=1)
    raw = jnp.concatenate([wide(as_column(grad_raw[c : c + 1])[0:64], width) for c in range(crops)], axis=1)
    ones = jnp.ones((8, lanes), bf16)
    sums_ref[...] = jnp.zeros_like(sums_ref)
    d2_ref[...] = jnp.zeros_like(d2_ref)
    d1_ref[...] = jnp.zeros_like(d1_ref)

    def masked(k, extra=None):
        coarse = rows_of(gc_ref, k * 64, 64)
        if extra is not None:
            coarse = coarse + extra
        grad = (coarse + raw).astype(bf16).astype(f32)
        h2 = rows_of(x3_ref, (k + 1) * 192 + 64, 64).astype(f32)
        put_rows(g2_ref, k * 192, three_columns(jnp.where(h2 > 0, grad, 0.0).astype(bf16), crops))

    up = jnp.where(edge[0] < 0, up_ref[...].astype(f32), 0.0)
    dn = jnp.where(edge[1] > rows, dn_ref[...].astype(f32), 0.0)
    masked(0, up[0:64])
    masked(1, up[64:128])
    masked(rows, dn[0:64])
    masked(rows + 1, dn[64:128])

    def inner(ks):
        for k in ks:
            masked(k + 2)

    repeat_rows(rows - 2, 2, inner)

    def backward(rs):
        gps = [dot(wd2_ref[...], rows_of(g2_ref, r * 192, 576)) for r in rs]
        gts = [dot(wht_ref[...], rows_of(go_ref, r * 16, 16)) for r in rs]
        d2, d1, sum_two, sum_one = 0.0, 0.0, 0.0, 0.0
        for r, gp, gt in zip(rs, gps, gts):
            g2 = rows_of(g2_ref, (r + 1) * 192 + 64, 64)
            d2 = d2 + dot_nt(rows_of(x2_ref, (r + 2) * 96, 288), g2)
            sum_two = sum_two + dot_nt(ones, g2)
            gp = 0.25 * gp.astype(bf16).astype(f32)
            g1 = (jnp.concatenate([gp] * 4, axis=0) + gt.astype(bf16).astype(f32)).astype(bf16).astype(f32)
            h1 = rows_of(h1_ref, (r + 3) * 128, 128).astype(f32)
            gb = jnp.where(h1 > 0, g1, 0.0).astype(bf16)
            sum_one = sum_one + dot_nt(ones, gb)
            d1 = d1 + dot_nt(rows_of(y_ref, (r + 3) * 16, 32), gb)
        d2_ref[...] += d2
        d1_ref[...] += d1
        sums_ref[0:1, :] += sum_one[0:1]
        sums_ref[1:2, 0:64] += sum_two[0:1]

    repeat_rows(rows, 2, backward)
    rest = jnp.concatenate([d2_ref[160:288, :], jnp.zeros((32, 64), f32)], axis=0)
    k2_ref[...] = jnp.concatenate([d2_ref[0:160, :], rest], axis=1)


def update_kernel(pixel_count, count_ref, sum_ref, *refs):
    olds, outs, loss_ref = refs[:18], refs[18:36], refs[36]
    starts = [sum(PART_ROWS[:k]) for k in range(len(PART_ROWS))]
    rate = 1.0 / (jnp.zeros((8, 128), f32) + (count_ref[0].astype(f32) + 1.0))

    def step(index, spot, grad):
        weight, momentum, average = (olds[3 * index + k][spot] for k in range(3))
        decayed = grad + decay_rate * weight
        momentum = momentum_rate * momentum + decayed
        new = weight - learn_rate * (decayed + momentum_rate * momentum)
        outs[3 * index][spot] = new
        outs[3 * index + 1][spot] = momentum
        outs[3 * index + 2][spot] = average + (new - average) * rate[0:1, 0:1]

    d1 = sum_ref[starts[2] : starts[2] + 32, :]
    total = jnp.zeros((32, 128), f32)
    for p in range(4):
        total = total + turn(turn(d1, -32 * p, 1), -(8 * (p // 2) + p % 2), 0)
    for a in range(3):
        for b in range(3):
            for i in range(2):
                k = 8 * a + 4 * i + b
                step(0, (a, b, slice(i, i + 1), slice(None)), total[k : k + 1, 0:32])
    for tap in range(9):
        a, b = tap // 3, tap % 3
        first = starts[1] + 32 * (tap % 5)
        half = 64 * (tap // 5)
        step(1, (a, b), sum_ref[first : first + 32, half : half + 64])
        if tap < 8:
            first = starts[0] + 32 * (tap // 2)
            lane = 64 * (tap % 2)
            grad = sum_ref[first : first + 32, lane : lane + 64]
        else:
            first = starts[0] + 128
            grad = jnp.concatenate([sum_ref[first : first + 16, 64 * k : 64 * (k + 1)] for k in range(2)], axis=0)
        step(2, (a, b), grad)
    first = starts[4]
    grad = jnp.concatenate([sum_ref[first : first + 16, 64 * k : 64 * (k + 1)] for k in range(2)], axis=0)
    step(3, (slice(None), slice(None)), grad)
    head = sum_ref[starts[3] : starts[3] + 16, :]
    total = jnp.zeros((16, 128), f32)
    for p in range(4):
        total = total + turn(turn(head, -32 * p, 1), -p, 0)
    total = jnp.concatenate([total[4 * o : 4 * o + 1] for o in range(OUT_CH)], axis=0)
    step(4, (slice(None), slice(None)), total[:, 0:32])
    sums = sum_ref[starts[5] : starts[5] + 8, :]
    one, three = over_phases(sums[0:1]), over_phases(sums[2:3])
    lane = lax.broadcasted_iota(jnp.int32, (1, 128), 1)
    low = jnp.where(lane < 32, one, jnp.where(lane < 96, turn(sums[1:2], 32, 1), three))
    ends = sums[3:4]
    ends = (ends + turn(ends, -1, 1)) + (turn(ends, -2, 1) + turn(ends, -3, 1))
    high = jnp.where(lane < 32, three, 0.0)
    for o in range(OUT_CH):
        high = jnp.where(lane == 32 + o, turn(ends, 32 + o - 4 * o, 1), high)
    grad = jnp.concatenate([low, high], axis=1)[:, 0 : olds[15].shape[0]]
    weight, momentum, average = (olds[15 + k][...].reshape(1, -1) for k in range(3))
    decayed = grad + decay_rate * weight
    momentum = momentum_rate * momentum + decayed
    new = weight - learn_rate * (decayed + momentum_rate * momentum)
    average = average + (new - average) * rate[0:1, 0:1]
    for k, value in enumerate((new, momentum, average)):
        outs[15 + k][...] = value.reshape(-1)
    loss_ref[0] = jnp.sum(sums[4:5]) / pixel_count


def on_device(
    images, nucleus, target_flow, cell_label, step_count,
    conv1_weight, conv1_momentum, conv1_average,
    conv2_weight, conv2_momentum, conv2_average,
    conv3_weight, conv3_momentum, conv3_average,
    style_weight, style_momentum, style_average,
    head_weight, head_momentum, head_average,
    biases, bias_momentum, bias_average,
):
    tiles = lax.axis_size("tile")
    crops, _, height, cols = images.shape
    rows, width = height // 2, cols // 2
    pixel_count = lax.axis_size("img") * tiles * crops * height * cols
    grad_scale = 1.0 / math.sqrt(pixel_count)
    coarse_count = tiles * rows * width

    def sds(shape, dtype=f32):
        return jax.ShapeDtypeStruct(shape, dtype)

    lanes = crops * width
    images_count = lax.axis_size("img")

    def params(mib):
        return pltpu.CompilerParams(vmem_limit_bytes=mib * 2**20)

    def remote(collective_id):
        return pltpu.CompilerParams(collective_id=collective_id, has_side_effects=True, vmem_limit_bytes=8 * 2**20)

    def other_way(w):
        return jnp.swapaxes(w, -1, -2)

    third = tuple(other_way(w) for w in (conv3_weight, conv3_momentum, conv3_average))
    style = tuple(other_way(w) for w in (style_weight, style_momentum, style_average))
    head = tuple(other_way(w) for w in (head_weight, head_momentum, head_average))

    edge = (crops, 2, HALO, cols)
    x_lo, x_hi, t_lo, t_hi = pl.pallas_call(
        lambda *refs: halo_kernel(tiles, *refs),
        out_shape=(sds(edge, bf16), sds(edge, bf16), sds(edge, jnp.int32), sds(edge, jnp.int32)),
        in_specs=[ANY] * 2,
        out_specs=[ANY] * 4,
        scratch_shapes=[DMA((4,)), DMA((4,))],
        compiler_params=remote(1),
        name="halo",
    )(images, target_flow)
    w1, w2, w3, wd3, wd2, wh, wht, b1, b2, b3, bh = pl.pallas_call(
        weight_kernel,
        out_shape=(
            sds((128, 32), bf16),
            sds((CH_TWO, 9 * CH_ONE), bf16),
            sds((256, 9 * CH_TWO), bf16),
            sds((128, 16 * CH_ONE), bf16),
            sds((CH_ONE, 9 * CH_TWO), bf16),
            sds((16, 128), bf16),
            sds((128, 16), bf16),
            sds((128, 128)),
            sds((64, 128)),
            sds((8, 128)),
            sds((16, 128)),
        ),
        in_specs=[VMEM] * 5,
        out_specs=[VMEM] * 11,
        scratch_shapes=[pltpu.VMEM((32, 128), f32)],
        compiler_params=params(8),
        name="weights",
    )(conv1_weight, conv2_weight, third[0], head[0], biases)

    y, targets, h1, x2, x3, style_part = pl.pallas_call(
        lambda *refs: first_kernel(tiles, *refs),
        out_shape=(
            sds((16 * (rows + 7), lanes), bf16),
            sds((lanes // 128, 16 * (rows + 2), 128)),
            sds((128 * (rows + 6), lanes), bf16),
            sds((96 * (rows + 6), lanes), bf16),
            sds((192 * (rows + 4), lanes), bf16),
            sds((8, 128)),
        ),
        in_specs=[SMEM] + [VMEM] * 11,
        out_specs=[VMEM] * 6,
        compiler_params=params(12),
        name="forward_one_two",
    )(nucleus, images, x_lo, x_hi, target_flow, t_lo, t_hi, cell_label, w1, b1, w2, b2)

    style_total = pl.pallas_call(
        lambda *refs: sum_kernel(tiles, *refs),
        out_shape=sds((8, 128)),
        in_specs=[VMEM],
        out_specs=VMEM,
        scratch_shapes=[pltpu.VMEM((tiles, 8, 128), f32), DMA((tiles,)), DMA((tiles,))],
        compiler_params=remote(2),
        name="style_sum",
    )(style_part)

    rim = (128, lanes)
    gc, rim_lo, rim_hi, go, k3, head_part, style_grad, sums_a, sg = pl.pallas_call(
        lambda *refs: second_kernel(tiles, crops, grad_scale, float(coarse_count), *refs),
        out_shape=(
            sds((64 * (rows + 2), lanes)),
            sds(rim, bf16),
            sds(rim, bf16),
            sds((16 * rows, lanes), bf16),
            sds((144, 128)),
            sds((16, 128)),
            sds((16, 128)),
            sds((8, 128)),
            sds((8, 128)),
        ),
        in_specs=[VMEM] * 11,
        out_specs=[VMEM] * 9,
        scratch_shapes=[
            pltpu.VMEM((128 * (rows + 2), lanes), bf16),
            pltpu.VMEM((128 * (rows + 2), lanes), bf16),
            pltpu.VMEM((lanes // 128, 16 * (rows + 2), 128), f32),
            pltpu.VMEM((lanes // 128, 16 * rows, 128), f32),
            pltpu.VMEM((256 * (rows + 4), lanes), bf16),
            pltpu.VMEM((9 * CH_TWO, 128), f32),
        ],
        compiler_params=params(30),
        name="forward_three_back",
    )(h1, x3, targets, style_total, b3, style[0], w3, wh, wht, wd3, bh)

    sg_total, rim_up, rim_dn = pl.pallas_call(
        lambda *refs: sum_rim_kernel(tiles, *refs),
        out_shape=(sds((8, 128)), sds(rim, bf16), sds(rim, bf16)),
        in_specs=[VMEM, ANY, ANY],
        out_specs=[VMEM, ANY, ANY],
        scratch_shapes=[
            pltpu.VMEM((tiles, 8, 128), f32), DMA((tiles,)), DMA((tiles,)), DMA((2,)), DMA((2,)),
        ],
        compiler_params=remote(3),
        name="style_grad_sum",
    )(sg, rim_lo, rim_hi)

    k2, d1, sums_b = pl.pallas_call(
        lambda *refs: third_kernel(tiles, crops, float(coarse_count), *refs),
        out_shape=(sds((160, 128)), sds((32, 128)), sds((8, 128))),
        in_specs=[VMEM] * 13,
        out_specs=[VMEM] * 3,
        scratch_shapes=[
            pltpu.VMEM((192 * (rows + 2), lanes), bf16),
            pltpu.VMEM((9 * CH_ONE, CH_TWO), f32),
        ],
        compiler_params=params(16),
        name="back_two_one",
    )(gc, rim_up, rim_dn, style_total, sg_total, style[0], x3, x2, h1, y, go, wd2, wht)

    part = 8 * pl.cdiv(sum(PART_ROWS), 8 * tiles)
    summed = pl.pallas_call(
        lambda *refs: reduce_kernel(tiles, images_count, part, *refs),
        out_shape=sds((part * tiles, 128)),
        in_specs=[VMEM] * 7,
        out_specs=VMEM,
        scratch_shapes=[
            pltpu.VMEM((part * tiles, 128), f32),
            pltpu.VMEM((tiles, part, 128), f32),
            pltpu.VMEM((part, 128), f32),
            pltpu.VMEM((images_count, part, 128), f32),
            pltpu.VMEM((part * tiles, 128), f32),
            DMA((tiles,)), DMA((tiles,)), DMA((images_count,)), DMA((images_count,)), DMA((tiles,)), DMA((tiles,)),
        ],
        compiler_params=remote(4),
        name="gradient_sum",
    )(k3, k2, d1, head_part, style_grad, sums_a, sums_b)

    olds = (
        (conv1_weight, conv1_momentum, conv1_average)
        + (conv2_weight, conv2_momentum, conv2_average)
        + third + style + head
        + (biases, bias_momentum, bias_average)
    )
    news = pl.pallas_call(
        lambda *refs: update_kernel(float(pixel_count), *refs),
        out_shape=tuple(sds(v.shape) for v in olds) + (sds((1,)),),
        in_specs=[SMEM] + [VMEM] * 19,
        out_specs=[VMEM] * 18 + [SMEM],
        compiler_params=params(16),
        name="update",
    )(step_count, summed, *olds)
    return (news[18], *news[0:6], *(other_way(w) for w in news[6:15]), *news[15:18])


def solution(mesh):
    return jax.shard_map(
        on_device,
        mesh=mesh,
        in_specs=(
            P("img", None, "tile", None),
            P("img"),
            P("img", None, "tile", None),
            P("img", "tile", None),
        )
        + (P(),) * 19,
        out_specs=(P(),) * 19,
        check_vma=False,
    )
```

```python
import math

import jax
import jax.numpy as jnp
from jax import lax
from jax.experimental import pallas as pl
from jax.experimental.pallas import tpu as pltpu
from jax.sharding import PartitionSpec as P

CH_ONE = 32
CH_TWO = 64
OUT_CH = 3

momentum_rate = 0.9
learn_rate = 0.02
decay_rate = 0.0001
norm_eps = 1e-05
highest = lax.Precision.HIGHEST
f32 = jnp.float32
bf16 = jnp.bfloat16

HALO = 8
VMEM = pl.BlockSpec(memory_space=pltpu.VMEM)
SMEM = pl.BlockSpec(memory_space=pltpu.SMEM)
ANY = pl.BlockSpec(memory_space=pl.ANY)
MESH = pl.DeviceIdType.MESH
DMA = pltpu.SemaphoreType.DMA

PART_ROWS = (144, 160, 32, 16, 16, 8)


def dot(a, b):
    return jnp.dot(a, b, preferred_element_type=f32)


def dot_nt(a, b, precision=None):
    return lax.dot_general(a, b, (((1,), (1,)), ((), ())), preferred_element_type=f32, precision=precision)


def from_left(x, crops=1):
    lane = lax.broadcasted_iota(jnp.int32, x.shape, 1)
    return jnp.where(lane % (x.shape[1] // crops) == 0, 0.0, pltpu.roll(x, 1, 1))


def from_right(x, crops=1):
    width = x.shape[1] // crops
    lane = lax.broadcasted_iota(jnp.int32, x.shape, 1)
    return jnp.where(lane % width == width - 1, 0.0, pltpu.roll(x, x.shape[1] - 1, 1))


def three_columns(mid, crops):
    x = mid.astype(f32)
    return jnp.concatenate([from_left(x, crops).astype(bf16), mid, from_right(x, crops).astype(bf16)], axis=0)


def crop_rows(crops, lanes):
    row = lax.broadcasted_iota(jnp.int32, (8, lanes), 0)
    lane = lax.broadcasted_iota(jnp.int32, (8, lanes), 1)
    return jnp.where(lane // (lanes // crops) == row, 1.0, 0.0).astype(bf16)


def repeat_rows(count, step, body):
    def run(k, carry):
        body([k * step + j for j in range(step)])
        return carry

    lax.fori_loop(0, count // step, run, 0)


def turn(x, by, axis):
    by = by % x.shape[axis]
    return pltpu.roll(x, by, axis) if by else x


def lane_group(x, group, size=32):
    lane = lax.broadcasted_iota(jnp.int32, x.shape, 1)
    return jnp.where(lane // size == group, x, 0.0)


def over_phases(x):
    return (x + turn(x, 32, 1)) + (turn(x, 64, 1) + turn(x, 96, 1))


def as_column(row):
    return jnp.transpose(jnp.broadcast_to(row, (128, 128)))


def fold_lanes(x):
    total = x[:, 0:128]
    for k in range(1, x.shape[1] // 128):
        total = total + x[:, 128 * k : 128 * (k + 1)]
    return total


def wide(tile, width):
    return jnp.concatenate([tile] * (width // 128), axis=1)


def rows_of(ref, start, size):
    return ref[pl.ds(pl.multiple_of(start, 16), size), :]


def put_rows(ref, start, value):
    ref[pl.ds(pl.multiple_of(start, 16), value.shape[0]), :] = value


def put_lanes(ref, start, value):
    for k in range(value.shape[1] // 128):
        ref[k, pl.ds(pl.multiple_of(start, 16), value.shape[0]), :] = value[:, 128 * k : 128 * (k + 1)]


def get_lanes(ref, start, size, stride=None):
    spot = pl.ds(start, size, stride=stride) if stride else pl.ds(pl.multiple_of(start, 16), size)
    return jnp.concatenate([ref[k, spot, :] for k in range(ref.shape[0])], axis=1)


def strip_edges(tiles, rows):
    me = lax.axis_index("tile")
    return -me * rows, (tiles - me) * rows


def valid(row, edge):
    return jnp.where((row >= edge[0]) & (row < edge[1]), 1.0, 0.0).astype(f32)


def greet(sizes):
    gate = pltpu.get_barrier_semaphore()
    for axis, count in sizes:
        me = lax.axis_index(axis)
        for j in range(1, count):
            pl.semaphore_signal(gate, inc=1, device_id={axis: lax.rem(me + j, count)}, device_id_type=MESH)
    return lambda: pl.semaphore_wait(gate, sum(count - 1 for _, count in sizes))


def meet(sizes):
    greet(sizes)()


def send_all(count, axis, source, target, send_sem, recv_sem):
    me = lax.axis_index(axis)
    copies = []
    for j in range(1, count):
        to = lax.rem(me + j, count)
        copy = pltpu.make_async_remote_copy(
            src_ref=source(to), dst_ref=target, send_sem=send_sem.at[j - 1], recv_sem=recv_sem.at[j - 1],
            device_id={axis: to}, device_id_type=MESH,
        )
        copy.start()
        copies.append(copy)
    return copies


def in_order(ref, count):
    total = ref[0]
    for k in range(1, count):
        total = total + ref[k]
    return total


def swap_edges(tiles, pairs, send_sem, recv_sem):
    me = lax.axis_index("tile")
    copies = []
    for k, (low, high, from_before, from_after) in enumerate(pairs):
        down = pltpu.make_async_remote_copy(
            src_ref=high, dst_ref=from_before, send_sem=send_sem.at[2 * k], recv_sem=recv_sem.at[2 * k],
            device_id={"tile": jnp.minimum(me + 1, tiles - 1)}, device_id_type=MESH,
        )
        up = pltpu.make_async_remote_copy(
            src_ref=low, dst_ref=from_after, send_sem=send_sem.at[2 * k + 1], recv_sem=recv_sem.at[2 * k + 1],
            device_id={"tile": jnp.maximum(me - 1, 0)}, device_id_type=MESH,
        )
        copies.append((down, up))

    @pl.when(me < tiles - 1)
    def _():
        for down, _up in copies:
            down.start()

    @pl.when(me > 0)
    def _():
        for _down, up in copies:
            up.start()

    def finish():
        @pl.when(me < tiles - 1)
        def _():
            for down, up in copies:
                down.wait_send()
                up.wait_recv()

        @pl.when(me > 0)
        def _():
            for down, up in copies:
                up.wait_send()
                down.wait_recv()

    return finish


def sum_over_tiles(tiles, source, got, send_sem, recv_sem):
    me = lax.axis_index("tile")
    got[me] = source[...]
    copies = send_all(tiles, "tile", lambda to: source, got.at[me], send_sem, recv_sem)
    for copy in copies:
        copy.wait()
    return in_order(got, tiles)


def sum_rim_kernel(tiles, x_ref, lo_ref, hi_ref, o_ref, up_ref, dn_ref, got, send_sem, recv_sem, rim_send, rim_recv):
    meet((("tile", tiles),))
    finish = swap_edges(tiles, [(lo_ref, hi_ref, up_ref, dn_ref)], rim_send, rim_recv)
    o_ref[...] = sum_over_tiles(tiles, x_ref, got, send_sem, recv_sem)
    finish()


def reduce_kernel(
    tiles, images, part, k3_ref, k2_ref, k1_ref, head_ref, style_ref, sums_a, sums_b, o_ref,
    pay, got, own, met, full, send_one, recv_one, send_two, recv_two, send_three, recv_three,
):
    me, mine = lax.axis_index("tile"), lax.axis_index("img")
    start = 0
    for ref, rows in zip((k3_ref, k2_ref, k1_ref, head_ref, style_ref), PART_ROWS):
        pay[start : start + rows, :] = ref[...]
        start += rows
    pay[start : start + 8, :] = sums_a[...] + sums_b[...]
    start += 8
    if start < part * tiles:
        pay[start : part * tiles, :] = jnp.zeros((part * tiles - start, 128), f32)
    meet((("tile", tiles), ("img", images)))

    def block(ref, k):
        return ref.at[pl.ds(pl.multiple_of(k * part, 8), part), :]

    got[me] = pay[pl.ds(pl.multiple_of(me * part, 8), part), :]
    for copy in send_all(tiles, "tile", lambda to: block(pay, to), got.at[me], send_one, recv_one):
        copy.wait()
    own[...] = in_order(got, tiles)
    met[mine] = own[...]
    for copy in send_all(images, "img", lambda to: own, met.at[mine], send_two, recv_two):
        copy.wait()
    total = in_order(met, images)
    full[pl.ds(pl.multiple_of(me * part, 8), part), :] = total
    copies = send_all(tiles, "tile", lambda to: block(full, me), block(full, me), send_three, recv_three)
    for copy in copies:
        copy.wait()
    o_ref[...] = full[...]


def weight_tables(
    k1_ref, k2_ref, k3_ref, kh_ref, bias_ref,
    w1_ref, w2_ref, w3_ref, wd3_ref, wd2_ref, wh_ref, wht_ref, b1_ref, b2_ref, b3_ref, bh_ref,
    base_ref,
):
    base_ref[...] = jnp.zeros_like(base_ref)
    for a in range(3):
        for b in range(3):
            for i in range(2):
                base_ref[8 * a + 4 * i + b : 8 * a + 4 * i + b + 1, 0:32] = k1_ref[a, b, i : i + 1, :]
    base = base_ref[...]
    w1t = jnp.zeros((32, 128), f32)
    for p in range(4):
        w1t = w1t + turn(turn(base, 8 * (p // 2) + p % 2, 0), 32 * p, 1)
    w1_ref[...] = jnp.transpose(w1t).astype(bf16)

    k2 = [[k2_ref[a, b].astype(bf16).astype(f32) for b in range(3)] for a in range(3)]
    w2t = jnp.concatenate([k2[a][b] for a in range(3) for b in range(3)], axis=0)
    w2_ref[...] = jnp.transpose(w2t).astype(bf16)
    wd2_ref[...] = jnp.concatenate([k2[2 - s][2 - t] for s in range(3) for t in range(3)], axis=1).astype(bf16)

    def tap_sum(first, second):
        total = None
        for a in first:
            for b in second:
                total = k3[a][b] if total is None else total + k3[a][b]
        return jnp.zeros((CH_ONE, CH_TWO), f32) if total is None else total

    k3 = [[k3_ref[a, b].astype(bf16).astype(f32) for b in range(3)] for a in range(3)]
    up = [[[a for a in range(3) if (p + a + 1) // 2 == r] for r in range(3)] for p in range(2)]
    for p in range(4):
        w3 = jnp.concatenate([tap_sum(up[p // 2][r], up[p % 2][c]) for r in range(3) for c in range(3)], axis=1)
        w3_hi = w3.astype(bf16)
        w3_ref[32 * p : 32 * (p + 1), :] = w3_hi
        w3_ref[128 + 32 * p : 160 + 32 * p, :] = (w3 - w3_hi.astype(f32)).astype(bf16)
    down = ((2,), (1, 2), (0, 1), (0,))
    wd3 = jnp.transpose(jnp.concatenate([tap_sum(down[r], down[c]) for r in range(4) for c in range(4)], axis=0))
    wd3_hi = wd3.astype(bf16)
    wd3_ref[0:64, :] = wd3_hi
    wd3_ref[64:128, :] = (wd3 - wd3_hi.astype(f32)).astype(bf16)

    row = lax.broadcasted_iota(jnp.int32, (16, 128), 0)
    lane = lax.broadcasted_iota(jnp.int32, (16, 128), 1)
    wh = jnp.zeros((16, 128), f32)
    for o in range(OUT_CH):
        one = jnp.concatenate([kh_ref[o : o + 1, :]] * 4, axis=1)
        wh = jnp.where(row // 4 == o, jnp.broadcast_to(one, (16, 128)), wh)
    wh = jnp.where(row % 4 == lane // 32, wh, 0.0)
    wh_ref[...] = wh.astype(bf16)
    wht_ref[...] = jnp.transpose(wh).astype(bf16)

    bias = bias_ref[...].reshape(1, -1)
    b1 = bias[:, 0:32]
    b1_ref[...] = as_column(jnp.concatenate([b1] * 4, axis=1))
    b2 = bias[:, 32:96]
    b2_ref[...] = as_column(jnp.concatenate([b2] * 2, axis=1))[0:64]
    b3_ref[...] = jnp.zeros_like(b3_ref)
    b3_ref[0:1, :] = jnp.concatenate([bias[:, 96:128] + bias[:, 128:160]] * 4, axis=1)
    bh = jnp.zeros((16, 128), f32)
    for o in range(OUT_CH):
        bh = jnp.where(row // 4 == o, jnp.broadcast_to(bias[:, 160 + o : 161 + o], (16, 128)), bh)
    bh_ref[...] = bh


def split_columns(x, select):
    even, odd = [], []
    for k in range(x.shape[1] // 256):
        piece = dot(x[:, 256 * k : 256 * (k + 1)], select)
        even.append(piece[:, 0:128])
        odd.append(piece[:, 128:256])
    return jnp.concatenate(even, axis=1), jnp.concatenate(odd, axis=1)


def first_kernel(
    tiles,
    nucleus_ref, x_ref, t_ref, label_ref, k1_ref, k2_ref, k3_ref, kh_ref, bias_ref,
    y_ref, t_out, h1_ref, x2_ref, x3_ref, total_ref, w3_ref, wd3_ref, wd2_ref, wh_ref, wht_ref, b3_ref, bh_ref,
    x_lo, x_hi, t_lo, t_hi, w1_ref, w2_ref, b1_ref, b2_ref, base_ref, style_ref, got,
    halo_send, halo_recv, send_sem, recv_sem,
):
    arrived = greet((("tile", tiles),))
    weight_tables(
        k1_ref, k2_ref, k3_ref, kh_ref, bias_ref,
        w1_ref, w2_ref, w3_ref, wd3_ref, wd2_ref, wh_ref, wht_ref, b1_ref, b2_ref, b3_ref, bh_ref,
        base_ref,
    )
    arrived()
    last = x_ref.shape[2] - HALO
    finish = swap_edges(
        tiles,
        [
            (ref.at[:, :, pl.ds(0, HALO), :], ref.at[:, :, pl.ds(last, HALO), :], lo, hi)
            for ref, lo, hi in ((x_ref, x_lo, x_hi), (t_ref, t_lo, t_hi))
        ],
        halo_send, halo_recv,
    )
    crops = x_ref.shape[0]
    width = x_ref.shape[3] // 2
    lanes = crops * width
    height = x_ref.shape[2]
    rows = height // 2
    edge = strip_edges(tiles, rows)
    r_id = lax.broadcasted_iota(jnp.int32, (256, 256), 0)
    c_id = lax.broadcasted_iota(jnp.int32, (256, 256), 1)
    select = jnp.where(r_id == 2 * (c_id % 128) + c_id // 128, 1.0, 0.0).astype(bf16)
    x_rows = 2 * (height + 2 * HALO)
    y_rows = y_ref.shape[0]
    ri = lax.broadcasted_iota(jnp.int32, (y_rows, 4 * x_rows), 0)
    ci = lax.broadcasted_iota(jnp.int32, (y_rows, 4 * x_rows), 1)
    fine = 2 * (ri // 16) + (ri // 8) % 2 - 7
    channel = (ri // 4) % 2
    source = jnp.where(
        fine < 0,
        channel * HALO + fine + HALO,
        jnp.where(
            fine < height,
            2 * HALO + channel * height + fine,
            2 * HALO + 2 * height + channel * HALO + fine - height,
        ),
    )
    perm_x = jnp.where(ci == (ri % 4) * x_rows + source, 1.0, 0.0).astype(bf16)
    t_rows = 3 * height + 4 * HALO
    ri = lax.broadcasted_iota(jnp.int32, (t_out.shape[1], 2 * t_rows), 0)
    ci = lax.broadcasted_iota(jnp.int32, (t_out.shape[1], 2 * t_rows), 1)
    part = (ri // 4) % 4
    fine = 2 * (ri // 16) + (ri // 2) % 2 - 2
    source = jnp.where(
        fine < 0,
        3 * height + part * HALO + fine + HALO,
        jnp.where(fine < height, part * height + fine, 3 * height + 2 * HALO + part * HALO + fine - height),
    )
    outside = (fine < 0) | (fine >= height)
    known = (part < 2) | ((part == 2) & jnp.logical_not(outside))
    perm_t = jnp.where((ci == (ri % 2) * t_rows + source) & known, 1.0, 0.0).astype(bf16)
    has_up, has_dn = edge[0] < 0, edge[1] > rows

    def both_columns(of_crop):
        even, odd = [], []
        for c in range(crops):
            first, second = split_columns(of_crop(c), select)
            even.append(first)
            odd.append(second)
        return jnp.concatenate(even, axis=1), jnp.concatenate(odd, axis=1)

    def image_rows(c):
        pieces = [jnp.where(has_up, x_lo[c, k].astype(f32), 0.0) for k in range(2)]
        pieces += [x_ref[c, k].astype(f32) for k in range(2)]
        pieces += [jnp.where(has_dn, x_hi[c, k].astype(f32), 0.0) for k in range(2)]
        return jnp.concatenate(pieces, axis=0).astype(bf16)

    def target_rows(c):
        pieces = [t_ref[c, 0].astype(f32), t_ref[c, 1].astype(f32), label_ref[c].astype(f32)]
        pieces += [jnp.where(has_up, t_lo[c, k], 0).astype(f32) for k in range(2)]
        pieces += [jnp.where(has_dn, t_hi[c, k], 0).astype(f32) for k in range(2)]
        return jnp.concatenate(pieces, axis=0).astype(bf16)

    finish()
    even, odd = both_columns(image_rows)
    row = lax.broadcasted_iota(jnp.int32, (x_rows, lanes), 0)
    crop = lax.broadcasted_iota(jnp.int32, (x_rows, lanes), 1) // width
    second = ((row >= HALO) & (row < 2 * HALO)) | (row >= x_rows - HALO)
    second = second | ((row >= 2 * HALO + height) & (row < 2 * HALO + 2 * height))
    gate = jnp.ones((x_rows, lanes), f32)
    for c in range(crops):
        gate = jnp.where(second & (crop == c), nucleus_ref[c].astype(f32), gate)
    even, odd = even * gate, odd * gate
    stack = jnp.concatenate([from_left(odd, crops), even, odd, from_right(even, crops)], axis=0)
    y_ref[...] = dot(perm_x, stack.astype(bf16)).astype(bf16)
    even, odd = both_columns(target_rows)
    put_lanes(t_out, 0, dot(perm_t, jnp.concatenate([even, odd], axis=0).astype(bf16)))
    ones = crop_rows(crops, lanes)
    style_ref[...] = jnp.zeros_like(style_ref)

    def conv_one(ks):
        pre = [dot(w1_ref[...], rows_of(y_ref, k * 16, 32)) for k in ks]
        for k, p in zip(ks, pre):
            keep = valid(k - 3, edge)
            hidden = (jnp.maximum(p + wide(b1_ref[...], lanes), 0.0) * keep).astype(bf16)
            put_rows(h1_ref, k * 128, hidden)
            h = hidden.astype(f32)
            pooled = (0.25 * ((h[0:32] + h[32:64]) + (h[64:96] + h[96:128]))).astype(bf16)
            put_rows(x2_ref, k * 96, three_columns(pooled, crops))

    def conv_two(qs):
        pre = [dot(w2_ref[...], rows_of(x2_ref, q * 96, 288)) for q in qs]
        sums = 0.0
        for q, p in zip(qs, pre):
            row = q - 2
            keep = valid(row, edge)
            own = jnp.where((row >= 0) & (row < rows), 1.0, 0.0).astype(f32)
            hidden = (jnp.maximum(p + wide(b2_ref[...], lanes), 0.0) * keep).astype(bf16)
            put_rows(x3_ref, q * 192, three_columns(hidden, crops))
            sums = sums + dot_nt(ones, hidden) * own
        style_ref[:, 0:64] += sums

    repeat_rows(rows + 6, 2, conv_one)
    repeat_rows(rows + 4, 2, conv_two)
    total_ref[...] = sum_over_tiles(tiles, style_ref, got, send_sem, recv_sem)


def second_kernel(
    tiles, crops, scale, coarse_count,
    h1_ref, x3_ref, t_ref, total_ref, b3_ref, ws_ref, w3_ref, wh_ref, wht_ref, wd3_ref, bh_ref,
    gc_ref, rim_lo, rim_hi, go_out, k3_ref, head_ref, style_ref, sums_ref, sg_ref,
    h3_ref, m_ref, fe_ref, go_ref, g3_ref, d3_ref,
):
    lanes = h1_ref.shape[1]
    width = lanes // crops
    rows = go_out.shape[0] // 16
    edge = strip_edges(tiles, rows)
    raw = total_ref[:, 0:64] / coarse_count
    unit = raw * lax.rsqrt(jnp.mean(raw * raw, axis=1, keepdims=True) + norm_eps)
    vec = dot_nt(unit, ws_ref[...], highest)
    vec = jnp.concatenate([vec] * 4, axis=1) + b3_ref[0:1, :]
    bias3 = [as_column(vec[c : c + 1]) for c in range(crops)]
    bias3 = jnp.concatenate([wide(b, width) for b in bias3], axis=1)
    ones = crop_rows(crops, lanes)

    def forward(ks):
        pre = [dot(w3_ref[...], rows_of(x3_ref, k * 192, 576)) for k in ks]
        hs = []
        for k, both in zip(ks, pre):
            p = both[0:128] + both[128:256] + bias3
            h1 = rows_of(h1_ref, (k + 2) * 128, 128).astype(f32)
            h3 = (jnp.maximum(p, 0.0) + h1).astype(bf16)
            put_rows(h3_ref, k * 128, h3)
            put_rows(m_ref, k * 128, jnp.where(p > 0, 1.0, 0.0).astype(bf16))
            hs.append(h3)
        outs = [dot(wh_ref[...], h) for h in hs]
        for k, o in zip(ks, outs):
            o = o + wide(bh_ref[...], lanes)
            t = get_lanes(t_ref, k * 16, 16)
            fe = (o[0:8] - 0.25 * t[0:8]) * valid(k - 1, edge)
            put_lanes(fe_ref, k * 16, jnp.concatenate([fe, o[8:16]], axis=0))

    repeat_rows(rows + 2, 2, forward)

    r_id = lax.broadcasted_iota(jnp.int32, (rows, lanes), 0)
    above = jnp.where(r_id - 1 >= edge[0], 1.0, 0.0)
    below = jnp.where(r_id + 1 < edge[1], 1.0, 0.0)
    go_ref[...] = jnp.zeros_like(go_ref)

    def at(part, off):
        return get_lanes(fe_ref, 16 * (1 + off) + part, rows, 16)

    def column_part(pr, off):
        odd, even = at(4 + 2 * pr + 1, off), at(4 + 2 * pr, off)
        return 0.5 * (odd - from_left(odd, crops)), 0.5 * (from_right(even, crops) - even)

    loss = jnp.zeros((rows, 128), f32)
    e0 = [at(k, 0) for k in range(4)]
    e1 = [at(4 + k, 0) for k in range(4)]
    cols0, cols1 = column_part(0, 0), column_part(1, 0)
    cols_up, cols_dn = column_part(1, -1), column_part(0, 1)
    spread = [None] * 4
    g_up, g_dn = [None] * 2, [None] * 2
    for pc in range(2):
        f_up, f_dn = at(2 + pc, -1), at(pc, 1)
        spread[pc] = 0.5 * (e0[2 + pc] - f_up) + cols0[pc]
        spread[2 + pc] = 0.5 * (f_dn - e0[pc]) + cols1[pc]
        g_up[pc] = 2.0 * scale * above * (0.5 * (e0[pc] - at(pc, -1)) + cols_up[pc])
        g_dn[pc] = 2.0 * scale * below * (0.5 * (at(2 + pc, 1) - e0[2 + pc]) + cols_dn[pc])
    g = [2.0 * scale * v for v in spread]
    for pr in range(2):
        even, odd = g[2 * pr], g[2 * pr + 1]
        col = [0.5 * (odd - from_left(odd, crops)), 0.5 * (from_right(even, crops) - even)]
        for pc in range(2):
            k = 2 * pr + pc
            if pr == 0:
                row_part = 0.5 * (g[2 + pc] - g_up[pc])
            else:
                row_part = 0.5 * (g_dn[pc] - g[pc])
            logit = at(8 + k, 0)
            label = get_lanes(t_ref, 16 + 8 + k, rows, 16)
            ex = jnp.exp(-jnp.abs(logit))
            sig = jnp.where(logit >= 0, 1.0, ex) / (1.0 + ex)
            grads = (2.0 * scale * e0[k] - row_part, 2.0 * scale * e1[k] - col[pc], scale * (sig - label))
            for part in range(OUT_CH):
                for j in range(lanes // 128):
                    go_ref[j, pl.ds(4 * part + k, rows, stride=16), :] = grads[part][:, 128 * j : 128 * (j + 1)]
            term = jnp.maximum(logit, 0.0) + jnp.log1p(ex) - label * logit
            loss = loss + fold_lanes(e0[k] * e0[k] + e1[k] * e1[k] + spread[k] * spread[k] + term)

    sums_ref[...] = jnp.zeros_like(sums_ref)
    sums_ref[4:5, :] = jnp.sum(loss, axis=0, keepdims=True)
    head_ref[...] = jnp.zeros_like(head_ref)
    sg_ref[...] = jnp.zeros_like(sg_ref)
    d3_ref[...] = jnp.zeros_like(d3_ref)
    for k in (0, 1, rows + 2, rows + 3):
        g3_ref[256 * k : 256 * (k + 1), :] = jnp.zeros((256, lanes), bf16)

    def backward(rs):
        gos = [get_lanes(go_ref, r * 16, 16).astype(bf16) for r in rs]
        gts = [dot(wht_ref[...], go) for go in gos]
        head, gsum, sg, d3 = 0.0, 0.0, 0.0, 0.0
        for r, go, gt in zip(rs, gos, gts):
            put_rows(go_out, r * 16, go)
            spot = (r + 1) * 128
            head = head + dot_nt(go, rows_of(h3_ref, spot, 128))
            gsum = gsum + dot_nt(ones, go)
            g = gt.astype(bf16).astype(f32) * rows_of(m_ref, spot, 128).astype(f32)
            gb = g.astype(bf16)
            sg = sg + dot_nt(ones, gb)
            parts = []
            for pr in range(2):
                even, odd = g[64 * pr : 64 * pr + 32], g[64 * pr + 32 : 64 * pr + 64]
                parts += [
                    from_left(odd, crops).astype(bf16),
                    gb[64 * pr : 64 * pr + 64],
                    from_right(even, crops).astype(bf16),
                ]
            put_rows(g3_ref, (r + 2) * 256, jnp.concatenate(parts, axis=0))
            d3 = d3 + dot_nt(rows_of(x3_ref, (r + 1) * 192, 576), gb)
        head_ref[...] += head
        sums_ref[3:4, 0:16] += jnp.sum(gsum, axis=0, keepdims=True)
        sg_ref[...] += sg
        d3_ref[...] += d3

    repeat_rows(rows, 2, backward)

    def down(ks):
        both = [dot(wd3_ref[...], rows_of(g3_ref, k * 256 + 128, 512)) for k in ks]
        for k, b in zip(ks, both):
            put_rows(gc_ref, k * 64, b[0:64] + b[64:128])

    repeat_rows(rows + 2, 2, down)
    rim_lo[...] = gc_ref[0:128, :].astype(bf16)
    rim_hi[...] = gc_ref[64 * rows : 64 * rows + 128, :].astype(bf16)

    d3 = jnp.transpose(d3_ref[...])
    for block in range(5):
        packed = jnp.zeros((CH_ONE, 128), f32)
        for tap in range(2 * block, min(2 * block + 2, 9)):
            a, b = tap // 3, tap % 3
            total = jnp.zeros((CH_ONE, CH_TWO), f32)
            for p in range(4):
                n = 3 * ((p // 2 + a + 1) // 2) + (p % 2 + b + 1) // 2
                total = total + d3[32 * p : 32 * (p + 1), 64 * n : 64 * (n + 1)]
            if tap % 2 == 0:
                packed = jnp.concatenate([total, packed[:, 64:128]], axis=1)
            else:
                packed = jnp.concatenate([packed[:, 0:64], total], axis=1)
        if block < 4:
            k3_ref[32 * block : 32 * (block + 1), :] = packed
        else:
            k3_ref[128:144, :] = jnp.concatenate([packed[0:16, 0:64], packed[16:32, 0:64]], axis=1)
    outer = jnp.zeros((CH_ONE, 128), f32)
    for c in range(crops):
        outer = outer + as_column(over_phases(sg_ref[c : c + 1, :]))[0:32] * jnp.concatenate([unit[c : c + 1]] * 2, axis=1)
        sums_ref[2:3, :] += sg_ref[c : c + 1, :]
    style_ref[...] = jnp.concatenate([outer[0:16, 0:64], outer[16:32, 0:64]], axis=1)


def third_kernel(
    tiles, crops, coarse_count,
    gc_ref, up_ref, dn_ref, total_ref, sg_ref, ws_ref, x3_ref, x2_ref, h1_ref, y_ref, go_ref, wd2_ref, wht_ref,
    k2_ref, d1_ref, sums_ref,
    g2_ref, d2_ref,
):
    lanes = h1_ref.shape[1]
    width = lanes // crops
    rows = go_ref.shape[0] // 16
    edge = strip_edges(tiles, rows)
    style_raw = total_ref[:, 0:64] / coarse_count
    inv = lax.rsqrt(jnp.mean(style_raw * style_raw, axis=1, keepdims=True) + norm_eps)
    style_grad = over_phases(sg_ref[...])[:, 0:32]
    grad_unit = jnp.dot(style_grad, ws_ref[...], precision=highest, preferred_element_type=f32)
    grad_raw = inv * grad_unit - inv * inv * inv * style_raw * jnp.mean(style_raw * grad_unit, axis=1, keepdims=True)
    grad_raw = jnp.concatenate([grad_raw / coarse_count] * 2, axis=1)
    raw = jnp.concatenate([wide(as_column(grad_raw[c : c + 1])[0:64], width) for c in range(crops)], axis=1)
    ones = jnp.ones((8, lanes), bf16)
    sums_ref[...] = jnp.zeros_like(sums_ref)
    d2_ref[...] = jnp.zeros_like(d2_ref)
    d1_ref[...] = jnp.zeros_like(d1_ref)

    def masked(k, extra=None):
        coarse = rows_of(gc_ref, k * 64, 64)
        if extra is not None:
            coarse = coarse + extra
        grad = (coarse + raw).astype(bf16).astype(f32)
        h2 = rows_of(x3_ref, (k + 1) * 192 + 64, 64).astype(f32)
        put_rows(g2_ref, k * 192, three_columns(jnp.where(h2 > 0, grad, 0.0).astype(bf16), crops))

    up = jnp.where(edge[0] < 0, up_ref[...].astype(f32), 0.0)
    dn = jnp.where(edge[1] > rows, dn_ref[...].astype(f32), 0.0)
    masked(0, up[0:64])
    masked(1, up[64:128])
    masked(rows, dn[0:64])
    masked(rows + 1, dn[64:128])

    def inner(ks):
        for k in ks:
            masked(k + 2)

    repeat_rows(rows - 2, 2, inner)

    def backward(rs):
        gps = [dot(wd2_ref[...], rows_of(g2_ref, r * 192, 576)) for r in rs]
        gts = [dot(wht_ref[...], rows_of(go_ref, r * 16, 16)) for r in rs]
        d2, d1, sum_two, sum_one = 0.0, 0.0, 0.0, 0.0
        for r, gp, gt in zip(rs, gps, gts):
            g2 = rows_of(g2_ref, (r + 1) * 192 + 64, 64)
            d2 = d2 + dot_nt(rows_of(x2_ref, (r + 2) * 96, 288), g2)
            sum_two = sum_two + dot_nt(ones, g2)
            gp = 0.25 * gp.astype(bf16).astype(f32)
            g1 = (jnp.concatenate([gp] * 4, axis=0) + gt.astype(bf16).astype(f32)).astype(bf16).astype(f32)
            h1 = rows_of(h1_ref, (r + 3) * 128, 128).astype(f32)
            gb = jnp.where(h1 > 0, g1, 0.0).astype(bf16)
            sum_one = sum_one + dot_nt(ones, gb)
            d1 = d1 + dot_nt(rows_of(y_ref, (r + 3) * 16, 32), gb)
        d2_ref[...] += d2
        d1_ref[...] += d1
        sums_ref[0:1, :] += sum_one[0:1]
        sums_ref[1:2, 0:64] += sum_two[0:1]

    repeat_rows(rows, 2, backward)
    rest = jnp.concatenate([d2_ref[160:288, :], jnp.zeros((32, 64), f32)], axis=0)
    k2_ref[...] = jnp.concatenate([d2_ref[0:160, :], rest], axis=1)


def update_kernel(pixel_count, count_ref, sum_ref, *refs):
    olds, outs, loss_ref = refs[:18], refs[18:36], refs[36]
    starts = [sum(PART_ROWS[:k]) for k in range(len(PART_ROWS))]
    rate = 1.0 / (jnp.zeros((8, 128), f32) + (count_ref[0].astype(f32) + 1.0))

    def step(index, spot, grad):
        weight, momentum, average = (olds[3 * index + k][spot] for k in range(3))
        decayed = grad + decay_rate * weight
        momentum = momentum_rate * momentum + decayed
        new = weight - learn_rate * (decayed + momentum_rate * momentum)
        outs[3 * index][spot] = new
        outs[3 * index + 1][spot] = momentum
        outs[3 * index + 2][spot] = average + (new - average) * rate[0:1, 0:1]

    d1 = sum_ref[starts[2] : starts[2] + 32, :]
    total = jnp.zeros((32, 128), f32)
    for p in range(4):
        total = total + turn(turn(d1, -32 * p, 1), -(8 * (p // 2) + p % 2), 0)
    for a in range(3):
        for b in range(3):
            for i in range(2):
                k = 8 * a + 4 * i + b
                step(0, (a, b, slice(i, i + 1), slice(None)), total[k : k + 1, 0:32])
    for tap in range(9):
        a, b = tap // 3, tap % 3
        first = starts[1] + 32 * (tap % 5)
        half = 64 * (tap // 5)
        step(1, (a, b), sum_ref[first : first + 32, half : half + 64])
        if tap < 8:
            first = starts[0] + 32 * (tap // 2)
            lane = 64 * (tap % 2)
            grad = sum_ref[first : first + 32, lane : lane + 64]
        else:
            first = starts[0] + 128
            grad = jnp.concatenate([sum_ref[first : first + 16, 64 * k : 64 * (k + 1)] for k in range(2)], axis=0)
        step(2, (a, b), grad)
    first = starts[4]
    grad = jnp.concatenate([sum_ref[first : first + 16, 64 * k : 64 * (k + 1)] for k in range(2)], axis=0)
    step(3, (slice(None), slice(None)), grad)
    head = sum_ref[starts[3] : starts[3] + 16, :]
    total = jnp.zeros((16, 128), f32)
    for p in range(4):
        total = total + turn(turn(head, -32 * p, 1), -p, 0)
    total = jnp.concatenate([total[4 * o : 4 * o + 1] for o in range(OUT_CH)], axis=0)
    step(4, (slice(None), slice(None)), total[:, 0:32])
    sums = sum_ref[starts[5] : starts[5] + 8, :]
    one, three = over_phases(sums[0:1]), over_phases(sums[2:3])
    lane = lax.broadcasted_iota(jnp.int32, (1, 128), 1)
    low = jnp.where(lane < 32, one, jnp.where(lane < 96, turn(sums[1:2], 32, 1), three))
    ends = sums[3:4]
    ends = (ends + turn(ends, -1, 1)) + (turn(ends, -2, 1) + turn(ends, -3, 1))
    high = jnp.where(lane < 32, three, 0.0)
    for o in range(OUT_CH):
        high = jnp.where(lane == 32 + o, turn(ends, 32 + o - 4 * o, 1), high)
    grad = jnp.concatenate([low, high], axis=1)[:, 0 : olds[15].shape[0]]
    weight, momentum, average = (olds[15 + k][...].reshape(1, -1) for k in range(3))
    decayed = grad + decay_rate * weight
    momentum = momentum_rate * momentum + decayed
    new = weight - learn_rate * (decayed + momentum_rate * momentum)
    average = average + (new - average) * rate[0:1, 0:1]
    for k, value in enumerate((new, momentum, average)):
        outs[15 + k][...] = value.reshape(-1)
    loss_ref[0] = jnp.sum(sums[4:5]) / pixel_count


def on_device(
    images, nucleus, target_flow, cell_label, step_count,
    conv1_weight, conv1_momentum, conv1_average,
    conv2_weight, conv2_momentum, conv2_average,
    conv3_weight, conv3_momentum, conv3_average,
    style_weight, style_momentum, style_average,
    head_weight, head_momentum, head_average,
    biases, bias_momentum, bias_average,
):
    tiles = lax.axis_size("tile")
    crops, _, height, cols = images.shape
    rows, width = height // 2, cols // 2
    pixel_count = lax.axis_size("img") * tiles * crops * height * cols
    grad_scale = 1.0 / math.sqrt(pixel_count)
    coarse_count = tiles * rows * width

    def sds(shape, dtype=f32):
        return jax.ShapeDtypeStruct(shape, dtype)

    lanes = crops * width
    images_count = lax.axis_size("img")

    def params(mib):
        return pltpu.CompilerParams(vmem_limit_bytes=mib * 2**20)

    def remote(collective_id, mib=8):
        return pltpu.CompilerParams(collective_id=collective_id, has_side_effects=True, vmem_limit_bytes=mib * 2**20)

    def other_way(w):
        return jnp.swapaxes(w, -1, -2)

    third = tuple(other_way(w) for w in (conv3_weight, conv3_momentum, conv3_average))
    style = tuple(other_way(w) for w in (style_weight, style_momentum, style_average))
    head = tuple(other_way(w) for w in (head_weight, head_momentum, head_average))

    edge = (crops, 2, HALO, cols)
    y, targets, h1, x2, x3, style_total, w3, wd3, wd2, wh, wht, b3, bh = pl.pallas_call(
        lambda *refs: first_kernel(tiles, *refs),
        out_shape=(
            sds((16 * (rows + 7), lanes), bf16),
            sds((lanes // 128, 16 * (rows + 2), 128)),
            sds((128 * (rows + 6), lanes), bf16),
            sds((96 * (rows + 6), lanes), bf16),
            sds((192 * (rows + 4), lanes), bf16),
            sds((8, 128)),
            sds((256, 9 * CH_TWO), bf16),
            sds((128, 16 * CH_ONE), bf16),
            sds((CH_ONE, 9 * CH_TWO), bf16),
            sds((16, 128), bf16),
            sds((128, 16), bf16),
            sds((8, 128)),
            sds((16, 128)),
        ),
        in_specs=[SMEM] + [VMEM] * 8,
        out_specs=[VMEM] * 13,
        scratch_shapes=[
            pltpu.VMEM(edge, bf16), pltpu.VMEM(edge, bf16), pltpu.VMEM(edge, jnp.int32), pltpu.VMEM(edge, jnp.int32),
            pltpu.VMEM((128, 32), bf16), pltpu.VMEM((CH_TWO, 9 * CH_ONE), bf16),
            pltpu.VMEM((128, 128), f32), pltpu.VMEM((64, 128), f32), pltpu.VMEM((32, 128), f32),
            pltpu.VMEM((8, 128), f32), pltpu.VMEM((tiles, 8, 128), f32),
            DMA((4,)), DMA((4,)), DMA((tiles,)), DMA((tiles,)),
        ],
        compiler_params=remote(1, 14),
        name="forward_one_two",
    )(nucleus, images, target_flow, cell_label, conv1_weight, conv2_weight, third[0], head[0], biases)

    rim = (128, lanes)
    gc, rim_lo, rim_hi, go, k3, head_part, style_grad, sums_a, sg = pl.pallas_call(
        lambda *refs: second_kernel(tiles, crops, grad_scale, float(coarse_count), *refs),
        out_shape=(
            sds((64 * (rows + 2), lanes)),
            sds(rim, bf16),
            sds(rim, bf16),
            sds((16 * rows, lanes), bf16),
            sds((144, 128)),
            sds((16, 128)),
            sds((16, 128)),
            sds((8, 128)),
            sds((8, 128)),
        ),
        in_specs=[VMEM] * 11,
        out_specs=[VMEM] * 9,
        scratch_shapes=[
            pltpu.VMEM((128 * (rows + 2), lanes), bf16),
            pltpu.VMEM((128 * (rows + 2), lanes), bf16),
            pltpu.VMEM((lanes // 128, 16 * (rows + 2), 128), f32),
            pltpu.VMEM((lanes // 128, 16 * rows, 128), f32),
            pltpu.VMEM((256 * (rows + 4), lanes), bf16),
            pltpu.VMEM((9 * CH_TWO, 128), f32),
        ],
        compiler_params=params(30),
        name="forward_three_back",
    )(h1, x3, targets, style_total, b3, style[0], w3, wh, wht, wd3, bh)

    sg_total, rim_up, rim_dn = pl.pallas_call(
        lambda *refs: sum_rim_kernel(tiles, *refs),
        out_shape=(sds((8, 128)), sds(rim, bf16), sds(rim, bf16)),
        in_specs=[VMEM, ANY, ANY],
        out_specs=[VMEM, ANY, ANY],
        scratch_shapes=[
            pltpu.VMEM((tiles, 8, 128), f32), DMA((tiles,)), DMA((tiles,)), DMA((2,)), DMA((2,)),
        ],
        compiler_params=remote(3),
        name="style_grad_sum",
    )(sg, rim_lo, rim_hi)

    k2, d1, sums_b = pl.pallas_call(
        lambda *refs: third_kernel(tiles, crops, float(coarse_count), *refs),
        out_shape=(sds((160, 128)), sds((32, 128)), sds((8, 128))),
        in_specs=[VMEM] * 13,
        out_specs=[VMEM] * 3,
        scratch_shapes=[
            pltpu.VMEM((192 * (rows + 2), lanes), bf16),
            pltpu.VMEM((9 * CH_ONE, CH_TWO), f32),
        ],
        compiler_params=params(16),
        name="back_two_one",
    )(gc, rim_up, rim_dn, style_total, sg_total, style[0], x3, x2, h1, y, go, wd2, wht)

    part = 8 * pl.cdiv(sum(PART_ROWS), 8 * tiles)
    summed = pl.pallas_call(
        lambda *refs: reduce_kernel(tiles, images_count, part, *refs),
        out_shape=sds((part * tiles, 128)),
        in_specs=[VMEM] * 7,
        out_specs=VMEM,
        scratch_shapes=[
            pltpu.VMEM((part * tiles, 128), f32),
            pltpu.VMEM((tiles, part, 128), f32),
            pltpu.VMEM((part, 128), f32),
            pltpu.VMEM((images_count, part, 128), f32),
            pltpu.VMEM((part * tiles, 128), f32),
            DMA((tiles,)), DMA((tiles,)), DMA((images_count,)), DMA((images_count,)), DMA((tiles,)), DMA((tiles,)),
        ],
        compiler_params=remote(4),
        name="gradient_sum",
    )(k3, k2, d1, head_part, style_grad, sums_a, sums_b)

    olds = (
        (conv1_weight, conv1_momentum, conv1_average)
        + (conv2_weight, conv2_momentum, conv2_average)
        + third + style + head
        + (biases, bias_momentum, bias_average)
    )
    news = pl.pallas_call(
        lambda *refs: update_kernel(float(pixel_count), *refs),
        out_shape=tuple(sds(v.shape) for v in olds) + (sds((1,)),),
        in_specs=[SMEM] + [VMEM] * 19,
        out_specs=[VMEM] * 18 + [SMEM],
        compiler_params=params(16),
        name="update",
    )(step_count, summed, *olds)
    return (news[18], *news[0:6], *(other_way(w) for w in news[6:15]), *news[15:18])


def solution(mesh):
    return jax.shard_map(
        on_device,
        mesh=mesh,
        in_specs=(
            P("img", None, "tile", None),
            P("img"),
            P("img", None, "tile", None),
            P("img", "tile", None),
        )
        + (P(),) * 19,
        out_specs=(P(),) * 19,
        check_vma=False,
    )
```

```python
import math

import jax
import jax.numpy as jnp
from jax import lax
from jax.experimental import pallas as pl
from jax.experimental.pallas import tpu as pltpu
from jax.sharding import PartitionSpec as P

CH_ONE = 32
CH_TWO = 64
OUT_CH = 3

momentum_rate = 0.9
learn_rate = 0.02
decay_rate = 0.0001
norm_eps = 1e-05
highest = lax.Precision.HIGHEST
f32 = jnp.float32
bf16 = jnp.bfloat16

HALO = 8
VMEM = pl.BlockSpec(memory_space=pltpu.VMEM)
SMEM = pl.BlockSpec(memory_space=pltpu.SMEM)
ANY = pl.BlockSpec(memory_space=pl.ANY)
MESH = pl.DeviceIdType.MESH
DMA = pltpu.SemaphoreType.DMA

BLOCK_ROWS = ((144, 16, 16, 8), (160, 8), (8, 8))


def dot(a, b):
    return jnp.dot(a, b, preferred_element_type=f32)


def dot_nt(a, b, precision=None):
    return lax.dot_general(a, b, (((1,), (1,)), ((), ())), preferred_element_type=f32, precision=precision)


def from_left(x, crops=1):
    lane = lax.broadcasted_iota(jnp.int32, x.shape, 1)
    return jnp.where(lane % (x.shape[1] // crops) == 0, 0.0, pltpu.roll(x, 1, 1))


def from_right(x, crops=1):
    width = x.shape[1] // crops
    lane = lax.broadcasted_iota(jnp.int32, x.shape, 1)
    return jnp.where(lane % width == width - 1, 0.0, pltpu.roll(x, x.shape[1] - 1, 1))


def three_columns(mid, crops):
    x = mid.astype(f32)
    return jnp.concatenate([from_left(x, crops).astype(bf16), mid, from_right(x, crops).astype(bf16)], axis=0)


def crop_rows(crops, lanes):
    row = lax.broadcasted_iota(jnp.int32, (8, lanes), 0)
    lane = lax.broadcasted_iota(jnp.int32, (8, lanes), 1)
    return jnp.where(lane // (lanes // crops) == row, 1.0, 0.0).astype(bf16)


def repeat_rows(count, step, body):
    def run(k, carry):
        body([k * step + j for j in range(step)])
        return carry

    lax.fori_loop(0, count // step, run, 0)


def turn(x, by, axis):
    by = by % x.shape[axis]
    return pltpu.roll(x, by, axis) if by else x


def lane_group(x, group, size=32):
    lane = lax.broadcasted_iota(jnp.int32, x.shape, 1)
    return jnp.where(lane // size == group, x, 0.0)


def over_phases(x):
    return (x + turn(x, 32, 1)) + (turn(x, 64, 1) + turn(x, 96, 1))


def as_column(row):
    return jnp.transpose(jnp.broadcast_to(row, (128, 128)))


def fold_lanes(x):
    total = x[:, 0:128]
    for k in range(1, x.shape[1] // 128):
        total = total + x[:, 128 * k : 128 * (k + 1)]
    return total


def wide(tile, width):
    return jnp.concatenate([tile] * (width // 128), axis=1)


def rows_of(ref, start, size):
    return ref[pl.ds(pl.multiple_of(start, 16), size), :]


def put_rows(ref, start, value):
    ref[pl.ds(pl.multiple_of(start, 16), value.shape[0]), :] = value


def put_lanes(ref, start, value):
    for k in range(value.shape[1] // 128):
        ref[k, pl.ds(pl.multiple_of(start, 16), value.shape[0]), :] = value[:, 128 * k : 128 * (k + 1)]


def get_lanes(ref, start, size, stride=None):
    spot = pl.ds(start, size, stride=stride) if stride else pl.ds(pl.multiple_of(start, 16), size)
    return jnp.concatenate([ref[k, spot, :] for k in range(ref.shape[0])], axis=1)


def strip_edges(tiles, rows):
    me = lax.axis_index("tile")
    return -me * rows, (tiles - me) * rows


def valid(row, edge):
    return jnp.where((row >= edge[0]) & (row < edge[1]), 1.0, 0.0).astype(f32)


def greet(sizes):
    gate = pltpu.get_barrier_semaphore()
    for axis, count in sizes:
        me = lax.axis_index(axis)
        for j in range(1, count):
            pl.semaphore_signal(gate, inc=1, device_id={axis: lax.rem(me + j, count)}, device_id_type=MESH)
    return lambda: pl.semaphore_wait(gate, sum(count - 1 for _, count in sizes))


def send_all(count, axis, source, target, send_sem, recv_sem):
    me = lax.axis_index(axis)
    copies = []
    for j in range(1, count):
        to = lax.rem(me + j, count)
        copy = pltpu.make_async_remote_copy(
            src_ref=source(to), dst_ref=target, send_sem=send_sem.at[j - 1], recv_sem=recv_sem.at[j - 1],
            device_id={axis: to}, device_id_type=MESH,
        )
        copy.start()
        copies.append(copy)
    return copies


def wait_all(copies):
    for copy in copies:
        copy.wait()


def in_order(ref, count):
    total = ref[0]
    for k in range(1, count):
        total = total + ref[k]
    return total


def swap_edges(tiles, pairs, send_sem, recv_sem):
    me = lax.axis_index("tile")
    copies = []
    for k, (low, high, from_before, from_after) in enumerate(pairs):
        down = pltpu.make_async_remote_copy(
            src_ref=high, dst_ref=from_before, send_sem=send_sem.at[2 * k], recv_sem=recv_sem.at[2 * k],
            device_id={"tile": jnp.minimum(me + 1, tiles - 1)}, device_id_type=MESH,
        )
        up = pltpu.make_async_remote_copy(
            src_ref=low, dst_ref=from_after, send_sem=send_sem.at[2 * k + 1], recv_sem=recv_sem.at[2 * k + 1],
            device_id={"tile": jnp.maximum(me - 1, 0)}, device_id_type=MESH,
        )
        copies.append((down, up))

    @pl.when(me < tiles - 1)
    def _():
        for down, _up in copies:
            down.start()

    @pl.when(me > 0)
    def _():
        for _down, up in copies:
            up.start()

    def finish():
        @pl.when(me < tiles - 1)
        def _():
            for down, up in copies:
                down.wait_send()
                up.wait_recv()

        @pl.when(me > 0)
        def _():
            for down, up in copies:
                up.wait_send()
                down.wait_recv()

    return finish


def share(count, axis, source, got, send_sem, recv_sem):
    me = lax.axis_index(axis)
    got[me] = source[...]
    return send_all(count, axis, lambda to: source, got.at[me], send_sem, recv_sem)


class Reduction:
    def __init__(self, tiles, images, pay, got, own, met, sems):
        self.tiles, self.images = tiles, images
        self.pay, self.got, self.own, self.met, self.sems = pay, got, own, met, sems
        self.part = own.shape[0]
        self.me = lax.axis_index("tile")

    def block(self, k):
        return pl.ds(pl.multiple_of(k * self.part, 8), self.part)

    def scatter(self):
        self.got[self.me] = self.pay[self.block(self.me), :]
        self.copies = send_all(
            self.tiles, "tile", lambda to: self.pay.at[self.block(to), :], self.got.at[self.me], self.sems[0], self.sems[1]
        )

    def across(self):
        wait_all(self.copies)
        self.own[...] = in_order(self.got, self.tiles)
        self.copies = share(self.images, "img", self.own, self.met, self.sems[2], self.sems[3])

    def gather(self, full):
        wait_all(self.copies)
        full[self.block(self.me), :] = in_order(self.met, self.images)
        here = full.at[self.block(self.me), :]
        self.copies = send_all(self.tiles, "tile", lambda to: here, here, self.sems[4], self.sems[5])

    def finish(self):
        wait_all(self.copies)


def first_tables(k1_ref, k2_ref, bias_ref, w1_ref, w2_ref, b1_ref, b2_ref, base_ref):
    base_ref[...] = jnp.zeros_like(base_ref)
    for a in range(3):
        for b in range(3):
            for i in range(2):
                base_ref[8 * a + 4 * i + b : 8 * a + 4 * i + b + 1, 0:32] = k1_ref[a, b, i : i + 1, :]
    base = base_ref[...]
    w1t = jnp.zeros((32, 128), f32)
    for p in range(4):
        w1t = w1t + turn(turn(base, 8 * (p // 2) + p % 2, 0), 32 * p, 1)
    w1_ref[...] = jnp.transpose(w1t).astype(bf16)

    k2 = [[k2_ref[a, b].astype(bf16).astype(f32) for b in range(3)] for a in range(3)]
    w2t = jnp.concatenate([k2[a][b] for a in range(3) for b in range(3)], axis=0)
    w2_ref[...] = jnp.transpose(w2t).astype(bf16)
    bias = bias_ref[...].reshape(1, -1)
    b1_ref[...] = as_column(jnp.concatenate([bias[:, 0:32]] * 4, axis=1))
    b2_ref[...] = as_column(jnp.concatenate([bias[:, 32:96]] * 2, axis=1))[0:64]


def later_tables(k2_ref, k3_ref, kh_ref, bias_ref, w3_ref, wd3_ref, wd2_ref, wh_ref, wht_ref, b3_ref, bh_ref):
    k2 = [[k2_ref[a, b].astype(bf16).astype(f32) for b in range(3)] for a in range(3)]
    wd2_ref[...] = jnp.concatenate([k2[2 - s][2 - t] for s in range(3) for t in range(3)], axis=1).astype(bf16)

    def tap_sum(first, second):
        total = None
        for a in first:
            for b in second:
                total = k3[a][b] if total is None else total + k3[a][b]
        return jnp.zeros((CH_ONE, CH_TWO), f32) if total is None else total

    k3 = [[k3_ref[a, b].astype(bf16).astype(f32) for b in range(3)] for a in range(3)]
    up = [[[a for a in range(3) if (p + a + 1) // 2 == r] for r in range(3)] for p in range(2)]
    for p in range(4):
        w3 = jnp.concatenate([tap_sum(up[p // 2][r], up[p % 2][c]) for r in range(3) for c in range(3)], axis=1)
        w3_hi = w3.astype(bf16)
        w3_ref[32 * p : 32 * (p + 1), :] = w3_hi
        w3_ref[128 + 32 * p : 160 + 32 * p, :] = (w3 - w3_hi.astype(f32)).astype(bf16)
    down = ((2,), (1, 2), (0, 1), (0,))
    wd3 = jnp.transpose(jnp.concatenate([tap_sum(down[r], down[c]) for r in range(4) for c in range(4)], axis=0))
    wd3_hi = wd3.astype(bf16)
    wd3_ref[0:64, :] = wd3_hi
    wd3_ref[64:128, :] = (wd3 - wd3_hi.astype(f32)).astype(bf16)

    row = lax.broadcasted_iota(jnp.int32, (16, 128), 0)
    lane = lax.broadcasted_iota(jnp.int32, (16, 128), 1)
    wh = jnp.zeros((16, 128), f32)
    for o in range(OUT_CH):
        one = jnp.concatenate([kh_ref[o : o + 1, :]] * 4, axis=1)
        wh = jnp.where(row // 4 == o, jnp.broadcast_to(one, (16, 128)), wh)
    wh = jnp.where(row % 4 == lane // 32, wh, 0.0)
    wh_ref[...] = wh.astype(bf16)
    wht_ref[...] = jnp.transpose(wh).astype(bf16)

    bias = bias_ref[...].reshape(1, -1)
    b3_ref[...] = jnp.zeros_like(b3_ref)
    b3_ref[0:1, :] = jnp.concatenate([bias[:, 96:128] + bias[:, 128:160]] * 4, axis=1)
    bh = jnp.zeros((16, 128), f32)
    for o in range(OUT_CH):
        bh = jnp.where(row // 4 == o, jnp.broadcast_to(bias[:, 160 + o : 161 + o], (16, 128)), bh)
    bh_ref[...] = bh


def split_columns(x, select):
    even, odd = [], []
    for k in range(x.shape[1] // 256):
        piece = dot(x[:, 256 * k : 256 * (k + 1)], select)
        even.append(piece[:, 0:128])
        odd.append(piece[:, 128:256])
    return jnp.concatenate(even, axis=1), jnp.concatenate(odd, axis=1)


def step_kernel(
    tiles, images, scale, coarse_count,
    nucleus_ref, x_ref, t_ref, label_ref, k1_ref, k2_ref, k3_ref, kh_ref, bias_ref, ws_ref,
    o_ref,
    x_lo, x_hi, t_lo, t_hi,
    w1_ref, w2_ref, w3_ref, wd3_ref, wd2_ref, wh_ref, wht_ref, b1_ref, b2_ref, b3_ref, bh_ref, base_ref,
    y_ref, t_out, h1_ref, x2_ref, x3_ref, h3_ref, m_ref, fe_ref, go_ref, go_out, g3_ref, gc_ref,
    rim_lo, rim_hi, rim_up, rim_dn,
    style_ref, style_got, sg_ref, sg_got, head_ref, sums_ref, d3_ref, d2_ref, d1_ref,
    pay_a, got_a, own_a, met_a, full_a, pay_b, got_b, own_b, met_b, full_b,
    pay_c, got_c, own_c, met_c,
    halo_send, halo_recv, s1_send, s1_recv, s2_send, s2_recv, rim_send, rim_recv,
    *sems,
):
    reduce_a = Reduction(tiles, images, pay_a, got_a, own_a, met_a, sems[0:6])
    reduce_b = Reduction(tiles, images, pay_b, got_b, own_b, met_b, sems[6:12])
    arrived = greet((("tile", tiles), ("img", images)))
    first_tables(k1_ref, k2_ref, bias_ref, w1_ref, w2_ref, b1_ref, b2_ref, base_ref)
    arrived()
    last = x_ref.shape[2] - HALO
    finish_halo = swap_edges(
        tiles,
        [
            (ref.at[:, :, pl.ds(0, HALO), :], ref.at[:, :, pl.ds(last, HALO), :], lo, hi)
            for ref, lo, hi in ((x_ref, x_lo, x_hi), (t_ref, t_lo, t_hi))
        ],
        halo_send, halo_recv,
    )
    crops = x_ref.shape[0]
    width = x_ref.shape[3] // 2
    lanes = crops * width
    height = x_ref.shape[2]
    rows = height // 2
    edge = strip_edges(tiles, rows)
    r_id = lax.broadcasted_iota(jnp.int32, (256, 256), 0)
    c_id = lax.broadcasted_iota(jnp.int32, (256, 256), 1)
    select = jnp.where(r_id == 2 * (c_id % 128) + c_id // 128, 1.0, 0.0).astype(bf16)
    x_rows = 2 * (height + 2 * HALO)
    y_rows = y_ref.shape[0]
    ri = lax.broadcasted_iota(jnp.int32, (y_rows, 4 * x_rows), 0)
    ci = lax.broadcasted_iota(jnp.int32, (y_rows, 4 * x_rows), 1)
    fine = 2 * (ri // 16) + (ri // 8) % 2 - 7
    channel = (ri // 4) % 2
    source = jnp.where(
        fine < 0,
        2 * height + channel * HALO + fine + HALO,
        jnp.where(
            fine < height, channel * height + fine, 2 * height + 2 * HALO + channel * HALO + fine - height
        ),
    )
    perm_x = jnp.where(ci == (ri % 4) * x_rows + source, 1.0, 0.0).astype(bf16)
    has_up, has_dn = edge[0] < 0, edge[1] > rows

    def both_columns(of_crop):
        even, odd = [], []
        for c in range(crops):
            first, second = split_columns(of_crop(c), select)
            even.append(first)
            odd.append(second)
        return jnp.concatenate(even, axis=1), jnp.concatenate(odd, axis=1)

    def own_rows(c):
        return jnp.concatenate([x_ref[c, k] for k in range(2)], axis=0)

    def halo_rows(c):
        pieces = [jnp.where(has_up, x_lo[c, k].astype(f32), 0.0) for k in range(2)]
        pieces += [jnp.where(has_dn, x_hi[c, k].astype(f32), 0.0) for k in range(2)]
        return jnp.concatenate(pieces, axis=0).astype(bf16)

    def target_rows(c):
        pieces = [t_ref[c, 0].astype(f32), t_ref[c, 1].astype(f32), label_ref[c].astype(f32)]
        pieces += [jnp.where(has_up, t_lo[c, k], 0).astype(f32) for k in range(2)]
        pieces += [jnp.where(has_dn, t_hi[c, k], 0).astype(f32) for k in range(2)]
        return jnp.concatenate(pieces, axis=0).astype(bf16)

    own_part = both_columns(own_rows)
    finish_halo()
    even, odd = (jnp.concatenate([a, b], axis=0) for a, b in zip(own_part, both_columns(halo_rows)))
    row = lax.broadcasted_iota(jnp.int32, (x_rows, lanes), 0)
    crop = lax.broadcasted_iota(jnp.int32, (x_rows, lanes), 1) // width
    second = jnp.where(row < 2 * height, row // height, (row - 2 * height) // HALO % 2) == 1
    gate = jnp.ones((x_rows, lanes), f32)
    for c in range(crops):
        gate = jnp.where(second & (crop == c), nucleus_ref[c].astype(f32), gate)
    even, odd = even * gate, odd * gate
    stack = jnp.concatenate([from_left(odd, crops), even, odd, from_right(even, crops)], axis=0)
    y_ref[...] = dot(perm_x, stack.astype(bf16)).astype(bf16)
    ones = crop_rows(crops, lanes)
    style_ref[...] = jnp.zeros_like(style_ref)

    def conv_one(ks):
        pre = [dot(w1_ref[...], rows_of(y_ref, k * 16, 32)) for k in ks]
        for k, p in zip(ks, pre):
            keep = valid(k - 3, edge)
            hidden = (jnp.maximum(p + wide(b1_ref[...], lanes), 0.0) * keep).astype(bf16)
            put_rows(h1_ref, k * 128, hidden)
            h = hidden.astype(f32)
            pooled = (0.25 * ((h[0:32] + h[32:64]) + (h[64:96] + h[96:128]))).astype(bf16)
            put_rows(x2_ref, k * 96, three_columns(pooled, crops))

    def conv_two(qs):
        pre = [dot(w2_ref[...], rows_of(x2_ref, q * 96, 288)) for q in qs]
        sums = 0.0
        for q, p in zip(qs, pre):
            row = q - 2
            keep = valid(row, edge)
            own = jnp.where((row >= 0) & (row < rows), 1.0, 0.0).astype(f32)
            hidden = (jnp.maximum(p + wide(b2_ref[...], lanes), 0.0) * keep).astype(bf16)
            put_rows(x3_ref, q * 192, three_columns(hidden, crops))
            sums = sums + dot_nt(ones, hidden) * own
        style_ref[:, 0:64] += sums

    repeat_rows(rows + 6, 2, conv_one)
    repeat_rows(rows + 4, 2, conv_two)
    style_copies = share(tiles, "tile", style_ref, style_got, s1_send, s1_recv)

    t_rows = 3 * height + 4 * HALO
    ri = lax.broadcasted_iota(jnp.int32, (t_out.shape[1], 2 * t_rows), 0)
    ci = lax.broadcasted_iota(jnp.int32, (t_out.shape[1], 2 * t_rows), 1)
    part = (ri // 4) % 4
    fine = 2 * (ri // 16) + (ri // 2) % 2 - 2
    source = jnp.where(
        fine < 0,
        3 * height + part * HALO + fine + HALO,
        jnp.where(fine < height, part * height + fine, 3 * height + 2 * HALO + part * HALO + fine - height),
    )
    outside = (fine < 0) | (fine >= height)
    known = (part < 2) | ((part == 2) & jnp.logical_not(outside))
    perm_t = jnp.where((ci == (ri % 2) * t_rows + source) & known, 1.0, 0.0).astype(bf16)
    even, odd = both_columns(target_rows)
    put_lanes(t_out, 0, dot(perm_t, jnp.concatenate([even, odd], axis=0).astype(bf16)))
    later_tables(k2_ref, k3_ref, kh_ref, bias_ref, w3_ref, wd3_ref, wd2_ref, wh_ref, wht_ref, b3_ref, bh_ref)
    wait_all(style_copies)
    style_raw = in_order(style_got, tiles)[:, 0:64] / coarse_count
    style_inv = lax.rsqrt(jnp.mean(style_raw * style_raw, axis=1, keepdims=True) + norm_eps)
    unit = style_raw * style_inv
    vec = dot_nt(unit, ws_ref[...], highest)
    vec = jnp.concatenate([vec] * 4, axis=1) + b3_ref[0:1, :]
    bias3 = [as_column(vec[c : c + 1]) for c in range(crops)]

    def forward(ks):
        pre = [dot(w3_ref[...], rows_of(x3_ref, k * 192, 576)) for k in ks]
        hs = []
        for k, both in zip(ks, pre):
            p = both[0:128] + both[128:256] + jnp.concatenate([wide(b, width) for b in bias3], axis=1)
            h1 = rows_of(h1_ref, (k + 2) * 128, 128).astype(f32)
            h3 = (jnp.maximum(p, 0.0) + h1).astype(bf16)
            put_rows(h3_ref, k * 128, h3)
            put_rows(m_ref, k * 128, jnp.where(p > 0, 1.0, 0.0).astype(bf16))
            hs.append(h3)
        outs = [dot(wh_ref[...], h) for h in hs]
        for k, o in zip(ks, outs):
            o = o + wide(bh_ref[...], lanes)
            t = get_lanes(t_out, k * 16, 16)
            fe = (o[0:8] - 0.25 * t[0:8]) * valid(k - 1, edge)
            put_lanes(fe_ref, k * 16, jnp.concatenate([fe, o[8:16]], axis=0))

    repeat_rows(rows + 2, 2, forward)

    r_id = lax.broadcasted_iota(jnp.int32, (rows, lanes), 0)
    above = jnp.where(r_id - 1 >= edge[0], 1.0, 0.0)
    below = jnp.where(r_id + 1 < edge[1], 1.0, 0.0)
    go_ref[...] = jnp.zeros_like(go_ref)

    def at(part, off):
        return get_lanes(fe_ref, 16 * (1 + off) + part, rows, 16)

    def column_part(pr, off):
        odd, even = at(4 + 2 * pr + 1, off), at(4 + 2 * pr, off)
        return 0.5 * (odd - from_left(odd, crops)), 0.5 * (from_right(even, crops) - even)

    loss = jnp.zeros((rows, 128), f32)
    e0 = [at(k, 0) for k in range(4)]
    e1 = [at(4 + k, 0) for k in range(4)]
    cols0, cols1 = column_part(0, 0), column_part(1, 0)
    cols_up, cols_dn = column_part(1, -1), column_part(0, 1)
    spread = [None] * 4
    g_up, g_dn = [None] * 2, [None] * 2
    for pc in range(2):
        f_up, f_dn = at(2 + pc, -1), at(pc, 1)
        spread[pc] = 0.5 * (e0[2 + pc] - f_up) + cols0[pc]
        spread[2 + pc] = 0.5 * (f_dn - e0[pc]) + cols1[pc]
        g_up[pc] = 2.0 * scale * above * (0.5 * (e0[pc] - at(pc, -1)) + cols_up[pc])
        g_dn[pc] = 2.0 * scale * below * (0.5 * (at(2 + pc, 1) - e0[2 + pc]) + cols_dn[pc])
    g = [2.0 * scale * v for v in spread]
    for pr in range(2):
        even, odd = g[2 * pr], g[2 * pr + 1]
        col = [0.5 * (odd - from_left(odd, crops)), 0.5 * (from_right(even, crops) - even)]
        for pc in range(2):
            k = 2 * pr + pc
            if pr == 0:
                row_part = 0.5 * (g[2 + pc] - g_up[pc])
            else:
                row_part = 0.5 * (g_dn[pc] - g[pc])
            logit = at(8 + k, 0)
            label = get_lanes(t_out, 16 + 8 + k, rows, 16)
            ex = jnp.exp(-jnp.abs(logit))
            sig = jnp.where(logit >= 0, 1.0, ex) / (1.0 + ex)
            grads = (2.0 * scale * e0[k] - row_part, 2.0 * scale * e1[k] - col[pc], scale * (sig - label))
            for part in range(OUT_CH):
                for j in range(lanes // 128):
                    go_ref[j, pl.ds(4 * part + k, rows, stride=16), :] = grads[part][:, 128 * j : 128 * (j + 1)]
            term = jnp.maximum(logit, 0.0) + jnp.log1p(ex) - label * logit
            loss = loss + fold_lanes(e0[k] * e0[k] + e1[k] * e1[k] + spread[k] * spread[k] + term)

    sums_ref[...] = jnp.zeros_like(sums_ref)
    sums_ref[4:5, :] = jnp.sum(loss, axis=0, keepdims=True)
    head_ref[...] = jnp.zeros_like(head_ref)
    sg_ref[...] = jnp.zeros_like(sg_ref)
    d3_ref[...] = jnp.zeros_like(d3_ref)
    for k in (0, 1, rows + 2, rows + 3):
        g3_ref[256 * k : 256 * (k + 1), :] = jnp.zeros((256, lanes), bf16)

    def backward(rs):
        gos = [get_lanes(go_ref, r * 16, 16).astype(bf16) for r in rs]
        gts = [dot(wht_ref[...], go) for go in gos]
        head, gsum, sg = 0.0, 0.0, 0.0
        for r, go, gt in zip(rs, gos, gts):
            put_rows(go_out, r * 16, go)
            spot = (r + 1) * 128
            head = head + dot_nt(go, rows_of(h3_ref, spot, 128))
            gsum = gsum + dot_nt(ones, go)
            g = gt.astype(bf16).astype(f32) * rows_of(m_ref, spot, 128).astype(f32)
            gb = g.astype(bf16)
            sg = sg + dot_nt(ones, gb)
            parts = []
            for pr in range(2):
                even, odd = g[64 * pr : 64 * pr + 32], g[64 * pr + 32 : 64 * pr + 64]
                parts += [
                    from_left(odd, crops).astype(bf16),
                    gb[64 * pr : 64 * pr + 64],
                    from_right(even, crops).astype(bf16),
                ]
            put_rows(g3_ref, (r + 2) * 256, jnp.concatenate(parts, axis=0))
        head_ref[...] += head
        sums_ref[3:4, 0:16] += jnp.sum(gsum, axis=0, keepdims=True)
        sg_ref[...] += sg

    repeat_rows(rows, 2, backward)
    sg_copies = share(tiles, "tile", sg_ref, sg_got, s2_send, s2_recv)

    def down(ks):
        both = [dot(wd3_ref[...], rows_of(g3_ref, k * 256 + 128, 512)) for k in ks]
        for k, b in zip(ks, both):
            put_rows(gc_ref, k * 64, b[0:64] + b[64:128])

    down([0, 1])
    rim_lo[...] = gc_ref[0:128, :].astype(bf16)
    down([rows, rows + 1])
    rim_hi[...] = gc_ref[64 * rows : 64 * rows + 128, :].astype(bf16)
    finish_rims = swap_edges(tiles, [(rim_lo, rim_hi, rim_up, rim_dn)], rim_send, rim_recv)
    repeat_rows(rows - 2, 2, lambda ks: down([k + 2 for k in ks]))

    def weights_three(rs):
        d3 = 0.0
        for r in rs:
            spot = (r + 2) * 256
            gb = jnp.concatenate([rows_of(g3_ref, spot + 32, 64), rows_of(g3_ref, spot + 160, 64)], axis=0)
            d3 = d3 + dot_nt(rows_of(x3_ref, (r + 1) * 192, 576), gb)
        d3_ref[...] += d3

    repeat_rows(rows, 2, weights_three)
    d3 = jnp.transpose(d3_ref[...])
    for block in range(5):
        packed = jnp.zeros((CH_ONE, 128), f32)
        for tap in range(2 * block, min(2 * block + 2, 9)):
            a, b = tap // 3, tap % 3
            total = jnp.zeros((CH_ONE, CH_TWO), f32)
            for p in range(4):
                n = 3 * ((p // 2 + a + 1) // 2) + (p % 2 + b + 1) // 2
                total = total + d3[32 * p : 32 * (p + 1), 64 * n : 64 * (n + 1)]
            if tap % 2 == 0:
                packed = jnp.concatenate([total, packed[:, 64:128]], axis=1)
            else:
                packed = jnp.concatenate([packed[:, 0:64], total], axis=1)
        if block < 4:
            pay_a[32 * block : 32 * (block + 1), :] = packed
        else:
            pay_a[128:144, :] = jnp.concatenate([packed[0:16, 0:64], packed[16:32, 0:64]], axis=1)
    outer = jnp.zeros((CH_ONE, 128), f32)
    for c in range(crops):
        outer = outer + as_column(over_phases(sg_ref[c : c + 1, :]))[0:32] * jnp.concatenate([unit[c : c + 1]] * 2, axis=1)
        sums_ref[2:3, :] += sg_ref[c : c + 1, :]
    pay_a[144:160, :] = head_ref[...]
    pay_a[160:176, :] = jnp.concatenate([outer[0:16, 0:64], outer[16:32, 0:64]], axis=1)
    pay_a[176:184, :] = sums_ref[...]
    if pay_a.shape[0] > 184:
        pay_a[184:, :] = jnp.zeros((pay_a.shape[0] - 184, 128), f32)
    reduce_a.scatter()

    wait_all(sg_copies)
    style_grad = over_phases(in_order(sg_got, tiles))[:, 0:32]
    grad_unit = jnp.dot(style_grad, ws_ref[...], precision=highest, preferred_element_type=f32)
    mixed = jnp.mean(style_raw * grad_unit, axis=1, keepdims=True)
    grad_raw = style_inv * grad_unit - style_inv * style_inv * style_inv * style_raw * mixed
    grad_raw = jnp.concatenate([grad_raw / coarse_count] * 2, axis=1)
    raw = [as_column(grad_raw[c : c + 1])[0:64] for c in range(crops)]
    pay_c[...] = jnp.zeros_like(pay_c)
    d2_ref[...] = jnp.zeros_like(d2_ref)
    d1_ref[...] = jnp.zeros_like(d1_ref)
    finish_rims()
    g2_ref = g3_ref

    def masked(k, extra=None):
        coarse = rows_of(gc_ref, k * 64, 64)
        if extra is not None:
            coarse = coarse + extra
        grad = (coarse + jnp.concatenate([wide(v, width) for v in raw], axis=1)).astype(bf16).astype(f32)
        h2 = rows_of(x3_ref, (k + 1) * 192 + 64, 64).astype(f32)
        put_rows(g2_ref, k * 192, three_columns(jnp.where(h2 > 0, grad, 0.0).astype(bf16), crops))

    up = jnp.where(edge[0] < 0, rim_up[...].astype(f32), 0.0)
    dn = jnp.where(edge[1] > rows, rim_dn[...].astype(f32), 0.0)
    masked(0, up[0:64])
    masked(1, up[64:128])
    masked(rows, dn[0:64])
    masked(rows + 1, dn[64:128])

    def inner(ks):
        for k in ks:
            masked(k + 2)

    repeat_rows(rows - 2, 2, inner)
    reduce_a.across()
    pay_b[...] = jnp.zeros_like(pay_b)

    def weights_two(rs):
        d2, sums = 0.0, 0.0
        for r in rs:
            g2 = rows_of(g2_ref, (r + 1) * 192 + 64, 64)
            d2 = d2 + dot_nt(rows_of(x2_ref, (r + 2) * 96, 288), g2)
            sums = sums + dot_nt(ones, g2)
        d2_ref[...] += d2
        pay_b[160:168, 0:64] += sums

    repeat_rows(rows, 2, weights_two)
    rest = jnp.concatenate([d2_ref[160:288, :], jnp.zeros((32, 64), f32)], axis=0)
    pay_b[0:160, :] = jnp.concatenate([d2_ref[0:160, :], rest], axis=1)
    reduce_b.scatter()
    reduce_a.gather(full_a)

    def last_back(rs):
        gps = [dot(wd2_ref[...], rows_of(g2_ref, r * 192, 576)) for r in rs]
        gts = [dot(wht_ref[...], rows_of(go_out, r * 16, 16)) for r in rs]
        d1, sums = 0.0, 0.0
        for r, gp, gt in zip(rs, gps, gts):
            gp = 0.25 * gp.astype(bf16).astype(f32)
            g1 = (jnp.concatenate([gp] * 4, axis=0) + gt.astype(bf16).astype(f32)).astype(bf16).astype(f32)
            h1 = rows_of(h1_ref, (r + 3) * 128, 128).astype(f32)
            gb = jnp.where(h1 > 0, g1, 0.0).astype(bf16)
            sums = sums + dot_nt(ones, gb)
            d1 = d1 + dot_nt(rows_of(y_ref, (r + 3) * 16, 32), gb)
        d1_ref[...] += d1
        pay_c[8:16, :] += sums

    half = rows // 2
    repeat_rows(half, 2, last_back)
    reduce_b.across()
    repeat_rows(rows - half, 2, lambda rs: last_back([r + half for r in rs]))
    total = jnp.zeros((32, 128), f32)
    for p in range(4):
        total = total + turn(turn(d1_ref[...], -32 * p, 1), -(8 * (p // 2) + p % 2), 0)
    packed = lane_group(total[0:8], 0)
    for k in range(1, 4):
        packed = packed + turn(lane_group(total[8 * k : 8 * (k + 1)], 0), 32 * k, 1)
    pay_c[0:8, :] = packed
    copies = share(tiles, "tile", pay_c, got_c, sems[12], sems[13])
    reduce_b.gather(full_b)
    wait_all(copies)
    own_c[...] = in_order(got_c, tiles)
    copies = share(images, "img", own_c, met_c, sems[14], sems[15])
    reduce_a.finish()
    size_a, size_b = full_a.shape[0], full_b.shape[0]
    o_ref[0:size_a, :] = full_a[...]
    reduce_b.finish()
    o_ref[size_a : size_a + size_b, :] = full_b[...]
    wait_all(copies)
    o_ref[size_a + size_b :, :] = in_order(met_c, images)


def update_kernel(pixel_count, second_at, third_at, count_ref, sum_ref, *refs):
    olds, outs, loss_ref = refs[:18], refs[18:36], refs[36]
    rate = 1.0 / (jnp.zeros((8, 128), f32) + (count_ref[0].astype(f32) + 1.0))

    def step(index, spot, grad):
        weight, momentum, average = (olds[3 * index + k][spot] for k in range(3))
        decayed = grad + decay_rate * weight
        momentum = momentum_rate * momentum + decayed
        new = weight - learn_rate * (decayed + momentum_rate * momentum)
        outs[3 * index][spot] = new
        outs[3 * index + 1][spot] = momentum
        outs[3 * index + 2][spot] = average + (new - average) * rate[0:1, 0:1]

    first = sum_ref[third_at : third_at + 8, :]
    for a in range(3):
        for b in range(3):
            for i in range(2):
                grad = first[4 * i + b : 4 * i + b + 1, 32 * a : 32 * (a + 1)]
                step(0, (a, b, slice(i, i + 1), slice(None)), grad)
    for tap in range(9):
        a, b = tap // 3, tap % 3
        first = second_at + 32 * (tap % 5)
        half = 64 * (tap // 5)
        step(1, (a, b), sum_ref[first : first + 32, half : half + 64])
        if tap < 8:
            first = 32 * (tap // 2)
            lane = 64 * (tap % 2)
            grad = sum_ref[first : first + 32, lane : lane + 64]
        else:
            first = 128
            grad = jnp.concatenate([sum_ref[first : first + 16, 64 * k : 64 * (k + 1)] for k in range(2)], axis=0)
        step(2, (a, b), grad)
    first = 160
    grad = jnp.concatenate([sum_ref[first : first + 16, 64 * k : 64 * (k + 1)] for k in range(2)], axis=0)
    step(3, (slice(None), slice(None)), grad)
    head = sum_ref[144:160, :]
    total = jnp.zeros((16, 128), f32)
    for p in range(4):
        total = total + turn(turn(head, -32 * p, 1), -p, 0)
    total = jnp.concatenate([total[4 * o : 4 * o + 1] for o in range(OUT_CH)], axis=0)
    step(4, (slice(None), slice(None)), total[:, 0:32])
    sums = sum_ref[176:184, :]
    one = over_phases(jnp.sum(sum_ref[third_at + 8 : third_at + 16, :], axis=0, keepdims=True))
    two = jnp.sum(sum_ref[second_at + 160 : second_at + 168, :], axis=0, keepdims=True)
    three = over_phases(sums[2:3])
    lane = lax.broadcasted_iota(jnp.int32, (1, 128), 1)
    low = jnp.where(lane < 32, one, jnp.where(lane < 96, turn(two, 32, 1), three))
    ends = sums[3:4]
    ends = (ends + turn(ends, -1, 1)) + (turn(ends, -2, 1) + turn(ends, -3, 1))
    high = jnp.where(lane < 32, three, 0.0)
    for o in range(OUT_CH):
        high = jnp.where(lane == 32 + o, turn(ends, 32 + o - 4 * o, 1), high)
    grad = jnp.concatenate([low, high], axis=1)[:, 0 : olds[15].shape[0]]
    weight, momentum, average = (olds[15 + k][...].reshape(1, -1) for k in range(3))
    decayed = grad + decay_rate * weight
    momentum = momentum_rate * momentum + decayed
    new = weight - learn_rate * (decayed + momentum_rate * momentum)
    average = average + (new - average) * rate[0:1, 0:1]
    for k, value in enumerate((new, momentum, average)):
        outs[15 + k][...] = value.reshape(-1)
    loss_ref[0] = jnp.sum(sums[4:5]) / pixel_count


def on_device(
    images, nucleus, target_flow, cell_label, step_count,
    conv1_weight, conv1_momentum, conv1_average,
    conv2_weight, conv2_momentum, conv2_average,
    conv3_weight, conv3_momentum, conv3_average,
    style_weight, style_momentum, style_average,
    head_weight, head_momentum, head_average,
    biases, bias_momentum, bias_average,
):
    tiles = lax.axis_size("tile")
    crops, _, height, cols = images.shape
    rows, width = height // 2, cols // 2
    pixel_count = lax.axis_size("img") * tiles * crops * height * cols
    grad_scale = 1.0 / math.sqrt(pixel_count)
    coarse_count = tiles * rows * width

    def sds(shape, dtype=f32):
        return jax.ShapeDtypeStruct(shape, dtype)

    lanes = crops * width
    images_count = lax.axis_size("img")

    def other_way(w):
        return jnp.swapaxes(w, -1, -2)

    third = tuple(other_way(w) for w in (conv3_weight, conv3_momentum, conv3_average))
    style = tuple(other_way(w) for w in (style_weight, style_momentum, style_average))
    head = tuple(other_way(w) for w in (head_weight, head_momentum, head_average))

    edge = (crops, 2, HALO, cols)
    rim = (128, lanes)
    parts = [8 * pl.cdiv(sum(block), 8 * tiles) for block in BLOCK_ROWS[:2]]
    small = sum(BLOCK_ROWS[2])

    def buf(shape, dtype=bf16):
        return pltpu.VMEM(shape, dtype)

    def block_bufs(part):
        return [
            buf((part * tiles, 128), f32), buf((tiles, part, 128), f32), buf((part, 128), f32),
            buf((images_count, part, 128), f32), buf((part * tiles, 128), f32),
        ]

    block_sems = [DMA((tiles,)), DMA((tiles,)), DMA((images_count,)), DMA((images_count,)), DMA((tiles,)), DMA((tiles,))]
    summed = pl.pallas_call(
        lambda *refs: step_kernel(tiles, images_count, grad_scale, float(coarse_count), *refs),
        out_shape=sds((sum(parts) * tiles + small, 128)),
        in_specs=[SMEM] + [VMEM] * 9,
        out_specs=VMEM,
        scratch_shapes=[
            buf(edge), buf(edge), buf(edge, jnp.int32), buf(edge, jnp.int32),
            buf((128, 32)), buf((CH_TWO, 9 * CH_ONE)), buf((256, 9 * CH_TWO)), buf((128, 16 * CH_ONE)),
            buf((CH_ONE, 9 * CH_TWO)), buf((16, 128)), buf((128, 16)),
            buf((128, 128), f32), buf((64, 128), f32), buf((8, 128), f32), buf((16, 128), f32), buf((32, 128), f32),
            buf((16 * (rows + 7), lanes)), buf((lanes // 128, 16 * (rows + 2), 128), f32),
            buf((128 * (rows + 6), lanes)), buf((96 * (rows + 6), lanes)), buf((192 * (rows + 4), lanes)),
            buf((128 * (rows + 2), lanes)), buf((128 * (rows + 2), lanes)),
            buf((lanes // 128, 16 * (rows + 2), 128), f32), buf((lanes // 128, 16 * rows, 128), f32),
            buf((16 * rows, lanes)), buf((256 * (rows + 4), lanes)), buf((64 * (rows + 2), lanes), f32),
            buf(rim), buf(rim), buf(rim), buf(rim),
            buf((8, 128), f32), buf((tiles, 8, 128), f32), buf((8, 128), f32), buf((tiles, 8, 128), f32),
            buf((16, 128), f32), buf((8, 128), f32),
            buf((9 * CH_TWO, 128), f32), buf((9 * CH_ONE, CH_TWO), f32), buf((32, 128), f32),
        ]
        + block_bufs(parts[0])
        + block_bufs(parts[1])
        + [buf((small, 128), f32), buf((tiles, small, 128), f32), buf((small, 128), f32), buf((images_count, small, 128), f32)]
        + [DMA((4,)), DMA((4,)), DMA((tiles,)), DMA((tiles,)), DMA((tiles,)), DMA((tiles,)), DMA((2,)), DMA((2,))]
        + block_sems * 2
        + [DMA((tiles,)), DMA((tiles,)), DMA((images_count,)), DMA((images_count,))],
        compiler_params=pltpu.CompilerParams(collective_id=1, has_side_effects=True, vmem_limit_bytes=62 * 2**20),
        name="step",
    )(
        nucleus, images, target_flow, cell_label,
        conv1_weight, conv2_weight, third[0], head[0], biases, style[0],
    )

    olds = (
        (conv1_weight, conv1_momentum, conv1_average)
        + (conv2_weight, conv2_momentum, conv2_average)
        + third + style + head
        + (biases, bias_momentum, bias_average)
    )
    news = pl.pallas_call(
        lambda *refs: update_kernel(float(pixel_count), parts[0] * tiles, sum(parts) * tiles, *refs),
        out_shape=tuple(sds(v.shape) for v in olds) + (sds((1,)),),
        in_specs=[SMEM] + [VMEM] * 19,
        out_specs=[VMEM] * 18 + [SMEM],
        compiler_params=pltpu.CompilerParams(vmem_limit_bytes=16 * 2**20),
        name="update",
    )(step_count, summed, *olds)
    return (news[18], *news[0:6], *(other_way(w) for w in news[6:15]), *news[15:18])


def solution(mesh):
    return jax.shard_map(
        on_device,
        mesh=mesh,
        in_specs=(
            P("img", None, "tile", None),
            P("img"),
            P("img", None, "tile", None),
            P("img", "tile", None),
        )
        + (P(),) * 19,
        out_specs=(P(),) * 19,
        check_vma=False,
    )
```

```python
import math

import jax
import jax.numpy as jnp
from jax import lax
from jax.experimental import pallas as pl
from jax.experimental.pallas import tpu as pltpu
from jax.sharding import PartitionSpec as P

CH_ONE = 32
CH_TWO = 64
OUT_CH = 3

momentum_rate = 0.9
learn_rate = 0.02
decay_rate = 0.0001
norm_eps = 1e-05
highest = lax.Precision.HIGHEST
f32 = jnp.float32
bf16 = jnp.bfloat16

HALO = 8
VMEM = pl.BlockSpec(memory_space=pltpu.VMEM)
SMEM = pl.BlockSpec(memory_space=pltpu.SMEM)
HBM = pl.BlockSpec(memory_space=pltpu.HBM)
MESH = pl.DeviceIdType.MESH
DMA = pltpu.SemaphoreType.DMA

BLOCK_ROWS = ((144, 16, 16, 8), (160, 8), (8, 8))


def dot(a, b):
    return jnp.dot(a, b, preferred_element_type=f32)


def dot_nt(a, b, precision=None):
    return lax.dot_general(a, b, (((1,), (1,)), ((), ())), preferred_element_type=f32, precision=precision)


def edge_select(x, crops, first):
    width = x.shape[1] // crops
    lane = lax.broadcasted_iota(jnp.int32, (x.shape[0], 128), 1)
    parts = []
    for c in range(crops):
        low, high = width * c, width * (c + 1)
        if first:
            parts += [jnp.where(lane == 0, 0.0, x[:, low : low + 128]), x[:, low + 128 : high]]
        else:
            parts += [x[:, low : high - 128], jnp.where(lane == 127, 0.0, x[:, high - 128 : high])]
    return jnp.concatenate(parts, axis=1)


def from_left(x, crops):
    return edge_select(pltpu.roll(x, 1, 1), crops, True)


def from_right(x, crops):
    return edge_select(pltpu.roll(x, x.shape[1] - 1, 1), crops, False)


def three_columns(mid, x, crops):
    return jnp.concatenate([from_left(x, crops).astype(bf16), mid, from_right(x, crops).astype(bf16)], axis=0)


def pieces_of(x):
    high = x.astype(bf16)
    rest = x - high.astype(f32)
    mid = rest.astype(bf16)
    return high.astype(f32), mid.astype(f32), rest - mid.astype(f32)


def repeat_rows(count, limit, body, first=0):
    step = max(k for k in range(1, limit + 1) if count % k == 0)

    def run(k, carry):
        body([first + k * step + j for j in range(step)])
        return carry

    lax.fori_loop(0, count // step, run, 0)


def turn(x, by, axis):
    by = by % x.shape[axis]
    return pltpu.roll(x, by, axis) if by else x


def lane_group(x, group, size=32):
    lane = lax.broadcasted_iota(jnp.int32, x.shape, 1)
    return jnp.where(lane // size == group, x, 0.0)


def over_phases(x):
    return (x + turn(x, 32, 1)) + (turn(x, 64, 1) + turn(x, 96, 1))


def as_column(row):
    return jnp.transpose(jnp.broadcast_to(row, (128, 128)))


def fold_lanes(x):
    parts = [x[:, 128 * k : 128 * (k + 1)] for k in range(x.shape[1] // 128)]
    while len(parts) > 1:
        parts = [a + b for a, b in zip(parts[0::2], parts[1::2])] + parts[len(parts) // 2 * 2 :]
    return parts[0]


def lane_sums(x):
    return dot_nt(jnp.ones((8, 128), f32), x, highest)


def wide(tile, width):
    return jnp.concatenate([tile] * (width // 128), axis=1)


def rows_of(ref, start, size):
    return ref[pl.ds(pl.multiple_of(start, 16), size), :]


def put_rows(ref, start, value):
    ref[pl.ds(pl.multiple_of(start, 16), value.shape[0]), :] = value


def put_lanes(ref, start, value):
    for k in range(value.shape[1] // 128):
        ref[k, pl.ds(pl.multiple_of(start, 16), value.shape[0]), :] = value[:, 128 * k : 128 * (k + 1)]


def get_lanes(ref, start, size, stride=None):
    spot = pl.ds(start, size, stride=stride) if stride else pl.ds(pl.multiple_of(start, 16), size)
    return jnp.concatenate([ref[k, spot, :] for k in range(ref.shape[0])], axis=1)


def strip_edges(tiles, rows):
    me = lax.axis_index("tile")
    return -me * rows, (tiles - me) * rows


def valid(row, edge):
    return jnp.where((row >= edge[0]) & (row < edge[1]), 1.0, 0.0).astype(f32)


def greet(sizes):
    gate = pltpu.get_barrier_semaphore()
    for axis, count in sizes:
        me = lax.axis_index(axis)
        for j in range(1, count):
            pl.semaphore_signal(gate, inc=1, device_id={axis: lax.rem(me + j, count)}, device_id_type=MESH)
    return lambda: pl.semaphore_wait(gate, sum(count - 1 for _, count in sizes))


def send_all(count, axis, source, target, send_sem, recv_sem):
    me = lax.axis_index(axis)
    copies = []
    for j in range(1, count):
        to = lax.rem(me + j, count)
        copy = pltpu.make_async_remote_copy(
            src_ref=source(to), dst_ref=target, send_sem=send_sem.at[j - 1], recv_sem=recv_sem.at[j - 1],
            device_id={axis: to}, device_id_type=MESH,
        )
        copy.start()
        copies.append(copy)
    return copies


def wait_all(copies):
    for copy in copies:
        copy.wait()


def in_order(ref, count):
    total = ref[0]
    for k in range(1, count):
        total = total + ref[k]
    return total


def swap_edges(tiles, pairs, send_sem, recv_sem):
    me = lax.axis_index("tile")
    copies = []
    for k, (low, high, from_before, from_after) in enumerate(pairs):
        down = pltpu.make_async_remote_copy(
            src_ref=high, dst_ref=from_before, send_sem=send_sem.at[2 * k], recv_sem=recv_sem.at[2 * k],
            device_id={"tile": jnp.minimum(me + 1, tiles - 1)}, device_id_type=MESH,
        )
        up = pltpu.make_async_remote_copy(
            src_ref=low, dst_ref=from_after, send_sem=send_sem.at[2 * k + 1], recv_sem=recv_sem.at[2 * k + 1],
            device_id={"tile": jnp.maximum(me - 1, 0)}, device_id_type=MESH,
        )
        copies.append((down, up))

    @pl.when(me < tiles - 1)
    def _():
        for down, _up in copies:
            down.start()

    @pl.when(me > 0)
    def _():
        for _down, up in copies:
            up.start()

    def finish():
        @pl.when(me < tiles - 1)
        def _():
            for down, up in copies:
                down.wait_send()
                up.wait_recv()

        @pl.when(me > 0)
        def _():
            for down, up in copies:
                up.wait_send()
                down.wait_recv()

    return finish


def share(count, axis, source, got, send_sem, recv_sem):
    me = lax.axis_index(axis)
    got[me] = source[...]
    return send_all(count, axis, lambda to: source, got.at[me], send_sem, recv_sem)


class Reduction:
    def __init__(self, tiles, images, pay, got, own, met, sems):
        self.tiles, self.images = tiles, images
        self.pay, self.got, self.own, self.met, self.sems = pay, got, own, met, sems
        self.part = own.shape[0]
        self.me = lax.axis_index("tile")

    def block(self, k):
        return pl.ds(pl.multiple_of(k * self.part, 8), self.part)

    def scatter(self):
        self.got[self.me] = self.pay[self.block(self.me), :]
        self.copies = send_all(
            self.tiles, "tile", lambda to: self.pay.at[self.block(to), :], self.got.at[self.me], self.sems[0], self.sems[1]
        )

    def across(self):
        wait_all(self.copies)
        self.own[...] = in_order(self.got, self.tiles)
        self.copies = share(self.images, "img", self.own, self.met, self.sems[2], self.sems[3])

    def gather(self, full):
        wait_all(self.copies)
        full[self.block(self.me), :] = in_order(self.met, self.images)
        here = full.at[self.block(self.me), :]
        self.copies = send_all(self.tiles, "tile", lambda to: here, here, self.sems[4], self.sems[5])

    def finish(self):
        wait_all(self.copies)


def first_tables(k1_ref, k2_ref, bias_ref, w1_ref, w2_ref, base_ref):
    base_ref[...] = jnp.zeros_like(base_ref)
    for a in range(3):
        for b in range(3):
            for i in range(2):
                base_ref[8 * a + 4 * i + b : 8 * a + 4 * i + b + 1, 0:32] = k1_ref[a, b, i : i + 1, :]
    base = base_ref[...]
    w1t = jnp.zeros((32, 128), f32)
    for p in range(4):
        w1t = w1t + turn(turn(base, 8 * (p // 2) + p % 2, 0), 32 * p, 1)
    bias = bias_ref[...].reshape(1, -1)
    row = lax.broadcasted_iota(jnp.int32, (16, 128), 0)

    def piece_rows(values):
        table = jnp.zeros((16, 128), f32)
        for k, piece in enumerate(pieces_of(values)):
            table = jnp.where(row == k, jnp.broadcast_to(piece, (16, 128)), table)
        return table

    b1 = piece_rows(jnp.concatenate([bias[:, 0:32]] * 4, axis=1))
    w1_ref[...] = jnp.transpose(jnp.concatenate([w1t, b1], axis=0)).astype(bf16)

    k2 = [[k2_ref[a, b].astype(bf16).astype(f32) for b in range(3)] for a in range(3)]
    w2t = jnp.concatenate([k2[a][b] for a in range(3) for b in range(3)], axis=0)
    b2 = piece_rows(jnp.concatenate([bias[:, 32:96]] * 2, axis=1))[:, 0:64]
    w2_ref[...] = jnp.transpose(jnp.concatenate([w2t, b2], axis=0)).astype(bf16)


def later_tables(k2_ref, k3_ref, kh_ref, bias_ref, w3_ref, wd3_ref, wd2_ref, wh_ref, wht_ref, b3_ref, bh_ref):
    k2 = [[k2_ref[a, b].astype(bf16).astype(f32) for b in range(3)] for a in range(3)]
    wd2_ref[...] = jnp.concatenate([k2[2 - s][2 - t] for s in range(3) for t in range(3)], axis=1).astype(bf16)

    def tap_sum(first, second):
        total = None
        for a in first:
            for b in second:
                total = k3[a][b] if total is None else total + k3[a][b]
        return jnp.zeros((CH_ONE, CH_TWO), f32) if total is None else total

    k3 = [[k3_ref[a, b].astype(bf16).astype(f32) for b in range(3)] for a in range(3)]
    up = [[[a for a in range(3) if (p + a + 1) // 2 == r] for r in range(3)] for p in range(2)]
    for p in range(4):
        w3 = jnp.concatenate([tap_sum(up[p // 2][r], up[p % 2][c]) for r in range(3) for c in range(3)], axis=1)
        w3_hi = w3.astype(bf16)
        low = w3 - w3_hi.astype(f32)
        low = jnp.concatenate([low[:, 64:128], low[:, 192:384], low[:, 448:512]], axis=1)
        w3_ref[32 * p : 32 * (p + 1), 0:896] = jnp.concatenate([w3_hi, low.astype(bf16)], axis=1)
    down = ((2,), (1, 2), (0, 1), (0,))
    wd3 = jnp.transpose(jnp.concatenate([tap_sum(down[r], down[c]) for r in range(4) for c in range(4)], axis=0))
    wd3_hi = wd3.astype(bf16)
    wd3_ref[0:64, :] = wd3_hi
    wd3_ref[64:128, :] = (wd3 - wd3_hi.astype(f32)).astype(bf16)

    row = lax.broadcasted_iota(jnp.int32, (16, 128), 0)
    lane = lax.broadcasted_iota(jnp.int32, (16, 128), 1)
    wh = jnp.zeros((16, 128), f32)
    for o in range(OUT_CH):
        one = jnp.concatenate([kh_ref[o : o + 1, :]] * 4, axis=1)
        wh = jnp.where(row // 4 == o, jnp.broadcast_to(one, (16, 128)), wh)
    wh = jnp.where(row % 4 == lane // 32, wh, 0.0)
    wh_ref[...] = wh.astype(bf16)
    wht_ref[...] = jnp.transpose(wh).astype(bf16)

    bias = bias_ref[...].reshape(1, -1)
    b3_ref[...] = jnp.zeros_like(b3_ref)
    b3_ref[0:1, :] = jnp.concatenate([bias[:, 96:128] + bias[:, 128:160]] * 4, axis=1)
    bh = jnp.zeros((16, 128), f32)
    for o in range(OUT_CH):
        bh = jnp.where(row // 4 == o, jnp.broadcast_to(bias[:, 160 + o : 161 + o], (16, 128)), bh)
    bh_ref[...] = bh


def split_columns(x, select):
    even, odd = [], []
    for k in range(x.shape[1] // 256):
        piece = dot(x[:, 256 * k : 256 * (k + 1)], select)
        even.append(piece[:, 0:128])
        odd.append(piece[:, 128:256])
    return jnp.concatenate(even, axis=1), jnp.concatenate(odd, axis=1)


def step_kernel(
    tiles, images, scale, coarse_count,
    nucleus_ref, x_hbm, t_hbm, label_hbm, k1_hbm, k2_hbm, k3_hbm, kh_hbm, bias_hbm, ws_hbm,
    o_ref,
    x_ref, t_ref, label_ref, k1_ref, k2_ref, k3_ref, kh_ref, bias_ref, ws_ref,
    x_lo, x_hi, t_lo, t_hi,
    w1_ref, w2_ref, w3_ref, wd3_ref, wd2_ref, wh_ref, wht_ref, b3_ref, bh_ref, base_ref, ones_ref, mark_ref,
    y_ref, t_out, h1_ref, x2_ref, x3_ref, h3_ref, m_ref, fe_ref, go_ref, go_out, g3_ref, gc_ref,
    rim_lo, rim_hi, rim_up, rim_dn,
    style_ref, style_got, sg_ref, sg_got, head_ref, sums_ref, d3_ref, d2_ref, d1_ref,
    style_sum, sg_sum, go_sum, g2_sum,
    pay_a, got_a, own_a, met_a, full_a, pay_b, got_b, own_b, met_b, full_b,
    pay_c, got_c, own_c, met_c,
    load_sems, halo_send, halo_recv, s1_send, s1_recv, s2_send, s2_recv, rim_send, rim_recv,
    *sems,
):
    reduce_a = Reduction(tiles, images, pay_a, got_a, own_a, met_a, sems[0:6])
    reduce_b = Reduction(tiles, images, pay_b, got_b, own_b, met_b, sems[6:12])
    arrived = greet((("tile", tiles), ("img", images)))
    loads = [
        pltpu.make_async_copy(source, target, load_sems.at[k])
        for k, (source, target) in enumerate(
            (
                (k1_hbm, k1_ref), (k2_hbm, k2_ref), (bias_hbm, bias_ref), (x_hbm, x_ref),
                (t_hbm, t_ref), (label_hbm, label_ref), (k3_hbm, k3_ref), (kh_hbm, kh_ref), (ws_hbm, ws_ref),
            )
        )
    ]
    for load in loads:
        load.start()
    ones_ref[...] = jnp.ones_like(ones_ref)
    arrived()
    last = x_ref.shape[2] - HALO
    finish_halo = swap_edges(
        tiles,
        [
            (ref.at[:, :, pl.ds(0, HALO), :], ref.at[:, :, pl.ds(last, HALO), :], lo, hi)
            for ref, lo, hi in ((x_hbm, x_lo, x_hi), (t_hbm, t_lo, t_hi))
        ],
        halo_send, halo_recv,
    )
    for load in loads[0:4]:
        load.wait()
    first_tables(k1_ref, k2_ref, bias_ref, w1_ref, w2_ref, base_ref)
    crops = x_ref.shape[0]
    width = x_ref.shape[3] // 2
    lanes = crops * width
    height = x_ref.shape[2]
    rows = height // 2
    edge = strip_edges(tiles, rows)
    r_id = lax.broadcasted_iota(jnp.int32, (256, 256), 0)
    c_id = lax.broadcasted_iota(jnp.int32, (256, 256), 1)
    select = jnp.where(r_id == 2 * (c_id % 128) + c_id // 128, 1.0, 0.0).astype(bf16)
    y_rows = y_ref.shape[0]
    ri = lax.broadcasted_iota(jnp.int32, (y_rows, 8 * height), 0)
    ci = lax.broadcasted_iota(jnp.int32, (y_rows, 8 * height), 1)
    fine = 2 * (ri // 16) + (ri // 8) % 2 - 7
    source = (ri % 4) * 2 * height + (ri // 4) % 2 * height + fine
    perm_x = jnp.where((ci == source) & (fine >= 0) & (fine < height), 1.0, 0.0).astype(bf16)
    ri = lax.broadcasted_iota(jnp.int32, (128, 16 * HALO), 0)
    ci = lax.broadcasted_iota(jnp.int32, (128, 16 * HALO), 1)
    fine = 2 * (ri // 16) + (ri // 8) % 2 - 7
    fine = jnp.where(ri < 64, fine, fine + y_rows // 8 - 16)
    source = jnp.where(fine < 0, fine + HALO, 2 * HALO + fine - height)
    source = (ri % 4) * 4 * HALO + (ri // 4) % 2 * HALO + source
    perm_h = jnp.where((ci == source) & ((fine < 0) | (fine >= height)), 1.0, 0.0).astype(bf16)
    has_up, has_dn = edge[0] < 0, edge[1] > rows

    def both_columns(of_crop):
        even, odd = [], []
        for c in range(crops):
            first, second = split_columns(of_crop(c), select)
            even.append(first)
            odd.append(second)
        return jnp.concatenate(even, axis=1), jnp.concatenate(odd, axis=1)

    def own_rows(c):
        return jnp.concatenate([x_ref[c, k] for k in range(2)], axis=0)

    def halo_rows(c):
        pieces = [jnp.where(has_up, x_lo[c, k].astype(f32), 0.0) for k in range(2)]
        pieces += [jnp.where(has_dn, x_hi[c, k].astype(f32), 0.0) for k in range(2)]
        return jnp.concatenate(pieces, axis=0).astype(bf16)

    def target_rows(c):
        pieces = [t_ref[c, 0].astype(f32), t_ref[c, 1].astype(f32), label_ref[c].astype(f32)]
        pieces += [jnp.where(has_up, t_lo[c, k], 0).astype(f32) for k in range(2)]
        pieces += [jnp.where(has_dn, t_hi[c, k], 0).astype(f32) for k in range(2)]
        return jnp.concatenate(pieces, axis=0).astype(bf16)

    def pixel_windows(of_crop, second):
        even, odd = both_columns(of_crop)
        row = lax.broadcasted_iota(jnp.int32, even.shape, 0)
        crop = lax.broadcasted_iota(jnp.int32, even.shape, 1) // width
        gate = jnp.ones(even.shape, f32)
        for c in range(crops):
            gate = jnp.where(second(row) & (crop == c), nucleus_ref[c].astype(f32), gate)
        even, odd = even * gate, odd * gate
        return jnp.concatenate([from_left(odd, crops), even, odd, from_right(even, crops)], axis=0).astype(bf16)

    y_ref[...] = dot(perm_x, pixel_windows(own_rows, lambda row: row >= height)).astype(bf16)

    def conv_one(ks, inside=True):
        pre = [
            dot(w1_ref[...], jnp.concatenate([rows_of(y_ref, k * 16, 32), ones_ref[...]], axis=0)) for k in ks
        ]
        for k, p in zip(ks, pre):
            p = jnp.maximum(p, 0.0)
            hidden = (p if inside else p * valid(k - 3, edge)).astype(bf16)
            put_rows(h1_ref, k * 128, hidden)
            h = hidden.astype(f32)
            pooled = (0.25 * ((h[0:32] + h[32:64]) + (h[64:96] + h[96:128]))).astype(bf16)
            put_rows(x2_ref, k * 96, three_columns(pooled, pooled.astype(f32), crops))

    def conv_two(qs, inside=True):
        pre = [
            dot(w2_ref[...], jnp.concatenate([rows_of(x2_ref, q * 96, 288), ones_ref[...]], axis=0)) for q in qs
        ]
        sums = [0.0] * crops
        for q, p in zip(qs, pre):
            p = jnp.maximum(p, 0.0)
            hidden = (p if inside else p * valid(q - 2, edge)).astype(bf16)
            h = hidden.astype(f32)
            put_rows(x3_ref, q * 192, three_columns(hidden, h, crops))
            for c in range(crops):
                sums[c] = sums[c] + fold_lanes(h[:, width * c : width * (c + 1)])
        if inside:
            for c in range(crops):
                style_sum[c] += sums[c]

    repeat_rows(rows - 2, 7, conv_one, 4)
    finish_halo()
    extra = dot(perm_h, pixel_windows(halo_rows, lambda row: row // HALO % 2 == 1))
    y_ref[0:64, :] = (y_ref[0:64, :].astype(f32) + extra[0:64]).astype(bf16)
    y_ref[y_rows - 64 : y_rows, :] = (y_ref[y_rows - 64 : y_rows, :].astype(f32) + extra[64:128]).astype(bf16)
    conv_one([0, 1, 2, 3], False)
    conv_one([rows + 2, rows + 3, rows + 4, rows + 5], False)
    style_sum[...] = jnp.zeros_like(style_sum)
    repeat_rows(rows, 8, conv_two, 2)
    style_ref[...] = jnp.zeros_like(style_ref)
    for c in range(crops):
        style_ref[c : c + 1, 0:64] = lane_sums(style_sum[c])[0:1]
    style_copies = share(tiles, "tile", style_ref, style_got, s1_send, s1_recv)

    conv_two([0, 1], False)
    conv_two([rows + 2, rows + 3], False)
    for load in loads[4:]:
        load.wait()
    t_rows = 3 * height + 4 * HALO
    ri = lax.broadcasted_iota(jnp.int32, (t_out.shape[1], 2 * t_rows), 0)
    ci = lax.broadcasted_iota(jnp.int32, (t_out.shape[1], 2 * t_rows), 1)
    part = (ri // 4) % 4
    fine = 2 * (ri // 16) + (ri // 2) % 2 - 2
    source = jnp.where(
        fine < 0,
        3 * height + part * HALO + fine + HALO,
        jnp.where(fine < height, part * height + fine, 3 * height + 2 * HALO + part * HALO + fine - height),
    )
    outside = (fine < 0) | (fine >= height)
    known = (part < 2) | ((part == 2) & jnp.logical_not(outside))
    perm_t = jnp.where((ci == (ri % 2) * t_rows + source) & known, 1.0, 0.0).astype(bf16)
    even, odd = both_columns(target_rows)
    put_lanes(t_out, 0, dot(perm_t, jnp.concatenate([even, odd], axis=0).astype(bf16)))
    later_tables(k2_ref, k3_ref, kh_ref, bias_ref, w3_ref, wd3_ref, wd2_ref, wh_ref, wht_ref, b3_ref, bh_ref)
    wait_all(style_copies)
    style_raw = in_order(style_got, tiles)[:, 0:64] / coarse_count
    style_inv = lax.rsqrt(jnp.mean(style_raw * style_raw, axis=1, keepdims=True) + norm_eps)
    unit = style_raw * style_inv
    vec = dot_nt(unit, ws_ref[...], highest)
    vec = jnp.concatenate([vec] * 4, axis=1) + b3_ref[0:1, :]
    row = lax.broadcasted_iota(jnp.int32, (16, lanes), 0)
    lane = lax.broadcasted_iota(jnp.int32, (16, lanes), 1)
    mark_ref[...] = jnp.where(row // 3 == lane // width, 1.0, 0.0).astype(bf16)
    row = lax.broadcasted_iota(jnp.int32, (128, 128), 0)
    table = jnp.zeros((128, 128), f32)
    for c in range(crops):
        for k, piece in enumerate(pieces_of(vec[c : c + 1])):
            table = jnp.where(row == 3 * c + k, jnp.broadcast_to(piece, (128, 128)), table)
    w3_ref[:, 896:912] = jnp.transpose(table)[:, 0:16].astype(bf16)

    def forward(ks):
        pre = []
        for k in ks:
            x = rows_of(x3_ref, k * 192, 576)
            x = jnp.concatenate([x, x[64:128], x[192:384], x[448:512], mark_ref[...]], axis=0)
            pre.append(dot(w3_ref[...], x))
        hs = []
        for k, p in zip(ks, pre):
            p = jnp.maximum(p, 0.0)
            h3 = (p + rows_of(h1_ref, (k + 2) * 128, 128).astype(f32)).astype(bf16)
            put_rows(h3_ref, k * 128, h3)
            put_rows(m_ref, k * 128, p.astype(bf16))
            hs.append(h3)
        outs = [dot(wh_ref[...], h) for h in hs]
        for k, o in zip(ks, outs):
            o = o + wide(bh_ref[...], lanes)
            t = get_lanes(t_out, k * 16, 16)
            fe = (o[0:8] - 0.25 * t[0:8]) * valid(k - 1, edge)
            put_lanes(fe_ref, k * 16, jnp.concatenate([fe, o[8:16]], axis=0))

    repeat_rows(rows + 2, 6, forward)

    r_id = lax.broadcasted_iota(jnp.int32, (rows, lanes), 0)
    above = jnp.where(r_id - 1 >= edge[0], 1.0, 0.0)
    below = jnp.where(r_id + 1 < edge[1], 1.0, 0.0)
    go_ref[...] = jnp.zeros_like(go_ref)

    def at(part, off):
        return get_lanes(fe_ref, 16 * (1 + off) + part, rows, 16)

    def column_part(pr, off):
        odd, even = at(4 + 2 * pr + 1, off), at(4 + 2 * pr, off)
        return 0.5 * (odd - from_left(odd, crops)), 0.5 * (from_right(even, crops) - even)

    loss = jnp.zeros((rows, 128), f32)
    e0 = [at(k, 0) for k in range(4)]
    e1 = [at(4 + k, 0) for k in range(4)]
    cols0, cols1 = column_part(0, 0), column_part(1, 0)
    cols_up, cols_dn = column_part(1, -1), column_part(0, 1)
    spread = [None] * 4
    g_up, g_dn = [None] * 2, [None] * 2
    for pc in range(2):
        f_up, f_dn = at(2 + pc, -1), at(pc, 1)
        spread[pc] = 0.5 * (e0[2 + pc] - f_up) + cols0[pc]
        spread[2 + pc] = 0.5 * (f_dn - e0[pc]) + cols1[pc]
        g_up[pc] = 2.0 * scale * above * (0.5 * (e0[pc] - at(pc, -1)) + cols_up[pc])
        g_dn[pc] = 2.0 * scale * below * (0.5 * (at(2 + pc, 1) - e0[2 + pc]) + cols_dn[pc])
    g = [2.0 * scale * v for v in spread]
    for pr in range(2):
        even, odd = g[2 * pr], g[2 * pr + 1]
        col = [0.5 * (odd - from_left(odd, crops)), 0.5 * (from_right(even, crops) - even)]
        for pc in range(2):
            k = 2 * pr + pc
            if pr == 0:
                row_part = 0.5 * (g[2 + pc] - g_up[pc])
            else:
                row_part = 0.5 * (g_dn[pc] - g[pc])
            logit = at(8 + k, 0)
            label = get_lanes(t_out, 16 + 8 + k, rows, 16)
            ex = jnp.exp(-jnp.abs(logit))
            sig = jnp.where(logit >= 0, 1.0, ex) / (1.0 + ex)
            grads = (2.0 * scale * e0[k] - row_part, 2.0 * scale * e1[k] - col[pc], scale * (sig - label))
            for part in range(OUT_CH):
                for j in range(lanes // 128):
                    go_ref[j, pl.ds(4 * part + k, rows, stride=16), :] = grads[part][:, 128 * j : 128 * (j + 1)]
            term = jnp.maximum(logit, 0.0) + jnp.log1p(ex) - label * logit
            loss = loss + fold_lanes(e0[k] * e0[k] + e1[k] * e1[k] + spread[k] * spread[k] + term)

    sums_ref[...] = jnp.zeros_like(sums_ref)
    sums_ref[4:5, :] = jnp.sum(loss, axis=0, keepdims=True)
    head_ref[...] = jnp.zeros_like(head_ref)
    sg_ref[...] = jnp.zeros_like(sg_ref)
    d3_ref[...] = jnp.zeros_like(d3_ref)
    for k in (0, 1, rows + 2, rows + 3):
        g3_ref[256 * k : 256 * (k + 1), :] = jnp.zeros((256, lanes), bf16)

    sg_sum[...] = jnp.zeros_like(sg_sum)
    go_sum[...] = jnp.zeros_like(go_sum)

    def backward(rs):
        gos = [get_lanes(go_ref, r * 16, 16).astype(bf16) for r in rs]
        gts = [dot(wht_ref[...], go) for go in gos]
        head, gsum, sums = 0.0, 0.0, [0.0] * crops
        for r, go, gt in zip(rs, gos, gts):
            put_rows(go_out, r * 16, go)
            spot = (r + 1) * 128
            head = head + dot_nt(rows_of(h3_ref, spot, 128), go)
            gsum = gsum + fold_lanes(go.astype(f32))
            g = jnp.where(rows_of(m_ref, spot, 128).astype(f32) > 0, gt.astype(bf16).astype(f32), 0.0)
            gb = g.astype(bf16)
            for c in range(crops):
                sums[c] = sums[c] + fold_lanes(g[:, width * c : width * (c + 1)])
            parts = []
            for pr in range(2):
                even, odd = g[64 * pr : 64 * pr + 32], g[64 * pr + 32 : 64 * pr + 64]
                parts += [
                    from_left(odd, crops).astype(bf16),
                    gb[64 * pr : 64 * pr + 64],
                    from_right(even, crops).astype(bf16),
                ]
            put_rows(g3_ref, (r + 2) * 256, jnp.concatenate(parts, axis=0))
        head_ref[...] += head
        go_sum[...] += gsum
        for c in range(crops):
            sg_sum[c] += sums[c]

    repeat_rows(rows, 4, backward)
    for c in range(crops):
        sg_ref[c : c + 1, :] = lane_sums(sg_sum[c])[0:1]
    sums_ref[3:4, 0:16] = lane_sums(go_sum[...])[0:1]
    sg_copies = share(tiles, "tile", sg_ref, sg_got, s2_send, s2_recv)

    def down(ks):
        both = [dot(wd3_ref[...], rows_of(g3_ref, k * 256 + 128, 512)) for k in ks]
        for k, b in zip(ks, both):
            put_rows(gc_ref, k * 64, b[0:64] + b[64:128])

    down([0, 1])
    rim_lo[...] = gc_ref[0:128, :].astype(bf16)
    down([rows, rows + 1])
    rim_hi[...] = gc_ref[64 * rows : 64 * rows + 128, :].astype(bf16)
    finish_rims = swap_edges(tiles, [(rim_lo, rim_hi, rim_up, rim_dn)], rim_send, rim_recv)
    repeat_rows(rows - 2, 7, down, 2)

    def weights_three(ks):
        d3 = 0.0
        for k in ks:
            gs = [rows_of(g3_ref, k * 256 + 128 * j + 160, 64) for j in range(4)]
            d3 = d3 + dot_nt(jnp.concatenate(gs, axis=0), rows_of(x3_ref, (k + 1) * 192, 192))
        d3_ref[...] += d3

    repeat_rows(rows + 2, 6, weights_three)
    for tap in range(9):
        a, b = tap // 3, tap % 3
        total = jnp.zeros((CH_ONE, CH_TWO), f32)
        for first in (2 - a, 3 - a):
            for pc in range(2):
                s = (pc + b + 1) // 2
                total = total + d3_ref[64 * first + 32 * pc : 64 * first + 32 * pc + 32, 64 * s : 64 * (s + 1)]
        if tap < 8:
            pay_a[32 * (tap // 2) : 32 * (tap // 2 + 1), 64 * (tap % 2) : 64 * (tap % 2 + 1)] = total
        else:
            pay_a[128:144, :] = jnp.concatenate([total[0:16], total[16:32]], axis=1)
    outer = jnp.zeros((CH_ONE, 128), f32)
    for c in range(crops):
        outer = outer + as_column(over_phases(sg_ref[c : c + 1, :]))[0:32] * jnp.concatenate([unit[c : c + 1]] * 2, axis=1)
        sums_ref[2:3, :] += sg_ref[c : c + 1, :]
    head = jnp.concatenate([head_ref[...], jnp.zeros((128, 112), f32)], axis=1)
    pay_a[144:160, :] = jnp.transpose(head)[0:16]
    pay_a[160:176, :] = jnp.concatenate([outer[0:16, 0:64], outer[16:32, 0:64]], axis=1)
    pay_a[176:184, :] = sums_ref[...]
    if pay_a.shape[0] > 184:
        pay_a[184:, :] = jnp.zeros((pay_a.shape[0] - 184, 128), f32)
    reduce_a.scatter()

    wait_all(sg_copies)
    style_grad = over_phases(in_order(sg_got, tiles))[:, 0:32]
    grad_unit = jnp.dot(style_grad, ws_ref[...], precision=highest, preferred_element_type=f32)
    mixed = jnp.mean(style_raw * grad_unit, axis=1, keepdims=True)
    grad_raw = style_inv * grad_unit - style_inv * style_inv * style_inv * style_raw * mixed
    grad_raw = jnp.concatenate([grad_raw / coarse_count] * 2, axis=1)
    raw = [as_column(grad_raw[c : c + 1])[0:64] for c in range(crops)]
    pay_c[...] = jnp.zeros_like(pay_c)
    d2_ref[...] = jnp.zeros_like(d2_ref)
    d1_ref[...] = jnp.zeros_like(d1_ref)
    g2_sum[...] = jnp.zeros_like(g2_sum)
    raw = jnp.concatenate([wide(v, width) for v in raw], axis=1)
    g2_ref = g3_ref

    def masked(ks, extras=None):
        sums = 0.0
        for j, k in enumerate(ks):
            coarse = rows_of(gc_ref, k * 64, 64)
            if extras is not None:
                coarse = coarse + extras[j]
            grad = (coarse + raw).astype(bf16).astype(f32)
            h2 = rows_of(x3_ref, (k + 1) * 192 + 64, 64).astype(f32)
            g = jnp.where(h2 > 0, grad, 0.0)
            if extras is None or 0 < j < 3:
                sums = sums + fold_lanes(g)
            put_rows(g2_ref, k * 192, three_columns(g.astype(bf16), g, crops))
        g2_sum[...] += sums

    repeat_rows(rows - 2, 7, masked, 2)
    finish_rims()
    up = jnp.where(edge[0] < 0, rim_up[...].astype(f32), 0.0)
    dn = jnp.where(edge[1] > rows, rim_dn[...].astype(f32), 0.0)
    masked([0, 1, rows, rows + 1], [up[0:64], up[64:128], dn[0:64], dn[64:128]])
    pay_b[...] = jnp.zeros_like(pay_b)

    pay_b[160:161, 0:64] = lane_sums(g2_sum[...])[0:1]

    def weights_two(rs):
        d2 = 0.0
        for r in rs:
            d2 = d2 + dot_nt(rows_of(x2_ref, (r + 2) * 96, 288), rows_of(g2_ref, (r + 1) * 192 + 64, 64))
        d2_ref[...] += d2

    repeat_rows(rows, 8, weights_two)
    reduce_a.across()
    rest = jnp.concatenate([d2_ref[160:288, :], jnp.zeros((32, 64), f32)], axis=0)
    pay_b[0:160, :] = jnp.concatenate([d2_ref[0:160, :], rest], axis=1)
    reduce_b.scatter()

    def last_back(rs):
        gps = [dot(wd2_ref[...], rows_of(g2_ref, r * 192, 576)) for r in rs]
        gts = [dot(wht_ref[...], rows_of(go_out, r * 16, 16)) for r in rs]
        d1 = 0.0
        for r, gp, gt in zip(rs, gps, gts):
            gp = 0.25 * gp.astype(bf16).astype(f32)
            g1 = (jnp.concatenate([gp] * 4, axis=0) + gt.astype(bf16).astype(f32)).astype(bf16).astype(f32)
            h1 = rows_of(h1_ref, (r + 3) * 128, 128).astype(f32)
            gb = jnp.where(h1 > 0, g1, 0.0).astype(bf16)
            d1 = d1 + dot_nt(gb, jnp.concatenate([rows_of(y_ref, (r + 3) * 16, 32), ones_ref[...]], axis=0))
        d1_ref[...] += d1

    half = rows // 2
    repeat_rows(half, 4, last_back)
    reduce_a.gather(full_a)
    reduce_b.across()
    repeat_rows(rows - half, 4, last_back, half)
    d1 = jnp.transpose(jnp.concatenate([d1_ref[...], jnp.zeros((128, 80), f32)], axis=1))
    pay_c[8:9, :] = d1[32:33]
    total = jnp.zeros((32, 128), f32)
    for p in range(4):
        total = total + turn(turn(d1[0:32], -32 * p, 1), -(8 * (p // 2) + p % 2), 0)
    packed = lane_group(total[0:8], 0)
    for k in range(1, 4):
        packed = packed + turn(lane_group(total[8 * k : 8 * (k + 1)], 0), 32 * k, 1)
    pay_c[0:8, :] = packed
    copies = share(tiles, "tile", pay_c, got_c, sems[12], sems[13])
    reduce_b.gather(full_b)
    wait_all(copies)
    own_c[...] = in_order(got_c, tiles)
    copies = share(images, "img", own_c, met_c, sems[14], sems[15])
    reduce_a.finish()
    size_a, size_b = full_a.shape[0], full_b.shape[0]
    o_ref[0:size_a, :] = full_a[...]
    reduce_b.finish()
    o_ref[size_a : size_a + size_b, :] = full_b[...]
    wait_all(copies)
    o_ref[size_a + size_b :, :] = in_order(met_c, images)


def update_kernel(pixel_count, second_at, third_at, count_ref, sum_ref, *refs):
    olds, outs, loss_ref = refs[:18], refs[18:36], refs[36]
    rate = 1.0 / (jnp.zeros((8, 128), f32) + (count_ref[0].astype(f32) + 1.0))

    def step(index, spot, grad):
        weight, momentum, average = (olds[3 * index + k][spot] for k in range(3))
        decayed = grad + decay_rate * weight
        momentum = momentum_rate * momentum + decayed
        new = weight - learn_rate * (decayed + momentum_rate * momentum)
        outs[3 * index][spot] = new
        outs[3 * index + 1][spot] = momentum
        outs[3 * index + 2][spot] = average + (new - average) * rate[0:1, 0:1]

    first = sum_ref[third_at : third_at + 8, :]
    for a in range(3):
        for b in range(3):
            for i in range(2):
                grad = first[4 * i + b : 4 * i + b + 1, 32 * a : 32 * (a + 1)]
                step(0, (a, b, slice(i, i + 1), slice(None)), grad)
    for tap in range(9):
        a, b = tap // 3, tap % 3
        first = second_at + 32 * (tap % 5)
        half = 64 * (tap // 5)
        step(1, (a, b), sum_ref[first : first + 32, half : half + 64])
        if tap < 8:
            first = 32 * (tap // 2)
            lane = 64 * (tap % 2)
            grad = sum_ref[first : first + 32, lane : lane + 64]
        else:
            first = 128
            grad = jnp.concatenate([sum_ref[first : first + 16, 64 * k : 64 * (k + 1)] for k in range(2)], axis=0)
        step(2, (a, b), grad)
    first = 160
    grad = jnp.concatenate([sum_ref[first : first + 16, 64 * k : 64 * (k + 1)] for k in range(2)], axis=0)
    step(3, (slice(None), slice(None)), grad)
    head = sum_ref[144:160, :]
    total = jnp.zeros((16, 128), f32)
    for p in range(4):
        total = total + turn(turn(head, -32 * p, 1), -p, 0)
    total = jnp.concatenate([total[4 * o : 4 * o + 1] for o in range(OUT_CH)], axis=0)
    step(4, (slice(None), slice(None)), total[:, 0:32])
    sums = sum_ref[176:184, :]
    one = over_phases(jnp.sum(sum_ref[third_at + 8 : third_at + 16, :], axis=0, keepdims=True))
    two = jnp.sum(sum_ref[second_at + 160 : second_at + 168, :], axis=0, keepdims=True)
    three = over_phases(sums[2:3])
    lane = lax.broadcasted_iota(jnp.int32, (1, 128), 1)
    low = jnp.where(lane < 32, one, jnp.where(lane < 96, turn(two, 32, 1), three))
    ends = sums[3:4]
    ends = (ends + turn(ends, -1, 1)) + (turn(ends, -2, 1) + turn(ends, -3, 1))
    high = jnp.where(lane < 32, three, 0.0)
    for o in range(OUT_CH):
        high = jnp.where(lane == 32 + o, turn(ends, 32 + o - 4 * o, 1), high)
    grad = jnp.concatenate([low, high], axis=1)[:, 0 : olds[15].shape[0]]
    weight, momentum, average = (olds[15 + k][...].reshape(1, -1) for k in range(3))
    decayed = grad + decay_rate * weight
    momentum = momentum_rate * momentum + decayed
    new = weight - learn_rate * (decayed + momentum_rate * momentum)
    average = average + (new - average) * rate[0:1, 0:1]
    for k, value in enumerate((new, momentum, average)):
        outs[15 + k][...] = value.reshape(-1)
    loss_ref[0] = jnp.sum(sums[4:5]) / pixel_count


def on_device(
    images, nucleus, target_flow, cell_label, step_count,
    conv1_weight, conv1_momentum, conv1_average,
    conv2_weight, conv2_momentum, conv2_average,
    conv3_weight, conv3_momentum, conv3_average,
    style_weight, style_momentum, style_average,
    head_weight, head_momentum, head_average,
    biases, bias_momentum, bias_average,
):
    tiles = lax.axis_size("tile")
    crops, _, height, cols = images.shape
    rows, width = height // 2, cols // 2
    pixel_count = lax.axis_size("img") * tiles * crops * height * cols
    grad_scale = 1.0 / math.sqrt(pixel_count)
    coarse_count = tiles * rows * width

    def sds(shape, dtype=f32):
        return jax.ShapeDtypeStruct(shape, dtype)

    lanes = crops * width
    images_count = lax.axis_size("img")

    def other_way(w):
        return jnp.swapaxes(w, -1, -2)

    third = tuple(other_way(w) for w in (conv3_weight, conv3_momentum, conv3_average))
    style = tuple(other_way(w) for w in (style_weight, style_momentum, style_average))
    head = tuple(other_way(w) for w in (head_weight, head_momentum, head_average))

    edge = (crops, 2, HALO, cols)
    rim = (128, lanes)
    parts = [8 * pl.cdiv(sum(block), 8 * tiles) for block in BLOCK_ROWS[:2]]
    small = sum(BLOCK_ROWS[2])

    def buf(shape, dtype=bf16):
        return pltpu.VMEM(shape, dtype)

    def block_bufs(part):
        return [
            buf((part * tiles, 128), f32), buf((tiles, part, 128), f32), buf((part, 128), f32),
            buf((images_count, part, 128), f32), buf((part * tiles, 128), f32),
        ]

    sources = (
        images, target_flow, cell_label, conv1_weight, conv2_weight, third[0], head[0], biases, style[0],
    )
    block_sems = [DMA((tiles,)), DMA((tiles,)), DMA((images_count,)), DMA((images_count,)), DMA((tiles,)), DMA((tiles,))]
    summed = pl.pallas_call(
        lambda *refs: step_kernel(tiles, images_count, grad_scale, float(coarse_count), *refs),
        out_shape=sds((sum(parts) * tiles + small, 128)),
        in_specs=[SMEM] + [HBM] * 9,
        out_specs=VMEM,
        scratch_shapes=[buf(v.shape, v.dtype) for v in sources]
        + [
            buf(edge), buf(edge), buf(edge, jnp.int32), buf(edge, jnp.int32),
            buf((128, 48)), buf((CH_TWO, 9 * CH_ONE + 16)), buf((128, 14 * CH_TWO + 16)), buf((128, 16 * CH_ONE)),
            buf((CH_ONE, 9 * CH_TWO)), buf((16, 128)), buf((128, 16)),
            buf((8, 128), f32), buf((16, 128), f32), buf((32, 128), f32), buf((16, lanes)), buf((16, lanes)),
            buf((16 * (rows + 7), lanes)), buf((lanes // 128, 16 * (rows + 2), 128), f32),
            buf((128 * (rows + 6), lanes)), buf((96 * (rows + 6), lanes)), buf((192 * (rows + 4), lanes)),
            buf((128 * (rows + 2), lanes)), buf((128 * (rows + 2), lanes)),
            buf((lanes // 128, 16 * (rows + 2), 128), f32), buf((lanes // 128, 16 * rows, 128), f32),
            buf((16 * rows, lanes)), buf((256 * (rows + 4), lanes)), buf((64 * (rows + 2), lanes), f32),
            buf(rim), buf(rim), buf(rim), buf(rim),
            buf((8, 128), f32), buf((tiles, 8, 128), f32), buf((8, 128), f32), buf((tiles, 8, 128), f32),
            buf((128, 16), f32), buf((8, 128), f32),
            buf((256, 3 * CH_TWO), f32), buf((9 * CH_ONE, CH_TWO), f32), buf((128, 48), f32),
            buf((crops, CH_TWO, 128), f32), buf((crops, 128, 128), f32), buf((16, 128), f32), buf((CH_TWO, 128), f32),
        ]
        + block_bufs(parts[0])
        + block_bufs(parts[1])
        + [buf((small, 128), f32), buf((tiles, small, 128), f32), buf((small, 128), f32), buf((images_count, small, 128), f32)]
        + [DMA((9,)), DMA((4,)), DMA((4,)), DMA((tiles,)), DMA((tiles,)), DMA((tiles,)), DMA((tiles,)), DMA((2,)), DMA((2,))]
        + block_sems * 2
        + [DMA((tiles,)), DMA((tiles,)), DMA((images_count,)), DMA((images_count,))],
        compiler_params=pltpu.CompilerParams(collective_id=1, has_side_effects=True, vmem_limit_bytes=60 * 2**20),
        name="step",
    )(nucleus, *sources)

    olds = (
        (conv1_weight, conv1_momentum, conv1_average)
        + (conv2_weight, conv2_momentum, conv2_average)
        + third + style + head
        + (biases, bias_momentum, bias_average)
    )
    news = pl.pallas_call(
        lambda *refs: update_kernel(float(pixel_count), parts[0] * tiles, sum(parts) * tiles, *refs),
        out_shape=tuple(sds(v.shape) for v in olds) + (sds((1,)),),
        in_specs=[SMEM] + [VMEM] * 19,
        out_specs=[VMEM] * 18 + [SMEM],
        compiler_params=pltpu.CompilerParams(vmem_limit_bytes=16 * 2**20),
        name="update",
    )(step_count, summed, *olds)
    return (news[18], *news[0:6], *(other_way(w) for w in news[6:15]), *news[15:18])


def solution(mesh):
    return jax.shard_map(
        on_device,
        mesh=mesh,
        in_specs=(
            P("img", None, "tile", None),
            P("img"),
            P("img", None, "tile", None),
            P("img", "tile", None),
        )
        + (P(),) * 19,
        out_specs=(P(),) * 19,
        check_vma=False,
    )
```

```python
import math

import jax
import jax.numpy as jnp
from jax import lax
from jax.experimental import pallas as pl
from jax.experimental.pallas import tpu as pltpu
from jax.sharding import PartitionSpec as P

CH_ONE = 32
CH_TWO = 64
OUT_CH = 3

momentum_rate = 0.9
learn_rate = 0.02
decay_rate = 0.0001
norm_eps = 1e-05
highest = lax.Precision.HIGHEST
f32 = jnp.float32
bf16 = jnp.bfloat16

HALO = 8
EARLY = 6
VMEM = pl.BlockSpec(memory_space=pltpu.VMEM)
SMEM = pl.BlockSpec(memory_space=pltpu.SMEM)
HBM = pl.BlockSpec(memory_space=pltpu.HBM)
MESH = pl.DeviceIdType.MESH
DMA = pltpu.SemaphoreType.DMA

BLOCK_ROWS = ((144, 16, 16, 8), (160, 8), (8,))


def dot(a, b):
    return jnp.dot(a, b, preferred_element_type=f32)


def dot_nt(a, b, precision=None):
    return lax.dot_general(a, b, (((1,), (1,)), ((), ())), preferred_element_type=f32, precision=precision)


def edge_select(x, crops, first):
    width = x.shape[1] // crops
    lane = lax.broadcasted_iota(jnp.int32, (x.shape[0], 128), 1)
    parts = []
    for c in range(crops):
        low, high = width * c, width * (c + 1)
        if first:
            parts += [jnp.where(lane == 0, 0.0, x[:, low : low + 128]), x[:, low + 128 : high]]
        else:
            parts += [x[:, low : high - 128], jnp.where(lane == 127, 0.0, x[:, high - 128 : high])]
    return jnp.concatenate(parts, axis=1)


def from_left(x, crops):
    return edge_select(pltpu.roll(x, 1, 1), crops, True)


def from_right(x, crops):
    return edge_select(pltpu.roll(x, x.shape[1] - 1, 1), crops, False)


def three_columns(mid, x, crops):
    return jnp.concatenate([from_left(x, crops).astype(bf16), mid, from_right(x, crops).astype(bf16)], axis=0)


def pieces_of(x):
    high = x.astype(bf16)
    rest = x - high.astype(f32)
    mid = rest.astype(bf16)
    return high.astype(f32), mid.astype(f32), rest - mid.astype(f32)


def repeat_rows(count, limit, body, first=0):
    step = max(k for k in range(1, limit + 1) if count % k == 0)

    def run(k, carry):
        body([first + k * step + j for j in range(step)])
        return carry

    lax.fori_loop(0, count // step, run, 0)


def turn(x, by, axis):
    by = by % x.shape[axis]
    return pltpu.roll(x, by, axis) if by else x


def lane_group(x, group, size=32):
    lane = lax.broadcasted_iota(jnp.int32, x.shape, 1)
    return jnp.where(lane // size == group, x, 0.0)


def over_phases(x):
    return (x + turn(x, 32, 1)) + (turn(x, 64, 1) + turn(x, 96, 1))


def as_column(row):
    return jnp.transpose(jnp.broadcast_to(row, (128, 128)))


def fold_lanes(x):
    parts = [x[:, 128 * k : 128 * (k + 1)] for k in range(x.shape[1] // 128)]
    while len(parts) > 1:
        parts = [a + b for a, b in zip(parts[0::2], parts[1::2])] + parts[len(parts) // 2 * 2 :]
    return parts[0]


def lane_sums(x):
    return dot_nt(jnp.ones((8, 128), f32), x, highest)


def wide(tile, width):
    return jnp.concatenate([tile] * (width // 128), axis=1)


def rows_of(ref, start, size):
    return ref[pl.ds(pl.multiple_of(start, 16), size), :]


def put_rows(ref, start, value):
    ref[pl.ds(pl.multiple_of(start, 16), value.shape[0]), :] = value


def put_lanes(ref, start, value):
    for k in range(value.shape[1] // 128):
        ref[k, pl.ds(pl.multiple_of(start, 16), value.shape[0]), :] = value[:, 128 * k : 128 * (k + 1)]


def get_lanes(ref, start, size, stride=None):
    spot = pl.ds(start, size, stride=stride) if stride else pl.ds(pl.multiple_of(start, 16), size)
    return jnp.concatenate([ref[k, spot, :] for k in range(ref.shape[0])], axis=1)


def strip_edges(tiles, rows):
    me = lax.axis_index("tile")
    return -me * rows, (tiles - me) * rows


def valid(row, edge):
    return jnp.where((row >= edge[0]) & (row < edge[1]), 1.0, 0.0).astype(f32)


def greet(sizes):
    gate = pltpu.get_barrier_semaphore()
    for axis, count in sizes:
        me = lax.axis_index(axis)
        for j in range(1, count):
            pl.semaphore_signal(gate, inc=1, device_id={axis: lax.rem(me + j, count)}, device_id_type=MESH)
    return lambda: pl.semaphore_wait(gate, sum(count - 1 for _, count in sizes))


def send_all(count, axis, source, target, send_sem, recv_sem):
    me = lax.axis_index(axis)
    copies = []
    for j in range(1, count):
        to = lax.rem(me + j, count)
        copy = pltpu.make_async_remote_copy(
            src_ref=source(to), dst_ref=target, send_sem=send_sem.at[j - 1], recv_sem=recv_sem.at[j - 1],
            device_id={axis: to}, device_id_type=MESH,
        )
        copy.start()
        copies.append(copy)
    return copies


def wait_all(copies):
    for copy in copies:
        copy.wait()


def in_order(ref, count):
    total = ref[0]
    for k in range(1, count):
        total = total + ref[k]
    return total


def swap_edges(tiles, pairs, send_sem, recv_sem):
    me = lax.axis_index("tile")
    copies = []
    for k, (low, high, from_before, from_after) in enumerate(pairs):
        down = pltpu.make_async_remote_copy(
            src_ref=high, dst_ref=from_before, send_sem=send_sem.at[2 * k], recv_sem=recv_sem.at[2 * k],
            device_id={"tile": jnp.minimum(me + 1, tiles - 1)}, device_id_type=MESH,
        )
        up = pltpu.make_async_remote_copy(
            src_ref=low, dst_ref=from_after, send_sem=send_sem.at[2 * k + 1], recv_sem=recv_sem.at[2 * k + 1],
            device_id={"tile": jnp.maximum(me - 1, 0)}, device_id_type=MESH,
        )
        copies.append((down, up))

    @pl.when(me < tiles - 1)
    def _():
        for down, _up in copies:
            down.start()

    @pl.when(me > 0)
    def _():
        for _down, up in copies:
            up.start()

    def finish():
        @pl.when(me < tiles - 1)
        def _():
            for down, up in copies:
                down.wait_send()
                up.wait_recv()

        @pl.when(me > 0)
        def _():
            for down, up in copies:
                up.wait_send()
                down.wait_recv()

    return finish


def share(count, axis, source, got, send_sem, recv_sem):
    me = lax.axis_index(axis)
    got[me] = source[...]
    return send_all(count, axis, lambda to: source, got.at[me], send_sem, recv_sem)


class Reduction:
    def __init__(self, tiles, images, pay, got, own, met, sems):
        self.tiles, self.images = tiles, images
        self.pay, self.got, self.own, self.met, self.sems = pay, got, own, met, sems
        self.part = own.shape[0]
        self.me = lax.axis_index("tile")

    def block(self, k):
        return pl.ds(pl.multiple_of(k * self.part, 8), self.part)

    def scatter(self):
        self.got[self.me] = self.pay[self.block(self.me), :]
        self.copies = send_all(
            self.tiles, "tile", lambda to: self.pay.at[self.block(to), :], self.got.at[self.me], self.sems[0], self.sems[1]
        )

    def across(self):
        wait_all(self.copies)
        self.own[...] = in_order(self.got, self.tiles)
        self.copies = share(self.images, "img", self.own, self.met, self.sems[2], self.sems[3])

    def gather(self, full):
        wait_all(self.copies)
        full[self.block(self.me), :] = in_order(self.met, self.images)
        here = full.at[self.block(self.me), :]
        self.copies = send_all(self.tiles, "tile", lambda to: here, here, self.sems[4], self.sems[5])

    def finish(self):
        wait_all(self.copies)


def first_tables(k1_ref, k2_ref, bias_ref, w1_ref, w2_ref, base_ref):
    base_ref[...] = jnp.zeros_like(base_ref)
    for a in range(3):
        for b in range(3):
            for i in range(2):
                base_ref[8 * a + 4 * i + b : 8 * a + 4 * i + b + 1, 0:32] = k1_ref[a, b, i : i + 1, :]
    base = base_ref[...]
    w1t = jnp.zeros((32, 128), f32)
    for p in range(4):
        w1t = w1t + turn(turn(base, 8 * (p // 2) + p % 2, 0), 32 * p, 1)
    bias = bias_ref[...].reshape(1, -1)
    row = lax.broadcasted_iota(jnp.int32, (16, 128), 0)

    def piece_rows(values):
        table = jnp.zeros((16, 128), f32)
        for k, piece in enumerate(pieces_of(values)):
            table = jnp.where(row == k, jnp.broadcast_to(piece, (16, 128)), table)
        return table

    b1 = piece_rows(jnp.concatenate([bias[:, 0:32]] * 4, axis=1))
    w1_ref[...] = jnp.transpose(jnp.concatenate([w1t, b1], axis=0)).astype(bf16)

    k2 = [[k2_ref[a, b].astype(bf16).astype(f32) for b in range(3)] for a in range(3)]
    w2t = jnp.concatenate([k2[a][b] for a in range(3) for b in range(3)], axis=0)
    b2 = piece_rows(jnp.concatenate([bias[:, 32:96]] * 2, axis=1))[:, 0:64]
    w2_ref[...] = jnp.transpose(jnp.concatenate([w2t, b2], axis=0)).astype(bf16)


def later_tables(k2_ref, k3_ref, kh_ref, bias_ref, w3_ref, wd3_ref, wd2_ref, wh_ref, wht_ref, b3_ref, bh_ref):
    k2 = [[k2_ref[a, b].astype(bf16).astype(f32) for b in range(3)] for a in range(3)]
    wd2_ref[...] = jnp.concatenate([k2[2 - s][2 - t] for s in range(3) for t in range(3)], axis=1).astype(bf16)

    def tap_sum(first, second):
        total = None
        for a in first:
            for b in second:
                total = k3[a][b] if total is None else total + k3[a][b]
        return jnp.zeros((CH_ONE, CH_TWO), f32) if total is None else total

    k3 = [[k3_ref[a, b].astype(bf16).astype(f32) for b in range(3)] for a in range(3)]
    up = [[[a for a in range(3) if (p + a + 1) // 2 == r] for r in range(3)] for p in range(2)]
    for p in range(4):
        w3 = jnp.concatenate([tap_sum(up[p // 2][r], up[p % 2][c]) for r in range(3) for c in range(3)], axis=1)
        w3_hi = w3.astype(bf16)
        low = w3 - w3_hi.astype(f32)
        low = jnp.concatenate([low[:, 64:128], low[:, 192:384], low[:, 448:512]], axis=1)
        w3_ref[32 * p : 32 * (p + 1), 0:896] = jnp.concatenate([w3_hi, low.astype(bf16)], axis=1)
    down = ((2,), (1, 2), (0, 1), (0,))
    wd3 = jnp.transpose(jnp.concatenate([tap_sum(down[r], down[c]) for r in range(4) for c in range(4)], axis=0))
    wd3_hi = wd3.astype(bf16)
    wd3_ref[0:64, :] = wd3_hi
    wd3_ref[64:128, :] = (wd3 - wd3_hi.astype(f32)).astype(bf16)

    row = lax.broadcasted_iota(jnp.int32, (16, 128), 0)
    lane = lax.broadcasted_iota(jnp.int32, (16, 128), 1)
    wh = jnp.zeros((16, 128), f32)
    for o in range(OUT_CH):
        one = jnp.concatenate([kh_ref[o : o + 1, :]] * 4, axis=1)
        wh = jnp.where(row // 4 == o, jnp.broadcast_to(one, (16, 128)), wh)
    wh = jnp.where(row % 4 == lane // 32, wh, 0.0)
    wh_ref[...] = wh.astype(bf16)
    wht_ref[...] = jnp.transpose(wh).astype(bf16)

    bias = bias_ref[...].reshape(1, -1)
    b3_ref[...] = jnp.zeros_like(b3_ref)
    b3_ref[0:1, :] = jnp.concatenate([bias[:, 96:128] + bias[:, 128:160]] * 4, axis=1)
    bh = jnp.zeros((16, 128), f32)
    for o in range(OUT_CH):
        bh = jnp.where(row // 4 == o, jnp.broadcast_to(bias[:, 160 + o : 161 + o], (16, 128)), bh)
    bh_ref[...] = bh


def split_columns(x, select):
    even, odd = [], []
    for k in range(x.shape[1] // 256):
        piece = dot(x[:, 256 * k : 256 * (k + 1)], select)
        even.append(piece[:, 0:128])
        odd.append(piece[:, 128:256])
    return jnp.concatenate(even, axis=1), jnp.concatenate(odd, axis=1)


def step_kernel(
    tiles, images, scale, coarse_count,
    nucleus_ref, x_hbm, t_hbm, label_hbm, k1_hbm, k2_hbm, k3_hbm, kh_hbm, bias_hbm, ws_hbm,
    o_ref,
    x_ref, t_ref, label_ref, k1_ref, k2_ref, k3_ref, kh_ref, bias_ref, ws_ref,
    x_lo, x_hi, t_lo, t_hi,
    w1_ref, w2_ref, w3_ref, wd3_ref, wd2_ref, wh_ref, wht_ref, b3_ref, bh_ref, base_ref, ones_ref, mark_ref,
    y_ref, t_out, h1_ref, x2_ref, x3_ref, h3_ref, m_ref, fe_ref, go_ref, g3_ref, gc_ref,
    rim_lo, rim_hi, rim_up, rim_dn,
    style_ref, style_got, sg_ref, sg_got, head_ref, sums_ref, d3_ref, d2_ref, d1_ref,
    style_sum, sg_sum, go_sum, g2_sum,
    pay_a, got_a, own_a, met_a, full_a, pay_b, got_b, own_b, met_b, full_b,
    pay_c, got_c, own_c, met_c,
    load_sems, halo_send, halo_recv, s1_send, s1_recv, s2_send, s2_recv, rim_send, rim_recv,
    *sems,
):
    pre_ref = gc_ref
    reduce_a = Reduction(tiles, images, pay_a, got_a, own_a, met_a, sems[0:6])
    reduce_b = Reduction(tiles, images, pay_b, got_b, own_b, met_b, sems[6:12])
    arrived = greet((("tile", tiles), ("img", images)))
    loads = [
        pltpu.make_async_copy(source, target, load_sems.at[k])
        for k, (source, target) in enumerate(
            (
                (k1_hbm, k1_ref), (k2_hbm, k2_ref), (bias_hbm, bias_ref), (x_hbm, x_ref),
                (t_hbm, t_ref), (label_hbm, label_ref), (k3_hbm, k3_ref), (kh_hbm, kh_ref), (ws_hbm, ws_ref),
            )
        )
    ]
    for load in loads:
        load.start()
    ones_ref[...] = jnp.ones_like(ones_ref)
    for load in loads[0:3]:
        load.wait()
    first_tables(k1_ref, k2_ref, bias_ref, w1_ref, w2_ref, base_ref)
    arrived()
    last = x_ref.shape[2] - HALO
    finish_halo = swap_edges(
        tiles,
        [
            (ref.at[:, :, pl.ds(0, HALO), :], ref.at[:, :, pl.ds(last, HALO), :], lo, hi)
            for ref, lo, hi in ((x_hbm, x_lo, x_hi), (t_hbm, t_lo, t_hi))
        ],
        halo_send, halo_recv,
    )
    loads[3].wait()
    crops = x_ref.shape[0]
    width = x_ref.shape[3] // 2
    lanes = crops * width
    height = x_ref.shape[2]
    rows = height // 2
    edge = strip_edges(tiles, rows)
    r_id = lax.broadcasted_iota(jnp.int32, (256, 256), 0)
    c_id = lax.broadcasted_iota(jnp.int32, (256, 256), 1)
    select = jnp.where(r_id == 2 * (c_id % 128) + c_id // 128, 1.0, 0.0).astype(bf16)
    y_rows = y_ref.shape[0]
    ri = lax.broadcasted_iota(jnp.int32, (y_rows, 8 * height), 0)
    ci = lax.broadcasted_iota(jnp.int32, (y_rows, 8 * height), 1)
    fine = 2 * (ri // 16) + (ri // 8) % 2 - 7
    source = (ri % 4) * 2 * height + (ri // 4) % 2 * height + fine
    perm_x = jnp.where((ci == source) & (fine >= 0) & (fine < height), 1.0, 0.0).astype(bf16)
    ri = lax.broadcasted_iota(jnp.int32, (128, 16 * HALO), 0)
    ci = lax.broadcasted_iota(jnp.int32, (128, 16 * HALO), 1)
    fine = 2 * (ri // 16) + (ri // 8) % 2 - 7
    fine = jnp.where(ri < 64, fine, fine + y_rows // 8 - 16)
    source = jnp.where(fine < 0, fine + HALO, 2 * HALO + fine - height)
    source = (ri % 4) * 4 * HALO + (ri // 4) % 2 * HALO + source
    perm_h = jnp.where((ci == source) & ((fine < 0) | (fine >= height)), 1.0, 0.0).astype(bf16)
    has_up, has_dn = edge[0] < 0, edge[1] > rows

    def both_columns(of_crop):
        even, odd = [], []
        for c in range(crops):
            first, second = split_columns(of_crop(c), select)
            even.append(first)
            odd.append(second)
        return jnp.concatenate(even, axis=1), jnp.concatenate(odd, axis=1)

    def own_rows(c):
        return jnp.concatenate([x_ref[c, k] for k in range(2)], axis=0)

    def halo_rows(c):
        pieces = [jnp.where(has_up, x_lo[c, k].astype(f32), 0.0) for k in range(2)]
        pieces += [jnp.where(has_dn, x_hi[c, k].astype(f32), 0.0) for k in range(2)]
        return jnp.concatenate(pieces, axis=0).astype(bf16)

    def target_rows(c):
        pieces = [t_ref[c, 0].astype(f32), t_ref[c, 1].astype(f32), label_ref[c].astype(f32)]
        pieces += [jnp.where(has_up, t_lo[c, k], 0).astype(f32) for k in range(2)]
        pieces += [jnp.where(has_dn, t_hi[c, k], 0).astype(f32) for k in range(2)]
        return jnp.concatenate(pieces, axis=0).astype(bf16)

    def pixel_windows(of_crop, second):
        even, odd = both_columns(of_crop)
        row = lax.broadcasted_iota(jnp.int32, even.shape, 0)
        crop = lax.broadcasted_iota(jnp.int32, even.shape, 1) // width
        gate = jnp.ones(even.shape, f32)
        for c in range(crops):
            gate = jnp.where(second(row) & (crop == c), nucleus_ref[c].astype(f32), gate)
        even, odd = even * gate, odd * gate
        return jnp.concatenate([from_left(odd, crops), even, odd, from_right(even, crops)], axis=0).astype(bf16)

    y_ref[...] = dot(perm_x, pixel_windows(own_rows, lambda row: row >= height)).astype(bf16)

    def conv_one(ks, inside=True):
        pre = [
            dot(w1_ref[...], jnp.concatenate([rows_of(y_ref, k * 16, 32), ones_ref[...]], axis=0)) for k in ks
        ]
        for k, p in zip(ks, pre):
            p = jnp.maximum(p, 0.0)
            hidden = (p if inside else p * valid(k - 3, edge)).astype(bf16)
            put_rows(h1_ref, k * 128, hidden)
            h = hidden.astype(f32)
            pooled = (0.25 * ((h[0:32] + h[32:64]) + (h[64:96] + h[96:128]))).astype(bf16)
            put_rows(x2_ref, k * 96, three_columns(pooled, pooled.astype(f32), crops))

    def conv_two(qs, inside=True):
        pre = [
            dot(w2_ref[...], jnp.concatenate([rows_of(x2_ref, q * 96, 288), ones_ref[...]], axis=0)) for q in qs
        ]
        sums = [0.0] * crops
        for q, p in zip(qs, pre):
            p = jnp.maximum(p, 0.0)
            hidden = (p if inside else p * valid(q - 2, edge)).astype(bf16)
            h = hidden.astype(f32)
            put_rows(x3_ref, q * 192, three_columns(hidden, h, crops))
            for c in range(crops):
                sums[c] = sums[c] + fold_lanes(h[:, width * c : width * (c + 1)])
        if inside:
            for c in range(crops):
                style_sum[c] += sums[c]

    repeat_rows(rows - 2, 7, conv_one, 4)
    finish_halo()
    extra = dot(perm_h, pixel_windows(halo_rows, lambda row: row // HALO % 2 == 1))
    y_ref[0:64, :] = (y_ref[0:64, :].astype(f32) + extra[0:64]).astype(bf16)
    y_ref[y_rows - 64 : y_rows, :] = (y_ref[y_rows - 64 : y_rows, :].astype(f32) + extra[64:128]).astype(bf16)
    conv_one([0, 1, 2, 3, rows + 2, rows + 3, rows + 4, rows + 5], False)
    style_sum[...] = jnp.zeros_like(style_sum)
    repeat_rows(rows, 8, conv_two, 2)
    style_ref[...] = jnp.zeros_like(style_ref)
    for c in range(crops):
        style_ref[c : c + 1, 0:64] = lane_sums(style_sum[c])[0:1]
    style_copies = share(tiles, "tile", style_ref, style_got, s1_send, s1_recv)

    conv_two([0, 1], False)
    conv_two([rows + 2, rows + 3], False)
    for load in loads[4:]:
        load.wait()
    t_rows = 3 * height + 4 * HALO
    ri = lax.broadcasted_iota(jnp.int32, (t_out.shape[1], 2 * t_rows), 0)
    ci = lax.broadcasted_iota(jnp.int32, (t_out.shape[1], 2 * t_rows), 1)
    part = (ri // 4) % 4
    fine = 2 * (ri // 16) + (ri // 2) % 2 - 2
    source = jnp.where(
        fine < 0,
        3 * height + part * HALO + fine + HALO,
        jnp.where(fine < height, part * height + fine, 3 * height + 2 * HALO + part * HALO + fine - height),
    )
    outside = (fine < 0) | (fine >= height)
    known = (part < 2) | ((part == 2) & jnp.logical_not(outside))
    perm_t = jnp.where((ci == (ri % 2) * t_rows + source) & known, 1.0, 0.0).astype(bf16)
    even, odd = both_columns(target_rows)
    put_lanes(t_out, 0, dot(perm_t, jnp.concatenate([even, odd], axis=0).astype(bf16)))
    later_tables(k2_ref, k3_ref, kh_ref, bias_ref, w3_ref, wd3_ref, wd2_ref, wh_ref, wht_ref, b3_ref, bh_ref)

    def third_input(k):
        x = rows_of(x3_ref, k * 192, 576)
        return jnp.concatenate([x, x[64:128], x[192:384], x[448:512]], axis=0)

    for k in range(EARLY):
        put_rows(pre_ref, k * 128, dot(w3_ref[:, 0:896], third_input(k)))
    wait_all(style_copies)
    style_raw = in_order(style_got, tiles)[:, 0:64] / coarse_count
    style_inv = lax.rsqrt(jnp.mean(style_raw * style_raw, axis=1, keepdims=True) + norm_eps)
    unit = style_raw * style_inv
    vec = dot_nt(unit, ws_ref[...], highest)
    vec = jnp.concatenate([vec] * 4, axis=1) + b3_ref[0:1, :]
    bias3 = jnp.concatenate([wide(as_column(vec[c : c + 1]), width) for c in range(crops)], axis=1)
    row = lax.broadcasted_iota(jnp.int32, (16, lanes), 0)
    lane = lax.broadcasted_iota(jnp.int32, (16, lanes), 1)
    mark_ref[...] = jnp.where(row // 3 == lane // width, 1.0, 0.0).astype(bf16)
    row = lax.broadcasted_iota(jnp.int32, (128, 128), 0)
    table = jnp.zeros((128, 128), f32)
    for c in range(crops):
        for k, piece in enumerate(pieces_of(vec[c : c + 1])):
            table = jnp.where(row == 3 * c + k, jnp.broadcast_to(piece, (128, 128)), table)
    w3_ref[:, 896:912] = jnp.transpose(table)[:, 0:16].astype(bf16)

    def forward(ks, early=False):
        pre = []
        for k in ks:
            if early:
                pre.append(rows_of(pre_ref, k * 128, 128) + bias3)
            else:
                pre.append(dot(w3_ref[...], jnp.concatenate([third_input(k), mark_ref[...]], axis=0)))
        hs = []
        for k, p in zip(ks, pre):
            p = jnp.maximum(p, 0.0)
            h3 = (p + rows_of(h1_ref, (k + 2) * 128, 128).astype(f32)).astype(bf16)
            put_rows(h3_ref, k * 128, h3)
            put_rows(m_ref, k * 128, p.astype(bf16))
            hs.append(h3)
        outs = [dot(wh_ref[...], h) for h in hs]
        for k, o in zip(ks, outs):
            o = o + wide(bh_ref[...], lanes)
            t = get_lanes(t_out, k * 16, 16)
            fe = (o[0:8] - 0.25 * t[0:8]) * valid(k - 1, edge)
            put_lanes(fe_ref, k * 16, jnp.concatenate([fe, o[8:16]], axis=0))

    forward(range(EARLY), True)
    repeat_rows(rows + 2 - EARLY, 12, forward, EARLY)

    r_id = lax.broadcasted_iota(jnp.int32, (rows, lanes), 0)
    above = jnp.where(r_id - 1 >= edge[0], 1.0, 0.0)
    below = jnp.where(r_id + 1 < edge[1], 1.0, 0.0)
    go_ref[...] = jnp.zeros_like(go_ref)

    def at(part, off):
        return get_lanes(fe_ref, 16 * (1 + off) + part, rows, 16)

    def column_part(pr, off):
        odd, even = at(4 + 2 * pr + 1, off), at(4 + 2 * pr, off)
        return 0.5 * (odd - from_left(odd, crops)), 0.5 * (from_right(even, crops) - even)

    loss = jnp.zeros((rows, 128), f32)
    e0 = [at(k, 0) for k in range(4)]
    e1 = [at(4 + k, 0) for k in range(4)]
    cols0, cols1 = column_part(0, 0), column_part(1, 0)
    cols_up, cols_dn = column_part(1, -1), column_part(0, 1)
    spread = [None] * 4
    g_up, g_dn = [None] * 2, [None] * 2
    for pc in range(2):
        f_up, f_dn = at(2 + pc, -1), at(pc, 1)
        spread[pc] = 0.5 * (e0[2 + pc] - f_up) + cols0[pc]
        spread[2 + pc] = 0.5 * (f_dn - e0[pc]) + cols1[pc]
        g_up[pc] = 2.0 * scale * above * (0.5 * (e0[pc] - at(pc, -1)) + cols_up[pc])
        g_dn[pc] = 2.0 * scale * below * (0.5 * (at(2 + pc, 1) - e0[2 + pc]) + cols_dn[pc])
    g = [2.0 * scale * v for v in spread]
    for pr in range(2):
        even, odd = g[2 * pr], g[2 * pr + 1]
        col = [0.5 * (odd - from_left(odd, crops)), 0.5 * (from_right(even, crops) - even)]
        for pc in range(2):
            k = 2 * pr + pc
            if pr == 0:
                row_part = 0.5 * (g[2 + pc] - g_up[pc])
            else:
                row_part = 0.5 * (g_dn[pc] - g[pc])
            logit = at(8 + k, 0)
            label = get_lanes(t_out, 16 + 8 + k, rows, 16)
            ex = jnp.exp(-jnp.abs(logit))
            sig = jnp.where(logit >= 0, 1.0, ex) / (1.0 + ex)
            grads = (2.0 * scale * e0[k] - row_part, 2.0 * scale * e1[k] - col[pc], scale * (sig - label))
            for part in range(OUT_CH):
                for j in range(lanes // 128):
                    go_ref[j, pl.ds(4 * part + k, rows, stride=16), :] = grads[part][:, 128 * j : 128 * (j + 1)]
            term = jnp.maximum(logit, 0.0) + jnp.log1p(ex) - label * logit
            loss = loss + fold_lanes(e0[k] * e0[k] + e1[k] * e1[k] + spread[k] * spread[k] + term)

    sums_ref[...] = jnp.zeros_like(sums_ref)
    sums_ref[4:5, :] = jnp.sum(loss, axis=0, keepdims=True)
    head_ref[...] = jnp.zeros_like(head_ref)
    sg_ref[...] = jnp.zeros_like(sg_ref)
    d3_ref[...] = jnp.zeros_like(d3_ref)
    for k in (0, 1, rows + 2, rows + 3):
        g3_ref[256 * k : 256 * (k + 1), :] = jnp.zeros((256, lanes), bf16)

    sg_sum[...] = jnp.zeros_like(sg_sum)
    go_sum[...] = jnp.zeros_like(go_sum)

    def backward(rs):
        gos = [get_lanes(go_ref, r * 16, 16).astype(bf16) for r in rs]
        gts = [dot(wht_ref[...], go) for go in gos]
        head, gsum, sums, kept = 0.0, 0.0, [0.0] * crops, []
        for r, go, gt in zip(rs, gos, gts):
            spot = (r + 1) * 128
            head = head + dot_nt(rows_of(h3_ref, spot, 128), go)
            gsum = gsum + fold_lanes(go.astype(f32))
            gt = gt.astype(bf16)
            gb = jnp.where(rows_of(m_ref, spot, 128) > 0, gt, jnp.zeros_like(gt))
            g = gb.astype(f32)
            kept.append(gt)
            for c in range(crops):
                sums[c] = sums[c] + fold_lanes(g[:, width * c : width * (c + 1)])
            parts = []
            for pr in range(2):
                even, odd = g[64 * pr : 64 * pr + 32], g[64 * pr + 32 : 64 * pr + 64]
                parts += [
                    from_left(odd, crops).astype(bf16),
                    gb[64 * pr : 64 * pr + 64],
                    from_right(even, crops).astype(bf16),
                ]
            put_rows(g3_ref, (r + 2) * 256, jnp.concatenate(parts, axis=0))
        for r, gt in zip(rs, kept):
            put_rows(h3_ref, (r + 1) * 128, gt)
        head_ref[...] += head
        go_sum[...] += gsum
        for c in range(crops):
            sg_sum[c] += sums[c]

    repeat_rows(rows, 4, backward)
    for c in range(crops):
        sg_ref[c : c + 1, :] = lane_sums(sg_sum[c])[0:1]
    sums_ref[3:4, 0:16] = lane_sums(go_sum[...])[0:1]
    sg_copies = share(tiles, "tile", sg_ref, sg_got, s2_send, s2_recv)

    def down(ks):
        both = [dot(wd3_ref[...], rows_of(g3_ref, k * 256 + 128, 512)) for k in ks]
        for k, b in zip(ks, both):
            put_rows(gc_ref, k * 64, b[0:64] + b[64:128])

    down([0, 1])
    rim_lo[...] = gc_ref[0:128, :].astype(bf16)
    down([rows, rows + 1])
    rim_hi[...] = gc_ref[64 * rows : 64 * rows + 128, :].astype(bf16)
    finish_rims = swap_edges(tiles, [(rim_lo, rim_hi, rim_up, rim_dn)], rim_send, rim_recv)
    repeat_rows(rows - 2, 7, down, 2)

    def weights_three(ks):
        d3 = 0.0
        for k in ks:
            gs = [rows_of(g3_ref, k * 256 + 128 * j + 160, 64) for j in range(4)]
            d3 = d3 + dot_nt(jnp.concatenate(gs, axis=0), rows_of(x3_ref, (k + 1) * 192, 192))
        d3_ref[...] += d3

    repeat_rows(rows + 2, 6, weights_three)
    for tap in range(9):
        a, b = tap // 3, tap % 3
        total = jnp.zeros((CH_ONE, CH_TWO), f32)
        for first in (2 - a, 3 - a):
            for pc in range(2):
                s = (pc + b + 1) // 2
                total = total + d3_ref[64 * first + 32 * pc : 64 * first + 32 * pc + 32, 64 * s : 64 * (s + 1)]
        if tap < 8:
            pay_a[32 * (tap // 2) : 32 * (tap // 2 + 1), 64 * (tap % 2) : 64 * (tap % 2 + 1)] = total
        else:
            pay_a[128:144, :] = jnp.concatenate([total[0:16], total[16:32]], axis=1)
    outer = jnp.zeros((CH_ONE, 128), f32)
    for c in range(crops):
        outer = outer + as_column(over_phases(sg_ref[c : c + 1, :]))[0:32] * jnp.concatenate([unit[c : c + 1]] * 2, axis=1)
        sums_ref[2:3, :] += sg_ref[c : c + 1, :]
    head = jnp.concatenate([head_ref[...], jnp.zeros((128, 112), f32)], axis=1)
    pay_a[144:160, :] = jnp.transpose(head)[0:16]
    pay_a[160:176, :] = jnp.concatenate([outer[0:16, 0:64], outer[16:32, 0:64]], axis=1)
    pay_a[176:184, :] = sums_ref[...]
    if pay_a.shape[0] > 184:
        pay_a[184:, :] = jnp.zeros((pay_a.shape[0] - 184, 128), f32)
    reduce_a.scatter()

    wait_all(sg_copies)
    style_grad = over_phases(in_order(sg_got, tiles))[:, 0:32]
    grad_unit = jnp.dot(style_grad, ws_ref[...], precision=highest, preferred_element_type=f32)
    mixed = jnp.mean(style_raw * grad_unit, axis=1, keepdims=True)
    grad_raw = style_inv * grad_unit - style_inv * style_inv * style_inv * style_raw * mixed
    grad_raw = jnp.concatenate([grad_raw / coarse_count] * 2, axis=1)
    raw = [as_column(grad_raw[c : c + 1])[0:64] for c in range(crops)]
    d2_ref[...] = jnp.zeros_like(d2_ref)
    d1_ref[...] = jnp.zeros_like(d1_ref)
    g2_sum[...] = jnp.zeros_like(g2_sum)
    raw = jnp.concatenate([wide(v, width) for v in raw], axis=1)
    g2_ref = g3_ref

    def masked(ks, extras=None):
        sums = 0.0
        for j, k in enumerate(ks):
            coarse = rows_of(gc_ref, k * 64, 64)
            if extras is not None:
                coarse = coarse + extras[j]
            grad = (coarse + raw).astype(bf16)
            gb = jnp.where(rows_of(x3_ref, (k + 1) * 192 + 64, 64) > 0, grad, jnp.zeros_like(grad))
            g = gb.astype(f32)
            if extras is None or 0 < j < 3:
                sums = sums + fold_lanes(g)
            put_rows(g2_ref, k * 192, three_columns(gb, g, crops))
        g2_sum[...] += sums

    repeat_rows(rows - 2, 7, masked, 2)
    finish_rims()
    up = jnp.where(edge[0] < 0, rim_up[...].astype(f32), 0.0)
    dn = jnp.where(edge[1] > rows, rim_dn[...].astype(f32), 0.0)
    masked([0, 1, rows, rows + 1], [up[0:64], up[64:128], dn[0:64], dn[64:128]])
    pay_b[...] = jnp.zeros_like(pay_b)

    pay_b[160:161, 0:64] = lane_sums(g2_sum[...])[0:1]

    def weights_two(rs):
        d2 = 0.0
        for r in rs:
            d2 = d2 + dot_nt(rows_of(x2_ref, (r + 2) * 96, 288), rows_of(g2_ref, (r + 1) * 192 + 64, 64))
        d2_ref[...] += d2

    repeat_rows(rows, 8, weights_two)
    reduce_a.across()
    rest = jnp.concatenate([d2_ref[160:288, :], jnp.zeros((32, 64), f32)], axis=0)
    pay_b[0:160, :] = jnp.concatenate([d2_ref[0:160, :], rest], axis=1)
    reduce_b.scatter()

    def last_back(rs):
        gps = [dot(wd2_ref[...], rows_of(g2_ref, r * 192, 576)) for r in rs]
        d1 = 0.0
        for r, gp in zip(rs, gps):
            gp = 0.25 * gp.astype(bf16).astype(f32)
            gt = rows_of(h3_ref, (r + 1) * 128, 128).astype(f32)
            g1 = (jnp.concatenate([gp] * 4, axis=0) + gt).astype(bf16)
            gb = jnp.where(rows_of(h1_ref, (r + 3) * 128, 128) > 0, g1, jnp.zeros_like(g1))
            d1 = d1 + dot_nt(gb, jnp.concatenate([rows_of(y_ref, (r + 3) * 16, 32), ones_ref[...]], axis=0))
        d1_ref[...] += d1

    half, quarter = rows // 2, rows // 4
    repeat_rows(half, 4, last_back)
    reduce_a.gather(full_a)
    repeat_rows(quarter, 4, last_back, half)
    reduce_b.across()
    repeat_rows(rows - half - quarter, 4, last_back, half + quarter)
    d1 = jnp.transpose(jnp.concatenate([d1_ref[...], jnp.zeros((128, 80), f32)], axis=1))
    total = jnp.zeros((32, 128), f32)
    for p in range(4):
        total = total + turn(turn(d1[0:32], -32 * p, 1), -(8 * (p // 2) + p % 2), 0)
    packed = lane_group(total[0:8], 0)
    for k in range(1, 3):
        packed = packed + turn(lane_group(total[8 * k : 8 * (k + 1)], 0), 32 * k, 1)
    pay_c[...] = packed + lane_group(jnp.broadcast_to(over_phases(d1[32:33]), (8, 128)), 3)
    copies = share(tiles, "tile", pay_c, got_c, sems[12], sems[13])
    reduce_b.gather(full_b)
    wait_all(copies)
    own_c[...] = in_order(got_c, tiles)
    copies = share(images, "img", own_c, met_c, sems[14], sems[15])
    reduce_a.finish()
    size_a, size_b = full_a.shape[0], full_b.shape[0]
    o_ref[0:size_a, :] = full_a[...]
    reduce_b.finish()
    o_ref[size_a : size_a + size_b, :] = full_b[...]
    wait_all(copies)
    o_ref[size_a + size_b :, :] = in_order(met_c, images)


def update_kernel(pixel_count, second_at, third_at, count_ref, sum_ref, *refs):
    olds, outs, loss_ref = refs[:18], refs[18:36], refs[36]
    rate = 1.0 / (jnp.zeros((8, 128), f32) + (count_ref[0].astype(f32) + 1.0))

    def step(index, spot, grad):
        weight, momentum, average = (olds[3 * index + k][spot] for k in range(3))
        decayed = grad + decay_rate * weight
        momentum = momentum_rate * momentum + decayed
        new = weight - learn_rate * (decayed + momentum_rate * momentum)
        outs[3 * index][spot] = new
        outs[3 * index + 1][spot] = momentum
        outs[3 * index + 2][spot] = average + (new - average) * rate[0:1, 0:1]

    first = sum_ref[third_at : third_at + 8, :]
    for a in range(3):
        for b in range(3):
            for i in range(2):
                grad = first[4 * i + b : 4 * i + b + 1, 32 * a : 32 * (a + 1)]
                step(0, (a, b, slice(i, i + 1), slice(None)), grad)
    for tap in range(9):
        a, b = tap // 3, tap % 3
        first = second_at + 32 * (tap % 5)
        half = 64 * (tap // 5)
        step(1, (a, b), sum_ref[first : first + 32, half : half + 64])
        if tap < 8:
            first = 32 * (tap // 2)
            lane = 64 * (tap % 2)
            grad = sum_ref[first : first + 32, lane : lane + 64]
        else:
            first = 128
            grad = jnp.concatenate([sum_ref[first : first + 16, 64 * k : 64 * (k + 1)] for k in range(2)], axis=0)
        step(2, (a, b), grad)
    first = 160
    grad = jnp.concatenate([sum_ref[first : first + 16, 64 * k : 64 * (k + 1)] for k in range(2)], axis=0)
    step(3, (slice(None), slice(None)), grad)
    head = sum_ref[144:160, :]
    total = jnp.zeros((16, 128), f32)
    for p in range(4):
        total = total + turn(turn(head, -32 * p, 1), -p, 0)
    total = jnp.concatenate([total[4 * o : 4 * o + 1] for o in range(OUT_CH)], axis=0)
    step(4, (slice(None), slice(None)), total[:, 0:32])
    sums = sum_ref[176:184, :]
    one = turn(sum_ref[third_at : third_at + 1, :], -96, 1)
    two = jnp.sum(sum_ref[second_at + 160 : second_at + 168, :], axis=0, keepdims=True)
    three = over_phases(sums[2:3])
    lane = lax.broadcasted_iota(jnp.int32, (1, 128), 1)
    low = jnp.where(lane < 32, one, jnp.where(lane < 96, turn(two, 32, 1), three))
    ends = sums[3:4]
    ends = (ends + turn(ends, -1, 1)) + (turn(ends, -2, 1) + turn(ends, -3, 1))
    high = jnp.where(lane < 32, three, 0.0)
    for o in range(OUT_CH):
        high = jnp.where(lane == 32 + o, turn(ends, 32 + o - 4 * o, 1), high)
    grad = jnp.concatenate([low, high], axis=1)[:, 0 : olds[15].shape[0]]
    weight, momentum, average = (olds[15 + k][...].reshape(1, -1) for k in range(3))
    decayed = grad + decay_rate * weight
    momentum = momentum_rate * momentum + decayed
    new = weight - learn_rate * (decayed + momentum_rate * momentum)
    average = average + (new - average) * rate[0:1, 0:1]
    for k, value in enumerate((new, momentum, average)):
        outs[15 + k][...] = value.reshape(-1)
    loss_ref[0] = jnp.sum(sums[4:5]) / pixel_count


def on_device(
    images, nucleus, target_flow, cell_label, step_count,
    conv1_weight, conv1_momentum, conv1_average,
    conv2_weight, conv2_momentum, conv2_average,
    conv3_weight, conv3_momentum, conv3_average,
    style_weight, style_momentum, style_average,
    head_weight, head_momentum, head_average,
    biases, bias_momentum, bias_average,
):
    tiles = lax.axis_size("tile")
    crops, _, height, cols = images.shape
    rows, width = height // 2, cols // 2
    pixel_count = lax.axis_size("img") * tiles * crops * height * cols
    grad_scale = 1.0 / math.sqrt(pixel_count)
    coarse_count = tiles * rows * width

    def sds(shape, dtype=f32):
        return jax.ShapeDtypeStruct(shape, dtype)

    lanes = crops * width
    images_count = lax.axis_size("img")

    def other_way(w):
        return jnp.swapaxes(w, -1, -2)

    third = tuple(other_way(w) for w in (conv3_weight, conv3_momentum, conv3_average))
    style = tuple(other_way(w) for w in (style_weight, style_momentum, style_average))
    head = tuple(other_way(w) for w in (head_weight, head_momentum, head_average))

    edge = (crops, 2, HALO, cols)
    rim = (128, lanes)
    parts = [8 * pl.cdiv(sum(block), 8 * tiles) for block in BLOCK_ROWS[:2]]
    small = sum(BLOCK_ROWS[2])

    def buf(shape, dtype=bf16):
        return pltpu.VMEM(shape, dtype)

    def block_bufs(part):
        return [
            buf((part * tiles, 128), f32), buf((tiles, part, 128), f32), buf((part, 128), f32),
            buf((images_count, part, 128), f32), buf((part * tiles, 128), f32),
        ]

    sources = (
        images, target_flow, cell_label, conv1_weight, conv2_weight, third[0], head[0], biases, style[0],
    )
    block_sems = [DMA((tiles,)), DMA((tiles,)), DMA((images_count,)), DMA((images_count,)), DMA((tiles,)), DMA((tiles,))]
    summed = pl.pallas_call(
        lambda *refs: step_kernel(tiles, images_count, grad_scale, float(coarse_count), *refs),
        out_shape=pltpu.VMEM((sum(parts) * tiles + small, 128), f32),
        in_specs=[SMEM] + [HBM] * 9,
        out_specs=VMEM,
        scratch_shapes=[buf(v.shape, v.dtype) for v in sources]
        + [
            buf(edge), buf(edge), buf(edge, jnp.int32), buf(edge, jnp.int32),
            buf((128, 48)), buf((CH_TWO, 9 * CH_ONE + 16)), buf((128, 14 * CH_TWO + 16)), buf((128, 16 * CH_ONE)),
            buf((CH_ONE, 9 * CH_TWO)), buf((16, 128)), buf((128, 16)),
            buf((8, 128), f32), buf((16, 128), f32), buf((32, 128), f32), buf((16, lanes)), buf((16, lanes)),
            buf((16 * (rows + 7), lanes)), buf((lanes // 128, 16 * (rows + 2), 128), f32),
            buf((128 * (rows + 6), lanes)), buf((96 * (rows + 6), lanes)), buf((192 * (rows + 4), lanes)),
            buf((128 * (rows + 2), lanes)), buf((128 * (rows + 2), lanes)),
            buf((lanes // 128, 16 * (rows + 2), 128), f32), buf((lanes // 128, 16 * rows, 128), f32),
            buf((256 * (rows + 4), lanes)), buf((64 * (rows + 2), lanes), f32),
            buf(rim), buf(rim), buf(rim), buf(rim),
            buf((8, 128), f32), buf((tiles, 8, 128), f32), buf((8, 128), f32), buf((tiles, 8, 128), f32),
            buf((128, 16), f32), buf((8, 128), f32),
            buf((256, 3 * CH_TWO), f32), buf((9 * CH_ONE, CH_TWO), f32), buf((128, 48), f32),
            buf((crops, CH_TWO, 128), f32), buf((crops, 128, 128), f32), buf((16, 128), f32), buf((CH_TWO, 128), f32),
        ]
        + block_bufs(parts[0])
        + block_bufs(parts[1])
        + [buf((small, 128), f32), buf((tiles, small, 128), f32), buf((small, 128), f32), buf((images_count, small, 128), f32)]
        + [DMA((9,)), DMA((4,)), DMA((4,)), DMA((tiles,)), DMA((tiles,)), DMA((tiles,)), DMA((tiles,)), DMA((2,)), DMA((2,))]
        + block_sems * 2
        + [DMA((tiles,)), DMA((tiles,)), DMA((images_count,)), DMA((images_count,))],
        compiler_params=pltpu.CompilerParams(collective_id=1, has_side_effects=True, vmem_limit_bytes=60 * 2**20),
        name="step",
    )(nucleus, *sources)

    olds = (
        (conv1_weight, conv1_momentum, conv1_average)
        + (conv2_weight, conv2_momentum, conv2_average)
        + third + style + head
        + (biases, bias_momentum, bias_average)
    )
    news = pl.pallas_call(
        lambda *refs: update_kernel(float(pixel_count), parts[0] * tiles, sum(parts) * tiles, *refs),
        out_shape=tuple(sds(v.shape) for v in olds) + (sds((1,)),),
        in_specs=[SMEM] + [VMEM] * 19,
        out_specs=[VMEM] * 18 + [SMEM],
        compiler_params=pltpu.CompilerParams(vmem_limit_bytes=16 * 2**20),
        name="update",
    )(step_count, summed, *olds)
    return (news[18], *news[0:6], *(other_way(w) for w in news[6:15]), *news[15:18])


def solution(mesh):
    return jax.shard_map(
        on_device,
        mesh=mesh,
        in_specs=(
            P("img", None, "tile", None),
            P("img"),
            P("img", None, "tile", None),
            P("img", "tile", None),
        )
        + (P(),) * 19,
        out_specs=(P(),) * 19,
        check_vma=False,
    )
```

```python
import math

import jax
import jax.numpy as jnp
from jax import lax
from jax.experimental import pallas as pl
from jax.experimental.pallas import tpu as pltpu
from jax.sharding import PartitionSpec as P

CH_ONE = 32
CH_TWO = 64
OUT_CH = 3

momentum_rate = 0.9
learn_rate = 0.02
decay_rate = 0.0001
norm_eps = 1e-05
highest = lax.Precision.HIGHEST
f32 = jnp.float32
bf16 = jnp.bfloat16

HALO = 8
BACK = 2
EARLY = 6
VMEM = pl.BlockSpec(memory_space=pltpu.VMEM)
SMEM = pl.BlockSpec(memory_space=pltpu.SMEM)
HBM = pl.BlockSpec(memory_space=pltpu.HBM)
MESH = pl.DeviceIdType.MESH
DMA = pltpu.SemaphoreType.DMA

BLOCK_ROWS = ((144, 16, 16, 8), (160, 8), (8,))


def dot(a, b):
    return jnp.dot(a, b, preferred_element_type=f32)


def dot_nt(a, b, precision=None):
    return lax.dot_general(a, b, (((1,), (1,)), ((), ())), preferred_element_type=f32, precision=precision)


def edge_select(x, crops, first):
    width = x.shape[1] // crops
    lane = lax.broadcasted_iota(jnp.int32, (x.shape[0], 128), 1)
    parts = []
    for c in range(crops):
        low, high = width * c, width * (c + 1)
        if first:
            parts += [jnp.where(lane == 0, 0.0, x[:, low : low + 128]), x[:, low + 128 : high]]
        else:
            parts += [x[:, low : high - 128], jnp.where(lane == 127, 0.0, x[:, high - 128 : high])]
    return jnp.concatenate(parts, axis=1)


def from_left(x, crops):
    return edge_select(pltpu.roll(x, 1, 1), crops, True)


def from_right(x, crops):
    return edge_select(pltpu.roll(x, x.shape[1] - 1, 1), crops, False)


def three_columns(mid, x, crops):
    return jnp.concatenate([from_left(x, crops).astype(bf16), mid, from_right(x, crops).astype(bf16)], axis=0)


def pieces_of(x):
    high = x.astype(bf16)
    rest = x - high.astype(f32)
    mid = rest.astype(bf16)
    return high.astype(f32), mid.astype(f32), rest - mid.astype(f32)


def repeat_rows(count, limit, body, first=0):
    step = max(k for k in range(1, limit + 1) if count % k == 0)

    def run(k, carry):
        body([first + k * step + j for j in range(step)])
        return carry

    lax.fori_loop(0, count // step, run, 0)


def turn(x, by, axis):
    by = by % x.shape[axis]
    return pltpu.roll(x, by, axis) if by else x


def lane_group(x, group, size=32):
    lane = lax.broadcasted_iota(jnp.int32, x.shape, 1)
    return jnp.where(lane // size == group, x, 0.0)


def over_phases(x):
    return (x + turn(x, 32, 1)) + (turn(x, 64, 1) + turn(x, 96, 1))


def as_column(row):
    return jnp.transpose(jnp.broadcast_to(row, (128, 128)))


def fold_lanes(x):
    parts = [x[:, 128 * k : 128 * (k + 1)] for k in range(x.shape[1] // 128)]
    while len(parts) > 1:
        parts = [a + b for a, b in zip(parts[0::2], parts[1::2])] + parts[len(parts) // 2 * 2 :]
    return parts[0]


def lane_sums(x):
    return dot_nt(jnp.ones((8, 128), f32), x, highest)


def wide(tile, width):
    return jnp.concatenate([tile] * (width // 128), axis=1)


def rows_of(ref, start, size):
    return ref[pl.ds(pl.multiple_of(start, 16), size), :]


def put_rows(ref, start, value):
    ref[pl.ds(pl.multiple_of(start, 16), value.shape[0]), :] = value


def put_lanes(ref, start, value):
    for k in range(value.shape[1] // 128):
        ref[k, pl.ds(pl.multiple_of(start, 16), value.shape[0]), :] = value[:, 128 * k : 128 * (k + 1)]


def get_lanes(ref, start, size, stride=None):
    spot = pl.ds(start, size, stride=stride) if stride else pl.ds(pl.multiple_of(start, 16), size)
    return jnp.concatenate([ref[k, spot, :] for k in range(ref.shape[0])], axis=1)


def strip_edges(tiles, rows):
    me = lax.axis_index("tile")
    return -me * rows, (tiles - me) * rows


def valid(row, edge):
    return jnp.where((row >= edge[0]) & (row < edge[1]), 1.0, 0.0).astype(f32)


def greet(sizes):
    gate = pltpu.get_barrier_semaphore()
    for axis, count in sizes:
        me = lax.axis_index(axis)
        for j in range(1, count):
            pl.semaphore_signal(gate, inc=1, device_id={axis: lax.rem(me + j, count)}, device_id_type=MESH)
    return lambda: pl.semaphore_wait(gate, sum(count - 1 for _, count in sizes))


def send_all(count, axis, source, target, send_sem, recv_sem):
    me = lax.axis_index(axis)
    copies = []
    for j in range(1, count):
        to = lax.rem(me + j, count)
        copy = pltpu.make_async_remote_copy(
            src_ref=source(to), dst_ref=target, send_sem=send_sem.at[j - 1], recv_sem=recv_sem.at[j - 1],
            device_id={axis: to}, device_id_type=MESH,
        )
        copy.start()
        copies.append(copy)
    return copies


def wait_all(copies):
    for copy in copies:
        copy.wait()


def in_order(ref, count):
    total = ref[0]
    for k in range(1, count):
        total = total + ref[k]
    return total


def swap_edges(tiles, pairs, send_sem, recv_sem):
    me = lax.axis_index("tile")
    copies = []
    for k, (low, high, from_before, from_after) in enumerate(pairs):
        down = pltpu.make_async_remote_copy(
            src_ref=high, dst_ref=from_before, send_sem=send_sem.at[2 * k], recv_sem=recv_sem.at[2 * k],
            device_id={"tile": jnp.minimum(me + 1, tiles - 1)}, device_id_type=MESH,
        )
        up = pltpu.make_async_remote_copy(
            src_ref=low, dst_ref=from_after, send_sem=send_sem.at[2 * k + 1], recv_sem=recv_sem.at[2 * k + 1],
            device_id={"tile": jnp.maximum(me - 1, 0)}, device_id_type=MESH,
        )
        copies.append((down, up))

    @pl.when(me < tiles - 1)
    def _():
        for down, _up in copies:
            down.start()

    @pl.when(me > 0)
    def _():
        for _down, up in copies:
            up.start()

    def finish():
        @pl.when(me < tiles - 1)
        def _():
            for down, up in copies:
                down.wait_send()
                up.wait_recv()

        @pl.when(me > 0)
        def _():
            for down, up in copies:
                up.wait_send()
                down.wait_recv()

    return finish


def share(count, axis, source, got, send_sem, recv_sem):
    me = lax.axis_index(axis)
    got[me] = source[...]
    return send_all(count, axis, lambda to: source, got.at[me], send_sem, recv_sem)


class Reduction:
    def __init__(self, tiles, images, pay, got, own, met, sems):
        self.tiles, self.images = tiles, images
        self.pay, self.got, self.own, self.met, self.sems = pay, got, own, met, sems
        self.part = own.shape[0]
        self.me = lax.axis_index("tile")

    def block(self, k):
        return pl.ds(pl.multiple_of(k * self.part, 8), self.part)

    def scatter(self):
        self.got[self.me] = self.pay[self.block(self.me), :]
        self.copies = send_all(
            self.tiles, "tile", lambda to: self.pay.at[self.block(to), :], self.got.at[self.me], self.sems[0], self.sems[1]
        )

    def across(self):
        wait_all(self.copies)
        self.own[...] = in_order(self.got, self.tiles)
        self.copies = share(self.images, "img", self.own, self.met, self.sems[2], self.sems[3])

    def gather(self, full):
        wait_all(self.copies)
        full[self.block(self.me), :] = in_order(self.met, self.images)
        here = full.at[self.block(self.me), :]
        self.copies = send_all(self.tiles, "tile", lambda to: here, here, self.sems[4], self.sems[5])

    def finish(self):
        wait_all(self.copies)


def first_tables(k1_ref, k2_ref, bias_ref, w1_ref, w2_ref, base_ref):
    base_ref[...] = jnp.zeros_like(base_ref)
    for a in range(3):
        for b in range(3):
            for i in range(2):
                base_ref[8 * a + 4 * i + b : 8 * a + 4 * i + b + 1, 0:32] = k1_ref[a, b, i : i + 1, :]
    base = base_ref[...]
    w1t = jnp.zeros((32, 128), f32)
    for p in range(4):
        w1t = w1t + turn(turn(base, 8 * (p // 2) + p % 2, 0), 32 * p, 1)
    bias = bias_ref[...].reshape(1, -1)
    row = lax.broadcasted_iota(jnp.int32, (16, 128), 0)

    def piece_rows(values):
        table = jnp.zeros((16, 128), f32)
        for k, piece in enumerate(pieces_of(values)):
            table = jnp.where(row == k, jnp.broadcast_to(piece, (16, 128)), table)
        return table

    b1 = piece_rows(jnp.concatenate([bias[:, 0:32]] * 4, axis=1))
    w1_ref[...] = jnp.transpose(jnp.concatenate([w1t, b1], axis=0)).astype(bf16)

    k2 = [[k2_ref[a, b].astype(bf16).astype(f32) for b in range(3)] for a in range(3)]
    w2t = jnp.concatenate([k2[a][b] for a in range(3) for b in range(3)], axis=0)
    b2 = piece_rows(jnp.concatenate([bias[:, 32:96]] * 2, axis=1))[:, 0:64]
    w2_ref[...] = jnp.transpose(jnp.concatenate([w2t, b2], axis=0)).astype(bf16)


def later_tables(k2_ref, k3_ref, kh_ref, bias_ref, w3_ref, wd3_ref, wd2_ref, wh_ref, wht_ref, b3_ref, bh_ref):
    k2 = [[k2_ref[a, b].astype(bf16).astype(f32) for b in range(3)] for a in range(3)]
    wd2_ref[...] = jnp.concatenate([k2[2 - s][2 - t] for s in range(3) for t in range(3)], axis=1).astype(bf16)

    def tap_sum(first, second):
        total = None
        for a in first:
            for b in second:
                total = k3[a][b] if total is None else total + k3[a][b]
        return jnp.zeros((CH_ONE, CH_TWO), f32) if total is None else total

    k3 = [[k3_ref[a, b].astype(bf16).astype(f32) for b in range(3)] for a in range(3)]
    up = [[[a for a in range(3) if (p + a + 1) // 2 == r] for r in range(3)] for p in range(2)]
    for p in range(4):
        w3 = jnp.concatenate([tap_sum(up[p // 2][r], up[p % 2][c]) for r in range(3) for c in range(3)], axis=1)
        w3_hi = w3.astype(bf16)
        low = w3 - w3_hi.astype(f32)
        low = jnp.concatenate([low[:, 64:128], low[:, 192:384], low[:, 448:512]], axis=1)
        w3_ref[32 * p : 32 * (p + 1), 0:896] = jnp.concatenate([w3_hi, low.astype(bf16)], axis=1)
    down = ((2,), (1, 2), (0, 1), (0,))
    wd3 = jnp.transpose(jnp.concatenate([tap_sum(down[r], down[c]) for r in range(4) for c in range(4)], axis=0))
    wd3_hi = wd3.astype(bf16)
    wd3_ref[0:64, :] = wd3_hi
    wd3_ref[64:128, :] = (wd3 - wd3_hi.astype(f32)).astype(bf16)

    row = lax.broadcasted_iota(jnp.int32, (16, 128), 0)
    lane = lax.broadcasted_iota(jnp.int32, (16, 128), 1)
    wh = jnp.zeros((16, 128), f32)
    for o in range(OUT_CH):
        one = jnp.concatenate([kh_ref[o : o + 1, :]] * 4, axis=1)
        wh = jnp.where(row // 4 == o, jnp.broadcast_to(one, (16, 128)), wh)
    wh = jnp.where(row % 4 == lane // 32, wh, 0.0)
    wh_ref[...] = wh.astype(bf16)
    wht_ref[...] = jnp.transpose(wh).astype(bf16)

    bias = bias_ref[...].reshape(1, -1)
    b3_ref[...] = jnp.zeros_like(b3_ref)
    b3_ref[0:1, :] = jnp.concatenate([bias[:, 96:128] + bias[:, 128:160]] * 4, axis=1)
    bh = jnp.zeros((16, 128), f32)
    for o in range(OUT_CH):
        bh = jnp.where(row // 4 == o, jnp.broadcast_to(bias[:, 160 + o : 161 + o], (16, 128)), bh)
    bh_ref[...] = bh


def split_columns(x, select):
    even, odd = [], []
    for k in range(x.shape[1] // 256):
        piece = dot(x[:, 256 * k : 256 * (k + 1)], select)
        even.append(piece[:, 0:128])
        odd.append(piece[:, 128:256])
    return jnp.concatenate(even, axis=1), jnp.concatenate(odd, axis=1)


def step_kernel(
    tiles, images, scale, coarse_count,
    nucleus_ref, x_hbm, t_hbm, label_hbm, k1_hbm, k2_hbm, k3_hbm, kh_hbm, bias_hbm, ws_hbm,
    o_ref,
    x_ref, t_ref, label_ref, k1_ref, k2_ref, k3_ref, kh_ref, bias_ref, ws_ref,
    x_lo, x_hi, t_lo, t_hi,
    w1_ref, w2_ref, w3_ref, wd3_ref, wd2_ref, wh_ref, wht_ref, b3_ref, bh_ref, base_ref, ones_ref, mark_ref,
    y_ref, t_out, h1_ref, x2_ref, x3_ref, h3_ref, m_ref, fe_ref, go_ref, g3_ref, gc_ref,
    rim_lo, rim_hi, rim_up, rim_dn,
    style_ref, style_got, sg_ref, sg_got, head_ref, sums_ref, d3_ref, d2_ref, d1_ref,
    style_sum, sg_sum, go_sum, g2_sum,
    pay_a, got_a, own_a, met_a, full_a, pay_b, got_b, own_b, met_b, full_b,
    pay_c, got_c, own_c, met_c,
    load_sems, halo_send, halo_recv, s1_send, s1_recv, s2_send, s2_recv, rim_send, rim_recv,
    *sems,
):
    pre_ref = gc_ref
    reduce_a = Reduction(tiles, images, pay_a, got_a, own_a, met_a, sems[0:6])
    reduce_b = Reduction(tiles, images, pay_b, got_b, own_b, met_b, sems[6:12])
    arrived = greet((("tile", tiles), ("img", images)))
    loads = [
        pltpu.make_async_copy(source, target, load_sems.at[k])
        for k, (source, target) in enumerate(
            (
                (k1_hbm, k1_ref), (k2_hbm, k2_ref), (bias_hbm, bias_ref), (x_hbm, x_ref),
                (t_hbm, t_ref), (label_hbm, label_ref), (k3_hbm, k3_ref), (kh_hbm, kh_ref), (ws_hbm, ws_ref),
            )
        )
    ]
    for load in loads:
        load.start()
    ones_ref[...] = jnp.ones_like(ones_ref)
    arrived()
    last = x_ref.shape[2] - HALO
    finish_halo = swap_edges(
        tiles,
        [
            (ref.at[:, :, pl.ds(0, HALO), :], ref.at[:, :, pl.ds(last, HALO), :], lo, hi)
            for ref, lo, hi in ((x_hbm, x_lo, x_hi), (t_hbm, t_lo, t_hi))
        ],
        halo_send, halo_recv,
    )
    for load in loads[0:4]:
        load.wait()
    first_tables(k1_ref, k2_ref, bias_ref, w1_ref, w2_ref, base_ref)
    crops = x_ref.shape[0]
    width = x_ref.shape[3] // 2
    lanes = crops * width
    height = x_ref.shape[2]
    rows = height // 2
    edge = strip_edges(tiles, rows)
    r_id = lax.broadcasted_iota(jnp.int32, (256, 256), 0)
    c_id = lax.broadcasted_iota(jnp.int32, (256, 256), 1)
    select = jnp.where(r_id == 2 * (c_id % 128) + c_id // 128, 1.0, 0.0).astype(bf16)
    y_rows = y_ref.shape[0]
    ri = lax.broadcasted_iota(jnp.int32, (y_rows, 8 * height), 0)
    ci = lax.broadcasted_iota(jnp.int32, (y_rows, 8 * height), 1)
    fine = 2 * (ri // 16) + (ri // 8) % 2 - 7
    source = (ri % 4) * 2 * height + (ri // 4) % 2 * height + fine
    perm_x = jnp.where((ci == source) & (fine >= 0) & (fine < height), 1.0, 0.0).astype(bf16)
    ri = lax.broadcasted_iota(jnp.int32, (128, 16 * HALO), 0)
    ci = lax.broadcasted_iota(jnp.int32, (128, 16 * HALO), 1)
    fine = 2 * (ri // 16) + (ri // 8) % 2 - 7
    fine = jnp.where(ri < 64, fine, fine + y_rows // 8 - 16)
    source = jnp.where(fine < 0, fine + HALO, 2 * HALO + fine - height)
    source = (ri % 4) * 4 * HALO + (ri // 4) % 2 * HALO + source
    perm_h = jnp.where((ci == source) & ((fine < 0) | (fine >= height)), 1.0, 0.0).astype(bf16)
    has_up, has_dn = edge[0] < 0, edge[1] > rows

    def both_columns(of_crop):
        even, odd = [], []
        for c in range(crops):
            first, second = split_columns(of_crop(c), select)
            even.append(first)
            odd.append(second)
        return jnp.concatenate(even, axis=1), jnp.concatenate(odd, axis=1)

    def own_rows(c):
        return jnp.concatenate([x_ref[c, k] for k in range(2)], axis=0)

    def halo_rows(c):
        pieces = [jnp.where(has_up, x_lo[c, k].astype(f32), 0.0) for k in range(2)]
        pieces += [jnp.where(has_dn, x_hi[c, k].astype(f32), 0.0) for k in range(2)]
        return jnp.concatenate(pieces, axis=0).astype(bf16)

    def target_rows(c):
        pieces = [t_ref[c, 0].astype(f32), t_ref[c, 1].astype(f32), label_ref[c].astype(f32)]
        pieces += [jnp.where(has_up, t_lo[c, k], 0).astype(f32) for k in range(2)]
        pieces += [jnp.where(has_dn, t_hi[c, k], 0).astype(f32) for k in range(2)]
        return jnp.concatenate(pieces, axis=0).astype(bf16)

    def pixel_windows(of_crop, second):
        even, odd = both_columns(of_crop)
        row = lax.broadcasted_iota(jnp.int32, even.shape, 0)
        crop = lax.broadcasted_iota(jnp.int32, even.shape, 1) // width
        gate = jnp.ones(even.shape, f32)
        for c in range(crops):
            gate = jnp.where(second(row) & (crop == c), nucleus_ref[c].astype(f32), gate)
        even, odd = even * gate, odd * gate
        return jnp.concatenate([from_left(odd, crops), even, odd, from_right(even, crops)], axis=0).astype(bf16)

    y_ref[...] = dot(perm_x, pixel_windows(own_rows, lambda row: row >= height)).astype(bf16)

    def conv_one(ks, inside=True):
        pre = [
            dot(w1_ref[...], jnp.concatenate([rows_of(y_ref, k * 16, 32), ones_ref[...]], axis=0)) for k in ks
        ]
        for k, p in zip(ks, pre):
            p = jnp.maximum(p, 0.0)
            hidden = (p if inside else p * valid(k - 3, edge)).astype(bf16)
            put_rows(h1_ref, k * 128, hidden)
            h = hidden.astype(f32)
            pooled = (0.25 * ((h[0:32] + h[32:64]) + (h[64:96] + h[96:128]))).astype(bf16)
            put_rows(x2_ref, k * 96, three_columns(pooled, pooled.astype(f32), crops))

    def conv_two(qs, inside=True):
        pre = [
            dot(w2_ref[...], jnp.concatenate([rows_of(x2_ref, q * 96, 288), ones_ref[...]], axis=0)) for q in qs
        ]
        sums = [0.0] * crops
        for q, p in zip(qs, pre):
            p = jnp.maximum(p, 0.0)
            hidden = (p if inside else p * valid(q - 2, edge)).astype(bf16)
            h = hidden.astype(f32)
            put_rows(x3_ref, q * 192, three_columns(hidden, h, crops))
            for c in range(crops):
                sums[c] = sums[c] + fold_lanes(h[:, width * c : width * (c + 1)])
        if inside:
            for c in range(crops):
                style_sum[c] += sums[c]

    repeat_rows(rows - 2, 7, conv_one, 4)
    finish_halo()
    extra = dot(perm_h, pixel_windows(halo_rows, lambda row: row // HALO % 2 == 1))
    y_ref[0:64, :] = (y_ref[0:64, :].astype(f32) + extra[0:64]).astype(bf16)
    y_ref[y_rows - 64 : y_rows, :] = (y_ref[y_rows - 64 : y_rows, :].astype(f32) + extra[64:128]).astype(bf16)
    conv_one([0, 1, 2, 3, rows + 2, rows + 3, rows + 4, rows + 5], False)
    style_sum[...] = jnp.zeros_like(style_sum)
    repeat_rows(rows, 8, conv_two, 2)
    style_ref[...] = jnp.zeros_like(style_ref)
    for c in range(crops):
        style_ref[c : c + 1, 0:64] = lane_sums(style_sum[c])[0:1]
    style_copies = share(tiles, "tile", style_ref, style_got, s1_send, s1_recv)

    conv_two([0, 1], False)
    conv_two([rows + 2, rows + 3], False)
    for load in loads[4:]:
        load.wait()
    t_rows = 3 * height + 4 * HALO
    ri = lax.broadcasted_iota(jnp.int32, (t_out.shape[1], 2 * t_rows), 0)
    ci = lax.broadcasted_iota(jnp.int32, (t_out.shape[1], 2 * t_rows), 1)
    part = (ri // 4) % 4
    fine = 2 * (ri // 16) + (ri // 2) % 2 - 2
    source = jnp.where(
        fine < 0,
        3 * height + part * HALO + fine + HALO,
        jnp.where(fine < height, part * height + fine, 3 * height + 2 * HALO + part * HALO + fine - height),
    )
    outside = (fine < 0) | (fine >= height)
    known = (part < 2) | ((part == 2) & jnp.logical_not(outside))
    perm_t = jnp.where((ci == (ri % 2) * t_rows + source) & known, 1.0, 0.0).astype(bf16)
    even, odd = both_columns(target_rows)
    put_lanes(t_out, 0, dot(perm_t, jnp.concatenate([even, odd], axis=0).astype(bf16)))
    later_tables(k2_ref, k3_ref, kh_ref, bias_ref, w3_ref, wd3_ref, wd2_ref, wh_ref, wht_ref, b3_ref, bh_ref)

    def third_input(k):
        x = rows_of(x3_ref, k * 192, 576)
        return jnp.concatenate([x, x[64:128], x[192:384], x[448:512]], axis=0)

    for k in range(EARLY):
        put_rows(pre_ref, k * 128, dot(w3_ref[:, 0:896], third_input(k)))
    wait_all(style_copies)
    style_raw = in_order(style_got, tiles)[:, 0:64] / coarse_count
    style_inv = lax.rsqrt(jnp.mean(style_raw * style_raw, axis=1, keepdims=True) + norm_eps)
    unit = style_raw * style_inv
    vec = dot_nt(unit, ws_ref[...], highest)
    vec = jnp.concatenate([vec] * 4, axis=1) + b3_ref[0:1, :]
    bias3 = jnp.concatenate([wide(as_column(vec[c : c + 1]), width) for c in range(crops)], axis=1)
    row = lax.broadcasted_iota(jnp.int32, (16, lanes), 0)
    lane = lax.broadcasted_iota(jnp.int32, (16, lanes), 1)
    mark_ref[...] = jnp.where(row // 3 == lane // width, 1.0, 0.0).astype(bf16)
    row = lax.broadcasted_iota(jnp.int32, (128, 128), 0)
    table = jnp.zeros((128, 128), f32)
    for c in range(crops):
        for k, piece in enumerate(pieces_of(vec[c : c + 1])):
            table = jnp.where(row == 3 * c + k, jnp.broadcast_to(piece, (128, 128)), table)
    w3_ref[:, 896:912] = jnp.transpose(table)[:, 0:16].astype(bf16)

    def forward(ks, early=False):
        pre = []
        for k in ks:
            if early:
                pre.append(rows_of(pre_ref, k * 128, 128) + bias3)
            else:
                pre.append(dot(w3_ref[...], jnp.concatenate([third_input(k), mark_ref[...]], axis=0)))
        hs = []
        for k, p in zip(ks, pre):
            p = jnp.maximum(p, 0.0)
            h3 = (p + rows_of(h1_ref, (k + 2) * 128, 128).astype(f32)).astype(bf16)
            put_rows(h3_ref, k * 128, h3)
            put_rows(m_ref, k * 128, p.astype(bf16))
            hs.append(h3)
        outs = [dot(wh_ref[...], h) for h in hs]
        for k, o in zip(ks, outs):
            o = o + wide(bh_ref[...], lanes)
            t = get_lanes(t_out, k * 16, 16)
            fe = (o[0:8] - 0.25 * t[0:8]) * valid(k - 1, edge)
            put_lanes(fe_ref, k * 16, jnp.concatenate([fe, o[8:16]], axis=0))

    forward(range(EARLY), True)
    repeat_rows(rows + 2 - EARLY, 12, forward, EARLY)

    r_id = lax.broadcasted_iota(jnp.int32, (rows, lanes), 0)
    above = jnp.where(r_id - 1 >= edge[0], 1.0, 0.0)
    below = jnp.where(r_id + 1 < edge[1], 1.0, 0.0)
    go_ref[...] = jnp.zeros_like(go_ref)

    def at(part, off):
        return get_lanes(fe_ref, 16 * (1 + off) + part, rows, 16)

    def column_part(pr, off):
        odd, even = at(4 + 2 * pr + 1, off), at(4 + 2 * pr, off)
        return 0.5 * (odd - from_left(odd, crops)), 0.5 * (from_right(even, crops) - even)

    loss = jnp.zeros((rows, 128), f32)
    e0 = [at(k, 0) for k in range(4)]
    e1 = [at(4 + k, 0) for k in range(4)]
    cols0, cols1 = column_part(0, 0), column_part(1, 0)
    cols_up, cols_dn = column_part(1, -1), column_part(0, 1)
    spread = [None] * 4
    g_up, g_dn = [None] * 2, [None] * 2
    for pc in range(2):
        f_up, f_dn = at(2 + pc, -1), at(pc, 1)
        spread[pc] = 0.5 * (e0[2 + pc] - f_up) + cols0[pc]
        spread[2 + pc] = 0.5 * (f_dn - e0[pc]) + cols1[pc]
        g_up[pc] = 2.0 * scale * above * (0.5 * (e0[pc] - at(pc, -1)) + cols_up[pc])
        g_dn[pc] = 2.0 * scale * below * (0.5 * (at(2 + pc, 1) - e0[2 + pc]) + cols_dn[pc])
    g = [2.0 * scale * v for v in spread]
    for pr in range(2):
        even, odd = g[2 * pr], g[2 * pr + 1]
        col = [0.5 * (odd - from_left(odd, crops)), 0.5 * (from_right(even, crops) - even)]
        for pc in range(2):
            k = 2 * pr + pc
            if pr == 0:
                row_part = 0.5 * (g[2 + pc] - g_up[pc])
            else:
                row_part = 0.5 * (g_dn[pc] - g[pc])
            logit = at(8 + k, 0)
            label = get_lanes(t_out, 16 + 8 + k, rows, 16)
            ex = jnp.exp(-jnp.abs(logit))
            sig = jnp.where(logit >= 0, 1.0, ex) / (1.0 + ex)
            grads = (2.0 * scale * e0[k] - row_part, 2.0 * scale * e1[k] - col[pc], scale * (sig - label))
            for part in range(OUT_CH):
                for j in range(lanes // 128):
                    go_ref[j, pl.ds(4 * part + k, rows, stride=16), :] = grads[part][:, 128 * j : 128 * (j + 1)]
            term = jnp.maximum(logit, 0.0) + jnp.log1p(ex) - label * logit
            loss = loss + fold_lanes(e0[k] * e0[k] + e1[k] * e1[k] + spread[k] * spread[k] + term)

    sums_ref[...] = jnp.zeros_like(sums_ref)
    sums_ref[4:5, :] = jnp.sum(loss, axis=0, keepdims=True)
    head_ref[...] = jnp.zeros_like(head_ref)
    sg_ref[...] = jnp.zeros_like(sg_ref)
    d3_ref[...] = jnp.zeros_like(d3_ref)
    for k in (0, 1, rows + 2, rows + 3):
        g3_ref[256 * k : 256 * (k + 1), :] = jnp.zeros((256, lanes), bf16)

    sg_sum[...] = jnp.zeros_like(sg_sum)
    go_sum[...] = jnp.zeros_like(go_sum)

    def down(ks):
        both = [dot(wd3_ref[...], rows_of(g3_ref, k * 256 + 128, 512)) for k in ks]
        return [b[0:64] + b[64:128] for b in both]

    def backward(rs, ready=()):
        coarse = down(ready)
        gos = [get_lanes(go_ref, r * 16, 16).astype(bf16) for r in rs]
        gts = [dot(wht_ref[...], go) for go in gos]
        head, gsum, sums, kept = 0.0, 0.0, [0.0] * crops, []
        for r, go, gt in zip(rs, gos, gts):
            spot = (r + 1) * 128
            head = head + dot_nt(rows_of(h3_ref, spot, 128), go)
            gsum = gsum + fold_lanes(go.astype(f32))
            gt = gt.astype(bf16)
            gb = jnp.where(rows_of(m_ref, spot, 128) > 0, gt, jnp.zeros_like(gt))
            g = gb.astype(f32)
            kept.append(gt)
            for c in range(crops):
                sums[c] = sums[c] + fold_lanes(g[:, width * c : width * (c + 1)])
            parts = []
            for pr in range(2):
                even, odd = g[64 * pr : 64 * pr + 32], g[64 * pr + 32 : 64 * pr + 64]
                parts += [
                    from_left(odd, crops).astype(bf16),
                    gb[64 * pr : 64 * pr + 64],
                    from_right(even, crops).astype(bf16),
                ]
            put_rows(g3_ref, (r + 2) * 256, jnp.concatenate(parts, axis=0))
        for r, gt in zip(rs, kept):
            put_rows(h3_ref, (r + 1) * 128, gt)
        for k, b in zip(ready, coarse):
            put_rows(gc_ref, k * 64, b)
        head_ref[...] += head
        go_sum[...] += gsum
        for c in range(crops):
            sg_sum[c] += sums[c]

    backward(range(BACK))
    repeat_rows(rows - BACK, BACK, lambda rs: backward(rs, [r - BACK for r in rs]), BACK)
    for c in range(crops):
        sg_ref[c : c + 1, :] = lane_sums(sg_sum[c])[0:1]
    sums_ref[3:4, 0:16] = lane_sums(go_sum[...])[0:1]
    sg_copies = share(tiles, "tile", sg_ref, sg_got, s2_send, s2_recv)
    rest = list(range(rows - BACK, rows + 2))
    for k, b in zip(rest, down(rest)):
        put_rows(gc_ref, k * 64, b)

    rim_lo[...] = gc_ref[0:128, :].astype(bf16)
    rim_hi[...] = gc_ref[64 * rows : 64 * rows + 128, :].astype(bf16)
    finish_rims = swap_edges(tiles, [(rim_lo, rim_hi, rim_up, rim_dn)], rim_send, rim_recv)

    def weights_three(ks):
        d3 = 0.0
        for k in ks:
            gs = [rows_of(g3_ref, k * 256 + 128 * j + 160, 64) for j in range(4)]
            d3 = d3 + dot_nt(jnp.concatenate(gs, axis=0), rows_of(x3_ref, (k + 1) * 192, 192))
        d3_ref[...] += d3

    repeat_rows(rows + 2, 6, weights_three)
    for tap in range(9):
        a, b = tap // 3, tap % 3
        total = jnp.zeros((CH_ONE, CH_TWO), f32)
        for first in (2 - a, 3 - a):
            for pc in range(2):
                s = (pc + b + 1) // 2
                total = total + d3_ref[64 * first + 32 * pc : 64 * first + 32 * pc + 32, 64 * s : 64 * (s + 1)]
        if tap < 8:
            pay_a[32 * (tap // 2) : 32 * (tap // 2 + 1), 64 * (tap % 2) : 64 * (tap % 2 + 1)] = total
        else:
            pay_a[128:144, :] = jnp.concatenate([total[0:16], total[16:32]], axis=1)
    outer = jnp.zeros((CH_ONE, 128), f32)
    for c in range(crops):
        outer = outer + as_column(over_phases(sg_ref[c : c + 1, :]))[0:32] * jnp.concatenate([unit[c : c + 1]] * 2, axis=1)
        sums_ref[2:3, :] += sg_ref[c : c + 1, :]
    head = jnp.concatenate([head_ref[...], jnp.zeros((128, 112), f32)], axis=1)
    pay_a[144:160, :] = jnp.transpose(head)[0:16]
    pay_a[160:176, :] = jnp.concatenate([outer[0:16, 0:64], outer[16:32, 0:64]], axis=1)
    pay_a[176:184, :] = sums_ref[...]
    if pay_a.shape[0] > 184:
        pay_a[184:, :] = jnp.zeros((pay_a.shape[0] - 184, 128), f32)
    reduce_a.scatter()

    wait_all(sg_copies)
    style_grad = over_phases(in_order(sg_got, tiles))[:, 0:32]
    grad_unit = jnp.dot(style_grad, ws_ref[...], precision=highest, preferred_element_type=f32)
    mixed = jnp.mean(style_raw * grad_unit, axis=1, keepdims=True)
    grad_raw = style_inv * grad_unit - style_inv * style_inv * style_inv * style_raw * mixed
    grad_raw = jnp.concatenate([grad_raw / coarse_count] * 2, axis=1)
    raw = [as_column(grad_raw[c : c + 1])[0:64] for c in range(crops)]
    d2_ref[...] = jnp.zeros_like(d2_ref)
    d1_ref[...] = jnp.zeros_like(d1_ref)
    g2_sum[...] = jnp.zeros_like(g2_sum)
    raw = jnp.concatenate([wide(v, width) for v in raw], axis=1)
    g2_ref = g3_ref

    def masked(ks, extras=None):
        sums, d2 = 0.0, 0.0
        for j, k in enumerate(ks):
            coarse = rows_of(gc_ref, k * 64, 64)
            if extras is not None:
                coarse = coarse + extras[j]
            grad = (coarse + raw).astype(bf16)
            gb = jnp.where(rows_of(x3_ref, (k + 1) * 192 + 64, 64) > 0, grad, jnp.zeros_like(grad))
            g = gb.astype(f32)
            if extras is None or 0 < j < 3:
                sums = sums + fold_lanes(g)
                d2 = d2 + dot_nt(rows_of(x2_ref, (k + 1) * 96, 288), gb)
            put_rows(g2_ref, k * 192, three_columns(gb, g, crops))
        g2_sum[...] += sums
        d2_ref[...] += d2

    repeat_rows(rows - 2, 7, masked, 2)
    finish_rims()
    up = jnp.where(edge[0] < 0, rim_up[...].astype(f32), 0.0)
    dn = jnp.where(edge[1] > rows, rim_dn[...].astype(f32), 0.0)
    masked([0, 1, rows, rows + 1], [up[0:64], up[64:128], dn[0:64], dn[64:128]])
    pay_b[...] = jnp.zeros_like(pay_b)

    pay_b[160:161, 0:64] = lane_sums(g2_sum[...])[0:1]

    rest = jnp.concatenate([d2_ref[160:288, :], jnp.zeros((32, 64), f32)], axis=0)
    pay_b[0:160, :] = jnp.concatenate([d2_ref[0:160, :], rest], axis=1)
    reduce_b.scatter()
    reduce_a.across()

    def last_back(rs):
        gps = [dot(wd2_ref[...], rows_of(g2_ref, r * 192, 576)) for r in rs]
        d1 = 0.0
        for r, gp in zip(rs, gps):
            gp = 0.25 * gp.astype(bf16).astype(f32)
            gt = rows_of(h3_ref, (r + 1) * 128, 128).astype(f32)
            g1 = (jnp.concatenate([gp] * 4, axis=0) + gt).astype(bf16)
            gb = jnp.where(rows_of(h1_ref, (r + 3) * 128, 128) > 0, g1, jnp.zeros_like(g1))
            d1 = d1 + dot_nt(gb, jnp.concatenate([rows_of(y_ref, (r + 3) * 16, 32), ones_ref[...]], axis=0))
        d1_ref[...] += d1

    quarter = rows // 4
    repeat_rows(rows // 2, 4, last_back)
    reduce_a.gather(full_a)
    repeat_rows(quarter, 4, last_back, rows // 2)
    reduce_b.across()
    repeat_rows(rows - rows // 2 - quarter, 4, last_back, rows // 2 + quarter)
    d1 = jnp.transpose(jnp.concatenate([d1_ref[...], jnp.zeros((128, 80), f32)], axis=1))
    total = jnp.zeros((32, 128), f32)
    for p in range(4):
        total = total + turn(turn(d1[0:32], -32 * p, 1), -(8 * (p // 2) + p % 2), 0)
    packed = lane_group(total[0:8], 0)
    for k in range(1, 3):
        packed = packed + turn(lane_group(total[8 * k : 8 * (k + 1)], 0), 32 * k, 1)
    pay_c[...] = packed + lane_group(jnp.broadcast_to(over_phases(d1[32:33]), (8, 128)), 3)
    copies = share(tiles, "tile", pay_c, got_c, sems[12], sems[13])
    reduce_b.gather(full_b)
    wait_all(copies)
    own_c[...] = in_order(got_c, tiles)
    copies = share(images, "img", own_c, met_c, sems[14], sems[15])
    reduce_a.finish()
    size_a, size_b = full_a.shape[0], full_b.shape[0]
    o_ref[0:size_a, :] = full_a[...]
    reduce_b.finish()
    o_ref[size_a : size_a + size_b, :] = full_b[...]
    wait_all(copies)
    o_ref[size_a + size_b :, :] = in_order(met_c, images)


def update_kernel(pixel_count, second_at, third_at, count_ref, sum_ref, *refs):
    olds, outs, loss_ref = refs[:18], refs[18:36], refs[36]
    rate = 1.0 / (jnp.zeros((8, 128), f32) + (count_ref[0].astype(f32) + 1.0))

    def step(index, spot, grad):
        weight, momentum, average = (olds[3 * index + k][spot] for k in range(3))
        decayed = grad + decay_rate * weight
        momentum = momentum_rate * momentum + decayed
        new = weight - learn_rate * (decayed + momentum_rate * momentum)
        outs[3 * index][spot] = new
        outs[3 * index + 1][spot] = momentum
        outs[3 * index + 2][spot] = average + (new - average) * rate[0:1, 0:1]

    first = sum_ref[third_at : third_at + 8, :]
    for a in range(3):
        for b in range(3):
            for i in range(2):
                grad = first[4 * i + b : 4 * i + b + 1, 32 * a : 32 * (a + 1)]
                step(0, (a, b, slice(i, i + 1), slice(None)), grad)
    for tap in range(9):
        a, b = tap // 3, tap % 3
        first = second_at + 32 * (tap % 5)
        half = 64 * (tap // 5)
        step(1, (a, b), sum_ref[first : first + 32, half : half + 64])
        if tap < 8:
            first = 32 * (tap // 2)
            lane = 64 * (tap % 2)
            grad = sum_ref[first : first + 32, lane : lane + 64]
        else:
            first = 128
            grad = jnp.concatenate([sum_ref[first : first + 16, 64 * k : 64 * (k + 1)] for k in range(2)], axis=0)
        step(2, (a, b), grad)
    first = 160
    grad = jnp.concatenate([sum_ref[first : first + 16, 64 * k : 64 * (k + 1)] for k in range(2)], axis=0)
    step(3, (slice(None), slice(None)), grad)
    head = sum_ref[144:160, :]
    total = jnp.zeros((16, 128), f32)
    for p in range(4):
        total = total + turn(turn(head, -32 * p, 1), -p, 0)
    total = jnp.concatenate([total[4 * o : 4 * o + 1] for o in range(OUT_CH)], axis=0)
    step(4, (slice(None), slice(None)), total[:, 0:32])
    sums = sum_ref[176:184, :]
    one = turn(sum_ref[third_at : third_at + 1, :], -96, 1)
    two = jnp.sum(sum_ref[second_at + 160 : second_at + 168, :], axis=0, keepdims=True)
    three = over_phases(sums[2:3])
    lane = lax.broadcasted_iota(jnp.int32, (1, 128), 1)
    low = jnp.where(lane < 32, one, jnp.where(lane < 96, turn(two, 32, 1), three))
    ends = sums[3:4]
    ends = (ends + turn(ends, -1, 1)) + (turn(ends, -2, 1) + turn(ends, -3, 1))
    high = jnp.where(lane < 32, three, 0.0)
    for o in range(OUT_CH):
        high = jnp.where(lane == 32 + o, turn(ends, 32 + o - 4 * o, 1), high)
    grad = jnp.concatenate([low, high], axis=1)[:, 0 : olds[15].shape[0]]
    weight, momentum, average = (olds[15 + k][...].reshape(1, -1) for k in range(3))
    decayed = grad + decay_rate * weight
    momentum = momentum_rate * momentum + decayed
    new = weight - learn_rate * (decayed + momentum_rate * momentum)
    average = average + (new - average) * rate[0:1, 0:1]
    for k, value in enumerate((new, momentum, average)):
        outs[15 + k][...] = value.reshape(-1)
    loss_ref[0] = jnp.sum(sums[4:5]) / pixel_count


def on_device(
    images, nucleus, target_flow, cell_label, step_count,
    conv1_weight, conv1_momentum, conv1_average,
    conv2_weight, conv2_momentum, conv2_average,
    conv3_weight, conv3_momentum, conv3_average,
    style_weight, style_momentum, style_average,
    head_weight, head_momentum, head_average,
    biases, bias_momentum, bias_average,
):
    tiles = lax.axis_size("tile")
    crops, _, height, cols = images.shape
    rows, width = height // 2, cols // 2
    pixel_count = lax.axis_size("img") * tiles * crops * height * cols
    grad_scale = 1.0 / math.sqrt(pixel_count)
    coarse_count = tiles * rows * width

    def sds(shape, dtype=f32):
        return jax.ShapeDtypeStruct(shape, dtype)

    lanes = crops * width
    images_count = lax.axis_size("img")

    def other_way(w):
        return jnp.swapaxes(w, -1, -2)

    third = tuple(other_way(w) for w in (conv3_weight, conv3_momentum, conv3_average))
    style = tuple(other_way(w) for w in (style_weight, style_momentum, style_average))
    head = tuple(other_way(w) for w in (head_weight, head_momentum, head_average))

    edge = (crops, 2, HALO, cols)
    rim = (128, lanes)
    parts = [8 * pl.cdiv(sum(block), 8 * tiles) for block in BLOCK_ROWS[:2]]
    small = sum(BLOCK_ROWS[2])

    def buf(shape, dtype=bf16):
        return pltpu.VMEM(shape, dtype)

    def block_bufs(part):
        return [
            buf((part * tiles, 128), f32), buf((tiles, part, 128), f32), buf((part, 128), f32),
            buf((images_count, part, 128), f32), buf((part * tiles, 128), f32),
        ]

    sources = (
        images, target_flow, cell_label, conv1_weight, conv2_weight, third[0], head[0], biases, style[0],
    )
    block_sems = [DMA((tiles,)), DMA((tiles,)), DMA((images_count,)), DMA((images_count,)), DMA((tiles,)), DMA((tiles,))]
    summed = pl.pallas_call(
        lambda *refs: step_kernel(tiles, images_count, grad_scale, float(coarse_count), *refs),
        out_shape=pltpu.VMEM((sum(parts) * tiles + small, 128), f32),
        in_specs=[SMEM] + [HBM] * 9,
        out_specs=VMEM,
        scratch_shapes=[buf(v.shape, v.dtype) for v in sources]
        + [
            buf(edge), buf(edge), buf(edge, jnp.int32), buf(edge, jnp.int32),
            buf((128, 48)), buf((CH_TWO, 9 * CH_ONE + 16)), buf((128, 14 * CH_TWO + 16)), buf((128, 16 * CH_ONE)),
            buf((CH_ONE, 9 * CH_TWO)), buf((16, 128)), buf((128, 16)),
            buf((8, 128), f32), buf((16, 128), f32), buf((32, 128), f32), buf((16, lanes)), buf((16, lanes)),
            buf((16 * (rows + 7), lanes)), buf((lanes // 128, 16 * (rows + 2), 128), f32),
            buf((128 * (rows + 6), lanes)), buf((96 * (rows + 6), lanes)), buf((192 * (rows + 4), lanes)),
            buf((128 * (rows + 2), lanes)), buf((128 * (rows + 2), lanes)),
            buf((lanes // 128, 16 * (rows + 2), 128), f32), buf((lanes // 128, 16 * rows, 128), f32),
            buf((256 * (rows + 4), lanes)), buf((64 * (rows + 2), lanes), f32),
            buf(rim), buf(rim), buf(rim), buf(rim),
            buf((8, 128), f32), buf((tiles, 8, 128), f32), buf((8, 128), f32), buf((tiles, 8, 128), f32),
            buf((128, 16), f32), buf((8, 128), f32),
            buf((256, 3 * CH_TWO), f32), buf((9 * CH_ONE, CH_TWO), f32), buf((128, 48), f32),
            buf((crops, CH_TWO, 128), f32), buf((crops, 128, 128), f32), buf((16, 128), f32), buf((CH_TWO, 128), f32),
        ]
        + block_bufs(parts[0])
        + block_bufs(parts[1])
        + [buf((small, 128), f32), buf((tiles, small, 128), f32), buf((small, 128), f32), buf((images_count, small, 128), f32)]
        + [DMA((9,)), DMA((4,)), DMA((4,)), DMA((tiles,)), DMA((tiles,)), DMA((tiles,)), DMA((tiles,)), DMA((2,)), DMA((2,))]
        + block_sems * 2
        + [DMA((tiles,)), DMA((tiles,)), DMA((images_count,)), DMA((images_count,))],
        compiler_params=pltpu.CompilerParams(collective_id=1, has_side_effects=True, vmem_limit_bytes=60 * 2**20),
        name="step",
    )(nucleus, *sources)

    olds = (
        (conv1_weight, conv1_momentum, conv1_average)
        + (conv2_weight, conv2_momentum, conv2_average)
        + third + style + head
        + (biases, bias_momentum, bias_average)
    )
    news = pl.pallas_call(
        lambda *refs: update_kernel(float(pixel_count), parts[0] * tiles, sum(parts) * tiles, *refs),
        out_shape=tuple(sds(v.shape) for v in olds) + (sds((1,)),),
        in_specs=[SMEM] + [VMEM] * 19,
        out_specs=[VMEM] * 18 + [SMEM],
        compiler_params=pltpu.CompilerParams(vmem_limit_bytes=16 * 2**20),
        name="update",
    )(step_count, summed, *olds)
    return (news[18], *news[0:6], *(other_way(w) for w in news[6:15]), *news[15:18])


def solution(mesh):
    return jax.shard_map(
        on_device,
        mesh=mesh,
        in_specs=(
            P("img", None, "tile", None),
            P("img"),
            P("img", None, "tile", None),
            P("img", "tile", None),
        )
        + (P(),) * 19,
        out_specs=(P(),) * 19,
        check_vma=False,
    )
```

```python
import math

import jax
import jax.numpy as jnp
from jax import lax
from jax.experimental import pallas as pl
from jax.experimental.pallas import tpu as pltpu
from jax.sharding import PartitionSpec as P

CH_ONE = 32
CH_TWO = 64
OUT_CH = 3

momentum_rate = 0.9
learn_rate = 0.02
decay_rate = 0.0001
norm_eps = 1e-05
highest = lax.Precision.HIGHEST
f32 = jnp.float32
bf16 = jnp.bfloat16

HALO = 8
BACK = 2
EARLY = 6
VMEM = pl.BlockSpec(memory_space=pltpu.VMEM)
SMEM = pl.BlockSpec(memory_space=pltpu.SMEM)
HBM = pl.BlockSpec(memory_space=pltpu.HBM)
MESH = pl.DeviceIdType.MESH
DMA = pltpu.SemaphoreType.DMA

BLOCK_ROWS = ((144, 16, 16, 8), (160, 8), (8,))


def dot(a, b):
    return jnp.dot(a, b, preferred_element_type=f32)


def dot_nt(a, b, precision=None):
    return lax.dot_general(a, b, (((1,), (1,)), ((), ())), preferred_element_type=f32, precision=precision)


def edge_select(x, crops, first):
    width = x.shape[1] // crops
    lane = lax.broadcasted_iota(jnp.int32, (x.shape[0], 128), 1)
    parts = []
    for c in range(crops):
        low, high = width * c, width * (c + 1)
        if first:
            parts += [jnp.where(lane == 0, 0.0, x[:, low : low + 128]), x[:, low + 128 : high]]
        else:
            parts += [x[:, low : high - 128], jnp.where(lane == 127, 0.0, x[:, high - 128 : high])]
    return jnp.concatenate(parts, axis=1)


def from_left(x, crops):
    return edge_select(pltpu.roll(x, 1, 1), crops, True)


def from_right(x, crops):
    return edge_select(pltpu.roll(x, x.shape[1] - 1, 1), crops, False)


def three_columns(mid, x, crops):
    return jnp.concatenate([from_left(x, crops).astype(bf16), mid, from_right(x, crops).astype(bf16)], axis=0)


def pieces_of(x):
    high = x.astype(bf16)
    rest = x - high.astype(f32)
    mid = rest.astype(bf16)
    return high.astype(f32), mid.astype(f32), rest - mid.astype(f32)


def repeat_rows(count, limit, body, first=0):
    step = max(k for k in range(1, limit + 1) if count % k == 0)

    def run(k, carry):
        body([first + k * step + j for j in range(step)])
        return carry

    lax.fori_loop(0, count // step, run, 0)


def turn(x, by, axis):
    by = by % x.shape[axis]
    return pltpu.roll(x, by, axis) if by else x


def lane_group(x, group, size=32):
    lane = lax.broadcasted_iota(jnp.int32, x.shape, 1)
    return jnp.where(lane // size == group, x, 0.0)


def over_phases(x):
    return (x + turn(x, 32, 1)) + (turn(x, 64, 1) + turn(x, 96, 1))


def as_column(row):
    return jnp.transpose(jnp.broadcast_to(row, (128, 128)))


def fold_lanes(x):
    parts = [x[:, 128 * k : 128 * (k + 1)] for k in range(x.shape[1] // 128)]
    while len(parts) > 1:
        parts = [a + b for a, b in zip(parts[0::2], parts[1::2])] + parts[len(parts) // 2 * 2 :]
    return parts[0]


def lane_sums(x):
    return dot_nt(jnp.ones((8, 128), f32), x, highest)


def wide(tile, width):
    return jnp.concatenate([tile] * (width // 128), axis=1)


def rows_of(ref, start, size):
    return ref[pl.ds(pl.multiple_of(start, 16), size), :]


def put_rows(ref, start, value):
    ref[pl.ds(pl.multiple_of(start, 16), value.shape[0]), :] = value


def put_lanes(ref, start, value):
    for k in range(value.shape[1] // 128):
        ref[k, pl.ds(pl.multiple_of(start, 16), value.shape[0]), :] = value[:, 128 * k : 128 * (k + 1)]


def get_lanes(ref, start, size, stride=None):
    spot = pl.ds(start, size, stride=stride) if stride else pl.ds(pl.multiple_of(start, 16), size)
    return jnp.concatenate([ref[k, spot, :] for k in range(ref.shape[0])], axis=1)


def strip_edges(tiles, rows):
    me = lax.axis_index("tile")
    return -me * rows, (tiles - me) * rows


def valid(row, edge):
    return jnp.where((row >= edge[0]) & (row < edge[1]), 1.0, 0.0).astype(f32)


def greet(sizes):
    gate = pltpu.get_barrier_semaphore()
    for axis, count in sizes:
        me = lax.axis_index(axis)
        for j in range(1, count):
            pl.semaphore_signal(gate, inc=1, device_id={axis: lax.rem(me + j, count)}, device_id_type=MESH)
    return lambda: pl.semaphore_wait(gate, sum(count - 1 for _, count in sizes))


def send_all(count, axis, source, target, send_sem, recv_sem):
    me = lax.axis_index(axis)
    copies = []
    for j in range(1, count):
        to = lax.rem(me + j, count)
        copy = pltpu.make_async_remote_copy(
            src_ref=source(to), dst_ref=target, send_sem=send_sem.at[j - 1], recv_sem=recv_sem.at[j - 1],
            device_id={axis: to}, device_id_type=MESH,
        )
        copy.start()
        copies.append(copy)
    return copies


def wait_all(copies):
    for copy in copies:
        copy.wait()


def in_order(ref, count):
    total = ref[0]
    for k in range(1, count):
        total = total + ref[k]
    return total


def swap_edges(tiles, pairs, send_sem, recv_sem):
    me = lax.axis_index("tile")
    copies = []
    for k, (low, high, from_before, from_after) in enumerate(pairs):
        down = pltpu.make_async_remote_copy(
            src_ref=high, dst_ref=from_before, send_sem=send_sem.at[2 * k], recv_sem=recv_sem.at[2 * k],
            device_id={"tile": jnp.minimum(me + 1, tiles - 1)}, device_id_type=MESH,
        )
        up = pltpu.make_async_remote_copy(
            src_ref=low, dst_ref=from_after, send_sem=send_sem.at[2 * k + 1], recv_sem=recv_sem.at[2 * k + 1],
            device_id={"tile": jnp.maximum(me - 1, 0)}, device_id_type=MESH,
        )
        copies.append((down, up))

    @pl.when(me < tiles - 1)
    def _():
        for down, _up in copies:
            down.start()

    @pl.when(me > 0)
    def _():
        for _down, up in copies:
            up.start()

    def finish():
        @pl.when(me < tiles - 1)
        def _():
            for down, up in copies:
                down.wait_send()
                up.wait_recv()

        @pl.when(me > 0)
        def _():
            for down, up in copies:
                up.wait_send()
                down.wait_recv()

    return finish


def share(count, axis, source, got, send_sem, recv_sem):
    me = lax.axis_index(axis)
    got[me] = source[...]
    return send_all(count, axis, lambda to: source, got.at[me], send_sem, recv_sem)


class Reduction:
    def __init__(self, tiles, images, pay, got, own, met, sems):
        self.tiles, self.images = tiles, images
        self.pay, self.got, self.own, self.met, self.sems = pay, got, own, met, sems
        self.part = own.shape[0]
        self.me = lax.axis_index("tile")

    def block(self, k):
        return pl.ds(pl.multiple_of(k * self.part, 8), self.part)

    def scatter(self):
        self.got[self.me] = self.pay[self.block(self.me), :]
        self.copies = send_all(
            self.tiles, "tile", lambda to: self.pay.at[self.block(to), :], self.got.at[self.me], self.sems[0], self.sems[1]
        )

    def across(self):
        wait_all(self.copies)
        self.own[...] = in_order(self.got, self.tiles)
        self.copies = share(self.images, "img", self.own, self.met, self.sems[2], self.sems[3])

    def gather(self, full):
        wait_all(self.copies)
        full[self.block(self.me), :] = in_order(self.met, self.images)
        here = full.at[self.block(self.me), :]
        self.copies = send_all(self.tiles, "tile", lambda to: here, here, self.sems[4], self.sems[5])

    def finish(self):
        wait_all(self.copies)


def first_tables(k1_ref, k2_ref, bias_ref, w1_ref, w2_ref, base_ref):
    base_ref[...] = jnp.zeros_like(base_ref)
    for a in range(3):
        for b in range(3):
            for i in range(2):
                base_ref[8 * a + 4 * i + b : 8 * a + 4 * i + b + 1, 0:32] = k1_ref[a, b, i : i + 1, :]
    base = base_ref[...]
    w1t = jnp.zeros((32, 128), f32)
    for p in range(4):
        w1t = w1t + turn(turn(base, 8 * (p // 2) + p % 2, 0), 32 * p, 1)
    bias = bias_ref[...].reshape(1, -1)
    row = lax.broadcasted_iota(jnp.int32, (16, 128), 0)

    def piece_rows(values):
        table = jnp.zeros((16, 128), f32)
        for k, piece in enumerate(pieces_of(values)):
            table = jnp.where(row == k, jnp.broadcast_to(piece, (16, 128)), table)
        return table

    b1 = piece_rows(jnp.concatenate([bias[:, 0:32]] * 4, axis=1))
    w1_ref[...] = jnp.transpose(jnp.concatenate([w1t, b1], axis=0)).astype(bf16)

    k2 = [[k2_ref[a, b].astype(bf16).astype(f32) for b in range(3)] for a in range(3)]
    w2t = jnp.concatenate([k2[a][b] for a in range(3) for b in range(3)], axis=0)
    b2 = piece_rows(jnp.concatenate([bias[:, 32:96]] * 2, axis=1))[:, 0:64]
    w2_ref[...] = jnp.transpose(jnp.concatenate([w2t, b2], axis=0)).astype(bf16)


def later_tables(k2_ref, k3_ref, kh_ref, bias_ref, w3_ref, wd3_ref, wd2_ref, wh_ref, wht_ref, b3_ref, bh_ref):
    k2 = [[k2_ref[a, b].astype(bf16).astype(f32) for b in range(3)] for a in range(3)]
    wd2_ref[...] = jnp.concatenate([k2[2 - s][2 - t] for s in range(3) for t in range(3)], axis=1).astype(bf16)

    def tap_sum(first, second):
        total = None
        for a in first:
            for b in second:
                total = k3[a][b] if total is None else total + k3[a][b]
        return jnp.zeros((CH_ONE, CH_TWO), f32) if total is None else total

    k3 = [[k3_ref[a, b].astype(bf16).astype(f32) for b in range(3)] for a in range(3)]
    up = [[[a for a in range(3) if (p + a + 1) // 2 == r] for r in range(3)] for p in range(2)]
    for p in range(4):
        w3 = jnp.concatenate([tap_sum(up[p // 2][r], up[p % 2][c]) for r in range(3) for c in range(3)], axis=1)
        w3_hi = w3.astype(bf16)
        low = w3 - w3_hi.astype(f32)
        low = jnp.concatenate([low[:, 64:128], low[:, 192:384], low[:, 448:512]], axis=1)
        w3_ref[32 * p : 32 * (p + 1), 0:896] = jnp.concatenate([w3_hi, low.astype(bf16)], axis=1)
    down = ((2,), (1, 2), (0, 1), (0,))
    wd3 = jnp.transpose(jnp.concatenate([tap_sum(down[r], down[c]) for r in range(4) for c in range(4)], axis=0))
    wd3_hi = wd3.astype(bf16)
    wd3_ref[0:64, :] = wd3_hi
    wd3_ref[64:128, :] = (wd3 - wd3_hi.astype(f32)).astype(bf16)

    row = lax.broadcasted_iota(jnp.int32, (16, 128), 0)
    lane = lax.broadcasted_iota(jnp.int32, (16, 128), 1)
    wh = jnp.zeros((16, 128), f32)
    for o in range(OUT_CH):
        one = jnp.concatenate([kh_ref[o : o + 1, :]] * 4, axis=1)
        wh = jnp.where(row // 4 == o, jnp.broadcast_to(one, (16, 128)), wh)
    wh = jnp.where(row % 4 == lane // 32, wh, 0.0)
    wh_ref[...] = wh.astype(bf16)
    wht_ref[...] = jnp.transpose(wh).astype(bf16)

    bias = bias_ref[...].reshape(1, -1)
    b3_ref[...] = jnp.zeros_like(b3_ref)
    b3_ref[0:1, :] = jnp.concatenate([bias[:, 96:128] + bias[:, 128:160]] * 4, axis=1)
    bh = jnp.zeros((16, 128), f32)
    for o in range(OUT_CH):
        bh = jnp.where(row // 4 == o, jnp.broadcast_to(bias[:, 160 + o : 161 + o], (16, 128)), bh)
    bh_ref[...] = bh


def split_columns(x, select):
    even, odd = [], []
    for k in range(x.shape[1] // 256):
        piece = dot(x[:, 256 * k : 256 * (k + 1)], select)
        even.append(piece[:, 0:128])
        odd.append(piece[:, 128:256])
    return jnp.concatenate(even, axis=1), jnp.concatenate(odd, axis=1)


def step_kernel(
    tiles, images, scale, coarse_count,
    nucleus_ref, x_hbm, t_hbm, label_hbm, k1_hbm, k2_hbm, k3_hbm, kh_hbm, bias_hbm, ws_hbm,
    o_ref,
    x_ref, t_ref, label_ref, k1_ref, k2_ref, k3_ref, kh_ref, bias_ref, ws_ref,
    x_lo, x_hi, t_lo, t_hi,
    w1_ref, w2_ref, w3_ref, wd3_ref, wd2_ref, wh_ref, wht_ref, b3_ref, bh_ref, base_ref, ones_ref, mark_ref,
    y_ref, t_out, h1_ref, x2_ref, x3_ref, h3_ref, m_ref, fe_ref, go_ref, g3_ref, gc_ref,
    rim_lo, rim_hi, rim_up, rim_dn,
    style_ref, style_got, sg_ref, sg_got, head_ref, sums_ref, d3_ref, d2_ref, d1_ref,
    style_sum, sg_sum, go_sum, g2_sum,
    pay_a, got_a, own_a, met_a, full_a, pay_b, got_b, own_b, met_b, full_b,
    pay_c, got_c, own_c, met_c,
    load_sems, halo_send, halo_recv, flow_send, flow_recv, s1_send, s1_recv, s2_send, s2_recv, rim_send, rim_recv,
    *sems,
):
    pre_ref = gc_ref
    reduce_a = Reduction(tiles, images, pay_a, got_a, own_a, met_a, sems[0:6])
    reduce_b = Reduction(tiles, images, pay_b, got_b, own_b, met_b, sems[6:12])
    arrived = greet((("tile", tiles), ("img", images)))
    loads = [
        pltpu.make_async_copy(source, target, load_sems.at[k])
        for k, (source, target) in enumerate(
            (
                (k1_hbm, k1_ref), (k2_hbm, k2_ref), (bias_hbm, bias_ref), (x_hbm, x_ref),
                (t_hbm, t_ref), (label_hbm, label_ref), (k3_hbm, k3_ref), (kh_hbm, kh_ref), (ws_hbm, ws_ref),
            )
        )
    ]
    for load in loads:
        load.start()
    ones_ref[...] = jnp.ones_like(ones_ref)
    arrived()
    last = x_ref.shape[2] - HALO
    finish_halo, finish_targets = (
        swap_edges(
            tiles, [(ref.at[:, :, pl.ds(0, HALO), :], ref.at[:, :, pl.ds(last, HALO), :], lo, hi)], send, recv
        )
        for ref, lo, hi, send, recv in (
            (x_hbm, x_lo, x_hi, halo_send, halo_recv),
            (t_hbm, t_lo, t_hi, flow_send, flow_recv),
        )
    )
    for load in loads[0:4]:
        load.wait()
    first_tables(k1_ref, k2_ref, bias_ref, w1_ref, w2_ref, base_ref)
    crops = x_ref.shape[0]
    width = x_ref.shape[3] // 2
    lanes = crops * width
    height = x_ref.shape[2]
    rows = height // 2
    edge = strip_edges(tiles, rows)
    r_id = lax.broadcasted_iota(jnp.int32, (256, 256), 0)
    c_id = lax.broadcasted_iota(jnp.int32, (256, 256), 1)
    select = jnp.where(r_id == 2 * (c_id % 128) + c_id // 128, 1.0, 0.0).astype(bf16)
    y_rows = y_ref.shape[0]
    ri = lax.broadcasted_iota(jnp.int32, (y_rows, 8 * height), 0)
    ci = lax.broadcasted_iota(jnp.int32, (y_rows, 8 * height), 1)
    fine = 2 * (ri // 16) + (ri // 8) % 2 - 7
    source = (ri % 4) * 2 * height + (ri // 4) % 2 * height + fine
    perm_x = jnp.where((ci == source) & (fine >= 0) & (fine < height), 1.0, 0.0).astype(bf16)
    ri = lax.broadcasted_iota(jnp.int32, (128, 16 * HALO), 0)
    ci = lax.broadcasted_iota(jnp.int32, (128, 16 * HALO), 1)
    fine = 2 * (ri // 16) + (ri // 8) % 2 - 7
    fine = jnp.where(ri < 64, fine, fine + y_rows // 8 - 16)
    source = jnp.where(fine < 0, fine + HALO, 2 * HALO + fine - height)
    source = (ri % 4) * 4 * HALO + (ri // 4) % 2 * HALO + source
    perm_h = jnp.where((ci == source) & ((fine < 0) | (fine >= height)), 1.0, 0.0).astype(bf16)
    has_up, has_dn = edge[0] < 0, edge[1] > rows

    def both_columns(of_crop):
        even, odd = [], []
        for c in range(crops):
            first, second = split_columns(of_crop(c), select)
            even.append(first)
            odd.append(second)
        return jnp.concatenate(even, axis=1), jnp.concatenate(odd, axis=1)

    def own_rows(c):
        return jnp.concatenate([x_ref[c, k] for k in range(2)], axis=0)

    def halo_rows(c):
        pieces = [jnp.where(has_up, x_lo[c, k].astype(f32), 0.0) for k in range(2)]
        pieces += [jnp.where(has_dn, x_hi[c, k].astype(f32), 0.0) for k in range(2)]
        return jnp.concatenate(pieces, axis=0).astype(bf16)

    def target_rows(c):
        pieces = [t_ref[c, 0].astype(f32), t_ref[c, 1].astype(f32), label_ref[c].astype(f32)]
        pieces += [jnp.where(has_up, t_lo[c, k], 0).astype(f32) for k in range(2)]
        pieces += [jnp.where(has_dn, t_hi[c, k], 0).astype(f32) for k in range(2)]
        return jnp.concatenate(pieces, axis=0).astype(bf16)

    def pixel_windows(of_crop, second):
        even, odd = both_columns(of_crop)
        row = lax.broadcasted_iota(jnp.int32, even.shape, 0)
        crop = lax.broadcasted_iota(jnp.int32, even.shape, 1) // width
        gate = jnp.ones(even.shape, f32)
        for c in range(crops):
            gate = jnp.where(second(row) & (crop == c), nucleus_ref[c].astype(f32), gate)
        even, odd = even * gate, odd * gate
        return jnp.concatenate([from_left(odd, crops), even, odd, from_right(even, crops)], axis=0).astype(bf16)

    y_ref[...] = dot(perm_x, pixel_windows(own_rows, lambda row: row >= height)).astype(bf16)

    def conv_one(ks, inside=True):
        pre = [
            dot(w1_ref[...], jnp.concatenate([rows_of(y_ref, k * 16, 32), ones_ref[...]], axis=0)) for k in ks
        ]
        for k, p in zip(ks, pre):
            p = jnp.maximum(p, 0.0)
            hidden = (p if inside else p * valid(k - 3, edge)).astype(bf16)
            put_rows(h1_ref, k * 128, hidden)
            h = hidden.astype(f32)
            pooled = (0.25 * ((h[0:32] + h[32:64]) + (h[64:96] + h[96:128]))).astype(bf16)
            put_rows(x2_ref, k * 96, three_columns(pooled, pooled.astype(f32), crops))

    def conv_two(qs, inside=True):
        pre = [
            dot(w2_ref[...], jnp.concatenate([rows_of(x2_ref, q * 96, 288), ones_ref[...]], axis=0)) for q in qs
        ]
        sums = [0.0] * crops
        for q, p in zip(qs, pre):
            p = jnp.maximum(p, 0.0)
            hidden = (p if inside else p * valid(q - 2, edge)).astype(bf16)
            h = hidden.astype(f32)
            put_rows(x3_ref, q * 192, three_columns(hidden, h, crops))
            for c in range(crops):
                sums[c] = sums[c] + fold_lanes(h[:, width * c : width * (c + 1)])
        if inside:
            for c in range(crops):
                style_sum[c] += sums[c]

    repeat_rows(rows - 2, 7, conv_one, 4)
    finish_halo()
    extra = dot(perm_h, pixel_windows(halo_rows, lambda row: row // HALO % 2 == 1))
    y_ref[0:64, :] = (y_ref[0:64, :].astype(f32) + extra[0:64]).astype(bf16)
    y_ref[y_rows - 64 : y_rows, :] = (y_ref[y_rows - 64 : y_rows, :].astype(f32) + extra[64:128]).astype(bf16)
    conv_one([0, 1, 2, 3, rows + 2, rows + 3, rows + 4, rows + 5], False)
    style_sum[...] = jnp.zeros_like(style_sum)
    repeat_rows(rows, 8, conv_two, 2)
    style_ref[...] = jnp.zeros_like(style_ref)
    for c in range(crops):
        style_ref[c : c + 1, 0:64] = lane_sums(style_sum[c])[0:1]
    style_copies = share(tiles, "tile", style_ref, style_got, s1_send, s1_recv)

    conv_two([0, 1], False)
    conv_two([rows + 2, rows + 3], False)
    for load in loads[4:]:
        load.wait()
    t_rows = 3 * height + 4 * HALO
    ri = lax.broadcasted_iota(jnp.int32, (t_out.shape[1], 2 * t_rows), 0)
    ci = lax.broadcasted_iota(jnp.int32, (t_out.shape[1], 2 * t_rows), 1)
    part = (ri // 4) % 4
    fine = 2 * (ri // 16) + (ri // 2) % 2 - 2
    source = jnp.where(
        fine < 0,
        3 * height + part * HALO + fine + HALO,
        jnp.where(fine < height, part * height + fine, 3 * height + 2 * HALO + part * HALO + fine - height),
    )
    outside = (fine < 0) | (fine >= height)
    known = (part < 2) | ((part == 2) & jnp.logical_not(outside))
    perm_t = jnp.where((ci == (ri % 2) * t_rows + source) & known, 1.0, 0.0).astype(bf16)
    finish_targets()
    even, odd = both_columns(target_rows)
    put_lanes(t_out, 0, dot(perm_t, jnp.concatenate([even, odd], axis=0).astype(bf16)))
    later_tables(k2_ref, k3_ref, kh_ref, bias_ref, w3_ref, wd3_ref, wd2_ref, wh_ref, wht_ref, b3_ref, bh_ref)

    def third_input(k):
        x = rows_of(x3_ref, k * 192, 576)
        return jnp.concatenate([x, x[64:128], x[192:384], x[448:512]], axis=0)

    for k in range(EARLY):
        put_rows(pre_ref, k * 128, dot(w3_ref[:, 0:896], third_input(k)))
    wait_all(style_copies)
    style_raw = in_order(style_got, tiles)[:, 0:64] / coarse_count
    style_inv = lax.rsqrt(jnp.mean(style_raw * style_raw, axis=1, keepdims=True) + norm_eps)
    unit = style_raw * style_inv
    vec = dot_nt(unit, ws_ref[...], highest)
    vec = jnp.concatenate([vec] * 4, axis=1) + b3_ref[0:1, :]
    bias3 = jnp.concatenate([wide(as_column(vec[c : c + 1]), width) for c in range(crops)], axis=1)
    row = lax.broadcasted_iota(jnp.int32, (16, lanes), 0)
    lane = lax.broadcasted_iota(jnp.int32, (16, lanes), 1)
    mark_ref[...] = jnp.where(row // 3 == lane // width, 1.0, 0.0).astype(bf16)
    row = lax.broadcasted_iota(jnp.int32, (128, 128), 0)
    table = jnp.zeros((128, 128), f32)
    for c in range(crops):
        for k, piece in enumerate(pieces_of(vec[c : c + 1])):
            table = jnp.where(row == 3 * c + k, jnp.broadcast_to(piece, (128, 128)), table)
    w3_ref[:, 896:912] = jnp.transpose(table)[:, 0:16].astype(bf16)

    def forward(ks, early=False):
        pre = []
        for k in ks:
            if early:
                pre.append(rows_of(pre_ref, k * 128, 128) + bias3)
            else:
                pre.append(dot(w3_ref[...], jnp.concatenate([third_input(k), mark_ref[...]], axis=0)))
        hs = []
        for k, p in zip(ks, pre):
            p = jnp.maximum(p, 0.0)
            h3 = (p + rows_of(h1_ref, (k + 2) * 128, 128).astype(f32)).astype(bf16)
            put_rows(h3_ref, k * 128, h3)
            put_rows(m_ref, k * 128, p.astype(bf16))
            hs.append(h3)
        outs = [dot(wh_ref[...], h) for h in hs]
        for k, o in zip(ks, outs):
            o = o + wide(bh_ref[...], lanes)
            t = get_lanes(t_out, k * 16, 16)
            fe = (o[0:8] - 0.25 * t[0:8]) * valid(k - 1, edge)
            put_lanes(fe_ref, k * 16, jnp.concatenate([fe, o[8:16]], axis=0))

    forward(range(EARLY), True)
    repeat_rows(rows + 2 - EARLY, 12, forward, EARLY)

    r_id = lax.broadcasted_iota(jnp.int32, (rows, lanes), 0)
    above = jnp.where(r_id - 1 >= edge[0], 1.0, 0.0)
    below = jnp.where(r_id + 1 < edge[1], 1.0, 0.0)
    go_ref[...] = jnp.zeros_like(go_ref)

    def at(part, off):
        return get_lanes(fe_ref, 16 * (1 + off) + part, rows, 16)

    def column_part(pr, off):
        odd, even = at(4 + 2 * pr + 1, off), at(4 + 2 * pr, off)
        return 0.5 * (odd - from_left(odd, crops)), 0.5 * (from_right(even, crops) - even)

    loss = jnp.zeros((rows, 128), f32)
    e0 = [at(k, 0) for k in range(4)]
    e1 = [at(4 + k, 0) for k in range(4)]
    cols0, cols1 = column_part(0, 0), column_part(1, 0)
    cols_up, cols_dn = column_part(1, -1), column_part(0, 1)
    spread = [None] * 4
    g_up, g_dn = [None] * 2, [None] * 2
    for pc in range(2):
        f_up, f_dn = at(2 + pc, -1), at(pc, 1)
        spread[pc] = 0.5 * (e0[2 + pc] - f_up) + cols0[pc]
        spread[2 + pc] = 0.5 * (f_dn - e0[pc]) + cols1[pc]
        g_up[pc] = 2.0 * scale * above * (0.5 * (e0[pc] - at(pc, -1)) + cols_up[pc])
        g_dn[pc] = 2.0 * scale * below * (0.5 * (at(2 + pc, 1) - e0[2 + pc]) + cols_dn[pc])
    g = [2.0 * scale * v for v in spread]
    for pr in range(2):
        even, odd = g[2 * pr], g[2 * pr + 1]
        col = [0.5 * (odd - from_left(odd, crops)), 0.5 * (from_right(even, crops) - even)]
        for pc in range(2):
            k = 2 * pr + pc
            if pr == 0:
                row_part = 0.5 * (g[2 + pc] - g_up[pc])
            else:
                row_part = 0.5 * (g_dn[pc] - g[pc])
            logit = at(8 + k, 0)
            label = get_lanes(t_out, 16 + 8 + k, rows, 16)
            ex = jnp.exp(-jnp.abs(logit))
            sig = jnp.where(logit >= 0, 1.0, ex) / (1.0 + ex)
            grads = (2.0 * scale * e0[k] - row_part, 2.0 * scale * e1[k] - col[pc], scale * (sig - label))
            for part in range(OUT_CH):
                for j in range(lanes // 128):
                    go_ref[j, pl.ds(4 * part + k, rows, stride=16), :] = grads[part][:, 128 * j : 128 * (j + 1)]
            term = jnp.maximum(logit, 0.0) + jnp.log1p(ex) - label * logit
            loss = loss + fold_lanes(e0[k] * e0[k] + e1[k] * e1[k] + spread[k] * spread[k] + term)

    sums_ref[...] = jnp.zeros_like(sums_ref)
    sums_ref[4:5, :] = jnp.sum(loss, axis=0, keepdims=True)
    head_ref[...] = jnp.zeros_like(head_ref)
    sg_ref[...] = jnp.zeros_like(sg_ref)
    d3_ref[...] = jnp.zeros_like(d3_ref)
    for k in (0, 1, rows + 2, rows + 3):
        g3_ref[256 * k : 256 * (k + 1), :] = jnp.zeros((256, lanes), bf16)

    sg_sum[...] = jnp.zeros_like(sg_sum)
    go_sum[...] = jnp.zeros_like(go_sum)

    def down(ks):
        both = [dot(wd3_ref[...], rows_of(g3_ref, k * 256 + 128, 512)) for k in ks]
        return [b[0:64] + b[64:128] for b in both]

    def backward(rs, ready=()):
        coarse = down(ready)
        gos = [get_lanes(go_ref, r * 16, 16).astype(bf16) for r in rs]
        gts = [dot(wht_ref[...], go) for go in gos]
        head, gsum, sums, kept = 0.0, 0.0, [0.0] * crops, []
        for r, go, gt in zip(rs, gos, gts):
            spot = (r + 1) * 128
            head = head + dot_nt(rows_of(h3_ref, spot, 128), go)
            gsum = gsum + fold_lanes(go.astype(f32))
            gt = gt.astype(bf16)
            gb = jnp.where(rows_of(m_ref, spot, 128) > 0, gt, jnp.zeros_like(gt))
            g = gb.astype(f32)
            kept.append(gt)
            for c in range(crops):
                sums[c] = sums[c] + fold_lanes(g[:, width * c : width * (c + 1)])
            parts = []
            for pr in range(2):
                even, odd = g[64 * pr : 64 * pr + 32], g[64 * pr + 32 : 64 * pr + 64]
                parts += [
                    from_left(odd, crops).astype(bf16),
                    gb[64 * pr : 64 * pr + 64],
                    from_right(even, crops).astype(bf16),
                ]
            put_rows(g3_ref, (r + 2) * 256, jnp.concatenate(parts, axis=0))
        for r, gt in zip(rs, kept):
            put_rows(h3_ref, (r + 1) * 128, gt)
        for k, b in zip(ready, coarse):
            put_rows(gc_ref, k * 64, b)
        head_ref[...] += head
        go_sum[...] += gsum
        for c in range(crops):
            sg_sum[c] += sums[c]

    backward(range(BACK))
    repeat_rows(rows - BACK, BACK, lambda rs: backward(rs, [r - BACK for r in rs]), BACK)
    for c in range(crops):
        sg_ref[c : c + 1, :] = lane_sums(sg_sum[c])[0:1]
    sums_ref[3:4, 0:16] = lane_sums(go_sum[...])[0:1]
    sg_copies = share(tiles, "tile", sg_ref, sg_got, s2_send, s2_recv)
    rest = list(range(rows - BACK, rows + 2))
    for k, b in zip(rest, down(rest)):
        put_rows(gc_ref, k * 64, b)

    rim_lo[...] = gc_ref[0:128, :].astype(bf16)
    rim_hi[...] = gc_ref[64 * rows : 64 * rows + 128, :].astype(bf16)
    finish_rims = swap_edges(tiles, [(rim_lo, rim_hi, rim_up, rim_dn)], rim_send, rim_recv)

    def weights_three(ks):
        d3 = 0.0
        for k in ks:
            gs = [rows_of(g3_ref, k * 256 + 128 * j + 160, 64) for j in range(4)]
            d3 = d3 + dot_nt(jnp.concatenate(gs, axis=0), rows_of(x3_ref, (k + 1) * 192, 192))
        d3_ref[...] += d3

    repeat_rows(rows + 2, 6, weights_three)
    for tap in range(9):
        a, b = tap // 3, tap % 3
        total = jnp.zeros((CH_ONE, CH_TWO), f32)
        for first in (2 - a, 3 - a):
            for pc in range(2):
                s = (pc + b + 1) // 2
                total = total + d3_ref[64 * first + 32 * pc : 64 * first + 32 * pc + 32, 64 * s : 64 * (s + 1)]
        if tap < 8:
            pay_a[32 * (tap // 2) : 32 * (tap // 2 + 1), 64 * (tap % 2) : 64 * (tap % 2 + 1)] = total
        else:
            pay_a[128:144, :] = jnp.concatenate([total[0:16], total[16:32]], axis=1)
    outer = jnp.zeros((CH_ONE, 128), f32)
    for c in range(crops):
        outer = outer + as_column(over_phases(sg_ref[c : c + 1, :]))[0:32] * jnp.concatenate([unit[c : c + 1]] * 2, axis=1)
        sums_ref[2:3, :] += sg_ref[c : c + 1, :]
    head = jnp.concatenate([head_ref[...], jnp.zeros((128, 112), f32)], axis=1)
    pay_a[144:160, :] = jnp.transpose(head)[0:16]
    pay_a[160:176, :] = jnp.concatenate([outer[0:16, 0:64], outer[16:32, 0:64]], axis=1)
    pay_a[176:184, :] = sums_ref[...]
    if pay_a.shape[0] > 184:
        pay_a[184:, :] = jnp.zeros((pay_a.shape[0] - 184, 128), f32)
    reduce_a.scatter()

    wait_all(sg_copies)
    style_grad = over_phases(in_order(sg_got, tiles))[:, 0:32]
    grad_unit = jnp.dot(style_grad, ws_ref[...], precision=highest, preferred_element_type=f32)
    mixed = jnp.mean(style_raw * grad_unit, axis=1, keepdims=True)
    grad_raw = style_inv * grad_unit - style_inv * style_inv * style_inv * style_raw * mixed
    grad_raw = jnp.concatenate([grad_raw / coarse_count] * 2, axis=1)
    raw = [as_column(grad_raw[c : c + 1])[0:64] for c in range(crops)]
    d2_ref[...] = jnp.zeros_like(d2_ref)
    d1_ref[...] = jnp.zeros_like(d1_ref)
    g2_sum[...] = jnp.zeros_like(g2_sum)
    raw = jnp.concatenate([wide(v, width) for v in raw], axis=1)
    g2_ref = g3_ref

    def masked(ks, extras=None):
        sums, d2 = 0.0, 0.0
        for j, k in enumerate(ks):
            coarse = rows_of(gc_ref, k * 64, 64)
            if extras is not None:
                coarse = coarse + extras[j]
            grad = (coarse + raw).astype(bf16)
            gb = jnp.where(rows_of(x3_ref, (k + 1) * 192 + 64, 64) > 0, grad, jnp.zeros_like(grad))
            g = gb.astype(f32)
            if extras is None or 0 < j < 3:
                sums = sums + fold_lanes(g)
                d2 = d2 + dot_nt(rows_of(x2_ref, (k + 1) * 96, 288), gb)
            put_rows(g2_ref, k * 192, three_columns(gb, g, crops))
        g2_sum[...] += sums
        d2_ref[...] += d2

    repeat_rows(rows - 2, 14, masked, 2)
    finish_rims()
    up = jnp.where(edge[0] < 0, rim_up[...].astype(f32), 0.0)
    dn = jnp.where(edge[1] > rows, rim_dn[...].astype(f32), 0.0)
    masked([0, 1, rows, rows + 1], [up[0:64], up[64:128], dn[0:64], dn[64:128]])
    pay_b[...] = jnp.zeros_like(pay_b)

    pay_b[160:161, 0:64] = lane_sums(g2_sum[...])[0:1]

    rest = jnp.concatenate([d2_ref[160:288, :], jnp.zeros((32, 64), f32)], axis=0)
    pay_b[0:160, :] = jnp.concatenate([d2_ref[0:160, :], rest], axis=1)
    reduce_b.scatter()
    reduce_a.across()

    def last_back(rs):
        gps = [dot(wd2_ref[...], rows_of(g2_ref, r * 192, 576)) for r in rs]
        d1 = 0.0
        for r, gp in zip(rs, gps):
            gp = 0.25 * gp.astype(bf16).astype(f32)
            gt = rows_of(h3_ref, (r + 1) * 128, 128).astype(f32)
            g1 = (jnp.concatenate([gp] * 4, axis=0) + gt).astype(bf16)
            gb = jnp.where(rows_of(h1_ref, (r + 3) * 128, 128) > 0, g1, jnp.zeros_like(g1))
            d1 = d1 + dot_nt(gb, jnp.concatenate([rows_of(y_ref, (r + 3) * 16, 32), ones_ref[...]], axis=0))
        d1_ref[...] += d1

    quarter = rows // 4
    repeat_rows(rows // 2, 4, last_back)
    reduce_a.gather(full_a)
    repeat_rows(quarter, 4, last_back, rows // 2)
    reduce_b.across()
    repeat_rows(rows - rows // 2 - quarter, 4, last_back, rows // 2 + quarter)
    d1 = jnp.transpose(jnp.concatenate([d1_ref[...], jnp.zeros((128, 80), f32)], axis=1))
    total = jnp.zeros((32, 128), f32)
    for p in range(4):
        total = total + turn(turn(d1[0:32], -32 * p, 1), -(8 * (p // 2) + p % 2), 0)
    packed = lane_group(total[0:8], 0)
    for k in range(1, 3):
        packed = packed + turn(lane_group(total[8 * k : 8 * (k + 1)], 0), 32 * k, 1)
    pay_c[...] = packed + lane_group(jnp.broadcast_to(over_phases(d1[32:33]), (8, 128)), 3)
    copies = share(tiles, "tile", pay_c, got_c, sems[12], sems[13])
    reduce_b.gather(full_b)
    wait_all(copies)
    own_c[...] = in_order(got_c, tiles)
    copies = share(images, "img", own_c, met_c, sems[14], sems[15])
    reduce_a.finish()
    size_a, size_b = full_a.shape[0], full_b.shape[0]
    o_ref[0:size_a, :] = full_a[...]
    reduce_b.finish()
    o_ref[size_a : size_a + size_b, :] = full_b[...]
    wait_all(copies)
    o_ref[size_a + size_b :, :] = in_order(met_c, images)


def update_kernel(pixel_count, second_at, third_at, count_ref, sum_ref, *refs):
    olds, outs, loss_ref = refs[:18], refs[18:36], refs[36]
    rate = 1.0 / (jnp.zeros((8, 128), f32) + (count_ref[0].astype(f32) + 1.0))

    def step(index, spot, grad):
        weight, momentum, average = (olds[3 * index + k][spot] for k in range(3))
        decayed = grad + decay_rate * weight
        momentum = momentum_rate * momentum + decayed
        new = weight - learn_rate * (decayed + momentum_rate * momentum)
        outs[3 * index][spot] = new
        outs[3 * index + 1][spot] = momentum
        outs[3 * index + 2][spot] = average + (new - average) * rate[0:1, 0:1]

    first = sum_ref[third_at : third_at + 8, :]
    for a in range(3):
        for b in range(3):
            for i in range(2):
                grad = first[4 * i + b : 4 * i + b + 1, 32 * a : 32 * (a + 1)]
                step(0, (a, b, slice(i, i + 1), slice(None)), grad)
    for tap in range(9):
        a, b = tap // 3, tap % 3
        first = second_at + 32 * (tap % 5)
        half = 64 * (tap // 5)
        step(1, (a, b), sum_ref[first : first + 32, half : half + 64])
        if tap < 8:
            first = 32 * (tap // 2)
            lane = 64 * (tap % 2)
            grad = sum_ref[first : first + 32, lane : lane + 64]
        else:
            first = 128
            grad = jnp.concatenate([sum_ref[first : first + 16, 64 * k : 64 * (k + 1)] for k in range(2)], axis=0)
        step(2, (a, b), grad)
    first = 160
    grad = jnp.concatenate([sum_ref[first : first + 16, 64 * k : 64 * (k + 1)] for k in range(2)], axis=0)
    step(3, (slice(None), slice(None)), grad)
    head = sum_ref[144:160, :]
    total = jnp.zeros((16, 128), f32)
    for p in range(4):
        total = total + turn(turn(head, -32 * p, 1), -p, 0)
    total = jnp.concatenate([total[4 * o : 4 * o + 1] for o in range(OUT_CH)], axis=0)
    step(4, (slice(None), slice(None)), total[:, 0:32])
    sums = sum_ref[176:184, :]
    one = turn(sum_ref[third_at : third_at + 1, :], -96, 1)
    two = jnp.sum(sum_ref[second_at + 160 : second_at + 168, :], axis=0, keepdims=True)
    three = over_phases(sums[2:3])
    lane = lax.broadcasted_iota(jnp.int32, (1, 128), 1)
    low = jnp.where(lane < 32, one, jnp.where(lane < 96, turn(two, 32, 1), three))
    ends = sums[3:4]
    ends = (ends + turn(ends, -1, 1)) + (turn(ends, -2, 1) + turn(ends, -3, 1))
    high = jnp.where(lane < 32, three, 0.0)
    for o in range(OUT_CH):
        high = jnp.where(lane == 32 + o, turn(ends, 32 + o - 4 * o, 1), high)
    grad = jnp.concatenate([low, high], axis=1)[:, 0 : olds[15].shape[0]]
    weight, momentum, average = (olds[15 + k][...].reshape(1, -1) for k in range(3))
    decayed = grad + decay_rate * weight
    momentum = momentum_rate * momentum + decayed
    new = weight - learn_rate * (decayed + momentum_rate * momentum)
    average = average + (new - average) * rate[0:1, 0:1]
    for k, value in enumerate((new, momentum, average)):
        outs[15 + k][...] = value.reshape(-1)
    loss_ref[0] = jnp.sum(sums[4:5]) / pixel_count


def on_device(
    images, nucleus, target_flow, cell_label, step_count,
    conv1_weight, conv1_momentum, conv1_average,
    conv2_weight, conv2_momentum, conv2_average,
    conv3_weight, conv3_momentum, conv3_average,
    style_weight, style_momentum, style_average,
    head_weight, head_momentum, head_average,
    biases, bias_momentum, bias_average,
):
    tiles = lax.axis_size("tile")
    crops, _, height, cols = images.shape
    rows, width = height // 2, cols // 2
    pixel_count = lax.axis_size("img") * tiles * crops * height * cols
    grad_scale = 1.0 / math.sqrt(pixel_count)
    coarse_count = tiles * rows * width

    def sds(shape, dtype=f32):
        return jax.ShapeDtypeStruct(shape, dtype)

    lanes = crops * width
    images_count = lax.axis_size("img")

    def other_way(w):
        return jnp.swapaxes(w, -1, -2)

    third = tuple(other_way(w) for w in (conv3_weight, conv3_momentum, conv3_average))
    style = tuple(other_way(w) for w in (style_weight, style_momentum, style_average))
    head = tuple(other_way(w) for w in (head_weight, head_momentum, head_average))

    edge = (crops, 2, HALO, cols)
    rim = (128, lanes)
    parts = [8 * pl.cdiv(sum(block), 8 * tiles) for block in BLOCK_ROWS[:2]]
    small = sum(BLOCK_ROWS[2])

    def buf(shape, dtype=bf16):
        return pltpu.VMEM(shape, dtype)

    def block_bufs(part):
        return [
            buf((part * tiles, 128), f32), buf((tiles, part, 128), f32), buf((part, 128), f32),
            buf((images_count, part, 128), f32), buf((part * tiles, 128), f32),
        ]

    sources = (
        images, target_flow, cell_label, conv1_weight, conv2_weight, third[0], head[0], biases, style[0],
    )
    block_sems = [DMA((tiles,)), DMA((tiles,)), DMA((images_count,)), DMA((images_count,)), DMA((tiles,)), DMA((tiles,))]
    summed = pl.pallas_call(
        lambda *refs: step_kernel(tiles, images_count, grad_scale, float(coarse_count), *refs),
        out_shape=pltpu.VMEM((sum(parts) * tiles + small, 128), f32),
        in_specs=[SMEM] + [HBM] * 9,
        out_specs=VMEM,
        scratch_shapes=[buf(v.shape, v.dtype) for v in sources]
        + [
            buf(edge), buf(edge), buf(edge, jnp.int32), buf(edge, jnp.int32),
            buf((128, 48)), buf((CH_TWO, 9 * CH_ONE + 16)), buf((128, 14 * CH_TWO + 16)), buf((128, 16 * CH_ONE)),
            buf((CH_ONE, 9 * CH_TWO)), buf((16, 128)), buf((128, 16)),
            buf((8, 128), f32), buf((16, 128), f32), buf((32, 128), f32), buf((16, lanes)), buf((16, lanes)),
            buf((16 * (rows + 7), lanes)), buf((lanes // 128, 16 * (rows + 2), 128), f32),
            buf((128 * (rows + 6), lanes)), buf((96 * (rows + 6), lanes)), buf((192 * (rows + 4), lanes)),
            buf((128 * (rows + 2), lanes)), buf((128 * (rows + 2), lanes)),
            buf((lanes // 128, 16 * (rows + 2), 128), f32), buf((lanes // 128, 16 * rows, 128), f32),
            buf((256 * (rows + 4), lanes)), buf((64 * (rows + 2), lanes), f32),
            buf(rim), buf(rim), buf(rim), buf(rim),
            buf((8, 128), f32), buf((tiles, 8, 128), f32), buf((8, 128), f32), buf((tiles, 8, 128), f32),
            buf((128, 16), f32), buf((8, 128), f32),
            buf((256, 3 * CH_TWO), f32), buf((9 * CH_ONE, CH_TWO), f32), buf((128, 48), f32),
            buf((crops, CH_TWO, 128), f32), buf((crops, 128, 128), f32), buf((16, 128), f32), buf((CH_TWO, 128), f32),
        ]
        + block_bufs(parts[0])
        + block_bufs(parts[1])
        + [buf((small, 128), f32), buf((tiles, small, 128), f32), buf((small, 128), f32), buf((images_count, small, 128), f32)]
        + [DMA((9,)), DMA((2,)), DMA((2,)), DMA((2,)), DMA((2,)), DMA((tiles,)), DMA((tiles,)), DMA((tiles,)), DMA((tiles,)), DMA((2,)), DMA((2,))]
        + block_sems * 2
        + [DMA((tiles,)), DMA((tiles,)), DMA((images_count,)), DMA((images_count,))],
        compiler_params=pltpu.CompilerParams(collective_id=1, has_side_effects=True, vmem_limit_bytes=60 * 2**20),
        name="step",
    )(nucleus, *sources)

    olds = (
        (conv1_weight, conv1_momentum, conv1_average)
        + (conv2_weight, conv2_momentum, conv2_average)
        + third + style + head
        + (biases, bias_momentum, bias_average)
    )
    news = pl.pallas_call(
        lambda *refs: update_kernel(float(pixel_count), parts[0] * tiles, sum(parts) * tiles, *refs),
        out_shape=tuple(sds(v.shape) for v in olds) + (sds((1,)),),
        in_specs=[SMEM] + [VMEM] * 19,
        out_specs=[VMEM] * 18 + [SMEM],
        compiler_params=pltpu.CompilerParams(vmem_limit_bytes=16 * 2**20),
        name="update",
    )(step_count, summed, *olds)
    return (news[18], *news[0:6], *(other_way(w) for w in news[6:15]), *news[15:18])


def solution(mesh):
    return jax.shard_map(
        on_device,
        mesh=mesh,
        in_specs=(
            P("img", None, "tile", None),
            P("img"),
            P("img", None, "tile", None),
            P("img", "tile", None),
        )
        + (P(),) * 19,
        out_specs=(P(),) * 19,
        check_vma=False,
    )
```
